32 devices in a mesh: dp: 8 (over z, core), seq: 4 (over y, x).
Axes of the slice: x: 2, y: 2, z: 4, core: 2. Of those that a mesh axis runs over, the one named last changes fastest.
Arguments:
- tokens: bfloat16 [32, 1024, 768], P('dp', 'seq'), may hold values from -6 to 6
- cotangent: bfloat16 [32, 1024, 768], P('dp', 'seq'), may hold values from -6 to 6
- segment_ids: int32 [32, 1024], P('dp'), may hold values from 0 to 5, never falling along the last dimension, each value on 1 to 512 neighbouring positions
- w_qkv: float32 [768, 2304], P(('dp', 'seq')), may hold values from -0.21875 to 0.21875
- m_qkv: float32 [768, 2304], P(('dp', 'seq')), may hold values from -160 to 160
- v_qkv: float32 [768, 2304], P(('dp', 'seq')), may hold values from 65.536 to 262.144
- w_out: float32 [768, 768], P(('dp', 'seq')), may hold values from -1.25 to 1.25
- m_out: float32 [768, 768], P(('dp', 'seq')), may hold values from -40 to 40
- v_out: float32 [768, 768], P(('dp', 'seq')), may hold values from 3.2768 to 13.1072
- w_up: float32 [768, 3072], P(('dp', 'seq')), may hold values from -0.21875 to 0.21875
- m_up: float32 [768, 3072], P(('dp', 'seq')), may hold values from -40 to 40
- v_up: float32 [768, 3072], P(('dp', 'seq')), may hold values from 3.2768 to 13.1072
- w_down: float32 [3072, 768], P(('dp', 'seq')), may hold values from -0.109375 to 0.109375
- m_down: float32 [3072, 768], P(('dp', 'seq')), may hold values from -64 to 64
- v_down: float32 [3072, 768], P(('dp', 'seq')), may hold values from 11.79648 to 47.18592
- vectors: float32 [8, 768], P(None, ('dp', 'seq')), may hold values from -1.2 to 1.8
- m_vectors: float32 [8, 768], P(None, ('dp', 'seq')), may hold values from -160 to 160
- v_vectors: float32 [8, 768], P(None, ('dp', 'seq')), may hold values from 65.536 to 262.144
- up_bias: float32 [3072], P(('dp', 'seq')), may hold values from -1.75 to 1.75
- m_up_bias: float32 [3072], P(('dp', 'seq')), may hold values from -40 to 40
- v_up_bias: float32 [3072], P(('dp', 'seq')), may hold values from 3.2768 to 13.1072
Outputs:
- mixed: bfloat16 [32, 1024, 768], P('dp', 'seq')
- input_grad: float32 [32, 1024, 768], P('dp', 'seq')
- grad_qkv: float32 [768, 2304], P(('dp', 'seq'))
- grad_out: float32 [768, 768], P(('dp', 'seq'))
- grad_up: float32 [768, 3072], P(('dp', 'seq'))
- grad_down: float32 [3072, 768], P(('dp', 'seq'))
- grad_vectors: float32 [8, 768], P(None, ('dp', 'seq'))
- grad_up_bias: float32 [3072], P(('dp', 'seq'))
- first_qkv: float32 [768, 2304], P(('dp', 'seq'))
- first_out: float32 [768, 768], P(('dp', 'seq'))
- first_up: float32 [768, 3072], P(('dp', 'seq'))
- first_down: float32 [3072, 768], P(('dp', 'seq'))
- first_vectors: float32 [8, 768], P(None, ('dp', 'seq'))
- first_up_bias: float32 [3072], P(('dp', 'seq'))
- second_qkv: float32 [768, 2304], P(('dp', 'seq'))
- second_out: float32 [768, 768], P(('dp', 'seq'))
- second_up: float32 [768, 3072], P(('dp', 'seq'))
- second_down: float32 [3072, 768], P(('dp', 'seq'))
- second_vectors: float32 [8, 768], P(None, ('dp', 'seq'))
- second_up_bias: float32 [3072], P(('dp', 'seq'))
- new_qkv: float32 [768, 2304], P(('dp', 'seq'))
- new_out: float32 [768, 768], P(('dp', 'seq'))
- new_up: float32 [768, 3072], P(('dp', 'seq'))
- new_down: float32 [3072, 768], P(('dp', 'seq'))
- new_vectors: float32 [8, 768], P(None, ('dp', 'seq'))
- new_up_bias: float32 [3072], P(('dp', 'seq'))
- copy_qkv: bfloat16 [768, 2304], P(('dp', 'seq'))
- copy_out: bfloat16 [768, 768], P(('dp', 'seq'))
- copy_up: bfloat16 [768, 3072], P(('dp', 'seq'))
- copy_down: bfloat16 [3072, 768], P(('dp', 'seq'))
The draws below stay inside these ranges and needn't reach their ends.
Inputs may be any that keep to these rules, and one draw needn't show every extreme that they name: `segment_ids`: within each row of 1024 positions the ids never fall; no document has more than 512 positions.
All inputs are finite; a program needn't handle non-finite values.
Results may differ from the reference program's by a relative error of at most 0.012.
The reference program's roundings to bfloat16 on the way count: a program that leaves them out, or rounds other values in their place, can miss the bound.
Values may be sent and summed in bfloat16 or wider, within the bound.
A program may use at most 384 MiB of HBM per device.

```python
import math
import jax
import jax.numpy as jnp
import numpy as np
from jax import lax

D = 768
HEADS = 12
HEAD_DIM = 64
FF = 3072
LENGTH = 1024
ROWS = 32
TOKENS = 32768


def draw_vectors(key, part):
    noise = jnp.clip(jax.random.normal(key, (8, D), jnp.float32), -4.0, 4.0)
    places = jnp.arange(8)
    gain_rows = (places == 0) | (places == 2)
    center = jnp.where(gain_rows, 1.0, 0.0)[:, None]
    spread = jnp.where(gain_rows, 0.2, 0.3)[:, None]
    return (center + spread * noise).astype(jnp.float32)


def steps_of(key, shape, pieces, smallest, top_value):
    level, own = 1.0, jax.random.fold_in(key, 6)
    for axis_at, blocks in pieces:
        draws = jnp.exp(jax.random.uniform(jax.random.fold_in(own, axis_at), (blocks,), jnp.float32, smallest / len(pieces), top_value / len(pieces)))
        level = level * jnp.repeat(draws, shape[axis_at] // blocks).reshape([-1 if axis == axis_at else 1 for axis in range(len(shape))])
    return level


def profile(amount, total, most, slope):
    portions = [(1 << 20) // math.isqrt(standing ** slope) + 1 for standing in range(2, amount + 1)]
    spare, given = total - most - (amount - 1), [1] * (amount - 1)
    while spare > 0:
        candidates = [i for i in range(amount - 1) if given[i] < most]
        mass, budget = sum([portions[i] for i in candidates]), spare
        for i in candidates:
            addition = min(most - given[i], max(1, budget * portions[i] // mass), spare)
            given[i] = given[i] + addition
            spare = spare - addition
    return np.array([most] + given)


def uneven(stream_key, amount, total, reach, lean):
    if amount == 2:
        one = jax.random.randint(stream_key, (), max(1, total - reach), min(reach, total - 1) + 1)
        return jnp.stack([one, total - one])
    lengths = jnp.asarray(profile(amount, total, reach, lean), jnp.int32)
    twos = (amount - 1) // 2
    giver, receiver = lengths[1:1 + 2 * twos:2], lengths[2:2 + 2 * twos:2]
    room = jnp.minimum(giver - 1, reach - receiver)
    shifted = jax.random.randint(jax.random.fold_in(stream_key, 1), (twos,), 0, 1 << 20) % (room + 1)
    lengths = lengths.at[1:1 + 2 * twos:2].set(giver - shifted).at[2:2 + 2 * twos:2].set(receiver + shifted)
    return lengths[jax.random.permutation(jax.random.fold_in(stream_key, 2), amount)]


def centred(key, shape, scale, most, shards=(), held_as=jnp.bfloat16):
    entries = jax.random.normal(key, shape, jnp.float32) * scale
    if len(shards) > 0:
        entries = steps_of(key, shape, shards, -0.22, 0.18) * entries
    return jnp.clip(entries, min=-most, max=most).astype(held_as)


def setup_inputs(seed: int = 0) -> dict:
    key_of = jax.random.split(jax.random.key(seed), 22)
    return {
        "tokens": centred(key_of[0], (ROWS, LENGTH, D), 1.0, 6.0, ((0, 8), (1, 4))),
        "cotangent": centred(key_of[1], (ROWS, LENGTH, D), 1.0, 6.0, ((0, 8), (1, 4))),
        "segment_ids": jax.vmap(lambda own: jnp.searchsorted(jnp.cumsum(uneven(own, 6, LENGTH, LENGTH // 2, 2)), jnp.arange(LENGTH), side="right"))(jax.random.split(key_of[2], ROWS)).reshape((ROWS, LENGTH)).astype(jnp.int32),
        "w_qkv": centred(key_of[3], (D, 3 * D), D ** -0.5, 0.21875, ((0, 32),), jnp.float32),
        "m_qkv": centred(key_of[4], (D, 3 * D), (0.16 * TOKENS ** 0.5), 160.0, ((0, 32),), jnp.float32),
        "v_qkv": jnp.clip(jnp.exp(math.log(262.144) - 1.3862944 * jax.random.uniform(key_of[5], (D, 3 * D), jnp.float32) ** steps_of(key_of[5], (D, 3 * D), ((0, 32),), -0.2, 0.2)), 65.536, 262.144),
        "w_out": centred(key_of[6], (D, D), (D // 32) ** -0.5, 1.25, ((0, 32),), jnp.float32),
        "m_out": centred(key_of[7], (D, D), (0.035 * TOKENS ** 0.5), 40.0, ((0, 32),), jnp.float32),
        "v_out": jnp.clip(jnp.exp(math.log(13.1072) - 1.3862944 * jax.random.uniform(key_of[8], (D, D), jnp.float32) ** steps_of(key_of[8], (D, D), ((0, 32),), -0.2, 0.2)), 3.2768, 13.1072),
        "w_up": centred(key_of[9], (D, FF), D ** -0.5, 0.21875, ((0, 32),), jnp.float32),
        "m_up": centred(key_of[10], (D, FF), (0.035 * TOKENS ** 0.5), 40.0, ((0, 32),), jnp.float32),
        "v_up": jnp.clip(jnp.exp(math.log(13.1072) - 1.3862944 * jax.random.uniform(key_of[11], (D, FF), jnp.float32) ** steps_of(key_of[11], (D, FF), ((0, 32),), -0.2, 0.2)), 3.2768, 13.1072),
        "w_down": centred(key_of[12], (FF, D), FF ** -0.5, 0.109375, ((0, 32),), jnp.float32),
        "m_down": centred(key_of[13], (FF, D), (0.066 * TOKENS ** 0.5), 64.0, ((0, 32),), jnp.float32),
        "v_down": jnp.clip(jnp.exp(math.log(47.18592) - 1.3862944 * jax.random.uniform(key_of[14], (FF, D), jnp.float32) ** steps_of(key_of[14], (FF, D), ((0, 32),), -0.2, 0.2)), 11.79648, 47.18592),
        "vectors": draw_vectors(jax.random.fold_in(key_of[21], 71), 0),
        "m_vectors": centred(key_of[16], (8, D), (0.16 * TOKENS ** 0.5), 160.0, ((1, 32),), jnp.float32),
        "v_vectors": jnp.clip(jnp.exp(math.log(262.144) - 1.3862944 * jax.random.uniform(key_of[17], (8, D), jnp.float32) ** steps_of(key_of[17], (8, D), ((1, 32),), -0.2, 0.2)), 65.536, 262.144),
        "up_bias": centred(key_of[18], (FF,), 0.3, 1.75, ((0, 32),), jnp.float32),
        "m_up_bias": centred(key_of[19], (FF,), (0.035 * TOKENS ** 0.5), 40.0, ((0, 32),), jnp.float32),
        "v_up_bias": jnp.clip(jnp.exp(math.log(13.1072) - 1.3862944 * jax.random.uniform(key_of[20], (FF,), jnp.float32) ** steps_of(key_of[20], (FF,), ((0, 32),), -0.2, 0.2)), 3.2768, 13.1072),
    }


BETA_ONE = 0.9
BETA_TWO = 0.999
ADAM_EPS = 1e-06
DECAY_RATE = 0.01
LEARN_RATE = 0.4
NORM_EPS = 1e-05
STEP_NUMBER = 10.0
top_precision = lax.Precision.HIGHEST

@jax.custom_vjp
def low(v):
    return lax.optimization_barrier(v.astype(jnp.bfloat16)).astype(jnp.float32)

@jax.custom_vjp
def low_back(v):
    return v

def low_keep(v):
    return (low(v), None)

def low_pass(kept, grad):
    return (grad,)

def back_keep(v):
    return (v, None)

def back_low(kept, grad):
    return (low(grad),)
low.defvjp(low_keep, low_pass)
low_back.defvjp(back_keep, back_low)

def layer_norm(values, norm_gain, norm_shift):
    center = values - lax.optimization_barrier(jnp.mean(values, axis=-1, keepdims=True))
    spread = lax.optimization_barrier(jnp.mean(center * center, axis=-1, keepdims=True))
    return center * lax.rsqrt(spread + NORM_EPS) * norm_gain + norm_shift

def matmul(left_side, right_side):
    return jnp.dot(left_side, right_side, precision=top_precision, preferred_element_type=jnp.float32)

def attend_row(queries, key_rows, value_rows, segments):
    seq_length = queries.shape[0]
    raw_scores = jnp.einsum('qhd,khd->hqk', queries, key_rows, precision=top_precision) * HEAD_DIM ** (-0.5)
    places = lax.iota(jnp.int32, seq_length)
    allowed = (segments[:, None] == segments[None, :]) & (places[None, :] <= places[:, None])
    scores = jnp.where(allowed[None], low_back(raw_scores), -1000000000.0)
    attn_probs = jax.nn.softmax(scores, axis=-1)
    return jnp.einsum('hqk,khd->qhd', low(attn_probs), value_rows, precision=top_precision)
checked_attend = jax.checkpoint(attend_row)

def attend_parts(parts):
    return checked_attend(parts[0], parts[1], parts[2], parts[3])

def forward(params, inputs, segments):
    w_qkv, w_out, w_up, w_down, vectors, up_bias = [low(tensor) for tensor in params]
    groups, seq_length, _ = inputs.shape
    flat = inputs.reshape(groups * seq_length, D)
    normed_one = low(layer_norm(flat, vectors[0], vectors[1]))
    projected = matmul(normed_one, w_qkv)
    queries = low_back(low(projected[:, :D] + vectors[4]))
    key_rows = low_back(low(projected[:, D:2 * D]))
    value_rows = low_back(low(projected[:, 2 * D:] + vectors[5]))
    head_shape = (groups, seq_length, HEADS, HEAD_DIM)
    context = lax.map(attend_parts, (queries.reshape(head_shape), key_rows.reshape(head_shape), value_rows.reshape(head_shape), segments))
    context = low_back(low(context.reshape(groups * seq_length, D)))
    attended = low_back(matmul(context, w_out) + vectors[6])
    resid_one = flat + attended
    normed_two = low(layer_norm(resid_one, vectors[2], vectors[3]))
    hidden_pre = low_back(matmul(normed_two, w_up) + up_bias)
    activated = low(jax.nn.gelu(hidden_pre, approximate=True))
    result = resid_one + matmul(activated, w_down) + vectors[7]
    return result.reshape(groups, seq_length, D)

def lamb_update(weight, first, second, grad, decay, corr_one, corr_two, axis):
    first_new = BETA_ONE * first + (1.0 - BETA_ONE) * grad
    second_new = BETA_TWO * second + (1.0 - BETA_TWO) * grad * grad
    update = first_new / corr_one / (jnp.sqrt(second_new / corr_two) + ADAM_EPS) + decay * weight
    weight_norm = jnp.sqrt(lax.optimization_barrier(jnp.sum(weight * weight, axis=axis, keepdims=True)))
    update_norm = jnp.sqrt(lax.optimization_barrier(jnp.sum(update * update, axis=axis, keepdims=True)))
    new_weight = weight - LEARN_RATE * (weight_norm / (update_norm + ADAM_EPS)) * update
    return (first_new, second_new, new_weight)

def reference(tokens, cotangent, segment_ids, w_qkv, m_qkv, v_qkv, w_out, m_out, v_out, w_up, m_up, v_up, w_down, m_down, v_down, vectors, m_vectors, v_vectors, up_bias, m_up_bias, v_up_bias):
    params = (w_qkv, w_out, w_up, w_down, vectors, up_bias)
    group_rows = 4
    group_count = ROWS // group_rows
    inputs = tokens.reshape(group_count, group_rows, LENGTH, D)
    backs = cotangent.reshape(group_count, group_rows, LENGTH, D)
    segs = segment_ids.reshape(group_count, group_rows, LENGTH)

    def accumulate(totals, parts):
        token_block, back_block, segment_block = parts

        def run(param_set, input_block):
            return forward(param_set, input_block, segment_block)
        result, pull = jax.vjp(run, params, token_block.astype(jnp.float32))
        grad_params, grad_input = pull(back_block.astype(jnp.float32))
        totals = jax.tree.map(jnp.add, totals, grad_params)
        return (totals, (result.astype(jnp.bfloat16), grad_input))
    zero_grads = jax.tree.map(jnp.zeros_like, params)
    grads, (mixed, input_grad) = lax.scan(accumulate, zero_grads, (inputs, backs, segs))
    mixed = mixed.reshape(ROWS, LENGTH, D)
    input_grad = input_grad.reshape(ROWS, LENGTH, D)
    count_float = jnp.asarray(STEP_NUMBER, jnp.float32)
    corr_one = 1.0 - jnp.power(jnp.asarray(BETA_ONE, jnp.float32), count_float)
    corr_two = 1.0 - jnp.power(jnp.asarray(BETA_TWO, jnp.float32), count_float)
    firsts = (m_qkv, m_out, m_up, m_down, m_vectors, m_up_bias)
    seconds = (v_qkv, v_out, v_up, v_down, v_vectors, v_up_bias)
    decays = (DECAY_RATE, DECAY_RATE, DECAY_RATE, DECAY_RATE, 0.0, 0.0)
    axes_list = (None, None, None, None, 1, None)
    first_out = []
    second_out = []
    weight_out = []
    for tensor_index in range(6):
        first_new, second_new, new_weight = lamb_update(params[tensor_index], firsts[tensor_index], seconds[tensor_index], grads[tensor_index], decays[tensor_index], corr_one, corr_two, axes_list[tensor_index])
        first_out.append(first_new)
        second_out.append(second_new)
        weight_out.append(new_weight)
    return (mixed, input_grad, grads[0], grads[1], grads[2], grads[3], grads[4], grads[5], first_out[0], first_out[1], first_out[2], first_out[3], first_out[4], first_out[5], second_out[0], second_out[1], second_out[2], second_out[3], second_out[4], second_out[5], weight_out[0], weight_out[1], weight_out[2], weight_out[3], weight_out[4], weight_out[5], weight_out[0].astype(jnp.bfloat16), weight_out[1].astype(jnp.bfloat16), weight_out[2].astype(jnp.bfloat16), weight_out[3].astype(jnp.bfloat16))
```

```python
import jax
import jax.numpy as jnp
from jax import lax
from jax.experimental import pallas as pl
from jax.experimental.pallas import tpu as pltpu
from jax.sharding import PartitionSpec as P

HEADS = 12
HEAD_DIM = 64
LONGEST = 512
QUERY_BLOCK = 256


BETA_ONE = 0.9
BETA_TWO = 0.999
ADAM_EPS = 1e-06
DECAY_RATE = 0.01
LEARN_RATE = 0.4
NORM_EPS = 1e-05
STEP_NUMBER = 10.0

BRAIN = jnp.bfloat16
FLOAT = jnp.float32


def matmul(left_side, right_side):
    return jnp.dot(left_side, right_side, preferred_element_type=FLOAT)


def inner_rows(left_side, right_side):
    return lax.dot_general(
        left_side, right_side, (((0,), (0,)), ((), ())), preferred_element_type=FLOAT
    )


def times_transposed(left_side, right_side):
    return lax.dot_general(
        left_side, right_side, (((1,), (1,)), ((), ())), preferred_element_type=FLOAT
    )


def gelu_tanh(values):
    return jax.nn.gelu(values, approximate=True)


def norm_forward(values, norm_gain, norm_shift):
    center = values - jnp.mean(values, axis=-1, keepdims=True)
    inverse = lax.rsqrt(jnp.mean(center * center, axis=-1, keepdims=True) + NORM_EPS)
    normed = center * inverse
    return (normed * norm_gain + norm_shift, normed, inverse)


def norm_backward(upstream, normed, inverse, norm_gain):
    scaled = upstream * norm_gain
    centered = scaled - jnp.mean(scaled, axis=-1, keepdims=True)
    return inverse * (centered - normed * jnp.mean(scaled * normed, axis=-1, keepdims=True))


def windows(length):
    return [
        (max(0, first - LONGEST), first + QUERY_BLOCK) for first in range(0, length, QUERY_BLOCK)
    ]


def fill_bias(seg_col, seg_row, bias, length):
    place = 0
    for index, (low, high) in enumerate(windows(length)):
        first = index * QUERY_BLOCK
        size = high - low
        keys = seg_col[0, low:high, :]
        queries = seg_row[0, :, first : first + QUERY_BLOCK]
        key_place = low + lax.broadcasted_iota(jnp.int32, (size, QUERY_BLOCK), 0)
        query_place = first + lax.broadcasted_iota(jnp.int32, (size, QUERY_BLOCK), 1)
        allowed = (keys == queries) & (key_place <= query_place)
        bias[place : place + size, :] = jnp.where(allowed, 0.0, -1000000000.0)
        place += size


def split_heads(pair):
    lane = lax.broadcasted_iota(jnp.int32, pair.shape, 1)
    zero = jnp.zeros_like(pair)
    return (jnp.where(lane < HEAD_DIM, pair, zero), jnp.where(lane < HEAD_DIM, zero, pair))


def attend_forward(seg_col, seg_row, q_ref, k_ref, v_ref, c_ref, lse_ref, bias):
    length = q_ref.shape[0]

    @pl.when(pl.program_id(1) == 0)
    def _():
        fill_bias(seg_col, seg_row, bias, length)

    v_turned = v_ref[...].T
    place = 0
    for index, (low, high) in enumerate(windows(length)):
        first = index * QUERY_BLOCK
        size = high - low
        queries = split_heads(q_ref[first : first + QUERY_BLOCK, :] * HEAD_DIM ** (-0.5))
        keys = k_ref[low:high, :]
        blocked = bias[place : place + size, :]
        parts = []
        for head in range(2):
            scores = times_transposed(keys, queries[head]) + blocked
            peak = jnp.max(scores, axis=0, keepdims=True)
            probs = jnp.exp(scores - peak)
            total = jnp.sum(probs, axis=0, keepdims=True)
            probs = (probs * (1.0 / total)).astype(BRAIN)
            lse_ref[0, 0, head : head + 1, first : first + QUERY_BLOCK] = peak + jnp.log(total)
            turned = v_turned[head * HEAD_DIM : (head + 1) * HEAD_DIM, low:high]
            parts.append(matmul(turned, probs))
        context = jnp.concatenate(parts, axis=0).T
        c_ref[first : first + QUERY_BLOCK, :] = context.astype(BRAIN)
        place += size


def attend_backward(
    seg_col, seg_row, q_ref, k_ref, v_ref, g_ref, lse_ref, out_ref, bias, key_sum, value_sum
):
    length = q_ref.shape[0]
    pair = pl.program_id(1)

    @pl.when(pair == 0)
    def _():
        fill_bias(seg_col, seg_row, bias, length)

    key_sum[...] = jnp.zeros_like(key_sum)
    value_sum[...] = jnp.zeros_like(value_sum)
    width = HEADS * HEAD_DIM
    k_turned = k_ref[...].T
    lanes = 2 * HEAD_DIM
    column = pl.multiple_of(pair * lanes, lanes)
    place = 0
    for index, (low, high) in enumerate(windows(length)):
        first = index * QUERY_BLOCK
        size = high - low
        rows = slice(first, first + QUERY_BLOCK)
        queries = split_heads(q_ref[rows, :] * HEAD_DIM ** (-0.5))
        grads = split_heads(g_ref[rows, :])
        keys = k_ref[low:high, :]
        values = v_ref[low:high, :]
        blocked = bias[place : place + size, :]
        all_probs = []
        all_scores = []
        parts = []
        for head in range(2):
            scores = times_transposed(keys, queries[head]) + blocked
            probs = jnp.exp(scores - lse_ref[0, 0, head : head + 1, rows])
            prob_grad = times_transposed(values, grads[head])
            row_dot = jnp.sum(probs * prob_grad, axis=0, keepdims=True)
            score_grad = (probs * (prob_grad - row_dot)).astype(BRAIN)
            all_probs.append(probs.astype(BRAIN))
            all_scores.append(score_grad)
            turned = k_turned[head * HEAD_DIM : (head + 1) * HEAD_DIM, low:high]
            parts.append(matmul(turned, score_grad))
        query_grad = jnp.concatenate(parts, axis=0).T * HEAD_DIM ** (-0.5)
        out_ref[rows, pl.ds(column, lanes)] = query_grad.astype(BRAIN)
        value_sum[low:high, :] += matmul(
            jnp.concatenate(all_probs, axis=1), jnp.concatenate(grads, axis=0)
        )
        key_sum[low:high, :] += matmul(
            jnp.concatenate(all_scores, axis=1), jnp.concatenate(queries, axis=0)
        )
        place += size
    out_ref[:, pl.ds(width + column, lanes)] = key_sum[...].astype(BRAIN)
    out_ref[:, pl.ds(2 * width + column, lanes)] = value_sum[...].astype(BRAIN)


def attention_specs(length):
    lanes = 2 * HEAD_DIM
    pairs = HEADS // 2
    spec = lambda shift: pl.BlockSpec((length, lanes), lambda r, j: (r, shift * pairs + j))
    segs = [
        pl.BlockSpec((1, length, 1), lambda r, j: (r, 0, 0)),
        pl.BlockSpec((1, 1, length), lambda r, j: (r, 0, 0)),
    ]
    lse = pl.BlockSpec((1, 1, 8, length), lambda r, j: (r, j, 0, 0))
    plain = pl.BlockSpec((length, lanes), lambda r, j: (r, j))
    bias = pltpu.VMEM((sum(high - low for low, high in windows(length)), QUERY_BLOCK), FLOAT)
    return segs, [spec(0), spec(1), spec(2)], plain, lse, bias


def attention_forward(segments, qkv, length):
    rows = segments.shape[0]
    segs, qkv_specs, plain, lse, bias = attention_specs(length)
    width = HEADS * HEAD_DIM
    return pl.pallas_call(
        attend_forward,
        grid=(rows, HEADS // 2),
        in_specs=segs + qkv_specs,
        out_specs=[plain, lse],
        out_shape=[
            jax.ShapeDtypeStruct((rows * length, width), BRAIN),
            jax.ShapeDtypeStruct((rows, HEADS // 2, 8, length), FLOAT),
        ],
        scratch_shapes=[bias],
        name="attend_forward",
        compiler_params=pltpu.CompilerParams(vmem_limit_bytes=48 * 1024 * 1024),
    )(segments[:, :, None], segments[:, None, :], qkv, qkv, qkv)


def attention_backward(segments, qkv, grads, lse_rows, length):
    rows = segments.shape[0]
    segs, qkv_specs, plain, lse, bias = attention_specs(length)
    width = HEADS * HEAD_DIM
    return pl.pallas_call(
        attend_backward,
        grid=(rows, HEADS // 2),
        in_specs=segs + qkv_specs + [plain, lse],
        out_specs=pl.BlockSpec((length, 3 * width), lambda r, j: (r, 0)),
        out_shape=jax.ShapeDtypeStruct((rows * length, 3 * width), BRAIN),
        scratch_shapes=[
            bias,
            pltpu.VMEM((length, 2 * HEAD_DIM), FLOAT),
            pltpu.VMEM((length, 2 * HEAD_DIM), FLOAT),
        ],
        name="attend_backward",
        compiler_params=pltpu.CompilerParams(vmem_limit_bytes=56 * 1024 * 1024),
    )(segments[:, :, None], segments[:, None, :], qkv, qkv, qkv, grads, lse_rows)


def lamb_parts(weight, first, second, grad, decay, corr_one, corr_two, axis):
    first_new = BETA_ONE * first + (1.0 - BETA_ONE) * grad
    second_new = BETA_TWO * second + (1.0 - BETA_TWO) * grad * grad
    update = first_new / corr_one / (jnp.sqrt(second_new / corr_two) + ADAM_EPS) + decay * weight
    weight_sq = jnp.reshape(jnp.sum(weight * weight, axis=axis), (-1,))
    update_sq = jnp.reshape(jnp.sum(update * update, axis=axis), (-1,))
    return (first_new, second_new, update, weight_sq, update_sq)


def body(
    tokens,
    cotangent,
    segment_ids,
    w_qkv,
    m_qkv,
    v_qkv,
    w_out,
    m_out,
    v_out,
    w_up,
    m_up,
    v_up,
    w_down,
    m_down,
    v_down,
    vectors,
    m_vectors,
    v_vectors,
    up_bias,
    m_up_bias,
    v_up_bias,
):
    both = ("dp", "seq")
    small = jnp.concatenate([vectors.reshape(-1), up_bias]).astype(BRAIN)
    small = lax.all_gather(small[None], both, axis=0, tiled=True)
    cut = vectors.size
    full_vectors = small[:, :cut].reshape(-1, vectors.shape[0], vectors.shape[1])
    vector_rows = full_vectors.transpose(1, 0, 2).reshape(vectors.shape[0], -1).astype(FLOAT)
    up_shift = small[:, cut:].reshape(-1).astype(FLOAT)
    full_qkv = lax.all_gather(w_qkv.astype(BRAIN), both, axis=0, tiled=True)
    full_out = lax.all_gather(w_out.astype(BRAIN), both, axis=0, tiled=True)
    full_up = lax.all_gather(w_up.astype(BRAIN), both, axis=0, tiled=True)
    full_down = lax.all_gather(w_down.astype(BRAIN), both, axis=0, tiled=True)

    width = tokens.shape[2]
    length = segment_ids.shape[1]
    token_rows = lax.all_to_all(tokens, "seq", split_axis=0, concat_axis=1, tiled=True)
    back_rows = lax.all_to_all(cotangent, "seq", split_axis=0, concat_axis=1, tiled=True)
    rows = token_rows.shape[0]
    segments = lax.dynamic_slice_in_dim(segment_ids, lax.axis_index("seq") * rows, rows, 0)
    count = rows * length
    token_part = token_rows.reshape(count, width).astype(FLOAT)
    back_part = back_rows.reshape(count, width)

    normed_one, plain_one, inverse_one = norm_forward(token_part, vector_rows[0], vector_rows[1])
    low_one = normed_one.astype(BRAIN)
    shifts = jnp.concatenate([vector_rows[4], jnp.zeros_like(vector_rows[4]), vector_rows[5]])
    qkv = (matmul(low_one, full_qkv) + shifts).astype(BRAIN)
    context, lse_rows = attention_forward(segments, qkv, length)
    resid_one = token_part + matmul(context, full_out) + vector_rows[6]
    normed_two, plain_two, inverse_two = norm_forward(resid_one, vector_rows[2], vector_rows[3])
    low_two = normed_two.astype(BRAIN)
    hidden_pre = matmul(low_two, full_up) + up_shift
    activated, gelu_pull = jax.vjp(gelu_tanh, hidden_pre)
    low_act = activated.astype(BRAIN)
    result = resid_one + matmul(low_act, full_down) + vector_rows[7]
    mixed = result.astype(BRAIN).reshape(rows, length, width)
    mixed = lax.all_to_all(mixed, "seq", split_axis=1, concat_axis=0, tiled=True)

    back_float = back_part.astype(FLOAT)
    grad_down = inner_rows(low_act, back_part)
    act_grad = times_transposed(back_part, full_down)
    hidden_grad = gelu_pull(act_grad)[0].astype(BRAIN)
    grad_up = inner_rows(low_two, hidden_grad)
    grad_up_bias = jnp.sum(hidden_grad.astype(FLOAT), axis=0)
    two_grad = times_transposed(hidden_grad, full_up)
    resid_grad = back_float + norm_backward(two_grad, plain_two, inverse_two, vector_rows[2])
    branch_grad = resid_grad.astype(BRAIN)
    grad_out = inner_rows(context, branch_grad)
    context_grad = times_transposed(branch_grad, full_out).astype(BRAIN)
    joined = attention_backward(segments, qkv, context_grad, lse_rows, length)
    grad_qkv = inner_rows(low_one, joined)
    one_grad = times_transposed(joined, full_qkv)
    input_rows = resid_grad + norm_backward(one_grad, plain_one, inverse_one, vector_rows[0])
    input_grad = input_rows.astype(BRAIN).reshape(rows, length, width)
    input_grad = lax.all_to_all(input_grad, "seq", split_axis=1, concat_axis=0, tiled=True)
    input_grad = input_grad.astype(FLOAT)
    joined_sum = jnp.sum(joined.astype(FLOAT), axis=0)
    grad_vectors = jnp.stack(
        [
            jnp.sum(one_grad * plain_one, axis=0),
            jnp.sum(one_grad, axis=0),
            jnp.sum(two_grad * plain_two, axis=0),
            jnp.sum(two_grad, axis=0),
            joined_sum[:width],
            joined_sum[2 * width :],
            jnp.sum(branch_grad.astype(FLOAT), axis=0),
            jnp.sum(back_float, axis=0),
        ]
    )
    devices = width // vectors.shape[1]
    small_grad = jnp.concatenate(
        [
            grad_vectors.reshape(vectors.shape[0], devices, -1).transpose(1, 0, 2).reshape(devices, -1),
            grad_up_bias.reshape(devices, -1),
        ],
        axis=1,
    )
    scatter = lambda value: lax.psum_scatter(value, both, scatter_dimension=0, tiled=True)
    small_share = scatter(small_grad)[0]
    shares = (
        scatter(grad_qkv),
        scatter(grad_out),
        scatter(grad_up),
        scatter(grad_down),
        small_share[:cut].reshape(vectors.shape),
        small_share[cut:],
    )
    count_float = jnp.asarray(STEP_NUMBER, FLOAT)
    corr_one = 1.0 - jnp.power(jnp.asarray(BETA_ONE, FLOAT), count_float)
    corr_two = 1.0 - jnp.power(jnp.asarray(BETA_TWO, FLOAT), count_float)
    weights = (w_qkv, w_out, w_up, w_down, vectors, up_bias)
    firsts = (m_qkv, m_out, m_up, m_down, m_vectors, m_up_bias)
    seconds = (v_qkv, v_out, v_up, v_down, v_vectors, v_up_bias)
    decays = (DECAY_RATE, DECAY_RATE, DECAY_RATE, DECAY_RATE, 0.0, 0.0)
    axes_list = (None, None, None, None, 1, None)
    parts = [
        lamb_parts(*each, corr_one, corr_two, axis)
        for *each, axis in zip(weights, firsts, seconds, shares, decays, axes_list)
    ]
    totals = lax.psum(
        jnp.stack(
            [
                jnp.concatenate([part[3] for part in parts]),
                jnp.concatenate([part[4] for part in parts]),
            ]
        ),
        both,
    )
    ratios = jnp.sqrt(totals[0]) / (jnp.sqrt(totals[1]) + ADAM_EPS)
    scales = [ratios[0], ratios[1], ratios[2], ratios[3], ratios[4:12][:, None], ratios[12]]
    news = [
        weight - LEARN_RATE * scale * part[2] for weight, scale, part in zip(weights, scales, parts)
    ]
    return (
        mixed,
        input_grad,
        *shares,
        *[part[0] for part in parts],
        *[part[1] for part in parts],
        *news,
        *[new.astype(BRAIN) for new in news[:4]],
    )


def solution(mesh):
    matrix = P(("dp", "seq"), None)
    rows = P("dp", "seq", None)
    vector = P(None, ("dp", "seq"))
    bias = P(("dp", "seq"))
    six = (matrix, matrix, matrix, matrix, vector, bias)
    in_specs = (rows, rows, P("dp", None)) + tuple(spec for spec in six for _ in range(3))
    out_specs = (rows, rows) + six * 4 + (matrix,) * 4
    return jax.shard_map(body, mesh=mesh, in_specs=in_specs, out_specs=out_specs, check_vma=False)
```

```python
import functools

import jax
import jax.numpy as jnp
from jax import lax
from jax.experimental import pallas as pl
from jax.experimental.pallas import tpu as pltpu
from jax.sharding import PartitionSpec as P

HEADS = 12
HEAD_DIM = 64
LONGEST = 512
QUERY_BLOCK = 256


BETA_ONE = 0.9
BETA_TWO = 0.999
ADAM_EPS = 1e-06
DECAY_RATE = 0.01
LEARN_RATE = 0.4
NORM_EPS = 1e-05
STEP_NUMBER = 10.0
CORR_ONE = 1.0 - BETA_ONE**STEP_NUMBER
CORR_TWO = 1.0 - BETA_TWO**STEP_NUMBER

BRAIN = jnp.bfloat16
FLOAT = jnp.float32


def matmul(left_side, right_side):
    return jnp.dot(left_side, right_side, preferred_element_type=FLOAT)


def inner_rows(left_side, right_side):
    return lax.dot_general(
        left_side, right_side, (((0,), (0,)), ((), ())), preferred_element_type=FLOAT
    )


def times_transposed(left_side, right_side):
    return lax.dot_general(
        left_side, right_side, (((1,), (1,)), ((), ())), preferred_element_type=FLOAT
    )


def gelu_tanh(values):
    return jax.nn.gelu(values, approximate=True)


def norm_forward(values, norm_gain, norm_shift):
    center = values - jnp.mean(values, axis=-1, keepdims=True)
    inverse = lax.rsqrt(jnp.mean(center * center, axis=-1, keepdims=True) + NORM_EPS)
    normed = center * inverse
    return (normed * norm_gain + norm_shift, normed, inverse)


def norm_backward(upstream, normed, inverse, norm_gain):
    scaled = upstream * norm_gain
    centered = scaled - jnp.mean(scaled, axis=-1, keepdims=True)
    return inverse * (centered - normed * jnp.mean(scaled * normed, axis=-1, keepdims=True))


def windows(length):
    return [
        (max(0, first - LONGEST), first + QUERY_BLOCK) for first in range(0, length, QUERY_BLOCK)
    ]


def fill_bias(seg_col, seg_row, bias, length):
    place = 0
    for index, (low, high) in enumerate(windows(length)):
        first = index * QUERY_BLOCK
        size = high - low
        keys = seg_col[0, low:high, :]
        queries = seg_row[0, :, first : first + QUERY_BLOCK]
        key_place = low + lax.broadcasted_iota(jnp.int32, (size, QUERY_BLOCK), 0)
        query_place = first + lax.broadcasted_iota(jnp.int32, (size, QUERY_BLOCK), 1)
        allowed = (keys == queries) & (key_place <= query_place)
        bias[place : place + size, :] = jnp.where(allowed, 0.0, -1000000000.0)
        place += size


def split_heads(pair):
    lane = lax.broadcasted_iota(jnp.int32, pair.shape, 1)
    zero = jnp.zeros_like(pair)
    return (jnp.where(lane < HEAD_DIM, pair, zero), jnp.where(lane < HEAD_DIM, zero, pair))


def attend_forward(seg_col, seg_row, q_ref, k_ref, v_ref, c_ref, lse_ref, bias):
    length = q_ref.shape[0]

    @pl.when(pl.program_id(1) == 0)
    def _():
        fill_bias(seg_col, seg_row, bias, length)

    v_turned = v_ref[...].T
    place = 0
    for index, (low, high) in enumerate(windows(length)):
        first = index * QUERY_BLOCK
        size = high - low
        queries = split_heads(q_ref[first : first + QUERY_BLOCK, :] * HEAD_DIM ** (-0.5))
        keys = k_ref[low:high, :]
        blocked = bias[place : place + size, :]
        parts = []
        for head in range(2):
            scores = times_transposed(keys, queries[head]) + blocked
            peak = jnp.max(scores, axis=0, keepdims=True)
            probs = jnp.exp(scores - peak)
            total = jnp.sum(probs, axis=0, keepdims=True)
            probs = (probs * (1.0 / total)).astype(BRAIN)
            lse_ref[0, 0, head : head + 1, first : first + QUERY_BLOCK] = peak + jnp.log(total)
            turned = v_turned[head * HEAD_DIM : (head + 1) * HEAD_DIM, low:high]
            parts.append(matmul(turned, probs))
        context = jnp.concatenate(parts, axis=0).T
        c_ref[first : first + QUERY_BLOCK, :] = context.astype(BRAIN)
        place += size


def attend_backward(
    seg_col, seg_row, q_ref, k_ref, v_ref, g_ref, lse_ref, out_ref, bias, key_sum, value_sum
):
    length = q_ref.shape[0]
    pair = pl.program_id(1)

    @pl.when(pair == 0)
    def _():
        fill_bias(seg_col, seg_row, bias, length)

    key_sum[...] = jnp.zeros_like(key_sum)
    value_sum[...] = jnp.zeros_like(value_sum)
    width = HEADS * HEAD_DIM
    k_turned = k_ref[...].T
    lanes = 2 * HEAD_DIM
    column = pl.multiple_of(pair * lanes, lanes)
    place = 0
    for index, (low, high) in enumerate(windows(length)):
        first = index * QUERY_BLOCK
        size = high - low
        rows = slice(first, first + QUERY_BLOCK)
        queries = split_heads(q_ref[rows, :] * HEAD_DIM ** (-0.5))
        grads = split_heads(g_ref[rows, :])
        keys = k_ref[low:high, :]
        values = v_ref[low:high, :]
        blocked = bias[place : place + size, :]
        all_probs = []
        all_scores = []
        parts = []
        for head in range(2):
            scores = times_transposed(keys, queries[head]) + blocked
            probs = jnp.exp(scores - lse_ref[0, 0, head : head + 1, rows])
            prob_grad = times_transposed(values, grads[head])
            row_dot = jnp.sum(probs * prob_grad, axis=0, keepdims=True)
            score_grad = (probs * (prob_grad - row_dot)).astype(BRAIN)
            all_probs.append(probs.astype(BRAIN))
            all_scores.append(score_grad)
            turned = k_turned[head * HEAD_DIM : (head + 1) * HEAD_DIM, low:high]
            parts.append(matmul(turned, score_grad))
        query_grad = jnp.concatenate(parts, axis=0).T * HEAD_DIM ** (-0.5)
        out_ref[rows, pl.ds(column, lanes)] = query_grad.astype(BRAIN)
        value_sum[low:high, :] += matmul(
            jnp.concatenate(all_probs, axis=1), jnp.concatenate(grads, axis=0)
        )
        key_sum[low:high, :] += matmul(
            jnp.concatenate(all_scores, axis=1), jnp.concatenate(queries, axis=0)
        )
        place += size
    out_ref[:, pl.ds(width + column, lanes)] = key_sum[...].astype(BRAIN)
    out_ref[:, pl.ds(2 * width + column, lanes)] = value_sum[...].astype(BRAIN)


def attention_specs(length):
    lanes = 2 * HEAD_DIM
    pairs = HEADS // 2
    spec = lambda shift: pl.BlockSpec((length, lanes), lambda r, j: (r, shift * pairs + j))
    segs = [
        pl.BlockSpec((1, length, 1), lambda r, j: (r, 0, 0)),
        pl.BlockSpec((1, 1, length), lambda r, j: (r, 0, 0)),
    ]
    lse = pl.BlockSpec((1, 1, 8, length), lambda r, j: (r, j, 0, 0))
    plain = pl.BlockSpec((length, lanes), lambda r, j: (r, j))
    bias = pltpu.VMEM((sum(high - low for low, high in windows(length)), QUERY_BLOCK), FLOAT)
    return segs, [spec(0), spec(1), spec(2)], plain, lse, bias


def attention_forward(segments, qkv, length):
    rows = segments.shape[0]
    segs, qkv_specs, plain, lse, bias = attention_specs(length)
    width = HEADS * HEAD_DIM
    return pl.pallas_call(
        attend_forward,
        grid=(rows, HEADS // 2),
        in_specs=segs + qkv_specs,
        out_specs=[plain, lse],
        out_shape=[
            jax.ShapeDtypeStruct((rows * length, width), BRAIN),
            jax.ShapeDtypeStruct((rows, HEADS // 2, 8, length), FLOAT),
        ],
        scratch_shapes=[bias],
        name="attend_forward",
        compiler_params=pltpu.CompilerParams(vmem_limit_bytes=48 * 1024 * 1024),
    )(segments[:, :, None], segments[:, None, :], qkv, qkv, qkv)


def attention_backward(segments, qkv, grads, lse_rows, length):
    rows = segments.shape[0]
    segs, qkv_specs, plain, lse, bias = attention_specs(length)
    width = HEADS * HEAD_DIM
    return pl.pallas_call(
        attend_backward,
        grid=(rows, HEADS // 2),
        in_specs=segs + qkv_specs + [plain, lse],
        out_specs=pl.BlockSpec((length, 3 * width), lambda r, j: (r, 0)),
        out_shape=jax.ShapeDtypeStruct((rows * length, 3 * width), BRAIN),
        scratch_shapes=[
            bias,
            pltpu.VMEM((length, 2 * HEAD_DIM), FLOAT),
            pltpu.VMEM((length, 2 * HEAD_DIM), FLOAT),
        ],
        name="attend_backward",
        compiler_params=pltpu.CompilerParams(vmem_limit_bytes=56 * 1024 * 1024),
    )(segments[:, :, None], segments[:, None, :], qkv, qkv, qkv, grads, lse_rows)


MESH = pl.DeviceIdType.MESH


def bits_of(count):
    return count.bit_length() - 1


def flipped(value, bit):
    step = 1 << bit
    return value + step * (1 - 2 * lax.rem(lax.div(value, step), 2))


def rounded_down(value, bit):
    return lax.div(value, 1 << bit) * (1 << bit)


def spread(value, bit, total):
    step = 1 << (bit + 1)
    return [lax.rem(value, step) + step * turn for turn in range(1 << (total - 1 - bit))]


def greet(peers):
    barrier = pltpu.get_barrier_semaphore()
    for peer in peers:
        pl.semaphore_signal(barrier, inc=1, device_id=peer, device_id_type=MESH)
    pl.semaphore_wait(barrier, len(peers))


def cube_peers(place, line, seq_count, half_count):
    peers = [{"dp": flipped(place, 0)}]
    peers += [{"dp": flipped(place, bit + 1)} for bit in range(bits_of(half_count))]
    peers += [{"seq": flipped(line, bit)} for bit in range(bits_of(seq_count))]
    return peers


def column_halves(width):
    if width % 256:
        return [slice(0, width)]
    return [slice(0, width // 2), slice(width // 2, width)]


def gather_stages(full, columns, backwards):
    half_count, _, seq_count = full.shape[:3]
    place, line = lax.axis_index("dp"), lax.axis_index("seq")
    chip, core = lax.div(place, 2), lax.rem(place, 2)
    stages = []
    for bit in range(bits_of(half_count)):
        block = pl.ds(rounded_down(chip, bit), 1 << bit)
        stages.append(([full.at[block, core, line, :, columns]], {"dp": flipped(place, bit + 1)}))
    total = bits_of(seq_count)
    for bit in reversed(range(total)) if backwards else range(total):
        if backwards:
            held = [full.at[:, core, at, :, columns] for at in spread(line, bit, total)]
        else:
            block = pl.ds(rounded_down(line, bit), 1 << bit)
            held = [full.at[:, core, block, :, columns]]
        stages.append((held, {"seq": flipped(line, bit)}))
    stages.append(([full.at[:, core, :, :, columns]], {"dp": flipped(place, 0)}))
    return stages


def gather_kernel(count, *refs):
    shards, fulls = refs[:count], refs[count : 2 * count]
    send_sem, recv_sem, own_sem = refs[2 * count :]
    half_count, _, seq_count = fulls[0].shape[:3]
    place, line = lax.axis_index("dp"), lax.axis_index("seq")
    chip, core = lax.div(place, 2), lax.rem(place, 2)
    owns = [
        pltpu.make_async_copy(shard, full.at[chip, core, line], own_sem.at[index])
        for index, (shard, full) in enumerate(zip(shards, fulls))
    ]
    for own in owns:
        own.start()
    greet(cube_peers(place, line, seq_count, half_count))
    slot = 0
    chunks = []
    for full in fulls:
        chunk = []
        for turn, columns in enumerate(column_halves(full.shape[-1])):
            stages = []
            for slices, peer in gather_stages(full, columns, turn == 1):
                copies = []
                for part in slices:
                    copies.append(
                        pltpu.make_async_remote_copy(
                            part,
                            part,
                            send_sem.at[slot],
                            recv_sem.at[slot],
                            device_id=peer,
                            device_id_type=MESH,
                        )
                    )
                    slot += 1
                stages.append(copies)
            chunk.append(stages)
        chunks.append(chunk)
    steps = len(chunks[0][0])
    for wave in range(count + steps):
        for index, chunk in enumerate(chunks):
            step = wave - index
            if step == 0:
                owns[index].wait()
            for stages in chunk:
                if 1 <= step <= steps:
                    for copy in stages[step - 1]:
                        copy.wait_recv()
                if 0 <= step < steps:
                    for copy in stages[step]:
                        copy.start()
    for chunk in chunks:
        for stages in chunk:
            for copies in stages:
                for copy in copies:
                    copy.wait_send()


def copies_in_all(widths, half_count, seq_count):
    single = bits_of(half_count) + bits_of(seq_count) + 1
    double = single + bits_of(half_count) + 1 + seq_count - 1
    return sum(double if len(column_halves(width)) == 2 else single for width in widths)


def gather_all(shards, dp_count, seq_count):
    half_count = dp_count // 2
    slots = copies_in_all([shard.shape[1] for shard in shards], half_count, seq_count)
    fulls = pl.pallas_call(
        functools.partial(gather_kernel, len(shards)),
        out_shape=[
            jax.ShapeDtypeStruct((half_count, 2, seq_count) + shard.shape, shard.dtype)
            for shard in shards
        ],
        in_specs=[pl.BlockSpec(memory_space=pltpu.VMEM)] * len(shards),
        out_specs=[pl.BlockSpec(memory_space=pl.ANY)] * len(shards),
        scratch_shapes=[
            pltpu.SemaphoreType.DMA((slots,)),
            pltpu.SemaphoreType.DMA((slots,)),
            pltpu.SemaphoreType.DMA((len(shards),)),
        ],
        name="gather_weights",
        compiler_params=pltpu.CompilerParams(collective_id=0, has_side_effects=True),
    )(*shards)
    return fulls


def lamb_pieces(weight, first, second, grad, decay):
    first_new = BETA_ONE * first + (1.0 - BETA_ONE) * grad
    second_new = BETA_TWO * second + (1.0 - BETA_TWO) * grad * grad
    spread_out = jnp.sqrt(second_new / CORR_TWO) + ADAM_EPS
    update = first_new / CORR_ONE / spread_out + decay * weight
    return (first_new, second_new, update)


def square_sum(values):
    return jnp.sum(jnp.sum(values * values, axis=1, keepdims=True), axis=0, keepdims=True)


def picked(small, rank, vector_size, bias_size):
    width = small.shape[1]
    row = lax.broadcasted_iota(jnp.int32, (width, 128), 0)
    lane = lax.broadcasted_iota(jnp.int32, (width, 128), 1)
    dot = functools.partial(jnp.dot, precision=lax.Precision.HIGHEST, preferred_element_type=FLOAT)
    chosen = (row == lane + rank * vector_size) & (lane < vector_size)
    vector_grad = dot(small[0:8, :], jnp.where(chosen, 1.0, 0.0))[:, :vector_size]
    start = rank * bias_size
    chosen = (row == lane + lax.rem(start, width)) & (lane < bias_size)
    tail = dot(small[8:16, :], jnp.where(chosen, 1.0, 0.0))
    tail_row = lax.broadcasted_iota(jnp.int32, tail.shape, 0)
    tail = jnp.sum(jnp.where(tail_row == lax.div(start, width), tail, 0.0), axis=0, keepdims=True)
    return vector_grad, tail[:, :bias_size]


def scatter_kernel(*refs):
    grads, small = refs[0:4], refs[4]
    weights, firsts, seconds = refs[5:11], refs[11:17], refs[17:23]
    shares, norm_out = refs[23:29], refs[29]
    owns, cores, lines = refs[30:34], refs[34:38], refs[38:46]
    chips = refs[46:54]
    small_sum, small_in, norm_mine, norm_dp, norm_line, norm_seq = refs[54:60]
    send_sem, recv_sem, own_sem, small_send, small_recv, norm_send, norm_recv = refs[60:67]

    half_count, _, seq_count = grads[0].shape[:3]
    dp_count = 2 * half_count
    place, line = lax.axis_index("dp"), lax.axis_index("seq")
    chip, core = lax.div(place, 2), lax.rem(place, 2)
    seq_bits, half_bits = bits_of(seq_count), bits_of(half_count)

    loads = [
        pltpu.make_async_copy(grad.at[:, core], own, own_sem.at[index])
        for index, (grad, own) in enumerate(zip(grads, owns))
    ]
    for load in loads:
        load.start()
    dp_peers = [{"dp": lax.rem(place + turn, dp_count)} for turn in range(1, dp_count)]
    seq_peers = [{"seq": lax.rem(line + turn, seq_count)} for turn in range(1, seq_count)]
    greet(dp_peers + seq_peers)

    slots = iter(range(send_sem.shape[0]))

    def remote(source, target, peer):
        slot = next(slots)
        return pltpu.make_async_remote_copy(
            source, target, send_sem.at[slot], recv_sem.at[slot], device_id=peer, device_id_type=MESH
        )

    def add_loop(own, held, columns, trips, where):
        def step(turn, carry):
            mine, theirs = where(turn)
            own[mine[0], mine[1], :, columns] = (
                own[mine[0], mine[1], :, columns] + held[theirs]
            )
            return carry

        lax.fori_loop(0, trips, step, 0)

    chunks = []
    for index, (grad, own, from_core) in enumerate(zip(grads, owns, cores)):
        for turn, columns in enumerate(column_halves(grad.shape[-1])):
            backwards = turn == 1
            from_line, from_chip = lines[2 * index + turn], chips[2 * index + turn]
            stages = []
            copies = [
                remote(
                    grad.at[:, 1 - core, :, :, columns],
                    from_core.at[:, :, :, columns],
                    {"dp": flipped(place, 0)},
                )
            ]

            def core_add(own=own, from_core=from_core, columns=columns):
                def step(at, carry):
                    one, two = lax.div(at, seq_count), lax.rem(at, seq_count)
                    own[one, two, :, columns] = (
                        own[one, two, :, columns] + from_core[one, two, :, columns]
                    )
                    return carry

                lax.fori_loop(0, half_count * seq_count, step, 0)

            stages.append((copies, core_add))
            base = 0
            for bit in range(seq_bits) if backwards else reversed(range(seq_bits)):
                peer_line = flipped(line, bit)
                if backwards:
                    away, kept = spread(peer_line, bit, seq_bits), spread(line, bit, seq_bits)
                else:
                    size = 1 << bit
                    away = [rounded_down(peer_line, bit) + at for at in range(size)]
                    kept = [rounded_down(line, bit) + at for at in range(size)]
                copies = [
                    remote(
                        own.at[:, at, :, columns],
                        from_line.at[base + order],
                        {"seq": peer_line},
                    )
                    for order, at in enumerate(away)
                ]

                def line_add(own=own, from_line=from_line, columns=columns, kept=kept, base=base):
                    for order, at in enumerate(kept):

                        def step(one, carry, at=at, order=order):
                            own[one, at, :, columns] = (
                                own[one, at, :, columns] + from_line[base + order, one]
                            )
                            return carry

                        lax.fori_loop(0, half_count, step, 0)

                stages.append((copies, line_add))
                base += len(away)
            base = 0
            for bit in reversed(range(half_bits)):
                size = 1 << bit
                peer_chip = flipped(chip, bit)
                away, kept = rounded_down(peer_chip, bit), rounded_down(chip, bit)
                copies = [
                    remote(
                        own.at[pl.ds(away, size), line, :, columns],
                        from_chip.at[pl.ds(base, size)],
                        {"dp": flipped(place, bit + 1)},
                    )
                ]
                if bit:

                    def chip_add(
                        own=own, from_chip=from_chip, columns=columns, kept=kept, base=base, size=size
                    ):
                        for at in range(size):
                            own[kept + at, line, :, columns] = (
                                own[kept + at, line, :, columns] + from_chip[base + at]
                            )
                else:

                    def chip_add(
                        own=own, from_chip=from_chip, columns=columns, base=base, share=shares[index]
                    ):
                        share[:, columns] = own[chip, line, :, columns].astype(FLOAT) + from_chip[
                            base
                        ].astype(FLOAT)

                stages.append((copies, chip_add))
                base += size
            chunks.append((index, stages))

    small_peers = cube_peers(place, line, seq_count, half_count)
    small_copies = [
        pltpu.make_async_remote_copy(
            small if step == 0 else small_sum.at[step - 1],
            small_in.at[step],
            small_send.at[step],
            small_recv.at[step],
            device_id=peer,
            device_id_type=MESH,
        )
        for step, peer in enumerate(small_peers)
    ]

    def start_small(step):
        if 1 <= step <= len(small_copies):
            small_copies[step - 1].wait_recv()
            before = small[...] if step == 1 else small_sum[step - 2]
            small_sum[step - 1] = before + small_in[step - 1]
        if 0 <= step < len(small_copies):
            small_copies[step].start()

    steps = len(chunks[0][1])
    order = [3, 2, 1, 0]
    for wave in range(len(order) + steps):
        start_small(wave)
        for at, index in enumerate(order):
            step = wave - at
            if step == 1:
                loads[index].wait()
            for owner, stages in chunks:
                if owner != index:
                    continue
                if 1 <= step <= steps:
                    copies, add = stages[step - 1]
                    for copy in copies:
                        copy.wait_recv()
                    add()
                if 0 <= step < steps:
                    for copy in stages[step][0]:
                        copy.start()

    rank = place * seq_count + line
    vector_grad, bias_grad = picked(
        small_sum[len(small_copies) - 1], rank, shares[4].shape[1], shares[5].shape[1]
    )
    shares[4][...] = vector_grad
    shares[5][...] = bias_grad

    lane = lax.broadcasted_iota(jnp.int32, (8, 128), 1)
    row = lax.broadcasted_iota(jnp.int32, (8, 128), 0)
    tile = jnp.zeros((8, 128), FLOAT)
    for index in (0, 1, 2, 3, 5):
        decay = DECAY_RATE if index < 4 else 0.0
        weight = weights[index][...]
        update = lamb_pieces(
            weight, firsts[index][...], seconds[index][...], shares[index][...], decay
        )[2]
        here = row == (index if index < 4 else 4)
        tile = jnp.where(here & (lane == 0), square_sum(weight), tile)
        tile = jnp.where(here & (lane == 1), square_sum(update), tile)
    norm_mine[0:8, :] = tile
    weight = weights[4][...]
    update = lamb_pieces(weight, firsts[4][...], seconds[4][...], vector_grad, 0.0)[2]
    weight_sq = jnp.sum(weight * weight, axis=1, keepdims=True)
    update_sq = jnp.sum(update * update, axis=1, keepdims=True)
    norm_mine[8:16, :] = jnp.where(lane == 0, weight_sq, jnp.where(lane == 1, update_sq, 0.0))

    def exchange(source, held, peers, at, base):
        copies = [
            pltpu.make_async_remote_copy(
                source,
                held.at[at],
                norm_send.at[base + turn],
                norm_recv.at[base + turn],
                device_id=peer,
                device_id_type=MESH,
            )
            for turn, peer in enumerate(peers)
        ]
        for copy in copies:
            copy.start()
        held[at] = source[...]
        for copy in copies:
            copy.wait_recv()
        total = held[0]
        for turn in range(1, held.shape[0]):
            total = total + held[turn]
        return copies, total

    sent, total = exchange(norm_mine, norm_dp, dp_peers, place, 0)
    norm_line[...] = total
    more, total = exchange(norm_line, norm_seq, seq_peers, line, len(dp_peers))
    norm_out[...] = total
    for copy in sent + more + small_copies:
        copy.wait_send()
    for _, stages in chunks:
        for copies, _ in stages:
            for copy in copies:
                copy.wait_send()


def scatter_all(grads, small, weights, firsts, seconds, dp_count, seq_count):
    half_count = dp_count // 2
    shapes = [weight.shape for weight in weights]
    views = [
        grad.reshape(half_count, 2, seq_count, shape[0], shape[1])
        for grad, shape in zip(grads, shapes)
    ]
    vmem = pl.BlockSpec(memory_space=pltpu.VMEM)
    halves = [(shape[0], shape[1] // 2) for shape in shapes[:4] for _ in range(2)]
    slots = copies_in_all([shape[1] for shape in shapes[:4]], half_count, seq_count)
    slots += 4 * (seq_count - 1 - bits_of(seq_count))
    stages = bits_of(dp_count) + bits_of(seq_count)
    return pl.pallas_call(
        scatter_kernel,
        out_shape=[jax.ShapeDtypeStruct(shape, FLOAT) for shape in shapes]
        + [jax.ShapeDtypeStruct((16, 128), FLOAT)],
        in_specs=[pl.BlockSpec(memory_space=pl.ANY)] * 4 + [vmem] * 19,
        out_specs=[vmem] * 7,
        scratch_shapes=[
            pltpu.VMEM((half_count, seq_count) + shape, BRAIN) for shape in shapes[:4]
        ]
        + [pltpu.VMEM((half_count, seq_count) + shape, BRAIN) for shape in shapes[:4]]
        + [pltpu.VMEM((seq_count - 1, half_count) + half, BRAIN) for half in halves]
        + [pltpu.VMEM((half_count - 1,) + half, BRAIN) for half in halves]
        + [
            pltpu.VMEM((stages,) + small.shape, FLOAT),
            pltpu.VMEM((stages,) + small.shape, FLOAT),
            pltpu.VMEM((16, 128), FLOAT),
            pltpu.VMEM((dp_count, 16, 128), FLOAT),
            pltpu.VMEM((16, 128), FLOAT),
            pltpu.VMEM((seq_count, 16, 128), FLOAT),
            pltpu.SemaphoreType.DMA((slots,)),
            pltpu.SemaphoreType.DMA((slots,)),
            pltpu.SemaphoreType.DMA((4,)),
            pltpu.SemaphoreType.DMA((stages,)),
            pltpu.SemaphoreType.DMA((stages,)),
            pltpu.SemaphoreType.DMA((dp_count + seq_count,)),
            pltpu.SemaphoreType.DMA((dp_count + seq_count,)),
        ],
        name="scatter_gradients",
        compiler_params=pltpu.CompilerParams(
            collective_id=1, has_side_effects=True, vmem_limit_bytes=60 * 1024 * 1024
        ),
    )(*views, small, *weights, *firsts, *seconds)


def lamb_kernel(*refs):
    grads, norms = refs[0:6], refs[6]
    weights, firsts, seconds = refs[7:13], refs[13:19], refs[19:25]
    grad_out, first_out, second_out, new_out = refs[25:31], refs[31:37], refs[37:43], refs[43:49]
    copy_out = refs[49:53]
    weight_norm = jnp.sqrt(norms[:, 0:1])
    scales = weight_norm / (jnp.sqrt(norms[:, 1:2]) + ADAM_EPS)
    for index in range(6):
        grad = grads[index][...]
        weight = weights[index][...]
        decay = DECAY_RATE if index < 4 else 0.0
        first_new, second_new, update = lamb_pieces(
            weight, firsts[index][...], seconds[index][...], grad, decay
        )
        scale = scales[8:16] if index == 4 else scales[min(index, 4) : min(index, 4) + 1]
        new = weight - LEARN_RATE * scale * update
        grad_out[index][...] = grad
        first_out[index][...] = first_new
        second_out[index][...] = second_new
        new_out[index][...] = new
        if index < 4:
            copy_out[index][...] = new.astype(BRAIN)


def lamb_all(grads, norms, weights, firsts, seconds):
    vmem = pl.BlockSpec(memory_space=pltpu.VMEM)
    shapes = [jax.ShapeDtypeStruct(weight.shape, FLOAT) for weight in weights]
    copies = [jax.ShapeDtypeStruct(weight.shape, BRAIN) for weight in weights[:4]]
    return pl.pallas_call(
        lamb_kernel,
        out_shape=shapes * 4 + copies,
        in_specs=[vmem] * 25,
        out_specs=[vmem] * 28,
        name="lamb_update",
        compiler_params=pltpu.CompilerParams(vmem_limit_bytes=48 * 1024 * 1024),
    )(*grads, norms, *weights, *firsts, *seconds)


def back_to_positions(values, shape):
    row_count, pos_count, width = shape
    seq_count = lax.axis_size("seq")
    parts = values.reshape(row_count // seq_count, seq_count, pos_count, width)
    parts = parts.transpose(1, 0, 2, 3)
    parts = lax.all_to_all(parts, "seq", split_axis=0, concat_axis=0, tiled=True)
    return parts.reshape(shape)


def body(
    tokens,
    cotangent,
    segment_ids,
    w_qkv,
    m_qkv,
    v_qkv,
    w_out,
    m_out,
    v_out,
    w_up,
    m_up,
    v_up,
    w_down,
    m_down,
    v_down,
    vectors,
    m_vectors,
    v_vectors,
    up_bias,
    m_up_bias,
    v_up_bias,
):
    dp_count, seq_count = lax.axis_size("dp"), lax.axis_size("seq")
    vector_size, bias_size = vectors.shape[1], up_bias.shape[0]
    small = jnp.concatenate(
        [
            jnp.pad(vectors, ((0, 0), (0, 128 - vector_size))),
            jnp.pad(up_bias[None], ((0, 7), (0, 128 - bias_size))),
        ]
    )
    shards = [part.astype(BRAIN) for part in (small, w_qkv, w_out, w_up, w_down)]
    fulls = gather_all(shards, dp_count, seq_count)
    small = fulls[0].reshape(dp_count * seq_count, 16, 128)
    full_vectors = small[:, :8, :vector_size].transpose(1, 0, 2)
    vector_rows = full_vectors.reshape(8, -1).astype(FLOAT)
    up_shift = small[:, 8, :bias_size].reshape(-1).astype(FLOAT)
    full_qkv, full_out, full_up, full_down = [
        full.reshape(-1, full.shape[-1]) for full in fulls[1:]
    ]

    width = tokens.shape[2]
    length = segment_ids.shape[1]
    token_rows = lax.all_to_all(tokens, "seq", split_axis=0, concat_axis=1, tiled=True)
    back_rows = lax.all_to_all(cotangent, "seq", split_axis=0, concat_axis=1, tiled=True)
    rows = token_rows.shape[0]
    segments = lax.dynamic_slice_in_dim(segment_ids, lax.axis_index("seq") * rows, rows, 0)
    count = rows * length
    token_part = token_rows.reshape(count, width).astype(FLOAT)
    back_part = back_rows.reshape(count, width)

    normed_one, plain_one, inverse_one = norm_forward(token_part, vector_rows[0], vector_rows[1])
    low_one = normed_one.astype(BRAIN)
    shifts = jnp.concatenate([vector_rows[4], jnp.zeros_like(vector_rows[4]), vector_rows[5]])
    qkv = (matmul(low_one, full_qkv) + shifts).astype(BRAIN)
    context, lse_rows = attention_forward(segments, qkv, length)
    resid_one = token_part + matmul(context, full_out) + vector_rows[6]
    normed_two, plain_two, inverse_two = norm_forward(resid_one, vector_rows[2], vector_rows[3])
    low_two = normed_two.astype(BRAIN)
    hidden_pre = matmul(low_two, full_up) + up_shift
    activated, gelu_pull = jax.vjp(gelu_tanh, hidden_pre)
    low_act = activated.astype(BRAIN)
    result = resid_one + matmul(low_act, full_down) + vector_rows[7]
    mixed = back_to_positions(result.astype(BRAIN), tokens.shape)

    back_float = back_part.astype(FLOAT)
    grad_down = inner_rows(low_act, back_part)
    act_grad = times_transposed(back_part, full_down)
    hidden_grad = gelu_pull(act_grad)[0].astype(BRAIN)
    grad_up = inner_rows(low_two, hidden_grad)
    grad_up_bias = jnp.sum(hidden_grad.astype(FLOAT), axis=0)
    two_grad = times_transposed(hidden_grad, full_up)
    resid_grad = back_float + norm_backward(two_grad, plain_two, inverse_two, vector_rows[2])
    branch_grad = resid_grad.astype(BRAIN)
    grad_out = inner_rows(context, branch_grad)
    context_grad = times_transposed(branch_grad, full_out).astype(BRAIN)
    joined = attention_backward(segments, qkv, context_grad, lse_rows, length)
    grad_qkv = inner_rows(low_one, joined)
    one_grad = times_transposed(joined, full_qkv)
    input_rows = resid_grad + norm_backward(one_grad, plain_one, inverse_one, vector_rows[0])
    input_grad = back_to_positions(input_rows.astype(BRAIN), tokens.shape).astype(FLOAT)
    joined_sum = jnp.sum(joined.astype(FLOAT), axis=0)
    grad_vectors = jnp.stack(
        [
            jnp.sum(one_grad * plain_one, axis=0),
            jnp.sum(one_grad, axis=0),
            jnp.sum(two_grad * plain_two, axis=0),
            jnp.sum(two_grad, axis=0),
            joined_sum[:width],
            joined_sum[2 * width :],
            jnp.sum(branch_grad.astype(FLOAT), axis=0),
            jnp.sum(back_float, axis=0),
        ]
    )
    small_grad = jnp.concatenate([grad_vectors, grad_up_bias.reshape(-1, width)])
    small_grad = jnp.pad(small_grad, ((0, 16 - small_grad.shape[0]), (0, 0)))
    as_row = lambda value: value.reshape(1, -1)
    weights = (w_qkv, w_out, w_up, w_down, vectors, as_row(up_bias))
    firsts = (m_qkv, m_out, m_up, m_down, m_vectors, as_row(m_up_bias))
    seconds = (v_qkv, v_out, v_up, v_down, v_vectors, as_row(v_up_bias))
    matrix_grads = [grad.astype(BRAIN) for grad in (grad_qkv, grad_out, grad_up, grad_down)]
    *shares, norms = scatter_all(
        matrix_grads, small_grad, weights, firsts, seconds, dp_count, seq_count
    )
    results = list(lamb_all(shares, norms, weights, firsts, seconds))
    for index in (5, 11, 17, 23):
        results[index] = results[index].reshape(-1)
    return (mixed, input_grad, *results)


def solution(mesh):
    matrix = P(("dp", "seq"), None)
    rows = P("dp", "seq", None)
    vector = P(None, ("dp", "seq"))
    bias = P(("dp", "seq"))
    six = (matrix, matrix, matrix, matrix, vector, bias)
    in_specs = (rows, rows, P("dp", None)) + tuple(spec for spec in six for _ in range(3))
    out_specs = (rows, rows) + six * 4 + (matrix,) * 4
    return jax.shard_map(body, mesh=mesh, in_specs=in_specs, out_specs=out_specs, check_vma=False)
```

```python
import functools

import jax
import jax.numpy as jnp
from jax import lax
from jax.experimental import pallas as pl
from jax.experimental.pallas import tpu as pltpu
from jax.sharding import PartitionSpec as P

HEADS = 12
HEAD_DIM = 64
LONGEST = 512
QUERY_BLOCK = 256


BETA_ONE = 0.9
BETA_TWO = 0.999
ADAM_EPS = 1e-06
DECAY_RATE = 0.01
LEARN_RATE = 0.4
NORM_EPS = 1e-05
STEP_NUMBER = 10.0
CORR_ONE = 1.0 - BETA_ONE**STEP_NUMBER
CORR_TWO = 1.0 - BETA_TWO**STEP_NUMBER

BRAIN = jnp.bfloat16
FLOAT = jnp.float32


def matmul(left_side, right_side):
    return jnp.dot(left_side, right_side, preferred_element_type=FLOAT)


def inner_rows(left_side, right_side):
    return lax.dot_general(
        left_side, right_side, (((0,), (0,)), ((), ())), preferred_element_type=FLOAT
    )


def times_transposed(left_side, right_side):
    return lax.dot_general(
        left_side, right_side, (((1,), (1,)), ((), ())), preferred_element_type=FLOAT
    )


def gelu_tanh(values):
    return jax.nn.gelu(values, approximate=True)


def norm_forward(values, norm_gain, norm_shift):
    center = values - jnp.mean(values, axis=-1, keepdims=True)
    inverse = lax.rsqrt(jnp.mean(center * center, axis=-1, keepdims=True) + NORM_EPS)
    normed = center * inverse
    return (normed * norm_gain + norm_shift, normed, inverse)


def norm_backward(upstream, normed, inverse, norm_gain):
    scaled = upstream * norm_gain
    centered = scaled - jnp.mean(scaled, axis=-1, keepdims=True)
    return inverse * (centered - normed * jnp.mean(scaled * normed, axis=-1, keepdims=True))


def windows(length):
    return [
        (max(0, first - LONGEST), first + QUERY_BLOCK) for first in range(0, length, QUERY_BLOCK)
    ]


def fill_bias(seg_col, seg_row, bias, length):
    place = 0
    for index, (low, high) in enumerate(windows(length)):
        first = index * QUERY_BLOCK
        size = high - low
        keys = seg_col[0, low:high, :]
        queries = seg_row[0, :, first : first + QUERY_BLOCK]
        key_place = low + lax.broadcasted_iota(jnp.int32, (size, QUERY_BLOCK), 0)
        query_place = first + lax.broadcasted_iota(jnp.int32, (size, QUERY_BLOCK), 1)
        allowed = (keys == queries) & (key_place <= query_place)
        bias[place : place + size, :] = jnp.where(allowed, 0.0, -1000000000.0)
        place += size


def split_heads(pair):
    lane = lax.broadcasted_iota(jnp.int32, pair.shape, 1)
    zero = jnp.zeros_like(pair)
    return (jnp.where(lane < HEAD_DIM, pair, zero), jnp.where(lane < HEAD_DIM, zero, pair))


def attend_forward(counts, splits, *refs):
    seg_col, seg_row, q_ref, k_ref, v_ref = refs[0:5]
    cotangent, shards = refs[5], refs[6:8]
    c_ref, lse_ref, back_rows, fulls = refs[8], refs[9], refs[10], refs[11:13]
    bias, bounces, bounce, send_sem, recv_sem, own_sem, move_sem = refs[13], refs[14:16], *refs[16:]
    length = q_ref.shape[0]
    here = Here(*counts)
    slots = Slots(send_sem, recv_sem)
    gathers = gathers_of(here, slots, shards, fulls, bounces, own_sem, splits)
    move = Exchange(here, slots, cotangent, back_rows, True, bounce, move_sem)
    waves = led_by(lambda: greet(here.near_peers()), waves_of(gathers))
    blocks = windows(length)
    beside = Beside(waves, HEADS // 2 * len(blocks), extra=(lambda: move.start(0), 5))

    @pl.when(pl.program_id(1) == 0)
    def _():
        fill_bias(seg_col, seg_row, bias, length)

    v_turned = v_ref[...].T
    place = 0
    for index, (low, high) in enumerate(blocks):
        beside.point(index, len(blocks))
        first = index * QUERY_BLOCK
        size = high - low
        queries = split_heads(q_ref[first : first + QUERY_BLOCK, :] * HEAD_DIM ** (-0.5))
        keys = k_ref[low:high, :]
        blocked = bias[place : place + size, :]
        parts = []
        for head in range(2):
            scores = times_transposed(keys, queries[head]) + blocked
            peak = jnp.max(scores, axis=0, keepdims=True)
            probs = jnp.exp(scores - peak)
            total = jnp.sum(probs, axis=0, keepdims=True)
            probs = (probs * (1.0 / total)).astype(BRAIN)
            lse_ref[0, 0, head : head + 1, first : first + QUERY_BLOCK] = peak + jnp.log(total)
            turned = v_turned[head * HEAD_DIM : (head + 1) * HEAD_DIM, low:high]
            parts.append(matmul(turned, probs))
        context = jnp.concatenate(parts, axis=0).T
        c_ref[first : first + QUERY_BLOCK, :] = context.astype(BRAIN)
        place += size

    @pl.when((pl.program_id(0) == pl.num_programs(0) - 1) & (pl.program_id(1) == HEADS // 2 - 1))
    def _():
        beside.rest()
        move.finish(0)
        drain_all(gathers + [move])


def led_by(ahead, waves):
    def both():
        ahead()
        waves[0]()

    return [both] + waves[1:]


class Beside:
    def __init__(self, waves, points, extra=None):
        self.waves, self.points = waves, points
        self.at = {}
        early = len(waves) - 1
        for index in range(early):
            self.at.setdefault(index * points // early, []).append(waves[index])
        if extra:
            self.at.setdefault(extra[1], []).append(extra[0])
        self.late = waves[early:]

    def point(self, index, per_step):
        for point, calls in self.at.items():
            if point % per_step == index:

                @pl.when((pl.program_id(0) == 0) & (pl.program_id(1) == point // per_step))
                def _(calls=calls):
                    for call in calls:
                        call()

    def rest(self):
        for call in self.late:
            call()


def attend_backward(counts, splits, *refs):
    seg_col, seg_row, q_ref, k_ref, v_ref, g_ref, lse_ref = refs[0:7]
    mixed_rows, grads = refs[7], refs[8:10]
    out_ref, mixed, shares = refs[10], refs[11], refs[12:14]
    bias, key_sum, value_sum = refs[14:17]
    buffers, bounce, send_sem, recv_sem, own_sem, move_sem = refs[17:25], *refs[25:]
    length = q_ref.shape[0]
    pair = pl.program_id(1)
    here = Here(*counts)
    slots = Slots(send_sem, recv_sem)
    scatters, loads = scatters_of(here, slots, grads, buffers, shares, own_sem, splits)
    move = Exchange(here, slots, mixed_rows, mixed, False, bounce, move_sem)

    def begin():
        for load in loads:
            load().start()
        greet(here.near_peers())

    waves = led_by(begin, waves_of(scatters))
    blocks = windows(length)
    beside = Beside(waves, HEADS // 2 * len(blocks), extra=(lambda: move.start(0), 5))

    @pl.when(pair == 0)
    def _():
        fill_bias(seg_col, seg_row, bias, length)

    key_sum[...] = jnp.zeros_like(key_sum)
    value_sum[...] = jnp.zeros_like(value_sum)
    width = HEADS * HEAD_DIM
    k_turned = k_ref[...].T
    lanes = 2 * HEAD_DIM
    column = pl.multiple_of(pair * lanes, lanes)
    place = 0
    for index, (low, high) in enumerate(blocks):
        beside.point(index, len(blocks))
        first = index * QUERY_BLOCK
        size = high - low
        rows = slice(first, first + QUERY_BLOCK)
        queries = split_heads(q_ref[rows, :] * HEAD_DIM ** (-0.5))
        grads = split_heads(g_ref[rows, :])
        keys = k_ref[low:high, :]
        values = v_ref[low:high, :]
        blocked = bias[place : place + size, :]
        all_probs = []
        all_scores = []
        parts = []
        for head in range(2):
            scores = times_transposed(keys, queries[head]) + blocked
            probs = jnp.exp(scores - lse_ref[0, 0, head : head + 1, rows])
            prob_grad = times_transposed(values, grads[head])
            row_dot = jnp.sum(probs * prob_grad, axis=0, keepdims=True)
            score_grad = (probs * (prob_grad - row_dot)).astype(BRAIN)
            all_probs.append(probs.astype(BRAIN))
            all_scores.append(score_grad)
            turned = k_turned[head * HEAD_DIM : (head + 1) * HEAD_DIM, low:high]
            parts.append(matmul(turned, score_grad))
        query_grad = jnp.concatenate(parts, axis=0).T * HEAD_DIM ** (-0.5)
        out_ref[rows, pl.ds(column, lanes)] = query_grad.astype(BRAIN)
        value_sum[low:high, :] += matmul(
            jnp.concatenate(all_probs, axis=1), jnp.concatenate(grads, axis=0)
        )
        key_sum[low:high, :] += matmul(
            jnp.concatenate(all_scores, axis=1), jnp.concatenate(queries, axis=0)
        )
        place += size
    out_ref[:, pl.ds(width + column, lanes)] = key_sum[...].astype(BRAIN)
    out_ref[:, pl.ds(2 * width + column, lanes)] = value_sum[...].astype(BRAIN)

    @pl.when((pl.program_id(0) == pl.num_programs(0) - 1) & (pair == HEADS // 2 - 1))
    def _():
        beside.rest()
        move.finish(0)
        drain_all(scatters + [move])


def attention_specs(length):
    lanes = 2 * HEAD_DIM
    pairs = HEADS // 2
    spec = lambda shift: pl.BlockSpec((length, lanes), lambda r, j: (r, shift * pairs + j))
    segs = [
        pl.BlockSpec((1, length, 1), lambda r, j: (r, 0, 0)),
        pl.BlockSpec((1, 1, length), lambda r, j: (r, 0, 0)),
    ]
    lse = pl.BlockSpec((1, 1, 8, length), lambda r, j: (r, j, 0, 0))
    plain = pl.BlockSpec((length, lanes), lambda r, j: (r, j))
    bias = pltpu.VMEM((sum(high - low for low, high in windows(length)), QUERY_BLOCK), FLOAT)
    return segs, [spec(0), spec(1), spec(2)], plain, lse, bias


def attention_forward(segments, qkv, length, cotangent, shards, counts):
    rows = segments.shape[0]
    segs, qkv_specs, plain, lse, bias = attention_specs(length)
    width = HEADS * HEAD_DIM
    row_count, pos_count, _ = cotangent.shape
    splits = [True] * len(shards)
    slots = slot_count(counts, [shard.shape for shard in shards], splits, 1)
    return pl.pallas_call(
        functools.partial(attend_forward, counts, splits),
        grid=(rows, HEADS // 2),
        in_specs=segs + qkv_specs + [ANYWHERE] * 3,
        out_specs=[plain, lse] + [ANYWHERE] * 3,
        out_shape=[
            jax.ShapeDtypeStruct((rows * length, width), BRAIN),
            jax.ShapeDtypeStruct((rows, HEADS // 2, 8, length), FLOAT),
            jax.ShapeDtypeStruct((rows, counts[1], pos_count, width), BRAIN),
        ]
        + [full_shape(shard, *counts) for shard in shards],
        scratch_shapes=[bias]
        + [pltpu.VMEM(shard.shape, shard.dtype) for shard in shards]
        + [
            pltpu.VMEM((rows, pos_count, width), BRAIN),
            pltpu.SemaphoreType.DMA((slots,)),
            pltpu.SemaphoreType.DMA((slots,)),
            pltpu.SemaphoreType.DMA((2 * len(shards),)),
            pltpu.SemaphoreType.DMA((2,)),
        ],
        name="attend_forward",
        compiler_params=pltpu.CompilerParams(
            collective_id=1, has_side_effects=True, vmem_limit_bytes=48 * 1024 * 1024
        ),
    )(segments[:, :, None], segments[:, None, :], qkv, qkv, qkv, cotangent, *shards)


def attention_backward(segments, qkv, context_grad, lse_rows, length, result, grads, shapes, counts):
    rows = segments.shape[0]
    segs, qkv_specs, plain, lse, bias = attention_specs(length)
    width = HEADS * HEAD_DIM
    seq_count = counts[1]
    pos_count = length // seq_count
    splits = [True] * len(shapes)
    slots = slot_count(counts, shapes, splits, 1)
    return pl.pallas_call(
        functools.partial(attend_backward, counts, splits),
        grid=(rows, HEADS // 2),
        in_specs=segs + qkv_specs + [plain, lse] + [ANYWHERE] * 3,
        out_specs=[pl.BlockSpec((length, 3 * width), lambda r, j: (r, 0)), ANYWHERE] + [WHOLE] * 2,
        out_shape=[
            jax.ShapeDtypeStruct((rows * length, 3 * width), BRAIN),
            jax.ShapeDtypeStruct((seq_count, rows, pos_count, width), BRAIN),
        ]
        + [jax.ShapeDtypeStruct(shape, FLOAT) for shape in shapes],
        scratch_shapes=[
            bias,
            pltpu.VMEM((length, 2 * HEAD_DIM), FLOAT),
            pltpu.VMEM((length, 2 * HEAD_DIM), FLOAT),
        ]
        + scatter_buffers(shapes, counts)
        + [
            pltpu.VMEM((rows, pos_count, width), BRAIN),
            pltpu.SemaphoreType.DMA((slots,)),
            pltpu.SemaphoreType.DMA((slots,)),
            pltpu.SemaphoreType.DMA((len(shapes),)),
            pltpu.SemaphoreType.DMA((2,)),
        ],
        name="attend_backward",
        compiler_params=pltpu.CompilerParams(
            collective_id=2, has_side_effects=True, vmem_limit_bytes=62 * 1024 * 1024
        ),
    )(
        segments[:, :, None],
        segments[:, None, :],
        qkv,
        qkv,
        qkv,
        context_grad,
        lse_rows,
        result.reshape(rows, seq_count, pos_count, width),
        *scatter_views(grads, shapes, counts),
    )


MESH = pl.DeviceIdType.MESH
ANYWHERE = pl.BlockSpec(memory_space=pl.ANY)
WHOLE = pl.BlockSpec(memory_space=pltpu.VMEM)


def bits_of(count):
    return count.bit_length() - 1


def flipped(value, bit):
    step = 1 << bit
    return value + step * (1 - 2 * lax.rem(lax.div(value, step), 2))


def rounded_down(value, bit):
    return lax.div(value, 1 << bit) * (1 << bit)


def spread(value, bit, total):
    step = 1 << (bit + 1)
    return [lax.rem(value, step) + step * turn for turn in range(1 << (total - 1 - bit))]


class Here:
    def __init__(self, dp_count, seq_count):
        self.dp_count, self.seq_count = dp_count, seq_count
        self.half_count = dp_count // 2
        self.seq_bits = bits_of(seq_count)
        self.place, self.line = lax.axis_index("dp"), lax.axis_index("seq")
        self.chip, self.core = lax.div(self.place, 2), lax.rem(self.place, 2)

    def core_peer(self):
        return {"dp": flipped(self.place, 0)}

    def line_peer(self, bit):
        return {"seq": flipped(self.line, bit)}

    def other_lines(self):
        return [lax.rem(self.line + turn, self.seq_count) for turn in range(1, self.seq_count)]

    def other_chips(self):
        return [lax.rem(self.chip + turn, self.half_count) for turn in range(1, self.half_count)]

    def chip_peers(self):
        return [{"dp": 2 * chip + self.core} for chip in self.other_chips()]

    def near_peers(self):
        peers = [self.core_peer()] + self.chip_peers()
        return peers + [{"seq": line} for line in self.other_lines()]

    def all_peers(self):
        peers = [{"dp": lax.rem(self.place + turn, self.dp_count)} for turn in range(1, self.dp_count)]
        return peers + [{"seq": line} for line in self.other_lines()]


def greet(peers):
    barrier = pltpu.get_barrier_semaphore()
    for peer in peers:
        pl.semaphore_signal(barrier, inc=1, device_id=peer, device_id_type=MESH)
    pl.semaphore_wait(barrier, len(peers))


class Slots:
    def __init__(self, send_sem, recv_sem):
        self.send_sem, self.recv_sem, self.used = send_sem, recv_sem, 0

    def take(self, count):
        first = self.used
        self.used += count
        return first

    def copy(self, slot, source, target, peer):
        return pltpu.make_async_remote_copy(
            source,
            target,
            self.send_sem.at[slot],
            self.recv_sem.at[slot],
            device_id=peer,
            device_id_type=MESH,
        )


def parts_of(shape, split):
    rows, width = shape
    tiles = width // 128
    if width % 128 or tiles < 2:
        return [[(slice(0, rows), slice(0, width), False)]]
    middle = tiles // 2 * 128
    first, second = (0, middle), (middle, width)
    every = slice(0, rows)
    if split and rows % 32 == 0:
        return [
            [(part, slice(*first), False), (part, slice(*second), True)]
            for part in (slice(0, rows // 2), slice(rows // 2, rows))
        ]
    if split and tiles >= 4:
        lists = [[], []]
        for (low, high), backwards in ((first, False), (second, True)):
            cut = low + (high - low) // 256 * 128
            lists[0].append((every, slice(low, cut), backwards))
            lists[1].append((every, slice(cut, high), backwards))
        return lists
    return [[(every, slice(*first), False), (every, slice(*second), True)]]


class Transfer:
    def start(self, stage):
        for copy in self.copies(stage):
            copy.start()

    def finish(self, stage):
        for copy in self.copies(stage):
            copy.wait_recv()
        self.use(stage)

    def use(self, stage):
        pass

    def drain(self):
        for stage in range(self.stages):
            for copy in self.copies(stage):
                copy.wait_send()


class Gather(Transfer):
    def __init__(self, here, slots, shard, full, pieces, own_done):
        self.here, self.slots, self.shard, self.full = here, slots, shard, full
        self.pieces, self.own_done = pieces, own_done
        self.stages = here.seq_bits + 2
        self.each = here.half_count + here.seq_count
        self.first = slots.take(self.each * len(pieces))

    def copies(self, stage):
        here, full = self.here, self.full
        found = []
        for index, (rows, columns, backwards) in enumerate(self.pieces):
            slot = self.first + self.each * index
            if stage == 0:
                target = full.at[here.chip, here.core, here.line, rows, columns]
                for turn, peer in enumerate(here.chip_peers()):
                    source = self.shard.at[rows, columns]
                    found.append(self.slots.copy(slot + turn, source, target, peer))
                continue
            slot += here.half_count - 1
            if stage == self.stages - 1:
                part = full.at[:, here.core, :, rows, columns]
                slot += here.seq_count - 1
                found.append(self.slots.copy(slot, part, part, here.core_peer()))
                continue
            if backwards:
                bit = here.seq_bits - stage
                slot += (1 << (stage - 1)) - 1
                parts = [
                    full.at[:, here.core, at, rows, columns]
                    for at in spread(here.line, bit, here.seq_bits)
                ]
            else:
                bit = stage - 1
                slot += bit
                block = pl.ds(rounded_down(here.line, bit), 1 << bit)
                parts = [full.at[:, here.core, block, rows, columns]]
            for turn, part in enumerate(parts):
                found.append(self.slots.copy(slot + turn, part, part, here.line_peer(bit)))
        return found

    def start(self, stage):
        if stage == 1:
            self.own_done()
        super().start(stage)


class Scatter(Transfer):
    def __init__(self, here, slots, grad, own, from_core, from_line, from_chip, share, pieces, load):
        self.here, self.slots, self.grad, self.own = here, slots, grad, own
        self.from_core, self.from_line, self.from_chip = from_core, from_line, from_chip
        self.share, self.pieces, self.load = share, pieces, load
        self.stages = here.seq_bits + 2
        self.each = here.half_count + here.seq_count
        self.first = slots.take(self.each * len(pieces))

    def line_stage(self, stage, backwards):
        here = self.here
        if backwards:
            bit = stage - 1
            away = spread(flipped(here.line, bit), bit, here.seq_bits)
            kept = spread(here.line, bit, here.seq_bits)
        else:
            bit = here.seq_bits - stage
            away = [rounded_down(flipped(here.line, bit), bit) + at for at in range(1 << bit)]
            kept = [rounded_down(here.line, bit) + at for at in range(1 << bit)]
        base = sum(1 << (here.seq_bits - past) for past in range(1, stage))
        return bit, away, kept, base

    def copies(self, stage):
        here = self.here
        found = []
        for index, (rows, columns, backwards) in enumerate(self.pieces):
            slot = self.first + self.each * index
            if stage == 0:
                found.append(
                    self.slots.copy(
                        slot,
                        self.grad.at[:, 1 - here.core, :, rows, columns],
                        self.from_core.at[:, :, rows, columns],
                        here.core_peer(),
                    )
                )
            elif stage == self.stages - 1:
                slot += here.seq_count
                for turn, chip in enumerate(here.other_chips()):
                    found.append(
                        self.slots.copy(
                            slot + turn,
                            self.own.at[chip, here.line, rows, columns],
                            self.from_chip.at[turn, rows, columns],
                            {"dp": 2 * chip + here.core},
                        )
                    )
            else:
                bit, away, _, base = self.line_stage(stage, backwards)
                for turn, at in enumerate(away):
                    found.append(
                        self.slots.copy(
                            slot + 1 + base + turn,
                            self.own.at[:, at, rows, columns],
                            self.from_line.at[base + turn, :, rows, columns],
                            here.line_peer(bit),
                        )
                    )
        return found

    def use(self, stage):
        here, own = self.here, self.own
        if stage == 0:
            self.load()
        for rows, columns, backwards in self.pieces:
            if stage == 0:

                def add(at, carry, rows=rows, columns=columns):
                    one, two = lax.div(at, here.seq_count), lax.rem(at, here.seq_count)
                    own[one, two, rows, columns] = (
                        own[one, two, rows, columns] + self.from_core[one, two, rows, columns]
                    )
                    return carry

                lax.fori_loop(0, here.half_count * here.seq_count, add, 0)
            elif stage == self.stages - 1:
                total = own[here.chip, here.line, rows, columns].astype(FLOAT)
                for turn in range(here.half_count - 1):
                    total = total + self.from_chip[turn, rows, columns].astype(FLOAT)
                self.share[rows, columns] = total
            else:
                _, _, kept, base = self.line_stage(stage, backwards)
                for turn, at in enumerate(kept):

                    def add(one, carry, rows=rows, columns=columns, at=at, place=base + turn):
                        own[one, at, rows, columns] = (
                            own[one, at, rows, columns] + self.from_line[place, one, rows, columns]
                        )
                        return carry

                    lax.fori_loop(0, here.half_count, add, 0)


class Exchange(Transfer):
    stages = 1

    def __init__(self, here, slots, source, target, to_rows, bounce, sem):
        self.here, self.slots, self.source, self.target = here, slots, source, target
        self.to_rows, self.bounce, self.sem = to_rows, bounce, sem
        self.first = slots.take(here.seq_count - 1)

    def ends(self, line):
        if self.to_rows:
            count = self.target.shape[0]
            block = self.source.at[pl.ds(line * count, count)]
            return block, self.target.at[:, self.here.line]
        return self.source.at[:, line], self.target.at[self.here.line]

    def copies(self, stage):
        return [
            self.slots.copy(self.first + turn, *self.ends(line), {"seq": line})
            for turn, line in enumerate(self.here.other_lines())
        ]

    def own_in(self):
        return pltpu.make_async_copy(self.ends(self.here.line)[0], self.bounce, self.sem.at[0])

    def own_out(self):
        return pltpu.make_async_copy(self.bounce, self.ends(self.here.line)[1], self.sem.at[1])

    def start(self, stage):
        self.own_in().start()
        super().start(stage)
        self.own_in().wait()
        self.own_out().start()

    def use(self, stage):
        self.own_out().wait()


def waves_of(transfers):
    def wave(count):
        for index, transfer in enumerate(transfers):
            stage = count - index
            if 1 <= stage <= transfer.stages:
                transfer.finish(stage - 1)
            if 0 <= stage < transfer.stages:
                transfer.start(stage)

    total = max(index + transfer.stages for index, transfer in enumerate(transfers)) + 1
    return [functools.partial(wave, count) for count in range(total)]


def drain_all(transfers):
    for transfer in transfers:
        transfer.drain()


def gathers_of(here, slots, shards, fulls, bounces, sem, splits):
    found = []
    for index, (shard, full, bounce) in enumerate(zip(shards, fulls, bounces)):
        inward = lambda shard=shard, bounce=bounce, index=index: pltpu.make_async_copy(
            shard, bounce, sem.at[2 * index]
        )
        outward = lambda full=full, bounce=bounce, index=index: pltpu.make_async_copy(
            bounce, full.at[here.chip, here.core, here.line], sem.at[2 * index + 1]
        )
        for order, pieces in enumerate(parts_of(shard.shape, splits[index])):

            def own_done(first=order == 0, inward=inward, outward=outward):
                if first:
                    inward().start()
                    inward().wait()
                    outward().start()
                    outward().wait()

            found.append(Gather(here, slots, shard, full, pieces, own_done))
    return found


def slot_count(here_shape, shapes, splits, exchanges):
    half_count, seq_count = here_shape[0] // 2, here_shape[1]
    each = half_count + seq_count
    pieces = sum(len(part) for shape, split in zip(shapes, splits) for part in parts_of(shape, split))
    return each * pieces + exchanges * (seq_count - 1)


def full_shape(shard, dp_count, seq_count):
    return jax.ShapeDtypeStruct((dp_count // 2, 2, seq_count) + shard.shape, shard.dtype)


def gather_kernel(counts, splits, count, *refs):
    tokens, shards, fulls = refs[0], refs[1 : 1 + count], refs[2 + count : 2 + 2 * count]
    token_rows = refs[1 + count]
    rest = refs[2 + 2 * count :]
    bounces, bounce, send_sem, recv_sem, own_sem, move_sem = rest[:count], *rest[count:]
    here = Here(*counts)
    slots = Slots(send_sem, recv_sem)
    gathers = gathers_of(here, slots, shards, fulls, bounces, own_sem, splits)
    move = Exchange(here, slots, tokens, token_rows, True, bounce, move_sem)
    greet(here.near_peers())
    waves = waves_of(gathers)
    waves[0]()
    move.start(0)
    for wave in waves[1:]:
        wave()
    move.finish(0)
    drain_all(gathers + [move])


def gather_first(tokens, shards, counts):
    dp_count, seq_count = counts
    row_count, pos_count, width = tokens.shape
    rows = row_count // seq_count
    splits = [False] * len(shards)
    slots = slot_count(counts, [shard.shape for shard in shards], splits, 1)
    return pl.pallas_call(
        functools.partial(gather_kernel, counts, splits, len(shards)),
        out_shape=[jax.ShapeDtypeStruct((rows, seq_count, pos_count, width), tokens.dtype)]
        + [full_shape(shard, *counts) for shard in shards],
        in_specs=[ANYWHERE] * (1 + len(shards)),
        out_specs=[ANYWHERE] * (1 + len(shards)),
        scratch_shapes=[pltpu.VMEM(shard.shape, shard.dtype) for shard in shards]
        + [
            pltpu.VMEM((rows, pos_count, width), tokens.dtype),
            pltpu.SemaphoreType.DMA((slots,)),
            pltpu.SemaphoreType.DMA((slots,)),
            pltpu.SemaphoreType.DMA((2 * len(shards),)),
            pltpu.SemaphoreType.DMA((2,)),
        ],
        name="gather_first",
        compiler_params=pltpu.CompilerParams(collective_id=0, has_side_effects=True),
    )(tokens, *shards)


def lamb_pieces(weight, first, second, grad, decay):
    first_new = BETA_ONE * first + (1.0 - BETA_ONE) * grad
    second_new = BETA_TWO * second + (1.0 - BETA_TWO) * grad * grad
    spread_out = jnp.sqrt(second_new / CORR_TWO) + ADAM_EPS
    update = first_new / CORR_ONE / spread_out + decay * weight
    return (first_new, second_new, update)


def square_sum(values):
    return jnp.sum(jnp.sum(values * values, axis=1, keepdims=True), axis=0, keepdims=True)


def picked(small, rank, vector_size, bias_size):
    width = small.shape[1]
    row = lax.broadcasted_iota(jnp.int32, (width, 128), 0)
    lane = lax.broadcasted_iota(jnp.int32, (width, 128), 1)
    dot = functools.partial(jnp.dot, precision=lax.Precision.HIGHEST, preferred_element_type=FLOAT)
    chosen = (row == lane + rank * vector_size) & (lane < vector_size)
    vector_grad = dot(small[0:8, :], jnp.where(chosen, 1.0, 0.0))[:, :vector_size]
    start = rank * bias_size
    chosen = (row == lane + lax.rem(start, width)) & (lane < bias_size)
    tail = dot(small[8:16, :], jnp.where(chosen, 1.0, 0.0))
    tail_row = lax.broadcasted_iota(jnp.int32, tail.shape, 0)
    tail = jnp.sum(jnp.where(tail_row == lax.div(start, width), tail, 0.0), axis=0, keepdims=True)
    return vector_grad, tail[:, :bias_size]


def scatters_of(here, slots, grads, buffers, shares, own_sem, splits):
    count = len(grads)
    found, loads = [], []
    for index, (grad, share) in enumerate(zip(grads, shares)):
        own, *arrivals = buffers[index::count]
        load = lambda grad=grad, own=own, index=index: pltpu.make_async_copy(
            grad.at[:, here.core], own, own_sem.at[index]
        )
        loads.append(load)
        for order, pieces in enumerate(parts_of(share.shape, splits[index])):
            wait = (lambda load=load: load().wait()) if order == 0 else (lambda: None)
            found.append(Scatter(here, slots, grad, own, *arrivals, share, pieces, wait))
    return found, loads


def scatter_buffers(shapes, counts):
    half_count, seq_count = counts[0] // 2, counts[1]
    leads = [(half_count, seq_count)] * 2 + [(seq_count - 1, half_count), (half_count - 1,)]
    return [pltpu.VMEM(lead + shape, BRAIN) for lead in leads for shape in shapes]


def scatter_views(grads, shapes, counts):
    lead = (counts[0] // 2, 2, counts[1])
    return [grad.reshape(lead + shape) for grad, shape in zip(grads, shapes)]


class SmallSum(Transfer):
    def __init__(self, here, small, sums, arrived, send_sem, recv_sem):
        self.slots = Slots(send_sem, recv_sem)
        self.small, self.sums, self.arrived = small, sums, arrived
        self.peers = [here.core_peer()]
        self.peers += [{"dp": flipped(here.place, bit + 1)} for bit in range(bits_of(here.half_count))]
        self.peers += [here.line_peer(bit) for bit in range(here.seq_bits)]
        self.stages = len(self.peers)

    def copies(self, stage):
        source = self.sums.at[stage - 1] if stage else self.small
        return [self.slots.copy(stage, source, self.arrived.at[stage], self.peers[stage])]

    def use(self, stage):
        before = self.sums[stage - 1] if stage else self.small[...]
        self.sums[stage] = before + self.arrived[stage]


def scatter_kernel(counts, splits, *refs):
    grads, small, input_rows = refs[0:2], refs[2], refs[3]
    ready = refs[4:6]
    weights, firsts, seconds = refs[6:12], refs[12:18], refs[18:24]
    shares, norm_out, input_grad = refs[24:28], refs[28], refs[29]
    buffers, bounce = refs[30:38], refs[38]
    small_sum, small_in, norm_mine, norm_dp, norm_line, norm_seq = refs[39:45]
    send_sem, recv_sem, own_sem, move_sem, small_send, small_recv, norm_send, norm_recv = refs[45:53]
    here = Here(*counts)
    slots = Slots(send_sem, recv_sem)
    scatters, loads = scatters_of(here, slots, grads, buffers, shares[0:2], own_sem, splits)
    move = Exchange(here, slots, input_rows, input_grad, False, bounce, move_sem)
    total = SmallSum(here, small, small_sum, small_in, small_send, small_recv)
    for load in loads:
        load().start()
    dp_peers, seq_peers = here.all_peers()[: here.dp_count - 1], here.all_peers()[here.dp_count - 1 :]
    greet(dp_peers + seq_peers)
    waves = waves_of(scatters)
    more = waves_of([total])
    for turn in range(max(len(waves), len(more))):
        if turn < len(waves):
            waves[turn]()
        if turn < len(more):
            more[turn]()
        if turn == 1:
            move.start(0)

    rank = here.place * here.seq_count + here.line
    vector_grad, bias_grad = picked(
        small_sum[total.stages - 1], rank, shares[2].shape[1], shares[3].shape[1]
    )
    shares[2][...] = vector_grad
    shares[3][...] = bias_grad
    grads_now = [shares[0], shares[1], ready[0], ready[1], shares[2], shares[3]]

    lane = lax.broadcasted_iota(jnp.int32, (8, 128), 1)
    row = lax.broadcasted_iota(jnp.int32, (8, 128), 0)
    tile = jnp.zeros((8, 128), FLOAT)
    for index in (0, 1, 2, 3, 5):
        decay = DECAY_RATE if index < 4 else 0.0
        weight = weights[index][...]
        update = lamb_pieces(
            weight, firsts[index][...], seconds[index][...], grads_now[index][...], decay
        )[2]
        at = row == (index if index < 4 else 4)
        tile = jnp.where(at & (lane == 0), square_sum(weight), tile)
        tile = jnp.where(at & (lane == 1), square_sum(update), tile)
    norm_mine[0:8, :] = tile
    weight = weights[4][...]
    update = lamb_pieces(weight, firsts[4][...], seconds[4][...], vector_grad, 0.0)[2]
    weight_sq = jnp.sum(weight * weight, axis=1, keepdims=True)
    update_sq = jnp.sum(update * update, axis=1, keepdims=True)
    norm_mine[8:16, :] = jnp.where(lane == 0, weight_sq, jnp.where(lane == 1, update_sq, 0.0))

    norm_slots = Slots(norm_send, norm_recv)

    def exchange(source, held, peers, at):
        base = norm_slots.take(len(peers))
        copies = [
            norm_slots.copy(base + turn, source, held.at[at], peer) for turn, peer in enumerate(peers)
        ]
        for copy in copies:
            copy.start()
        held[at] = source[...]
        for copy in copies:
            copy.wait_recv()
        found = held[0]
        for turn in range(1, held.shape[0]):
            found = found + held[turn]
        return copies, found

    sent, found = exchange(norm_mine, norm_dp, dp_peers, here.place)
    norm_line[...] = found
    also, found = exchange(norm_line, norm_seq, seq_peers, here.line)
    norm_out[...] = found
    move.finish(0)
    for copy in sent + also:
        copy.wait_send()
    drain_all(scatters + [total, move])


def scatter_last(grads, small, input_rows, ready, weights, firsts, seconds, counts):
    dp_count, seq_count = counts
    shapes = [weight.shape for weight in weights]
    splits = [False, False]
    slots = slot_count(counts, shapes[:2], splits, 1)
    stages = bits_of(dp_count) + bits_of(seq_count)
    return pl.pallas_call(
        functools.partial(scatter_kernel, counts, splits),
        out_shape=[jax.ShapeDtypeStruct(shapes[at], FLOAT) for at in (0, 1, 4, 5)]
        + [
            jax.ShapeDtypeStruct((16, 128), FLOAT),
            jax.ShapeDtypeStruct((seq_count,) + input_rows.shape[0:1] + input_rows.shape[2:], BRAIN),
        ],
        in_specs=[ANYWHERE] * 2 + [WHOLE] + [ANYWHERE] + [WHOLE] * 20,
        out_specs=[WHOLE] * 5 + [ANYWHERE],
        scratch_shapes=scatter_buffers(shapes[:2], counts)
        + [
            pltpu.VMEM(input_rows.shape[0:1] + input_rows.shape[2:], BRAIN),
            pltpu.VMEM((stages,) + small.shape, FLOAT),
            pltpu.VMEM((stages,) + small.shape, FLOAT),
            pltpu.VMEM((16, 128), FLOAT),
            pltpu.VMEM((dp_count, 16, 128), FLOAT),
            pltpu.VMEM((16, 128), FLOAT),
            pltpu.VMEM((seq_count, 16, 128), FLOAT),
            pltpu.SemaphoreType.DMA((slots,)),
            pltpu.SemaphoreType.DMA((slots,)),
            pltpu.SemaphoreType.DMA((2,)),
            pltpu.SemaphoreType.DMA((2,)),
            pltpu.SemaphoreType.DMA((stages,)),
            pltpu.SemaphoreType.DMA((stages,)),
            pltpu.SemaphoreType.DMA((dp_count + seq_count,)),
            pltpu.SemaphoreType.DMA((dp_count + seq_count,)),
        ],
        name="scatter_last",
        compiler_params=pltpu.CompilerParams(
            collective_id=3, has_side_effects=True, vmem_limit_bytes=56 * 1024 * 1024
        ),
    )(*scatter_views(grads, shapes, counts), small, input_rows, *ready, *weights, *firsts, *seconds)


def lamb_kernel(*refs):
    grads, norms = refs[0:6], refs[6]
    weights, firsts, seconds = refs[7:13], refs[13:19], refs[19:25]
    grad_out, first_out, second_out, new_out = refs[25:31], refs[31:37], refs[37:43], refs[43:49]
    copy_out = refs[49:53]
    weight_norm = jnp.sqrt(norms[:, 0:1])
    scales = weight_norm / (jnp.sqrt(norms[:, 1:2]) + ADAM_EPS)
    for index in range(6):
        grad = grads[index][...]
        weight = weights[index][...]
        decay = DECAY_RATE if index < 4 else 0.0
        first_new, second_new, update = lamb_pieces(
            weight, firsts[index][...], seconds[index][...], grad, decay
        )
        scale = scales[8:16] if index == 4 else scales[min(index, 4) : min(index, 4) + 1]
        new = weight - LEARN_RATE * scale * update
        grad_out[index][...] = grad
        first_out[index][...] = first_new
        second_out[index][...] = second_new
        new_out[index][...] = new
        if index < 4:
            copy_out[index][...] = new.astype(BRAIN)


def lamb_all(grads, norms, weights, firsts, seconds):
    vmem = pl.BlockSpec(memory_space=pltpu.VMEM)
    shapes = [jax.ShapeDtypeStruct(weight.shape, FLOAT) for weight in weights]
    copies = [jax.ShapeDtypeStruct(weight.shape, BRAIN) for weight in weights[:4]]
    return pl.pallas_call(
        lamb_kernel,
        out_shape=shapes * 4 + copies,
        in_specs=[vmem] * 25,
        out_specs=[vmem] * 28,
        name="lamb_update",
        compiler_params=pltpu.CompilerParams(vmem_limit_bytes=48 * 1024 * 1024),
    )(*grads, norms, *weights, *firsts, *seconds)


def body(
    tokens,
    cotangent,
    segment_ids,
    w_qkv,
    m_qkv,
    v_qkv,
    w_out,
    m_out,
    v_out,
    w_up,
    m_up,
    v_up,
    w_down,
    m_down,
    v_down,
    vectors,
    m_vectors,
    v_vectors,
    up_bias,
    m_up_bias,
    v_up_bias,
):
    dp_count, seq_count = lax.axis_size("dp"), lax.axis_size("seq")
    vector_size, bias_size = vectors.shape[1], up_bias.shape[0]
    small = jnp.concatenate(
        [
            jnp.pad(vectors, ((0, 0), (0, 128 - vector_size))),
            jnp.pad(up_bias[None], ((0, 7), (0, 128 - bias_size))),
        ]
    )
    shards = [part.astype(BRAIN) for part in (small, w_qkv, w_out, w_up, w_down)]
    counts = (dp_count, seq_count)
    token_rows, *fulls = gather_first(tokens, shards[:3], counts)
    small = fulls[0].reshape(dp_count * seq_count, 16, 128)
    full_vectors = small[:, :8, :vector_size].transpose(1, 0, 2)
    vector_rows = full_vectors.reshape(8, -1).astype(FLOAT)
    up_shift = small[:, 8, :bias_size].reshape(-1).astype(FLOAT)
    as_matrix = lambda full: full.reshape(-1, full.shape[-1])
    full_qkv, full_out = as_matrix(fulls[1]), as_matrix(fulls[2])

    width = tokens.shape[2]
    length = segment_ids.shape[1]
    rows = token_rows.shape[0]
    segments = lax.dynamic_slice_in_dim(segment_ids, lax.axis_index("seq") * rows, rows, 0)
    count = rows * length
    token_part = token_rows.reshape(count, width).astype(FLOAT)

    normed_one, plain_one, inverse_one = norm_forward(token_part, vector_rows[0], vector_rows[1])
    low_one = normed_one.astype(BRAIN)
    shifts = jnp.concatenate([vector_rows[4], jnp.zeros_like(vector_rows[4]), vector_rows[5]])
    qkv = (matmul(low_one, full_qkv) + shifts).astype(BRAIN)
    context, lse_rows, back_rows, *fulls = attention_forward(
        segments, qkv, length, cotangent, shards[3:], counts
    )
    full_up, full_down = as_matrix(fulls[0]), as_matrix(fulls[1])
    back_part = back_rows.reshape(count, width)
    resid_one = token_part + matmul(context, full_out) + vector_rows[6]
    normed_two, plain_two, inverse_two = norm_forward(resid_one, vector_rows[2], vector_rows[3])
    low_two = normed_two.astype(BRAIN)
    hidden_pre = matmul(low_two, full_up) + up_shift
    activated, gelu_pull = jax.vjp(gelu_tanh, hidden_pre)
    low_act = activated.astype(BRAIN)
    result = resid_one + matmul(low_act, full_down) + vector_rows[7]

    back_float = back_part.astype(FLOAT)
    grad_down = inner_rows(low_act, back_part)
    act_grad = times_transposed(back_part, full_down)
    hidden_grad = gelu_pull(act_grad)[0].astype(BRAIN)
    grad_up = inner_rows(low_two, hidden_grad)
    grad_up_bias = jnp.sum(hidden_grad.astype(FLOAT), axis=0)
    two_grad = times_transposed(hidden_grad, full_up)
    resid_grad = back_float + norm_backward(two_grad, plain_two, inverse_two, vector_rows[2])
    branch_grad = resid_grad.astype(BRAIN)
    grad_out = inner_rows(context, branch_grad)
    context_grad = times_transposed(branch_grad, full_out).astype(BRAIN)
    joined, mixed, share_up, share_down = attention_backward(
        segments,
        qkv,
        context_grad,
        lse_rows,
        length,
        result.astype(BRAIN),
        [grad_up.astype(BRAIN), grad_down.astype(BRAIN)],
        [w_up.shape, w_down.shape],
        counts,
    )
    grad_qkv = inner_rows(low_one, joined)
    one_grad = times_transposed(joined, full_qkv)
    input_rows = resid_grad + norm_backward(one_grad, plain_one, inverse_one, vector_rows[0])
    joined_sum = jnp.sum(joined.astype(FLOAT), axis=0)
    grad_vectors = jnp.stack(
        [
            jnp.sum(one_grad * plain_one, axis=0),
            jnp.sum(one_grad, axis=0),
            jnp.sum(two_grad * plain_two, axis=0),
            jnp.sum(two_grad, axis=0),
            joined_sum[:width],
            joined_sum[2 * width :],
            jnp.sum(branch_grad.astype(FLOAT), axis=0),
            jnp.sum(back_float, axis=0),
        ]
    )
    small_grad = jnp.concatenate([grad_vectors, grad_up_bias.reshape(-1, width)])
    small_grad = jnp.pad(small_grad, ((0, 16 - small_grad.shape[0]), (0, 0)))
    as_row = lambda value: value.reshape(1, -1)
    weights = (w_qkv, w_out, w_up, w_down, vectors, as_row(up_bias))
    firsts = (m_qkv, m_out, m_up, m_down, m_vectors, as_row(m_up_bias))
    seconds = (v_qkv, v_out, v_up, v_down, v_vectors, as_row(v_up_bias))
    share_qkv, share_out, share_vectors, share_bias, norms, input_grad = scatter_last(
        [grad_qkv.astype(BRAIN), grad_out.astype(BRAIN)],
        small_grad,
        input_rows.astype(BRAIN).reshape(rows, seq_count, length // seq_count, width),
        [share_up, share_down],
        weights,
        firsts,
        seconds,
        counts,
    )
    shares = [share_qkv, share_out, share_up, share_down, share_vectors, share_bias]
    results = list(lamb_all(shares, norms, weights, firsts, seconds))
    mixed = mixed.reshape(tokens.shape)
    input_grad = input_grad.reshape(tokens.shape).astype(FLOAT)
    for index in (5, 11, 17, 23):
        results[index] = results[index].reshape(-1)
    return (mixed, input_grad, *results)


def solution(mesh):
    matrix = P(("dp", "seq"), None)
    rows = P("dp", "seq", None)
    vector = P(None, ("dp", "seq"))
    bias = P(("dp", "seq"))
    six = (matrix, matrix, matrix, matrix, vector, bias)
    in_specs = (rows, rows, P("dp", None)) + tuple(spec for spec in six for _ in range(3))
    out_specs = (rows, rows) + six * 4 + (matrix,) * 4
    return jax.shard_map(body, mesh=mesh, in_specs=in_specs, out_specs=out_specs, check_vma=False)
```

```python
import functools

import jax
import jax.numpy as jnp
from jax import lax
from jax.experimental import pallas as pl
from jax.experimental.pallas import tpu as pltpu
from jax.sharding import PartitionSpec as P

HEADS = 12
HEAD_DIM = 64
LONGEST = 512
QUERY_BLOCK = 256


BETA_ONE = 0.9
BETA_TWO = 0.999
ADAM_EPS = 1e-06
DECAY_RATE = 0.01
LEARN_RATE = 0.4
NORM_EPS = 1e-05
STEP_NUMBER = 10.0
CORR_ONE = 1.0 - BETA_ONE**STEP_NUMBER
CORR_TWO = 1.0 - BETA_TWO**STEP_NUMBER

BRAIN = jnp.bfloat16
FLOAT = jnp.float32


def matmul(left_side, right_side):
    return jnp.dot(left_side, right_side, preferred_element_type=FLOAT)


def inner_rows(left_side, right_side):
    return lax.dot_general(
        left_side, right_side, (((0,), (0,)), ((), ())), preferred_element_type=FLOAT
    )


def times_transposed(left_side, right_side):
    return lax.dot_general(
        left_side, right_side, (((1,), (1,)), ((), ())), preferred_element_type=FLOAT
    )


def gelu_tanh(values):
    return jax.nn.gelu(values, approximate=True)


def norm_forward(values, norm_gain, norm_shift):
    center = values - jnp.mean(values, axis=-1, keepdims=True)
    inverse = lax.rsqrt(jnp.mean(center * center, axis=-1, keepdims=True) + NORM_EPS)
    normed = center * inverse
    return (normed * norm_gain + norm_shift, normed, inverse)


def norm_backward(upstream, normed, inverse, norm_gain):
    scaled = upstream * norm_gain
    centered = scaled - jnp.mean(scaled, axis=-1, keepdims=True)
    return inverse * (centered - normed * jnp.mean(scaled * normed, axis=-1, keepdims=True))


def windows(length):
    return [
        (max(0, first - LONGEST), first + QUERY_BLOCK) for first in range(0, length, QUERY_BLOCK)
    ]


def fill_bias(seg_col, seg_row, bias, length):
    place = 0
    for index, (low, high) in enumerate(windows(length)):
        first = index * QUERY_BLOCK
        size = high - low
        keys = seg_col[0, low:high, :]
        queries = seg_row[0, :, first : first + QUERY_BLOCK]
        key_place = low + lax.broadcasted_iota(jnp.int32, (size, QUERY_BLOCK), 0)
        query_place = first + lax.broadcasted_iota(jnp.int32, (size, QUERY_BLOCK), 1)
        allowed = (keys == queries) & (key_place <= query_place)
        bias[place : place + size, :] = jnp.where(allowed, 0.0, -1000000000.0)
        place += size


def split_heads(pair):
    lane = lax.broadcasted_iota(jnp.int32, pair.shape, 1)
    zero = jnp.zeros_like(pair)
    return (jnp.where(lane < HEAD_DIM, pair, zero), jnp.where(lane < HEAD_DIM, zero, pair))


def attend_forward(counts, splits, *refs):
    seg_col, seg_row, q_ref, k_ref, v_ref = refs[0:5]
    shards, c_ref, lse_ref, fulls = refs[5:8], refs[8], refs[9], refs[10:13]
    bias, bounces, send_sem, recv_sem, own_sem = refs[13], refs[14:17], *refs[17:]
    length = q_ref.shape[0]
    here = Here(*counts)
    slots = Slots(send_sem, recv_sem)
    gathers = gathers_of(here, slots, shards, fulls, bounces, own_sem, splits)
    groups = [gathers[:2]] + [[each] for each in gathers[2:]]
    waves = led_by(lambda: greet(here.near_peers()), waves_of(groups))
    blocks = windows(length)
    beside = Beside(waves, HEADS // 2 * len(blocks))

    @pl.when(pl.program_id(1) == 0)
    def _():
        fill_bias(seg_col, seg_row, bias, length)

    v_turned = v_ref[...].T
    place = 0
    for index, (low, high) in enumerate(blocks):
        beside.point(index, len(blocks))
        first = index * QUERY_BLOCK
        size = high - low
        queries = split_heads(q_ref[first : first + QUERY_BLOCK, :] * HEAD_DIM ** (-0.5))
        keys = k_ref[low:high, :]
        blocked = bias[place : place + size, :]
        parts = []
        for head in range(2):
            scores = times_transposed(keys, queries[head]) + blocked
            peak = jnp.max(scores, axis=0, keepdims=True)
            probs = jnp.exp(scores - peak)
            total = jnp.sum(probs, axis=0, keepdims=True)
            probs = (probs * (1.0 / total)).astype(BRAIN)
            lse_ref[0, 0, head : head + 1, first : first + QUERY_BLOCK] = peak + jnp.log(total)
            turned = v_turned[head * HEAD_DIM : (head + 1) * HEAD_DIM, low:high]
            parts.append(matmul(turned, probs))
        context = jnp.concatenate(parts, axis=0).T
        c_ref[first : first + QUERY_BLOCK, :] = context.astype(BRAIN)
        place += size

    @pl.when((pl.program_id(0) == pl.num_programs(0) - 1) & (pl.program_id(1) == HEADS // 2 - 1))
    def _():
        beside.rest()
        drain_all(gathers)


def led_by(ahead, waves):
    def both():
        ahead()
        waves[0]()

    return [both] + waves[1:]


class Beside:
    def __init__(self, waves, points):
        self.at = {}
        early = len(waves) - 1
        for index in range(early):
            self.at.setdefault(index * points // early, []).append(waves[index])
        self.late = waves[early:]

    def point(self, index, per_step):
        for point, calls in self.at.items():
            if point % per_step == index:

                @pl.when((pl.program_id(0) == 0) & (pl.program_id(1) == point // per_step))
                def _(calls=calls):
                    for call in calls:
                        call()

    def rest(self):
        for call in self.late:
            call()


def attend_backward(counts, splits, *refs):
    seg_col, seg_row, q_ref, k_ref, v_ref, g_ref, lse_ref = refs[0:7]
    grads, out_ref, shares = refs[7:10], refs[10], refs[11:14]
    bias, key_sum, value_sum = refs[14:17]
    buffers, send_sem, recv_sem, own_sem = refs[17:29], *refs[29:]
    length = q_ref.shape[0]
    pair = pl.program_id(1)
    here = Here(*counts)
    slots = Slots(send_sem, recv_sem)
    scatters, loads = scatters_of(here, slots, grads, buffers, shares, own_sem, splits)

    def begin():
        for load in loads:
            load().start()
        greet(here.near_peers())

    groups = [[each] for each in scatters[:-2]] + [scatters[-2:]]
    waves = led_by(begin, waves_of(groups))
    blocks = windows(length)
    beside = Beside(waves, HEADS // 2 * len(blocks))

    @pl.when(pair == 0)
    def _():
        fill_bias(seg_col, seg_row, bias, length)

    key_sum[...] = jnp.zeros_like(key_sum)
    value_sum[...] = jnp.zeros_like(value_sum)
    width = HEADS * HEAD_DIM
    k_turned = k_ref[...].T
    lanes = 2 * HEAD_DIM
    column = pl.multiple_of(pair * lanes, lanes)
    place = 0
    for index, (low, high) in enumerate(blocks):
        beside.point(index, len(blocks))
        first = index * QUERY_BLOCK
        size = high - low
        rows = slice(first, first + QUERY_BLOCK)
        queries = split_heads(q_ref[rows, :] * HEAD_DIM ** (-0.5))
        grads = split_heads(g_ref[rows, :])
        keys = k_ref[low:high, :]
        values = v_ref[low:high, :]
        blocked = bias[place : place + size, :]
        all_probs = []
        all_scores = []
        parts = []
        for head in range(2):
            scores = times_transposed(keys, queries[head]) + blocked
            probs = jnp.exp(scores - lse_ref[0, 0, head : head + 1, rows])
            prob_grad = times_transposed(values, grads[head])
            row_dot = jnp.sum(probs * prob_grad, axis=0, keepdims=True)
            score_grad = (probs * (prob_grad - row_dot)).astype(BRAIN)
            all_probs.append(probs.astype(BRAIN))
            all_scores.append(score_grad)
            turned = k_turned[head * HEAD_DIM : (head + 1) * HEAD_DIM, low:high]
            parts.append(matmul(turned, score_grad))
        query_grad = jnp.concatenate(parts, axis=0).T * HEAD_DIM ** (-0.5)
        out_ref[rows, pl.ds(column, lanes)] = query_grad.astype(BRAIN)
        value_sum[low:high, :] += matmul(
            jnp.concatenate(all_probs, axis=1), jnp.concatenate(grads, axis=0)
        )
        key_sum[low:high, :] += matmul(
            jnp.concatenate(all_scores, axis=1), jnp.concatenate(queries, axis=0)
        )
        place += size
    out_ref[:, pl.ds(width + column, lanes)] = key_sum[...].astype(BRAIN)
    out_ref[:, pl.ds(2 * width + column, lanes)] = value_sum[...].astype(BRAIN)

    @pl.when((pl.program_id(0) == pl.num_programs(0) - 1) & (pair == HEADS // 2 - 1))
    def _():
        beside.rest()
        drain_all(scatters)


def attention_specs(length):
    lanes = 2 * HEAD_DIM
    pairs = HEADS // 2
    spec = lambda shift: pl.BlockSpec((length, lanes), lambda r, j: (r, shift * pairs + j))
    segs = [
        pl.BlockSpec((1, length, 1), lambda r, j: (r, 0, 0)),
        pl.BlockSpec((1, 1, length), lambda r, j: (r, 0, 0)),
    ]
    lse = pl.BlockSpec((1, 1, 8, length), lambda r, j: (r, j, 0, 0))
    plain = pl.BlockSpec((length, lanes), lambda r, j: (r, j))
    bias = pltpu.VMEM((sum(high - low for low, high in windows(length)), QUERY_BLOCK), FLOAT)
    return segs, [spec(0), spec(1), spec(2)], plain, lse, bias


def attention_forward(segments, qkv, length, shards, counts):
    rows = segments.shape[0]
    segs, qkv_specs, plain, lse, bias = attention_specs(length)
    width = HEADS * HEAD_DIM
    splits = [False] + [True] * (len(shards) - 1)
    slots = slot_count(counts, [shard.shape for shard in shards], splits, 0)
    return pl.pallas_call(
        functools.partial(attend_forward, counts, splits),
        grid=(rows, HEADS // 2),
        in_specs=segs + qkv_specs + [ANYWHERE] * 3,
        out_specs=[plain, lse] + [ANYWHERE] * 3,
        out_shape=[
            jax.ShapeDtypeStruct((rows * length, width), BRAIN),
            jax.ShapeDtypeStruct((rows, HEADS // 2, 8, length), FLOAT),
        ]
        + [full_shape(shard, *counts) for shard in shards],
        scratch_shapes=[bias]
        + [pltpu.VMEM(shard.shape, shard.dtype) for shard in shards]
        + [
            pltpu.SemaphoreType.DMA((slots,)),
            pltpu.SemaphoreType.DMA((slots,)),
            pltpu.SemaphoreType.DMA((2 * len(shards),)),
        ],
        name="attend_forward",
        compiler_params=pltpu.CompilerParams(
            collective_id=1, has_side_effects=True, vmem_limit_bytes=48 * 1024 * 1024
        ),
    )(segments[:, :, None], segments[:, None, :], qkv, qkv, qkv, *shards)


def attention_backward(segments, qkv, context_grad, lse_rows, length, grads, shapes, counts):
    rows = segments.shape[0]
    segs, qkv_specs, plain, lse, bias = attention_specs(length)
    width = HEADS * HEAD_DIM
    splits = [True] * (len(shapes) - 1) + [False]
    slots = slot_count(counts, shapes, splits, 0)
    return pl.pallas_call(
        functools.partial(attend_backward, counts, splits),
        grid=(rows, HEADS // 2),
        in_specs=segs + qkv_specs + [plain, lse] + [ANYWHERE] * 3,
        out_specs=[pl.BlockSpec((length, 3 * width), lambda r, j: (r, 0))] + [WHOLE] * 3,
        out_shape=[
            jax.ShapeDtypeStruct((rows * length, 3 * width), BRAIN),
        ]
        + [jax.ShapeDtypeStruct(shape, FLOAT) for shape in shapes],
        scratch_shapes=[
            bias,
            pltpu.VMEM((length, 2 * HEAD_DIM), FLOAT),
            pltpu.VMEM((length, 2 * HEAD_DIM), FLOAT),
        ]
        + scatter_buffers(shapes, counts)
        + [
            pltpu.SemaphoreType.DMA((slots,)),
            pltpu.SemaphoreType.DMA((slots,)),
            pltpu.SemaphoreType.DMA((len(shapes),)),
        ],
        name="attend_backward",
        compiler_params=pltpu.CompilerParams(
            collective_id=2, has_side_effects=True, vmem_limit_bytes=62 * 1024 * 1024
        ),
    )(
        segments[:, :, None],
        segments[:, None, :],
        qkv,
        qkv,
        qkv,
        context_grad,
        lse_rows,
        *scatter_views(grads, shapes, counts),
    )


MESH = pl.DeviceIdType.MESH
ANYWHERE = pl.BlockSpec(memory_space=pl.ANY)
WHOLE = pl.BlockSpec(memory_space=pltpu.VMEM)


def bits_of(count):
    return count.bit_length() - 1


def flipped(value, bit):
    step = 1 << bit
    return value + step * (1 - 2 * lax.rem(lax.div(value, step), 2))


def rounded_down(value, bit):
    return lax.div(value, 1 << bit) * (1 << bit)


def spread(value, bit, total):
    step = 1 << (bit + 1)
    return [lax.rem(value, step) + step * turn for turn in range(1 << (total - 1 - bit))]


class Here:
    def __init__(self, dp_count, seq_count):
        self.dp_count, self.seq_count = dp_count, seq_count
        self.half_count = dp_count // 2
        self.seq_bits = bits_of(seq_count)
        self.place, self.line = lax.axis_index("dp"), lax.axis_index("seq")
        self.chip, self.core = lax.div(self.place, 2), lax.rem(self.place, 2)

    def core_peer(self):
        return {"dp": flipped(self.place, 0)}

    def line_peer(self, bit):
        return {"seq": flipped(self.line, bit)}

    def other_lines(self):
        return [lax.rem(self.line + turn, self.seq_count) for turn in range(1, self.seq_count)]

    def other_chips(self):
        return [lax.rem(self.chip + turn, self.half_count) for turn in range(1, self.half_count)]

    def chip_peers(self):
        return [{"dp": 2 * chip + self.core} for chip in self.other_chips()]

    def near_peers(self):
        peers = [self.core_peer()] + self.chip_peers()
        return peers + [{"seq": line} for line in self.other_lines()]

    def all_peers(self):
        peers = [{"dp": lax.rem(self.place + turn, self.dp_count)} for turn in range(1, self.dp_count)]
        return peers + [{"seq": line} for line in self.other_lines()]


def greet(peers):
    barrier = pltpu.get_barrier_semaphore()
    for peer in peers:
        pl.semaphore_signal(barrier, inc=1, device_id=peer, device_id_type=MESH)
    pl.semaphore_wait(barrier, len(peers))


class Slots:
    def __init__(self, send_sem, recv_sem):
        self.send_sem, self.recv_sem, self.used = send_sem, recv_sem, 0

    def take(self, count):
        first = self.used
        self.used += count
        return first

    def copy(self, slot, source, target, peer):
        return pltpu.make_async_remote_copy(
            source,
            target,
            self.send_sem.at[slot],
            self.recv_sem.at[slot],
            device_id=peer,
            device_id_type=MESH,
        )


def parts_of(shape, split):
    rows, width = shape
    tiles = width // 128
    if width % 128 or tiles < 2:
        return [[(slice(0, rows), slice(0, width), False)]]
    middle = tiles // 2 * 128
    first, second = (0, middle), (middle, width)
    every = slice(0, rows)
    if split and rows % 32 == 0:
        return [
            [(part, slice(*first), False), (part, slice(*second), True)]
            for part in (slice(0, rows // 2), slice(rows // 2, rows))
        ]
    if split and tiles >= 4:
        lists = [[], []]
        for (low, high), backwards in ((first, False), (second, True)):
            cut = low + (high - low) // 256 * 128
            lists[0].append((every, slice(low, cut), backwards))
            lists[1].append((every, slice(cut, high), backwards))
        return lists
    return [[(every, slice(*first), False), (every, slice(*second), True)]]


class Transfer:
    def start(self, stage):
        for copy in self.copies(stage):
            copy.start()

    def finish(self, stage):
        for copy in self.copies(stage):
            copy.wait_recv()
        self.use(stage)

    def use(self, stage):
        pass

    def drain(self):
        for stage in range(self.stages):
            for copy in self.copies(stage):
                copy.wait_send()


class Gather(Transfer):
    def __init__(self, here, slots, shard, full, pieces, own_done):
        self.here, self.slots, self.shard, self.full = here, slots, shard, full
        self.pieces, self.own_done = pieces, own_done
        self.stages = here.seq_bits + 2
        self.each = here.half_count + here.seq_count
        self.first = slots.take(self.each * len(pieces))

    def copies(self, stage):
        here, full = self.here, self.full
        found = []
        for index, (rows, columns, backwards) in enumerate(self.pieces):
            slot = self.first + self.each * index
            if stage == 0:
                target = full.at[here.chip, here.core, here.line, rows, columns]
                for turn, peer in enumerate(here.chip_peers()):
                    source = self.shard.at[rows, columns]
                    found.append(self.slots.copy(slot + turn, source, target, peer))
                continue
            slot += here.half_count - 1
            if stage == self.stages - 1:
                part = full.at[:, here.core, :, rows, columns]
                slot += here.seq_count - 1
                found.append(self.slots.copy(slot, part, part, here.core_peer()))
                continue
            if backwards:
                bit = here.seq_bits - stage
                slot += (1 << (stage - 1)) - 1
                parts = [
                    full.at[:, here.core, at, rows, columns]
                    for at in spread(here.line, bit, here.seq_bits)
                ]
            else:
                bit = stage - 1
                slot += bit
                block = pl.ds(rounded_down(here.line, bit), 1 << bit)
                parts = [full.at[:, here.core, block, rows, columns]]
            for turn, part in enumerate(parts):
                found.append(self.slots.copy(slot + turn, part, part, here.line_peer(bit)))
        return found

    def start(self, stage):
        if stage == 1:
            self.own_done()
        super().start(stage)


class Scatter(Transfer):
    def __init__(self, here, slots, grad, own, from_core, from_line, from_chip, share, pieces, load):
        self.here, self.slots, self.grad, self.own = here, slots, grad, own
        self.from_core, self.from_line, self.from_chip = from_core, from_line, from_chip
        self.share, self.pieces, self.load = share, pieces, load
        self.stages = here.seq_bits + 2
        self.each = here.half_count + here.seq_count
        self.first = slots.take(self.each * len(pieces))

    def line_stage(self, stage, backwards):
        here = self.here
        if backwards:
            bit = stage - 1
            away = spread(flipped(here.line, bit), bit, here.seq_bits)
            kept = spread(here.line, bit, here.seq_bits)
        else:
            bit = here.seq_bits - stage
            away = [rounded_down(flipped(here.line, bit), bit) + at for at in range(1 << bit)]
            kept = [rounded_down(here.line, bit) + at for at in range(1 << bit)]
        base = sum(1 << (here.seq_bits - past) for past in range(1, stage))
        return bit, away, kept, base

    def copies(self, stage):
        here = self.here
        found = []
        for index, (rows, columns, backwards) in enumerate(self.pieces):
            slot = self.first + self.each * index
            if stage == 0:
                found.append(
                    self.slots.copy(
                        slot,
                        self.grad.at[:, 1 - here.core, :, rows, columns],
                        self.from_core.at[:, :, rows, columns],
                        here.core_peer(),
                    )
                )
            elif stage == self.stages - 1:
                slot += here.seq_count
                for turn, chip in enumerate(here.other_chips()):
                    found.append(
                        self.slots.copy(
                            slot + turn,
                            self.own.at[chip, here.line, rows, columns],
                            self.from_chip.at[turn, rows, columns],
                            {"dp": 2 * chip + here.core},
                        )
                    )
            else:
                bit, away, _, base = self.line_stage(stage, backwards)
                for turn, at in enumerate(away):
                    found.append(
                        self.slots.copy(
                            slot + 1 + base + turn,
                            self.own.at[:, at, rows, columns],
                            self.from_line.at[base + turn, :, rows, columns],
                            here.line_peer(bit),
                        )
                    )
        return found

    def use(self, stage):
        here, own = self.here, self.own
        if stage == 0:
            self.load()
        for rows, columns, backwards in self.pieces:
            if stage == 0:

                def add(at, carry, rows=rows, columns=columns):
                    one, two = lax.div(at, here.seq_count), lax.rem(at, here.seq_count)
                    own[one, two, rows, columns] = (
                        own[one, two, rows, columns] + self.from_core[one, two, rows, columns]
                    )
                    return carry

                lax.fori_loop(0, here.half_count * here.seq_count, add, 0)
            elif stage == self.stages - 1:
                total = own[here.chip, here.line, rows, columns].astype(FLOAT)
                for turn in range(here.half_count - 1):
                    total = total + self.from_chip[turn, rows, columns].astype(FLOAT)
                self.share[rows, columns] = total
            else:
                _, _, kept, base = self.line_stage(stage, backwards)
                for turn, at in enumerate(kept):

                    def add(one, carry, rows=rows, columns=columns, at=at, place=base + turn):
                        own[one, at, rows, columns] = (
                            own[one, at, rows, columns] + self.from_line[place, one, rows, columns]
                        )
                        return carry

                    lax.fori_loop(0, here.half_count, add, 0)


class Exchange(Transfer):
    stages = 1

    def __init__(self, here, slots, source, target, to_rows, bounce, sem):
        self.here, self.slots, self.source, self.target = here, slots, source, target
        self.to_rows, self.bounce, self.sem = to_rows, bounce, sem
        self.first = slots.take(here.seq_count - 1)

    def ends(self, line):
        if self.to_rows:
            count = self.target.shape[0]
            block = self.source.at[pl.ds(line * count, count)]
            return block, self.target.at[:, self.here.line]
        return self.source.at[:, line], self.target.at[self.here.line]

    def copies(self, stage):
        return [
            self.slots.copy(self.first + turn, *self.ends(line), {"seq": line})
            for turn, line in enumerate(self.here.other_lines())
        ]

    def own_in(self):
        return pltpu.make_async_copy(self.ends(self.here.line)[0], self.bounce, self.sem.at[0])

    def own_out(self):
        return pltpu.make_async_copy(self.bounce, self.ends(self.here.line)[1], self.sem.at[1])

    def start(self, stage):
        self.own_in().start()
        super().start(stage)
        self.own_in().wait()
        self.own_out().start()

    def use(self, stage):
        self.own_out().wait()


def waves_of(groups):
    def wave(count):
        for index, group in enumerate(groups):
            stage = count - index
            for transfer in group:
                if 1 <= stage <= transfer.stages:
                    transfer.finish(stage - 1)
            for transfer in group:
                if 0 <= stage < transfer.stages:
                    transfer.start(stage)

    total = max(index + transfer.stages for index, group in enumerate(groups) for transfer in group)
    return [functools.partial(wave, count) for count in range(total + 1)]


def drain_all(transfers):
    for transfer in transfers:
        transfer.drain()


def gathers_of(here, slots, shards, fulls, bounces, sem, splits):
    found = []
    for index, (shard, full, bounce) in enumerate(zip(shards, fulls, bounces)):
        inward = lambda shard=shard, bounce=bounce, index=index: pltpu.make_async_copy(
            shard, bounce, sem.at[2 * index]
        )
        outward = lambda full=full, bounce=bounce, index=index: pltpu.make_async_copy(
            bounce, full.at[here.chip, here.core, here.line], sem.at[2 * index + 1]
        )
        for order, pieces in enumerate(parts_of(shard.shape, splits[index])):

            def own_done(first=order == 0, inward=inward, outward=outward):
                if first:
                    inward().start()
                    inward().wait()
                    outward().start()
                    outward().wait()

            found.append(Gather(here, slots, shard, full, pieces, own_done))
    return found


def slot_count(here_shape, shapes, splits, exchanges):
    half_count, seq_count = here_shape[0] // 2, here_shape[1]
    each = half_count + seq_count
    pieces = sum(len(part) for shape, split in zip(shapes, splits) for part in parts_of(shape, split))
    return each * pieces + exchanges * (seq_count - 1)


def full_shape(shard, dp_count, seq_count):
    return jax.ShapeDtypeStruct((dp_count // 2, 2, seq_count) + shard.shape, shard.dtype)


def gather_kernel(counts, splits, count, *refs):
    tokens, shards, fulls = refs[0], refs[1 : 1 + count], refs[2 + count : 2 + 2 * count]
    token_rows = refs[1 + count]
    rest = refs[2 + 2 * count :]
    bounces, bounce, send_sem, recv_sem, own_sem, move_sem = rest[:count], *rest[count:]
    here = Here(*counts)
    slots = Slots(send_sem, recv_sem)
    gathers = gathers_of(here, slots, shards, fulls, bounces, own_sem, splits)
    move = Exchange(here, slots, tokens, token_rows, True, bounce, move_sem)
    greet(here.near_peers())
    waves = waves_of([gathers[:2]] + [[each] for each in gathers[2:]])
    waves[0]()
    move.start(0)
    for wave in waves[1:]:
        wave()
    move.finish(0)
    drain_all(gathers + [move])


def gather_first(tokens, shards, counts):
    dp_count, seq_count = counts
    row_count, pos_count, width = tokens.shape
    rows = row_count // seq_count
    splits = [True] * len(shards)
    slots = slot_count(counts, [shard.shape for shard in shards], splits, 1)
    return pl.pallas_call(
        functools.partial(gather_kernel, counts, splits, len(shards)),
        out_shape=[jax.ShapeDtypeStruct((rows, seq_count, pos_count, width), tokens.dtype)]
        + [full_shape(shard, *counts) for shard in shards],
        in_specs=[ANYWHERE] * (1 + len(shards)),
        out_specs=[ANYWHERE] * (1 + len(shards)),
        scratch_shapes=[pltpu.VMEM(shard.shape, shard.dtype) for shard in shards]
        + [
            pltpu.VMEM((rows, pos_count, width), tokens.dtype),
            pltpu.SemaphoreType.DMA((slots,)),
            pltpu.SemaphoreType.DMA((slots,)),
            pltpu.SemaphoreType.DMA((2 * len(shards),)),
            pltpu.SemaphoreType.DMA((2,)),
        ],
        name="gather_first",
        compiler_params=pltpu.CompilerParams(collective_id=0, has_side_effects=True),
    )(tokens, *shards)


def lamb_pieces(weight, first, second, grad, decay):
    first_new = BETA_ONE * first + (1.0 - BETA_ONE) * grad
    second_new = BETA_TWO * second + (1.0 - BETA_TWO) * grad * grad
    spread_out = jnp.sqrt(second_new / CORR_TWO) + ADAM_EPS
    update = first_new / CORR_ONE / spread_out + decay * weight
    return (first_new, second_new, update)


def square_sum(values):
    return jnp.sum(jnp.sum(values * values, axis=1, keepdims=True), axis=0, keepdims=True)


def picked(small, rank, vector_size, bias_size):
    width = small.shape[1]
    row = lax.broadcasted_iota(jnp.int32, (width, 128), 0)
    lane = lax.broadcasted_iota(jnp.int32, (width, 128), 1)
    dot = functools.partial(jnp.dot, precision=lax.Precision.HIGHEST, preferred_element_type=FLOAT)
    chosen = (row == lane + rank * vector_size) & (lane < vector_size)
    vector_grad = dot(small[0:8, :], jnp.where(chosen, 1.0, 0.0))[:, :vector_size]
    start = rank * bias_size
    chosen = (row == lane + lax.rem(start, width)) & (lane < bias_size)
    tail = dot(small[8:16, :], jnp.where(chosen, 1.0, 0.0))
    tail_row = lax.broadcasted_iota(jnp.int32, tail.shape, 0)
    tail = jnp.sum(jnp.where(tail_row == lax.div(start, width), tail, 0.0), axis=0, keepdims=True)
    return vector_grad, tail[:, :bias_size]


def scatters_of(here, slots, grads, buffers, shares, own_sem, splits):
    count = len(grads)
    found, loads = [], []
    for index, (grad, share) in enumerate(zip(grads, shares)):
        own, *arrivals = buffers[index::count]
        load = lambda grad=grad, own=own, index=index: pltpu.make_async_copy(
            grad.at[:, here.core], own, own_sem.at[index]
        )
        loads.append(load)
        for order, pieces in enumerate(parts_of(share.shape, splits[index])):
            wait = (lambda load=load: load().wait()) if order == 0 else (lambda: None)
            found.append(Scatter(here, slots, grad, own, *arrivals, share, pieces, wait))
    return found, loads


def scatter_buffers(shapes, counts):
    half_count, seq_count = counts[0] // 2, counts[1]
    leads = [(half_count, seq_count)] * 2 + [(seq_count - 1, half_count), (half_count - 1,)]
    return [pltpu.VMEM(lead + shape, BRAIN) for lead in leads for shape in shapes]


def scatter_views(grads, shapes, counts):
    lead = (counts[0] // 2, 2, counts[1])
    return [grad.reshape(lead + shape) for grad, shape in zip(grads, shapes)]


class SmallSum(Transfer):
    def __init__(self, here, small, sums, arrived, send_sem, recv_sem):
        self.slots = Slots(send_sem, recv_sem)
        self.small, self.sums, self.arrived = small, sums, arrived
        self.peers = [here.core_peer()]
        self.peers += [{"dp": flipped(here.place, bit + 1)} for bit in range(bits_of(here.half_count))]
        self.peers += [here.line_peer(bit) for bit in range(here.seq_bits)]
        self.stages = len(self.peers)

    def copies(self, stage):
        source = self.sums.at[stage - 1] if stage else self.small
        return [self.slots.copy(stage, source, self.arrived.at[stage], self.peers[stage])]

    def use(self, stage):
        before = self.sums[stage - 1] if stage else self.small[...]
        self.sums[stage] = before + self.arrived[stage]


def scatter_kernel(counts, splits, *refs):
    grads, small, input_rows = refs[0:1], refs[1], refs[2]
    ready = refs[3:6]
    weights, firsts, seconds = refs[6:12], refs[12:18], refs[18:24]
    shares, norm_out, input_grad = refs[24:27], refs[27], refs[28]
    buffers, bounce = refs[29:33], refs[33]
    small_sum, small_in, norm_mine, norm_dp, norm_line, norm_seq = refs[34:40]
    send_sem, recv_sem, own_sem, move_sem, small_send, small_recv, norm_send, norm_recv = refs[40:48]
    here = Here(*counts)
    slots = Slots(send_sem, recv_sem)
    scatters, loads = scatters_of(here, slots, grads, buffers, shares[0:1], own_sem, splits)
    move = Exchange(here, slots, input_rows, input_grad, False, bounce, move_sem)
    total = SmallSum(here, small, small_sum, small_in, small_send, small_recv)
    for load in loads:
        load().start()
    dp_peers, seq_peers = here.all_peers()[: here.dp_count - 1], here.all_peers()[here.dp_count - 1 :]
    greet(dp_peers + seq_peers)
    waves = waves_of([[each] for each in scatters])
    more = waves_of([[total]])
    for turn in range(max(len(waves), len(more))):
        if turn < len(waves):
            waves[turn]()
        if turn < len(more):
            more[turn]()
        if turn == here.seq_bits + 1:
            move.start(0)

    rank = here.place * here.seq_count + here.line
    vector_grad, bias_grad = picked(
        small_sum[total.stages - 1], rank, shares[1].shape[1], shares[2].shape[1]
    )
    shares[1][...] = vector_grad
    shares[2][...] = bias_grad
    grads_now = [shares[0], *ready, shares[1], shares[2]]

    lane = lax.broadcasted_iota(jnp.int32, (8, 128), 1)
    row = lax.broadcasted_iota(jnp.int32, (8, 128), 0)
    tile = jnp.zeros((8, 128), FLOAT)
    for index in (0, 1, 2, 3, 5):
        decay = DECAY_RATE if index < 4 else 0.0
        weight = weights[index][...]
        update = lamb_pieces(
            weight, firsts[index][...], seconds[index][...], grads_now[index][...], decay
        )[2]
        at = row == (index if index < 4 else 4)
        tile = jnp.where(at & (lane == 0), square_sum(weight), tile)
        tile = jnp.where(at & (lane == 1), square_sum(update), tile)
    norm_mine[0:8, :] = tile
    weight = weights[4][...]
    update = lamb_pieces(weight, firsts[4][...], seconds[4][...], vector_grad, 0.0)[2]
    weight_sq = jnp.sum(weight * weight, axis=1, keepdims=True)
    update_sq = jnp.sum(update * update, axis=1, keepdims=True)
    norm_mine[8:16, :] = jnp.where(lane == 0, weight_sq, jnp.where(lane == 1, update_sq, 0.0))

    norm_slots = Slots(norm_send, norm_recv)

    def exchange(source, held, peers, at):
        base = norm_slots.take(len(peers))
        copies = [
            norm_slots.copy(base + turn, source, held.at[at], peer) for turn, peer in enumerate(peers)
        ]
        for copy in copies:
            copy.start()
        held[at] = source[...]
        for copy in copies:
            copy.wait_recv()
        found = held[0]
        for turn in range(1, held.shape[0]):
            found = found + held[turn]
        return copies, found

    sent, found = exchange(norm_mine, norm_dp, dp_peers, here.place)
    norm_line[...] = found
    also, found = exchange(norm_line, norm_seq, seq_peers, here.line)
    norm_out[...] = found
    move.finish(0)
    for copy in sent + also:
        copy.wait_send()
    drain_all(scatters + [total, move])


def scatter_last(grads, small, input_rows, ready, weights, firsts, seconds, counts):
    dp_count, seq_count = counts
    shapes = [weight.shape for weight in weights]
    splits = [True]
    slots = slot_count(counts, shapes[:1], splits, 1)
    stages = bits_of(dp_count) + bits_of(seq_count)
    return pl.pallas_call(
        functools.partial(scatter_kernel, counts, splits),
        out_shape=[jax.ShapeDtypeStruct(shapes[at], FLOAT) for at in (0, 4, 5)]
        + [
            jax.ShapeDtypeStruct((16, 128), FLOAT),
            jax.ShapeDtypeStruct((seq_count,) + input_rows.shape[0:1] + input_rows.shape[2:], BRAIN),
        ],
        in_specs=[ANYWHERE, WHOLE, ANYWHERE] + [WHOLE] * 21,
        out_specs=[WHOLE] * 4 + [ANYWHERE],
        scratch_shapes=scatter_buffers(shapes[:1], counts)
        + [
            pltpu.VMEM(input_rows.shape[0:1] + input_rows.shape[2:], BRAIN),
            pltpu.VMEM((stages,) + small.shape, FLOAT),
            pltpu.VMEM((stages,) + small.shape, FLOAT),
            pltpu.VMEM((16, 128), FLOAT),
            pltpu.VMEM((dp_count, 16, 128), FLOAT),
            pltpu.VMEM((16, 128), FLOAT),
            pltpu.VMEM((seq_count, 16, 128), FLOAT),
            pltpu.SemaphoreType.DMA((slots,)),
            pltpu.SemaphoreType.DMA((slots,)),
            pltpu.SemaphoreType.DMA((1,)),
            pltpu.SemaphoreType.DMA((2,)),
            pltpu.SemaphoreType.DMA((stages,)),
            pltpu.SemaphoreType.DMA((stages,)),
            pltpu.SemaphoreType.DMA((dp_count + seq_count,)),
            pltpu.SemaphoreType.DMA((dp_count + seq_count,)),
        ],
        name="scatter_last",
        compiler_params=pltpu.CompilerParams(
            collective_id=3, has_side_effects=True, vmem_limit_bytes=56 * 1024 * 1024
        ),
    )(*scatter_views(grads, shapes, counts), small, input_rows, *ready, *weights, *firsts, *seconds)


def lamb_kernel(*refs):
    grads, norms = refs[0:6], refs[6]
    weights, firsts, seconds = refs[7:13], refs[13:19], refs[19:25]
    grad_out, first_out, second_out, new_out = refs[25:31], refs[31:37], refs[37:43], refs[43:49]
    copy_out = refs[49:53]
    weight_norm = jnp.sqrt(norms[:, 0:1])
    scales = weight_norm / (jnp.sqrt(norms[:, 1:2]) + ADAM_EPS)
    for index in range(6):
        grad = grads[index][...]
        weight = weights[index][...]
        decay = DECAY_RATE if index < 4 else 0.0
        first_new, second_new, update = lamb_pieces(
            weight, firsts[index][...], seconds[index][...], grad, decay
        )
        scale = scales[8:16] if index == 4 else scales[min(index, 4) : min(index, 4) + 1]
        new = weight - LEARN_RATE * scale * update
        grad_out[index][...] = grad
        first_out[index][...] = first_new
        second_out[index][...] = second_new
        new_out[index][...] = new
        if index < 4:
            copy_out[index][...] = new.astype(BRAIN)


def lamb_all(grads, norms, weights, firsts, seconds):
    vmem = pl.BlockSpec(memory_space=pltpu.VMEM)
    shapes = [jax.ShapeDtypeStruct(weight.shape, FLOAT) for weight in weights]
    copies = [jax.ShapeDtypeStruct(weight.shape, BRAIN) for weight in weights[:4]]
    return pl.pallas_call(
        lamb_kernel,
        out_shape=shapes * 4 + copies,
        in_specs=[vmem] * 25,
        out_specs=[vmem] * 28,
        name="lamb_update",
        compiler_params=pltpu.CompilerParams(vmem_limit_bytes=48 * 1024 * 1024),
    )(*grads, norms, *weights, *firsts, *seconds)


def body(
    tokens,
    cotangent,
    segment_ids,
    w_qkv,
    m_qkv,
    v_qkv,
    w_out,
    m_out,
    v_out,
    w_up,
    m_up,
    v_up,
    w_down,
    m_down,
    v_down,
    vectors,
    m_vectors,
    v_vectors,
    up_bias,
    m_up_bias,
    v_up_bias,
):
    dp_count, seq_count = lax.axis_size("dp"), lax.axis_size("seq")
    vector_size, bias_size = vectors.shape[1], up_bias.shape[0]
    small = jnp.concatenate(
        [
            jnp.pad(vectors, ((0, 0), (0, 128 - vector_size))),
            jnp.pad(up_bias[None], ((0, 7), (0, 128 - bias_size))),
        ]
    )
    shards = [part.astype(BRAIN) for part in (small, w_qkv, w_out, w_up, w_down)]
    counts = (dp_count, seq_count)
    token_rows, *fulls = gather_first(tokens, shards[:2], counts)
    small = fulls[0].reshape(dp_count * seq_count, 16, 128)
    full_vectors = small[:, :8, :vector_size].transpose(1, 0, 2)
    vector_rows = full_vectors.reshape(8, -1).astype(FLOAT)
    up_shift = small[:, 8, :bias_size].reshape(-1).astype(FLOAT)
    as_matrix = lambda full: full.reshape(-1, full.shape[-1])
    full_qkv = as_matrix(fulls[1])

    width = tokens.shape[2]
    length = segment_ids.shape[1]
    rows = token_rows.shape[0]
    segments = lax.dynamic_slice_in_dim(segment_ids, lax.axis_index("seq") * rows, rows, 0)
    count = rows * length
    token_part = token_rows.reshape(count, width).astype(FLOAT)

    normed_one, plain_one, inverse_one = norm_forward(token_part, vector_rows[0], vector_rows[1])
    low_one = normed_one.astype(BRAIN)
    shifts = jnp.concatenate([vector_rows[4], jnp.zeros_like(vector_rows[4]), vector_rows[5]])
    qkv = (matmul(low_one, full_qkv) + shifts).astype(BRAIN)
    context, lse_rows, *fulls = attention_forward(segments, qkv, length, shards[2:], counts)
    full_out, full_up, full_down = [as_matrix(full) for full in fulls]
    back_rows = lax.optimization_barrier((cotangent, context))[0]
    back_rows = lax.all_to_all(back_rows, "seq", split_axis=0, concat_axis=0, tiled=True)
    back_rows = back_rows.reshape(seq_count, rows, -1, width).transpose(1, 0, 2, 3)
    back_part = back_rows.reshape(count, width)
    resid_one = token_part + matmul(context, full_out) + vector_rows[6]
    normed_two, plain_two, inverse_two = norm_forward(resid_one, vector_rows[2], vector_rows[3])
    low_two = normed_two.astype(BRAIN)
    hidden_pre = matmul(low_two, full_up) + up_shift
    activated, gelu_pull = jax.vjp(gelu_tanh, hidden_pre)
    low_act = activated.astype(BRAIN)
    result = resid_one + matmul(low_act, full_down) + vector_rows[7]

    back_float = back_part.astype(FLOAT)
    grad_down = inner_rows(low_act, back_part)
    act_grad = times_transposed(back_part, full_down)
    hidden_grad = gelu_pull(act_grad)[0].astype(BRAIN)
    grad_up = inner_rows(low_two, hidden_grad)
    grad_up_bias = jnp.sum(hidden_grad.astype(FLOAT), axis=0)
    two_grad = times_transposed(hidden_grad, full_up)
    resid_grad = back_float + norm_backward(two_grad, plain_two, inverse_two, vector_rows[2])
    branch_grad = resid_grad.astype(BRAIN)
    grad_out = inner_rows(context, branch_grad)
    context_grad = times_transposed(branch_grad, full_out).astype(BRAIN)
    mixed = result.astype(BRAIN).reshape(rows, seq_count, -1, width).transpose(1, 0, 2, 3)
    mixed = lax.all_to_all(mixed, "seq", split_axis=0, concat_axis=0, tiled=True)
    joined, share_down, share_up, share_out = attention_backward(
        segments,
        qkv,
        context_grad,
        lse_rows,
        length,
        [grad_down.astype(BRAIN), grad_up.astype(BRAIN), grad_out.astype(BRAIN)],
        [w_down.shape, w_up.shape, w_out.shape],
        counts,
    )
    grad_qkv = inner_rows(low_one, joined)
    one_grad = times_transposed(joined, full_qkv)
    input_rows = resid_grad + norm_backward(one_grad, plain_one, inverse_one, vector_rows[0])
    joined_sum = jnp.sum(joined.astype(FLOAT), axis=0)
    grad_vectors = jnp.stack(
        [
            jnp.sum(one_grad * plain_one, axis=0),
            jnp.sum(one_grad, axis=0),
            jnp.sum(two_grad * plain_two, axis=0),
            jnp.sum(two_grad, axis=0),
            joined_sum[:width],
            joined_sum[2 * width :],
            jnp.sum(branch_grad.astype(FLOAT), axis=0),
            jnp.sum(back_float, axis=0),
        ]
    )
    small_grad = jnp.concatenate([grad_vectors, grad_up_bias.reshape(-1, width)])
    small_grad = jnp.pad(small_grad, ((0, 16 - small_grad.shape[0]), (0, 0)))
    as_row = lambda value: value.reshape(1, -1)
    weights = (w_qkv, w_out, w_up, w_down, vectors, as_row(up_bias))
    firsts = (m_qkv, m_out, m_up, m_down, m_vectors, as_row(m_up_bias))
    seconds = (v_qkv, v_out, v_up, v_down, v_vectors, as_row(v_up_bias))
    share_qkv, share_vectors, share_bias, norms, input_grad = scatter_last(
        [grad_qkv.astype(BRAIN)],
        small_grad,
        input_rows.astype(BRAIN).reshape(rows, seq_count, length // seq_count, width),
        [share_out, share_up, share_down],
        weights,
        firsts,
        seconds,
        counts,
    )
    shares = [share_qkv, share_out, share_up, share_down, share_vectors, share_bias]
    results = list(lamb_all(shares, norms, weights, firsts, seconds))
    mixed = mixed.reshape(tokens.shape)
    input_grad = input_grad.reshape(tokens.shape).astype(FLOAT)
    for index in (5, 11, 17, 23):
        results[index] = results[index].reshape(-1)
    return (mixed, input_grad, *results)


def solution(mesh):
    matrix = P(("dp", "seq"), None)
    rows = P("dp", "seq", None)
    vector = P(None, ("dp", "seq"))
    bias = P(("dp", "seq"))
    six = (matrix, matrix, matrix, matrix, vector, bias)
    in_specs = (rows, rows, P("dp", None)) + tuple(spec for spec in six for _ in range(3))
    out_specs = (rows, rows) + six * 4 + (matrix,) * 4
    return jax.shard_map(body, mesh=mesh, in_specs=in_specs, out_specs=out_specs, check_vma=False)
```

```python
import functools

import jax
import jax.numpy as jnp
from jax import lax
from jax.experimental import pallas as pl
from jax.experimental.pallas import tpu as pltpu
from jax.sharding import PartitionSpec as P

HEADS = 12
HEAD_DIM = 64
LONGEST = 512
QUERY_BLOCK = 256


BETA_ONE = 0.9
BETA_TWO = 0.999
ADAM_EPS = 1e-06
DECAY_RATE = 0.01
LEARN_RATE = 0.4
NORM_EPS = 1e-05
STEP_NUMBER = 10.0
CORR_ONE = 1.0 - BETA_ONE**STEP_NUMBER
CORR_TWO = 1.0 - BETA_TWO**STEP_NUMBER

BRAIN = jnp.bfloat16
FLOAT = jnp.float32


def matmul(left_side, right_side):
    return jnp.dot(left_side, right_side, preferred_element_type=FLOAT)


def inner_rows(left_side, right_side):
    return lax.dot_general(
        left_side, right_side, (((0,), (0,)), ((), ())), preferred_element_type=FLOAT
    )


def times_transposed(left_side, right_side):
    return lax.dot_general(
        left_side, right_side, (((1,), (1,)), ((), ())), preferred_element_type=FLOAT
    )


def norm_forward(values, norm_gain, norm_shift):
    center = values - jnp.mean(values, axis=-1, keepdims=True)
    inverse = lax.rsqrt(jnp.mean(center * center, axis=-1, keepdims=True) + NORM_EPS)
    normed = center * inverse
    return (normed * norm_gain + norm_shift, normed, inverse)


def norm_backward(upstream, normed, inverse, norm_gain):
    scaled = upstream * norm_gain
    centered = scaled - jnp.mean(scaled, axis=-1, keepdims=True)
    return inverse * (centered - normed * jnp.mean(scaled * normed, axis=-1, keepdims=True))


def windows(length):
    return [
        (max(0, first - LONGEST), first + QUERY_BLOCK) for first in range(0, length, QUERY_BLOCK)
    ]


def fill_bias(seg_col, seg_row, bias, length):
    place = 0
    for index, (low, high) in enumerate(windows(length)):
        first = index * QUERY_BLOCK
        size = high - low
        keys = seg_col[0, low:high, :]
        queries = seg_row[0, :, first : first + QUERY_BLOCK]
        key_place = low + lax.broadcasted_iota(jnp.int32, (size, QUERY_BLOCK), 0)
        query_place = first + lax.broadcasted_iota(jnp.int32, (size, QUERY_BLOCK), 1)
        allowed = (keys == queries) & (key_place <= query_place)
        bias[place : place + size, :] = jnp.where(allowed, 0.0, -1000000000.0)
        place += size


def split_heads(pair):
    lane = lax.broadcasted_iota(jnp.int32, pair.shape, 1)
    zero = jnp.zeros_like(pair)
    return (jnp.where(lane < HEAD_DIM, pair, zero), jnp.where(lane < HEAD_DIM, zero, pair))


def attend_forward(counts, splits, *refs):
    seg_col, seg_row, q_ref, k_ref, v_ref = refs[0:5]
    shards, c_ref, lse_ref, fulls = refs[5:8], refs[8], refs[9], refs[10:13]
    bias, bounces, send_sem, recv_sem, own_sem = refs[13], refs[14:17], *refs[17:]
    length = q_ref.shape[0]
    here = Here(*counts)
    slots = Slots(send_sem, recv_sem)
    gathers = gathers_of(here, slots, shards, fulls, bounces, own_sem, splits)
    groups = [gathers[:2]] + [[each] for each in gathers[2:]]
    waves = led_by(lambda: greet(here.near_peers()), waves_of(groups))
    blocks = windows(length)
    beside = Beside(waves, HEADS // 2 * len(blocks))

    @pl.when(pl.program_id(1) == 0)
    def _():
        fill_bias(seg_col, seg_row, bias, length)

    v_turned = v_ref[...].T
    place = 0
    for index, (low, high) in enumerate(blocks):
        beside.point(index, len(blocks))
        first = index * QUERY_BLOCK
        size = high - low
        queries = split_heads(q_ref[first : first + QUERY_BLOCK, :] * HEAD_DIM ** (-0.5))
        keys = k_ref[low:high, :]
        blocked = bias[place : place + size, :]
        parts = []
        for head in range(2):
            scores = times_transposed(keys, queries[head]) + blocked
            peak = jnp.max(scores, axis=0, keepdims=True)
            probs = jnp.exp(scores - peak)
            total = jnp.sum(probs, axis=0, keepdims=True)
            probs = (probs * (1.0 / total)).astype(BRAIN)
            lse_ref[0, 0, head : head + 1, first : first + QUERY_BLOCK] = peak + jnp.log(total)
            turned = v_turned[head * HEAD_DIM : (head + 1) * HEAD_DIM, low:high]
            parts.append(matmul(turned, probs))
        context = jnp.concatenate(parts, axis=0).T
        c_ref[first : first + QUERY_BLOCK, :] = context.astype(BRAIN)
        place += size

    @pl.when((pl.program_id(0) == pl.num_programs(0) - 1) & (pl.program_id(1) == HEADS // 2 - 1))
    def _():
        beside.rest()
        drain_all(gathers)


def led_by(ahead, waves):
    def both():
        ahead()
        waves[0]()

    return [both] + waves[1:]


class Beside:
    def __init__(self, waves, points):
        self.at = {}
        early = len(waves) - 1
        for index in range(early):
            self.at.setdefault(index * points // early, []).append(waves[index])
        self.late = waves[early:]

    def point(self, index, per_step):
        for point, calls in self.at.items():
            if point % per_step == index:

                @pl.when((pl.program_id(0) == 0) & (pl.program_id(1) == point // per_step))
                def _(calls=calls):
                    for call in calls:
                        call()

    def rest(self):
        for call in self.late:
            call()


def attend_backward(counts, splits, *refs):
    seg_col, seg_row, q_ref, k_ref, v_ref, g_ref, lse_ref = refs[0:7]
    grads, out_ref, shares = refs[7:10], refs[10], refs[11:14]
    bias, key_sum, value_sum = refs[14:17]
    buffers, send_sem, recv_sem, own_sem = refs[17:29], *refs[29:]
    length = q_ref.shape[0]
    pair = pl.program_id(1)
    here = Here(*counts)
    slots = Slots(send_sem, recv_sem)
    scatters, loads = scatters_of(here, slots, grads, buffers, shares, own_sem, splits)

    def begin():
        for load in loads:
            load().start()
        greet(here.near_peers())

    groups = [[each] for each in scatters[:-2]] + [scatters[-2:]]
    waves = led_by(begin, waves_of(groups))
    blocks = windows(length)
    beside = Beside(waves, HEADS // 2 * len(blocks))

    @pl.when(pair == 0)
    def _():
        fill_bias(seg_col, seg_row, bias, length)

    key_sum[...] = jnp.zeros_like(key_sum)
    value_sum[...] = jnp.zeros_like(value_sum)
    width = HEADS * HEAD_DIM
    k_turned = k_ref[...].T
    lanes = 2 * HEAD_DIM
    column = pl.multiple_of(pair * lanes, lanes)
    place = 0
    for index, (low, high) in enumerate(blocks):
        beside.point(index, len(blocks))
        first = index * QUERY_BLOCK
        size = high - low
        rows = slice(first, first + QUERY_BLOCK)
        queries = split_heads(q_ref[rows, :] * HEAD_DIM ** (-0.5))
        grads = split_heads(g_ref[rows, :])
        keys = k_ref[low:high, :]
        values = v_ref[low:high, :]
        blocked = bias[place : place + size, :]
        all_probs = []
        all_scores = []
        parts = []
        for head in range(2):
            scores = times_transposed(keys, queries[head]) + blocked
            probs = jnp.exp(scores - lse_ref[0, 0, head : head + 1, rows])
            prob_grad = times_transposed(values, grads[head])
            row_dot = jnp.sum(probs * prob_grad, axis=0, keepdims=True)
            score_grad = (probs * (prob_grad - row_dot)).astype(BRAIN)
            all_probs.append(probs.astype(BRAIN))
            all_scores.append(score_grad)
            turned = k_turned[head * HEAD_DIM : (head + 1) * HEAD_DIM, low:high]
            parts.append(matmul(turned, score_grad))
        query_grad = jnp.concatenate(parts, axis=0).T * HEAD_DIM ** (-0.5)
        out_ref[rows, pl.ds(column, lanes)] = query_grad.astype(BRAIN)
        value_sum[low:high, :] += matmul(
            jnp.concatenate(all_probs, axis=1), jnp.concatenate(grads, axis=0)
        )
        key_sum[low:high, :] += matmul(
            jnp.concatenate(all_scores, axis=1), jnp.concatenate(queries, axis=0)
        )
        place += size
    out_ref[:, pl.ds(width + column, lanes)] = key_sum[...].astype(BRAIN)
    out_ref[:, pl.ds(2 * width + column, lanes)] = value_sum[...].astype(BRAIN)

    @pl.when((pl.program_id(0) == pl.num_programs(0) - 1) & (pair == HEADS // 2 - 1))
    def _():
        beside.rest()
        drain_all(scatters)


def attention_specs(length):
    lanes = 2 * HEAD_DIM
    pairs = HEADS // 2
    spec = lambda shift: pl.BlockSpec((length, lanes), lambda r, j: (r, shift * pairs + j))
    segs = [
        pl.BlockSpec((1, length, 1), lambda r, j: (r, 0, 0)),
        pl.BlockSpec((1, 1, length), lambda r, j: (r, 0, 0)),
    ]
    lse = pl.BlockSpec((1, 1, 8, length), lambda r, j: (r, j, 0, 0))
    plain = pl.BlockSpec((length, lanes), lambda r, j: (r, j))
    bias = pltpu.VMEM((sum(high - low for low, high in windows(length)), QUERY_BLOCK), FLOAT)
    return segs, [spec(0), spec(1), spec(2)], plain, lse, bias


def attention_forward(segments, qkv, length, shards, counts):
    rows = segments.shape[0]
    segs, qkv_specs, plain, lse, bias = attention_specs(length)
    width = HEADS * HEAD_DIM
    splits = [False] + [True] * (len(shards) - 1)
    slots = slot_count(counts, [shard.shape for shard in shards], splits, 0)
    return pl.pallas_call(
        functools.partial(attend_forward, counts, splits),
        grid=(rows, HEADS // 2),
        in_specs=segs + qkv_specs + [ANYWHERE] * 3,
        out_specs=[plain, lse] + [ANYWHERE] * 3,
        out_shape=[
            jax.ShapeDtypeStruct((rows * length, width), BRAIN),
            jax.ShapeDtypeStruct((rows, HEADS // 2, 8, length), FLOAT),
        ]
        + [full_shape(shard, *counts) for shard in shards],
        scratch_shapes=[bias]
        + [pltpu.VMEM(shard.shape, shard.dtype) for shard in shards]
        + [
            pltpu.SemaphoreType.DMA((slots,)),
            pltpu.SemaphoreType.DMA((slots,)),
            pltpu.SemaphoreType.DMA((2 * len(shards),)),
        ],
        name="attend_forward",
        compiler_params=pltpu.CompilerParams(
            collective_id=1, has_side_effects=True, vmem_limit_bytes=48 * 1024 * 1024
        ),
    )(segments[:, :, None], segments[:, None, :], qkv, qkv, qkv, *shards)


def attention_backward(segments, qkv, context_grad, lse_rows, length, grads, shapes, counts):
    rows = segments.shape[0]
    segs, qkv_specs, plain, lse, bias = attention_specs(length)
    width = HEADS * HEAD_DIM
    splits = [True] * (len(shapes) - 1) + [False]
    slots = slot_count(counts, shapes, splits, 0)
    return pl.pallas_call(
        functools.partial(attend_backward, counts, splits),
        grid=(rows, HEADS // 2),
        in_specs=segs + qkv_specs + [plain, lse] + [ANYWHERE] * 3,
        out_specs=[pl.BlockSpec((length, 3 * width), lambda r, j: (r, 0))] + [WHOLE] * 3,
        out_shape=[
            jax.ShapeDtypeStruct((rows * length, 3 * width), BRAIN),
        ]
        + [jax.ShapeDtypeStruct(shape, FLOAT) for shape in shapes],
        scratch_shapes=[
            bias,
            pltpu.VMEM((length, 2 * HEAD_DIM), FLOAT),
            pltpu.VMEM((length, 2 * HEAD_DIM), FLOAT),
        ]
        + scatter_buffers(shapes, counts)
        + [
            pltpu.SemaphoreType.DMA((slots,)),
            pltpu.SemaphoreType.DMA((slots,)),
            pltpu.SemaphoreType.DMA((len(shapes),)),
        ],
        name="attend_backward",
        compiler_params=pltpu.CompilerParams(
            collective_id=2, has_side_effects=True, vmem_limit_bytes=62 * 1024 * 1024
        ),
    )(
        segments[:, :, None],
        segments[:, None, :],
        qkv,
        qkv,
        qkv,
        context_grad,
        lse_rows,
        *scatter_views(grads, shapes, counts),
    )


MESH = pl.DeviceIdType.MESH
ANYWHERE = pl.BlockSpec(memory_space=pl.ANY)
WHOLE = pl.BlockSpec(memory_space=pltpu.VMEM)


def bits_of(count):
    return count.bit_length() - 1


def flipped(value, bit):
    step = 1 << bit
    return value + step * (1 - 2 * lax.rem(lax.div(value, step), 2))


def rounded_down(value, bit):
    return lax.div(value, 1 << bit) * (1 << bit)


def spread(value, bit, total):
    step = 1 << (bit + 1)
    return [lax.rem(value, step) + step * turn for turn in range(1 << (total - 1 - bit))]


class Here:
    def __init__(self, dp_count, seq_count):
        self.dp_count, self.seq_count = dp_count, seq_count
        self.half_count = dp_count // 2
        self.seq_bits = bits_of(seq_count)
        self.place, self.line = lax.axis_index("dp"), lax.axis_index("seq")
        self.chip, self.core = lax.div(self.place, 2), lax.rem(self.place, 2)

    def core_peer(self):
        return {"dp": flipped(self.place, 0)}

    def line_peer(self, bit):
        return {"seq": flipped(self.line, bit)}

    def other_lines(self):
        return [lax.rem(self.line + turn, self.seq_count) for turn in range(1, self.seq_count)]

    def other_chips(self):
        return [lax.rem(self.chip + turn, self.half_count) for turn in range(1, self.half_count)]

    def chip_peers(self):
        return [{"dp": 2 * chip + self.core} for chip in self.other_chips()]

    def near_peers(self):
        peers = [self.core_peer()] + self.chip_peers()
        return peers + [{"seq": line} for line in self.other_lines()]

    def all_peers(self):
        peers = [{"dp": lax.rem(self.place + turn, self.dp_count)} for turn in range(1, self.dp_count)]
        return peers + [{"seq": line} for line in self.other_lines()]


def greet(peers):
    barrier = pltpu.get_barrier_semaphore()
    for peer in peers:
        pl.semaphore_signal(barrier, inc=1, device_id=peer, device_id_type=MESH)
    pl.semaphore_wait(barrier, len(peers))


class Slots:
    def __init__(self, send_sem, recv_sem):
        self.send_sem, self.recv_sem, self.used = send_sem, recv_sem, 0

    def take(self, count):
        first = self.used
        self.used += count
        return first

    def copy(self, slot, source, target, peer):
        return pltpu.make_async_remote_copy(
            source,
            target,
            self.send_sem.at[slot],
            self.recv_sem.at[slot],
            device_id=peer,
            device_id_type=MESH,
        )


def parts_of(shape, split):
    rows, width = shape
    tiles = width // 128
    if width % 128 or tiles < 2:
        return [[(slice(0, rows), slice(0, width), False)]]
    middle = tiles // 2 * 128
    first, second = (0, middle), (middle, width)
    every = slice(0, rows)
    if split and rows % 32 == 0:
        return [
            [(part, slice(*first), False), (part, slice(*second), True)]
            for part in (slice(0, rows // 2), slice(rows // 2, rows))
        ]
    if split and tiles >= 4:
        lists = [[], []]
        for (low, high), backwards in ((first, False), (second, True)):
            cut = low + (high - low) // 256 * 128
            lists[0].append((every, slice(low, cut), backwards))
            lists[1].append((every, slice(cut, high), backwards))
        return lists
    return [[(every, slice(*first), False), (every, slice(*second), True)]]


class Transfer:
    def start(self, stage):
        for copy in self.copies(stage):
            copy.start()

    def finish(self, stage):
        for copy in self.copies(stage):
            copy.wait_recv()
        self.use(stage)

    def use(self, stage):
        pass

    def drain(self):
        for stage in range(self.stages):
            for copy in self.copies(stage):
                copy.wait_send()


class Gather(Transfer):
    def __init__(self, here, slots, shard, full, pieces, own_done):
        self.here, self.slots, self.shard, self.full = here, slots, shard, full
        self.pieces, self.own_done = pieces, own_done
        self.stages = here.seq_bits + 2
        self.each = here.half_count + here.seq_count
        self.first = slots.take(self.each * len(pieces))

    def copies(self, stage):
        here, full = self.here, self.full
        found = []
        for index, (rows, columns, backwards) in enumerate(self.pieces):
            slot = self.first + self.each * index
            if stage == 0:
                target = full.at[here.chip, here.core, here.line, rows, columns]
                for turn, peer in enumerate(here.chip_peers()):
                    source = self.shard.at[rows, columns]
                    found.append(self.slots.copy(slot + turn, source, target, peer))
                continue
            slot += here.half_count - 1
            if stage == self.stages - 1:
                part = full.at[:, here.core, :, rows, columns]
                slot += here.seq_count - 1
                found.append(self.slots.copy(slot, part, part, here.core_peer()))
                continue
            if backwards:
                bit = here.seq_bits - stage
                slot += (1 << (stage - 1)) - 1
                parts = [
                    full.at[:, here.core, at, rows, columns]
                    for at in spread(here.line, bit, here.seq_bits)
                ]
            else:
                bit = stage - 1
                slot += bit
                block = pl.ds(rounded_down(here.line, bit), 1 << bit)
                parts = [full.at[:, here.core, block, rows, columns]]
            for turn, part in enumerate(parts):
                found.append(self.slots.copy(slot + turn, part, part, here.line_peer(bit)))
        return found

    def start(self, stage):
        if stage == 1:
            self.own_done()
        super().start(stage)


class Scatter(Transfer):
    def __init__(self, here, slots, grad, own, from_core, from_line, from_chip, share, pieces, load):
        self.here, self.slots, self.grad, self.own = here, slots, grad, own
        self.from_core, self.from_line, self.from_chip = from_core, from_line, from_chip
        self.share, self.pieces, self.load = share, pieces, load
        self.stages = here.seq_bits + 2
        self.each = here.half_count + here.seq_count
        self.first = slots.take(self.each * len(pieces))

    def line_stage(self, stage, backwards):
        here = self.here
        if backwards:
            bit = stage - 1
            away = spread(flipped(here.line, bit), bit, here.seq_bits)
            kept = spread(here.line, bit, here.seq_bits)
        else:
            bit = here.seq_bits - stage
            away = [rounded_down(flipped(here.line, bit), bit) + at for at in range(1 << bit)]
            kept = [rounded_down(here.line, bit) + at for at in range(1 << bit)]
        base = sum(1 << (here.seq_bits - past) for past in range(1, stage))
        return bit, away, kept, base

    def copies(self, stage):
        here = self.here
        found = []
        for index, (rows, columns, backwards) in enumerate(self.pieces):
            slot = self.first + self.each * index
            if stage == 0:
                found.append(
                    self.slots.copy(
                        slot,
                        self.grad.at[:, 1 - here.core, :, rows, columns],
                        self.from_core.at[:, :, rows, columns],
                        here.core_peer(),
                    )
                )
            elif stage == self.stages - 1:
                slot += here.seq_count
                for turn, chip in enumerate(here.other_chips()):
                    found.append(
                        self.slots.copy(
                            slot + turn,
                            self.own.at[chip, here.line, rows, columns],
                            self.from_chip.at[turn, rows, columns],
                            {"dp": 2 * chip + here.core},
                        )
                    )
            else:
                bit, away, _, base = self.line_stage(stage, backwards)
                for turn, at in enumerate(away):
                    found.append(
                        self.slots.copy(
                            slot + 1 + base + turn,
                            self.own.at[:, at, rows, columns],
                            self.from_line.at[base + turn, :, rows, columns],
                            here.line_peer(bit),
                        )
                    )
        return found

    def use(self, stage):
        here, own = self.here, self.own
        if stage == 0:
            self.load()
        for rows, columns, backwards in self.pieces:
            if stage == 0:

                def add(at, carry, rows=rows, columns=columns):
                    one, two = lax.div(at, here.seq_count), lax.rem(at, here.seq_count)
                    own[one, two, rows, columns] = (
                        own[one, two, rows, columns] + self.from_core[one, two, rows, columns]
                    )
                    return carry

                lax.fori_loop(0, here.half_count * here.seq_count, add, 0)
            elif stage == self.stages - 1:
                total = own[here.chip, here.line, rows, columns].astype(FLOAT)
                for turn in range(here.half_count - 1):
                    total = total + self.from_chip[turn, rows, columns].astype(FLOAT)
                self.share[rows, columns] = total
            else:
                _, _, kept, base = self.line_stage(stage, backwards)
                for turn, at in enumerate(kept):

                    def add(one, carry, rows=rows, columns=columns, at=at, place=base + turn):
                        own[one, at, rows, columns] = (
                            own[one, at, rows, columns] + self.from_line[place, one, rows, columns]
                        )
                        return carry

                    lax.fori_loop(0, here.half_count, add, 0)


class Exchange(Transfer):
    stages = 1

    def __init__(self, here, slots, source, target, to_rows, bounce, sem):
        self.here, self.slots, self.source, self.target = here, slots, source, target
        self.to_rows, self.bounce, self.sem = to_rows, bounce, sem
        self.first = slots.take(here.seq_count - 1)

    def ends(self, line):
        if self.to_rows:
            count = self.target.shape[0]
            block = self.source.at[pl.ds(line * count, count)]
            return block, self.target.at[:, self.here.line]
        return self.source.at[:, line], self.target.at[self.here.line]

    def copies(self, stage):
        return [
            self.slots.copy(self.first + turn, *self.ends(line), {"seq": line})
            for turn, line in enumerate(self.here.other_lines())
        ]

    def own_in(self):
        return pltpu.make_async_copy(self.ends(self.here.line)[0], self.bounce, self.sem.at[0])

    def own_out(self):
        source, target = self.ends(self.here.line)
        source = source if self.bounce is None else self.bounce
        return pltpu.make_async_copy(source, target, self.sem.at[1])

    def start(self, stage):
        if self.bounce is not None:
            self.own_in().start()
        super().start(stage)
        if self.bounce is not None:
            self.own_in().wait()
        self.own_out().start()

    def use(self, stage):
        self.own_out().wait()


def waves_of(groups):
    def wave(count):
        for index, group in enumerate(groups):
            stage = count - index
            for transfer in group:
                if 1 <= stage <= transfer.stages:
                    transfer.finish(stage - 1)
            for transfer in group:
                if 0 <= stage < transfer.stages:
                    transfer.start(stage)

    total = max(index + transfer.stages for index, group in enumerate(groups) for transfer in group)
    return [functools.partial(wave, count) for count in range(total + 1)]


def drain_all(transfers):
    for transfer in transfers:
        transfer.drain()


def gathers_of(here, slots, shards, fulls, bounces, sem, splits):
    found = []
    for index, (shard, full, bounce) in enumerate(zip(shards, fulls, bounces)):
        inward = lambda shard=shard, bounce=bounce, index=index: pltpu.make_async_copy(
            shard, bounce, sem.at[2 * index]
        )
        outward = lambda full=full, bounce=bounce, index=index: pltpu.make_async_copy(
            bounce, full.at[here.chip, here.core, here.line], sem.at[2 * index + 1]
        )
        for order, pieces in enumerate(parts_of(shard.shape, splits[index])):

            def own_done(first=order == 0, inward=inward, outward=outward):
                if first:
                    inward().start()
                    inward().wait()
                    outward().start()
                    outward().wait()

            found.append(Gather(here, slots, shard, full, pieces, own_done))
    return found


def slot_count(here_shape, shapes, splits, exchanges):
    half_count, seq_count = here_shape[0] // 2, here_shape[1]
    each = half_count + seq_count
    pieces = sum(len(part) for shape, split in zip(shapes, splits) for part in parts_of(shape, split))
    return each * pieces + exchanges * (seq_count - 1)


def full_shape(shard, dp_count, seq_count):
    return jax.ShapeDtypeStruct((dp_count // 2, 2, seq_count) + shard.shape, shard.dtype)


def gather_kernel(counts, splits, count, *refs):
    tokens, shards, fulls = refs[0], refs[1 : 1 + count], refs[2 + count : 2 + 2 * count]
    token_rows = refs[1 + count]
    rest = refs[2 + 2 * count :]
    bounces, bounce, send_sem, recv_sem, own_sem, move_sem = rest[:count], *rest[count:]
    here = Here(*counts)
    slots = Slots(send_sem, recv_sem)
    gathers = gathers_of(here, slots, shards, fulls, bounces, own_sem, splits)
    move = Exchange(here, slots, tokens, token_rows, True, bounce, move_sem)
    greet(here.near_peers())
    waves = waves_of([gathers[:2]] + [[each] for each in gathers[2:]])
    waves[0]()
    move.start(0)
    for wave in waves[1:]:
        wave()
    move.finish(0)
    drain_all(gathers + [move])


def gather_first(tokens, shards, counts):
    dp_count, seq_count = counts
    row_count, pos_count, width = tokens.shape
    rows = row_count // seq_count
    splits = [True] * len(shards)
    slots = slot_count(counts, [shard.shape for shard in shards], splits, 1)
    return pl.pallas_call(
        functools.partial(gather_kernel, counts, splits, len(shards)),
        out_shape=[jax.ShapeDtypeStruct((rows, seq_count, pos_count, width), tokens.dtype)]
        + [full_shape(shard, *counts) for shard in shards],
        in_specs=[ANYWHERE] * (1 + len(shards)),
        out_specs=[ANYWHERE] * (1 + len(shards)),
        scratch_shapes=[pltpu.VMEM(shard.shape, shard.dtype) for shard in shards]
        + [
            pltpu.VMEM((rows, pos_count, width), tokens.dtype),
            pltpu.SemaphoreType.DMA((slots,)),
            pltpu.SemaphoreType.DMA((slots,)),
            pltpu.SemaphoreType.DMA((2 * len(shards),)),
            pltpu.SemaphoreType.DMA((2,)),
        ],
        name="gather_first",
        compiler_params=pltpu.CompilerParams(collective_id=0, has_side_effects=True),
    )(tokens, *shards)


ROW_BLOCK = 256
HIDDEN_BLOCK = 512
GELU_SCALE = 0.7978845608028654
GELU_CUBE = 0.044715


def gelu_both(values):
    square = values * values
    turned = jnp.tanh(GELU_SCALE * values * (1.0 + GELU_CUBE * square))
    half = 0.5 + 0.5 * turned
    inner = GELU_SCALE * (1.0 + 3.0 * GELU_CUBE * square)
    return values * half, half + 0.5 * values * (1.0 - turned * turned) * inner


def row_blocks(count):
    return [slice(first, first + ROW_BLOCK) for first in range(0, count, ROW_BLOCK)]


def norm_parts(values):
    center = values - jnp.mean(values, axis=-1, keepdims=True)
    inverse = lax.rsqrt(jnp.mean(center * center, axis=-1, keepdims=True) + NORM_EPS)
    return center * inverse, inverse


def forward_start(context, tokens, w_out, vectors, resid, low_two, low_turned):
    for rows in row_blocks(resid.shape[0]):
        values = tokens[rows, :].astype(FLOAT) + (matmul(context[rows, :], w_out[...]) + vectors[6:7, :])
        resid[rows, :] = values
        normed, _ = norm_parts(values)
        low = (normed * vectors[2:3, :] + vectors[3:4, :]).astype(BRAIN)
        low_two[rows, :] = low
        low_turned[:, rows] = low.T


def backward_end(
    context, w_out, vectors, resid, total, back, gc_ref, gr_ref, gwo_ref, sum_ref, low_turned
):
    width = resid.shape[1]
    sums = [jnp.zeros((1, width), FLOAT) for _ in range(4)]
    for rows in row_blocks(resid.shape[0]):
        normed, inverse = norm_parts(resid[rows, :])
        upstream = total[rows, :]
        given = back(rows).astype(FLOAT)
        scaled = upstream * vectors[2:3, :]
        centered = scaled - jnp.mean(scaled, axis=-1, keepdims=True)
        inward = centered - normed * jnp.mean(scaled * normed, axis=-1, keepdims=True)
        grad = given + inverse * inward
        low = grad.astype(BRAIN)
        gr_ref[rows, :] = grad
        gc_ref[rows, :] = times_transposed(low, w_out[...]).astype(BRAIN)
        low_turned[:, rows] = context[rows, :].T
        total[rows, :] = low.astype(FLOAT)
        for index, values in enumerate((upstream * normed, upstream, low.astype(FLOAT), given)):
            sums[index] = sums[index] + jnp.sum(values, axis=0, keepdims=True)
    for index in range(4):
        sum_ref[index : index + 1, :] = sums[index]
    sum_ref[4:8, :] = jnp.zeros((4, width), FLOAT)
    gwo_ref[...] = matmul(low_turned[...], total[...].astype(BRAIN)).astype(BRAIN)


def mlp_kernel(counts, *refs):
    context, tokens, w_out, w_up, w_down, vectors, up_shift, cotangent = refs[0:8]
    gup_ref, gdown_ref, gub_ref, gwo_ref, gc_ref, gr_ref, sum_ref, mixed = refs[8:16]
    acts, slopes, low_two, low_turned, resid, total, hidden, back, mixed_rows = refs[16:25]
    send_sem, recv_sem, move_sem = refs[25:28]
    here = Here(*counts)
    slots = Slots(send_sem, recv_sem)
    arrive = Exchange(here, slots, cotangent, back, True, None, move_sem.at[pl.ds(0, 2)])
    leave = Exchange(here, slots, mixed_rows, mixed, False, None, move_sem.at[pl.ds(2, 2)])
    step = pl.program_id(0)
    half = pl.num_programs(0) // 2
    count = resid.shape[0]
    pos_count = back.shape[2]

    def back_rows(rows):
        parts = []
        for first in range(rows.start, rows.stop, pos_count):
            size = min(pos_count, rows.stop - first)
            row, rest = divmod(first, pos_count * counts[1])
            line, offset = divmod(rest, pos_count)
            parts.append(back[row, line, offset : offset + size, :])
        return parts[0] if len(parts) == 1 else jnp.concatenate(parts, axis=0)

    @pl.when(step == 0)
    def _():
        greet(here.near_peers())
        arrive.start(0)
        forward_start(context, tokens, w_out, vectors, resid, low_two, low_turned)
        total[...] = jnp.zeros_like(total)

    @pl.when(step < half)
    def _():
        for rows in row_blocks(count):
            values = matmul(low_two[rows, :], w_up[...]) + up_shift[...]
            act, slope = gelu_both(values)
            low = act.astype(BRAIN)
            acts[step, rows, :] = low
            slopes[step, rows, :] = slope
            total[rows, :] += matmul(low, w_down[...])

    @pl.when(step == half)
    def _():
        for first in range(0, count, pos_count):
            row, line = divmod(first // pos_count, counts[1])
            rows = slice(first, first + pos_count)
            values = resid[rows, :] + (total[rows, :] + vectors[7:8, :])
            mixed_rows[row, line] = values.astype(BRAIN)
        total[...] = jnp.zeros_like(total)
        leave.start(0)
        arrive.finish(0)

    @pl.when(step >= half)
    def _():
        at = step - half
        sums = jnp.zeros((1, hidden.shape[1]), FLOAT)
        for rows in row_blocks(count):
            grad = times_transposed(back_rows(rows), w_down[...]) * slopes[at, rows, :]
            low = grad.astype(BRAIN)
            hidden[rows, :] = low
            sums = sums + jnp.sum(low.astype(FLOAT), axis=0, keepdims=True)
            total[rows, :] += times_transposed(low, w_up[...])
        gub_ref[...] = sums
        gup_ref[...] = matmul(low_turned[...], hidden[...]).astype(BRAIN)
        every = back_rows(slice(0, count))
        gdown_ref[...] = inner_rows(acts[at], every).astype(BRAIN)

    @pl.when(step == 2 * half - 1)
    def _():
        backward_end(
            context, w_out, vectors, resid, total, back_rows, gc_ref, gr_ref, gwo_ref, sum_ref, low_turned
        )
        leave.finish(0)
        drain_all([arrive, leave])


def feed_forward(context, tokens, w_out, w_up, w_down, vectors, up_shift, cotangent, counts):
    count, width = context.shape
    hidden = w_up.shape[1]
    half = hidden // HIDDEN_BLOCK
    seq_count = counts[1]
    row_count, pos_count, _ = cotangent.shape
    rows = row_count // seq_count
    once = lambda shape: pl.BlockSpec(shape, lambda j: (0, 0), pipeline_mode=pl.Buffered(1))
    later = lambda j: jnp.maximum(j - half, 0)
    around = lambda j: lax.rem(j, half)
    block = HIDDEN_BLOCK
    slots = 2 * (seq_count - 1)
    return pl.pallas_call(
        functools.partial(mlp_kernel, counts),
        grid=(2 * half,),
        in_specs=[
            once((count, width)),
            once((count, width)),
            once((width, width)),
            pl.BlockSpec((width, block), lambda j: (0, around(j))),
            pl.BlockSpec((block, width), lambda j: (around(j), 0)),
            once((8, width)),
            pl.BlockSpec((1, block), lambda j: (0, around(j))),
            ANYWHERE,
        ],
        out_specs=[
            pl.BlockSpec((width, block), lambda j: (0, later(j))),
            pl.BlockSpec((block, width), lambda j: (later(j), 0)),
            pl.BlockSpec((1, block), lambda j: (0, later(j))),
            once((width, width)),
            once((count, width)),
            once((count, width)),
            once((8, width)),
            ANYWHERE,
        ],
        out_shape=[
            jax.ShapeDtypeStruct((width, hidden), BRAIN),
            jax.ShapeDtypeStruct((hidden, width), BRAIN),
            jax.ShapeDtypeStruct((1, hidden), FLOAT),
            jax.ShapeDtypeStruct((width, width), BRAIN),
            jax.ShapeDtypeStruct((count, width), BRAIN),
            jax.ShapeDtypeStruct((count, width), FLOAT),
            jax.ShapeDtypeStruct((8, width), FLOAT),
            jax.ShapeDtypeStruct((seq_count, rows, pos_count, width), BRAIN),
        ],
        scratch_shapes=[
            pltpu.VMEM((half, count, block), BRAIN),
            pltpu.VMEM((half, count, block), FLOAT),
            pltpu.VMEM((count, width), BRAIN),
            pltpu.VMEM((width, count), BRAIN),
            pltpu.VMEM((count, width), FLOAT),
            pltpu.VMEM((count, width), FLOAT),
            pltpu.VMEM((count, block), BRAIN),
            pltpu.VMEM((rows, seq_count, pos_count, width), BRAIN),
            pltpu.VMEM((rows, seq_count, pos_count, width), BRAIN),
            pltpu.SemaphoreType.DMA((slots,)),
            pltpu.SemaphoreType.DMA((slots,)),
            pltpu.SemaphoreType.DMA((4,)),
        ],
        name="feed_forward",
        compiler_params=pltpu.CompilerParams(
            collective_id=4, has_side_effects=True, vmem_limit_bytes=63 * 1024 * 1024
        ),
    )(context, tokens, w_out, w_up, w_down, vectors, up_shift, cotangent)


def lamb_pieces(weight, first, second, grad, decay):
    first_new = BETA_ONE * first + (1.0 - BETA_ONE) * grad
    second_new = BETA_TWO * second + (1.0 - BETA_TWO) * grad * grad
    spread_out = jnp.sqrt(second_new / CORR_TWO) + ADAM_EPS
    update = first_new / CORR_ONE / spread_out + decay * weight
    return (first_new, second_new, update)


def square_sum(values):
    return jnp.sum(jnp.sum(values * values, axis=1, keepdims=True), axis=0, keepdims=True)


def picked(small, rank, vector_size, bias_size):
    width = small.shape[1]
    row = lax.broadcasted_iota(jnp.int32, (width, 128), 0)
    lane = lax.broadcasted_iota(jnp.int32, (width, 128), 1)
    dot = functools.partial(jnp.dot, precision=lax.Precision.HIGHEST, preferred_element_type=FLOAT)
    chosen = (row == lane + rank * vector_size) & (lane < vector_size)
    vector_grad = dot(small[0:8, :], jnp.where(chosen, 1.0, 0.0))[:, :vector_size]
    start = rank * bias_size
    chosen = (row == lane + lax.rem(start, width)) & (lane < bias_size)
    tail = dot(small[8:16, :], jnp.where(chosen, 1.0, 0.0))
    tail_row = lax.broadcasted_iota(jnp.int32, tail.shape, 0)
    tail = jnp.sum(jnp.where(tail_row == lax.div(start, width), tail, 0.0), axis=0, keepdims=True)
    return vector_grad, tail[:, :bias_size]


def scatters_of(here, slots, grads, buffers, shares, own_sem, splits):
    count = len(grads)
    found, loads = [], []
    for index, (grad, share) in enumerate(zip(grads, shares)):
        own, *arrivals = buffers[index::count]
        load = lambda grad=grad, own=own, index=index: pltpu.make_async_copy(
            grad.at[:, here.core], own, own_sem.at[index]
        )
        loads.append(load)
        for order, pieces in enumerate(parts_of(share.shape, splits[index])):
            wait = (lambda load=load: load().wait()) if order == 0 else (lambda: None)
            found.append(Scatter(here, slots, grad, own, *arrivals, share, pieces, wait))
    return found, loads


def scatter_buffers(shapes, counts):
    half_count, seq_count = counts[0] // 2, counts[1]
    leads = [(half_count, seq_count)] * 2 + [(seq_count - 1, half_count), (half_count - 1,)]
    return [pltpu.VMEM(lead + shape, BRAIN) for lead in leads for shape in shapes]


def scatter_views(grads, shapes, counts):
    lead = (counts[0] // 2, 2, counts[1])
    return [grad.reshape(lead + shape) for grad, shape in zip(grads, shapes)]


class SmallSum(Transfer):
    def __init__(self, here, small, sums, arrived, send_sem, recv_sem):
        self.slots = Slots(send_sem, recv_sem)
        self.small, self.sums, self.arrived = small, sums, arrived
        self.peers = [here.core_peer()]
        self.peers += [{"dp": flipped(here.place, bit + 1)} for bit in range(bits_of(here.half_count))]
        self.peers += [here.line_peer(bit) for bit in range(here.seq_bits)]
        self.stages = len(self.peers)

    def copies(self, stage):
        source = self.sums.at[stage - 1] if stage else self.small
        return [self.slots.copy(stage, source, self.arrived.at[stage], self.peers[stage])]

    def use(self, stage):
        before = self.sums[stage - 1] if stage else self.small[...]
        self.sums[stage] = before + self.arrived[stage]


def scatter_kernel(counts, splits, *refs):
    grads, small, input_rows = refs[0:1], refs[1], refs[2]
    ready = refs[3:6]
    weights, firsts, seconds = refs[6:12], refs[12:18], refs[18:24]
    shares, norm_out, input_grad = refs[24:27], refs[27], refs[28]
    buffers, bounce = refs[29:33], refs[33]
    small_sum, small_in, norm_mine, norm_dp, norm_line, norm_seq = refs[34:40]
    send_sem, recv_sem, own_sem, move_sem, small_send, small_recv, norm_send, norm_recv = refs[40:48]
    here = Here(*counts)
    slots = Slots(send_sem, recv_sem)
    scatters, loads = scatters_of(here, slots, grads, buffers, shares[0:1], own_sem, splits)
    move = Exchange(here, slots, input_rows, input_grad, False, bounce, move_sem)
    total = SmallSum(here, small, small_sum, small_in, small_send, small_recv)
    for load in loads:
        load().start()
    dp_peers, seq_peers = here.all_peers()[: here.dp_count - 1], here.all_peers()[here.dp_count - 1 :]
    greet(dp_peers + seq_peers)
    waves = waves_of([[each] for each in scatters])
    more = waves_of([[total]])
    for turn in range(max(len(waves), len(more))):
        if turn < len(waves):
            waves[turn]()
        if turn < len(more):
            more[turn]()
        if turn == here.seq_bits + 1:
            move.start(0)

    rank = here.place * here.seq_count + here.line
    vector_grad, bias_grad = picked(
        small_sum[total.stages - 1], rank, shares[1].shape[1], shares[2].shape[1]
    )
    shares[1][...] = vector_grad
    shares[2][...] = bias_grad
    grads_now = [shares[0], *ready, shares[1], shares[2]]

    lane = lax.broadcasted_iota(jnp.int32, (8, 128), 1)
    row = lax.broadcasted_iota(jnp.int32, (8, 128), 0)
    tile = jnp.zeros((8, 128), FLOAT)
    for index in (0, 1, 2, 3, 5):
        decay = DECAY_RATE if index < 4 else 0.0
        weight = weights[index][...]
        update = lamb_pieces(
            weight, firsts[index][...], seconds[index][...], grads_now[index][...], decay
        )[2]
        at = row == (index if index < 4 else 4)
        tile = jnp.where(at & (lane == 0), square_sum(weight), tile)
        tile = jnp.where(at & (lane == 1), square_sum(update), tile)
    norm_mine[0:8, :] = tile
    weight = weights[4][...]
    update = lamb_pieces(weight, firsts[4][...], seconds[4][...], vector_grad, 0.0)[2]
    weight_sq = jnp.sum(weight * weight, axis=1, keepdims=True)
    update_sq = jnp.sum(update * update, axis=1, keepdims=True)
    norm_mine[8:16, :] = jnp.where(lane == 0, weight_sq, jnp.where(lane == 1, update_sq, 0.0))

    norm_slots = Slots(norm_send, norm_recv)

    def exchange(source, held, peers, at):
        base = norm_slots.take(len(peers))
        copies = [
            norm_slots.copy(base + turn, source, held.at[at], peer) for turn, peer in enumerate(peers)
        ]
        for copy in copies:
            copy.start()
        held[at] = source[...]
        for copy in copies:
            copy.wait_recv()
        found = held[0]
        for turn in range(1, held.shape[0]):
            found = found + held[turn]
        return copies, found

    sent, found = exchange(norm_mine, norm_dp, dp_peers, here.place)
    norm_line[...] = found
    also, found = exchange(norm_line, norm_seq, seq_peers, here.line)
    norm_out[...] = found
    move.finish(0)
    for copy in sent + also:
        copy.wait_send()
    drain_all(scatters + [total, move])


def scatter_last(grads, small, input_rows, ready, weights, firsts, seconds, counts):
    dp_count, seq_count = counts
    shapes = [weight.shape for weight in weights]
    splits = [True]
    slots = slot_count(counts, shapes[:1], splits, 1)
    stages = bits_of(dp_count) + bits_of(seq_count)
    return pl.pallas_call(
        functools.partial(scatter_kernel, counts, splits),
        out_shape=[jax.ShapeDtypeStruct(shapes[at], FLOAT) for at in (0, 4, 5)]
        + [
            jax.ShapeDtypeStruct((16, 128), FLOAT),
            jax.ShapeDtypeStruct((seq_count,) + input_rows.shape[0:1] + input_rows.shape[2:], BRAIN),
        ],
        in_specs=[ANYWHERE, WHOLE, ANYWHERE] + [WHOLE] * 21,
        out_specs=[WHOLE] * 4 + [ANYWHERE],
        scratch_shapes=scatter_buffers(shapes[:1], counts)
        + [
            pltpu.VMEM(input_rows.shape[0:1] + input_rows.shape[2:], BRAIN),
            pltpu.VMEM((stages,) + small.shape, FLOAT),
            pltpu.VMEM((stages,) + small.shape, FLOAT),
            pltpu.VMEM((16, 128), FLOAT),
            pltpu.VMEM((dp_count, 16, 128), FLOAT),
            pltpu.VMEM((16, 128), FLOAT),
            pltpu.VMEM((seq_count, 16, 128), FLOAT),
            pltpu.SemaphoreType.DMA((slots,)),
            pltpu.SemaphoreType.DMA((slots,)),
            pltpu.SemaphoreType.DMA((1,)),
            pltpu.SemaphoreType.DMA((2,)),
            pltpu.SemaphoreType.DMA((stages,)),
            pltpu.SemaphoreType.DMA((stages,)),
            pltpu.SemaphoreType.DMA((dp_count + seq_count,)),
            pltpu.SemaphoreType.DMA((dp_count + seq_count,)),
        ],
        name="scatter_last",
        compiler_params=pltpu.CompilerParams(
            collective_id=3, has_side_effects=True, vmem_limit_bytes=56 * 1024 * 1024
        ),
    )(*scatter_views(grads, shapes, counts), small, input_rows, *ready, *weights, *firsts, *seconds)


def lamb_kernel(*refs):
    grads, norms = refs[0:6], refs[6]
    weights, firsts, seconds = refs[7:13], refs[13:19], refs[19:25]
    grad_out, first_out, second_out, new_out = refs[25:31], refs[31:37], refs[37:43], refs[43:49]
    copy_out = refs[49:53]
    weight_norm = jnp.sqrt(norms[:, 0:1])
    scales = weight_norm / (jnp.sqrt(norms[:, 1:2]) + ADAM_EPS)
    for index in range(6):
        grad = grads[index][...]
        weight = weights[index][...]
        decay = DECAY_RATE if index < 4 else 0.0
        first_new, second_new, update = lamb_pieces(
            weight, firsts[index][...], seconds[index][...], grad, decay
        )
        scale = scales[8:16] if index == 4 else scales[min(index, 4) : min(index, 4) + 1]
        new = weight - LEARN_RATE * scale * update
        grad_out[index][...] = grad
        first_out[index][...] = first_new
        second_out[index][...] = second_new
        new_out[index][...] = new
        if index < 4:
            copy_out[index][...] = new.astype(BRAIN)


def lamb_all(grads, norms, weights, firsts, seconds):
    vmem = pl.BlockSpec(memory_space=pltpu.VMEM)
    shapes = [jax.ShapeDtypeStruct(weight.shape, FLOAT) for weight in weights]
    copies = [jax.ShapeDtypeStruct(weight.shape, BRAIN) for weight in weights[:4]]
    return pl.pallas_call(
        lamb_kernel,
        out_shape=shapes * 4 + copies,
        in_specs=[vmem] * 25,
        out_specs=[vmem] * 28,
        name="lamb_update",
        compiler_params=pltpu.CompilerParams(vmem_limit_bytes=48 * 1024 * 1024),
    )(*grads, norms, *weights, *firsts, *seconds)


def body(
    tokens,
    cotangent,
    segment_ids,
    w_qkv,
    m_qkv,
    v_qkv,
    w_out,
    m_out,
    v_out,
    w_up,
    m_up,
    v_up,
    w_down,
    m_down,
    v_down,
    vectors,
    m_vectors,
    v_vectors,
    up_bias,
    m_up_bias,
    v_up_bias,
):
    dp_count, seq_count = lax.axis_size("dp"), lax.axis_size("seq")
    vector_size, bias_size = vectors.shape[1], up_bias.shape[0]
    small = jnp.concatenate(
        [
            jnp.pad(vectors, ((0, 0), (0, 128 - vector_size))),
            jnp.pad(up_bias[None], ((0, 7), (0, 128 - bias_size))),
        ]
    )
    shards = [part.astype(BRAIN) for part in (small, w_qkv, w_out, w_up, w_down)]
    counts = (dp_count, seq_count)
    token_rows, *fulls = gather_first(tokens, shards[:2], counts)
    small = fulls[0].reshape(dp_count * seq_count, 16, 128)
    full_vectors = small[:, :8, :vector_size].transpose(1, 0, 2)
    vector_rows = full_vectors.reshape(8, -1).astype(FLOAT)
    up_shift = small[:, 8, :bias_size].reshape(-1).astype(FLOAT)
    as_matrix = lambda full: full.reshape(-1, full.shape[-1])
    full_qkv = as_matrix(fulls[1])

    width = tokens.shape[2]
    length = segment_ids.shape[1]
    rows = token_rows.shape[0]
    segments = lax.dynamic_slice_in_dim(segment_ids, lax.axis_index("seq") * rows, rows, 0)
    count = rows * length
    token_part = token_rows.reshape(count, width).astype(FLOAT)

    normed_one, plain_one, inverse_one = norm_forward(token_part, vector_rows[0], vector_rows[1])
    low_one = normed_one.astype(BRAIN)
    shifts = jnp.concatenate([vector_rows[4], jnp.zeros_like(vector_rows[4]), vector_rows[5]])
    qkv = (matmul(low_one, full_qkv) + shifts).astype(BRAIN)
    context, lse_rows, *fulls = attention_forward(segments, qkv, length, shards[2:], counts)
    full_out, full_up, full_down = [as_matrix(full) for full in fulls]
    grad_up, grad_down, grad_up_bias, grad_out, context_grad, resid_grad, sums, mixed = feed_forward(
        context,
        token_rows.reshape(count, width),
        full_out,
        full_up,
        full_down,
        vector_rows,
        up_shift[None],
        cotangent,
        counts,
    )
    joined, share_down, share_up, share_out = attention_backward(
        segments,
        qkv,
        context_grad,
        lse_rows,
        length,
        [grad_down, grad_up, grad_out],
        [w_down.shape, w_up.shape, w_out.shape],
        counts,
    )
    grad_qkv = inner_rows(low_one, joined)
    one_grad = times_transposed(joined, full_qkv)
    input_rows = resid_grad + norm_backward(one_grad, plain_one, inverse_one, vector_rows[0])
    joined_sum = jnp.sum(joined.astype(FLOAT), axis=0)
    grad_vectors = jnp.stack(
        [
            jnp.sum(one_grad * plain_one, axis=0),
            jnp.sum(one_grad, axis=0),
            sums[0],
            sums[1],
            joined_sum[:width],
            joined_sum[2 * width :],
            sums[2],
            sums[3],
        ]
    )
    small_grad = jnp.concatenate([grad_vectors, grad_up_bias.reshape(-1, width)])
    small_grad = jnp.pad(small_grad, ((0, 16 - small_grad.shape[0]), (0, 0)))
    as_row = lambda value: value.reshape(1, -1)
    weights = (w_qkv, w_out, w_up, w_down, vectors, as_row(up_bias))
    firsts = (m_qkv, m_out, m_up, m_down, m_vectors, as_row(m_up_bias))
    seconds = (v_qkv, v_out, v_up, v_down, v_vectors, as_row(v_up_bias))
    share_qkv, share_vectors, share_bias, norms, input_grad = scatter_last(
        [grad_qkv.astype(BRAIN)],
        small_grad,
        input_rows.astype(BRAIN).reshape(rows, seq_count, length // seq_count, width),
        [share_out, share_up, share_down],
        weights,
        firsts,
        seconds,
        counts,
    )
    shares = [share_qkv, share_out, share_up, share_down, share_vectors, share_bias]
    results = list(lamb_all(shares, norms, weights, firsts, seconds))
    mixed = mixed.reshape(tokens.shape)
    input_grad = input_grad.reshape(tokens.shape).astype(FLOAT)
    for index in (5, 11, 17, 23):
        results[index] = results[index].reshape(-1)
    return (mixed, input_grad, *results)


def solution(mesh):
    matrix = P(("dp", "seq"), None)
    rows = P("dp", "seq", None)
    vector = P(None, ("dp", "seq"))
    bias = P(("dp", "seq"))
    six = (matrix, matrix, matrix, matrix, vector, bias)
    in_specs = (rows, rows, P("dp", None)) + tuple(spec for spec in six for _ in range(3))
    out_specs = (rows, rows) + six * 4 + (matrix,) * 4
    return jax.shard_map(body, mesh=mesh, in_specs=in_specs, out_specs=out_specs, check_vma=False)
```

```python
import functools

import jax
import jax.numpy as jnp
from jax import lax
from jax.experimental import pallas as pl
from jax.experimental.pallas import tpu as pltpu
from jax.sharding import PartitionSpec as P

HEADS = 12
HEAD_DIM = 64
LONGEST = 512
QUERY_BLOCK = 256
ROW_BLOCK = 256


BETA_ONE = 0.9
BETA_TWO = 0.999
ADAM_EPS = 1e-06
DECAY_RATE = 0.01
LEARN_RATE = 0.4
NORM_EPS = 1e-05
STEP_NUMBER = 10.0
CORR_ONE = 1.0 - BETA_ONE**STEP_NUMBER
CORR_TWO = 1.0 - BETA_TWO**STEP_NUMBER

BRAIN = jnp.bfloat16
FLOAT = jnp.float32


def matmul(left_side, right_side):
    return jnp.dot(left_side, right_side, preferred_element_type=FLOAT)


def inner_rows(left_side, right_side):
    return lax.dot_general(
        left_side, right_side, (((0,), (0,)), ((), ())), preferred_element_type=FLOAT
    )


def times_transposed(left_side, right_side):
    return lax.dot_general(
        left_side, right_side, (((1,), (1,)), ((), ())), preferred_element_type=FLOAT
    )


def norm_parts(values):
    center = values - jnp.mean(values, axis=-1, keepdims=True)
    inverse = lax.rsqrt(jnp.mean(center * center, axis=-1, keepdims=True) + NORM_EPS)
    return center * inverse, inverse


def row_blocks(count):
    return [slice(first, first + ROW_BLOCK) for first in range(0, count, ROW_BLOCK)]


def windows(length):
    return [
        (max(0, first - LONGEST), first + QUERY_BLOCK) for first in range(0, length, QUERY_BLOCK)
    ]


def fill_bias(seg_col, seg_row, bias, length):
    place = 0
    for index, (low, high) in enumerate(windows(length)):
        first = index * QUERY_BLOCK
        size = high - low
        keys = seg_col[0, low:high, :]
        queries = seg_row[0, :, first : first + QUERY_BLOCK]
        key_place = low + lax.broadcasted_iota(jnp.int32, (size, QUERY_BLOCK), 0)
        query_place = first + lax.broadcasted_iota(jnp.int32, (size, QUERY_BLOCK), 1)
        allowed = (keys == queries) & (key_place <= query_place)
        bias[place : place + size, :] = jnp.where(allowed, 0.0, -1000000000.0)
        place += size


def split_heads(pair):
    lane = lax.broadcasted_iota(jnp.int32, pair.shape, 1)
    zero = jnp.zeros_like(pair)
    return (jnp.where(lane < HEAD_DIM, pair, zero), jnp.where(lane < HEAD_DIM, zero, pair))


def attend_forward(counts, plan, *refs):
    seg_col, seg_row, tokens, norms, shifts, wq_ref, wk_ref, wv_ref = refs[0:8]
    shards, q_ref, k_ref, v_ref, c_ref, lse_ref = refs[8:11], *refs[11:16]
    fulls, bias, low_one, bounces = refs[16:19], refs[19], refs[20], refs[21:24]
    send_sem, recv_sem, own_sem = refs[24:]
    length = q_ref.shape[0]
    here = Here(*counts)
    slots = Slots(send_sem, recv_sem)
    gathers = gathers_of(here, slots, shards, fulls, bounces, own_sem, plan)
    groups = [gathers[:2]] + [[each] for each in gathers[2:]]
    waves = led_by(lambda: greet(here.near_peers()), waves_of(groups))
    blocks = windows(length)
    beside = Beside(waves, HEADS // 2 * len(blocks))

    @pl.when(pl.program_id(0) == 0)
    def _():
        beside.point(0, len(blocks))
        fill_bias(seg_col, seg_row, bias, length)
        for rows in row_blocks(length):
            normed, _ = norm_parts(tokens[rows, :].astype(FLOAT))
            low_one[rows, :] = (normed * norms[0:1, :] + norms[1:2, :]).astype(BRAIN)

    lanes = 2 * HEAD_DIM
    joined = jnp.concatenate([wq_ref[...], wk_ref[...], wv_ref[...]], axis=1)
    for rows in row_blocks(length):
        projected = matmul(low_one[rows, :], joined)
        q_ref[rows, :] = (projected[:, :lanes] + shifts[4:5, :]).astype(BRAIN)
        k_ref[rows, :] = projected[:, lanes : 2 * lanes].astype(BRAIN)
        v_ref[rows, :] = (projected[:, 2 * lanes :] + shifts[5:6, :]).astype(BRAIN)
    v_turned = v_ref[...].T
    place = 0
    for index, (low, high) in enumerate(blocks):
        if index:
            beside.point(index, len(blocks))
        else:
            beside.point(0, len(blocks), skip_first=True)
        first = index * QUERY_BLOCK
        size = high - low
        queries = split_heads(q_ref[first : first + QUERY_BLOCK, :] * HEAD_DIM ** (-0.5))
        keys = k_ref[low:high, :]
        blocked = bias[place : place + size, :]
        parts = []
        for head in range(2):
            scores = times_transposed(keys, queries[head]) + blocked
            peak = jnp.max(scores, axis=0, keepdims=True)
            probs = jnp.exp(scores - peak)
            total = jnp.sum(probs, axis=0, keepdims=True)
            probs = (probs * (1.0 / total)).astype(BRAIN)
            lse_ref[0, head : head + 1, first : first + QUERY_BLOCK] = peak + jnp.log(total)
            turned = v_turned[head * HEAD_DIM : (head + 1) * HEAD_DIM, low:high]
            parts.append(matmul(turned, probs))
        context = jnp.concatenate(parts, axis=0).T
        c_ref[first : first + QUERY_BLOCK, :] = context.astype(BRAIN)
        place += size

    @pl.when(pl.program_id(0) == HEADS // 2 - 1)
    def _():
        beside.rest()
        drain_all(gathers)


def led_by(ahead, waves):
    def both():
        ahead()
        waves[0]()

    return [both] + waves[1:]


class Beside:
    def __init__(self, waves, points):
        self.at = {}
        early = len(waves) - 1
        for index in range(early):
            self.at.setdefault(index * points // early, []).append(waves[index])
        self.late = waves[early:]

    def point(self, index, per_step, skip_first=False):
        for point, calls in self.at.items():
            if point % per_step == index and (index or skip_first == (point > 0)):

                @pl.when(pl.program_id(0) == point // per_step)
                def _(calls=calls):
                    for call in calls:
                        call()

    def rest(self):
        for call in self.late:
            call()


def attend_backward(counts, plan, *refs):
    seg_col, seg_row, q_ref, k_ref, v_ref, g_ref, lse_ref = refs[0:7]
    tokens, norms, resid_grad, wq_ref, wk_ref, wv_ref = refs[7:13]
    grads, gq_ref, gk_ref, gv_ref, shift_ref, sum_ref, input_ref = refs[13:16], *refs[16:22]
    shares, bias, key_sum, value_sum, low_turned, total, joined = refs[22:25], *refs[25:31]
    buffers, send_sem, recv_sem, own_sem = refs[31:43], *refs[43:]
    length = q_ref.shape[0]
    pair = pl.program_id(0)
    here = Here(*counts)
    slots = Slots(send_sem, recv_sem)
    scatters, loads = scatters_of(here, slots, grads, buffers, shares, own_sem, plan)

    def begin():
        for load in loads:
            load().start()
        greet(here.near_peers())

    groups = [[each] for each in scatters[:-2]] + [scatters[-2:]]
    waves = led_by(begin, waves_of(groups))
    blocks = windows(length)
    beside = Beside(waves, HEADS // 2 * len(blocks))

    @pl.when(pair == 0)
    def _():
        beside.point(0, len(blocks))
        fill_bias(seg_col, seg_row, bias, length)
        for rows in row_blocks(length):
            normed, _ = norm_parts(tokens[rows, :].astype(FLOAT))
            low_turned[:, rows] = (normed * norms[0:1, :] + norms[1:2, :]).astype(BRAIN).T
        total[...] = jnp.zeros_like(total)

    key_sum[...] = jnp.zeros_like(key_sum)
    value_sum[...] = jnp.zeros_like(value_sum)
    k_turned = k_ref[...].T
    lanes = 2 * HEAD_DIM
    place = 0
    for index, (low, high) in enumerate(blocks):
        if index:
            beside.point(index, len(blocks))
        else:
            beside.point(0, len(blocks), skip_first=True)
        first = index * QUERY_BLOCK
        size = high - low
        rows = slice(first, first + QUERY_BLOCK)
        queries = split_heads(q_ref[rows, :] * HEAD_DIM ** (-0.5))
        grads = split_heads(g_ref[rows, :])
        keys = k_ref[low:high, :]
        values = v_ref[low:high, :]
        blocked = bias[place : place + size, :]
        all_probs = []
        all_scores = []
        parts = []
        for head in range(2):
            scores = times_transposed(keys, queries[head]) + blocked
            probs = jnp.exp(scores - lse_ref[0, head : head + 1, rows])
            prob_grad = times_transposed(values, grads[head])
            row_dot = jnp.sum(probs * prob_grad, axis=0, keepdims=True)
            score_grad = (probs * (prob_grad - row_dot)).astype(BRAIN)
            all_probs.append(probs.astype(BRAIN))
            all_scores.append(score_grad)
            turned = k_turned[head * HEAD_DIM : (head + 1) * HEAD_DIM, low:high]
            parts.append(matmul(turned, score_grad))
        query_grad = jnp.concatenate(parts, axis=0).T * HEAD_DIM ** (-0.5)
        joined[rows, :lanes] = query_grad.astype(BRAIN)
        value_sum[low:high, :] += matmul(
            jnp.concatenate(all_probs, axis=1), jnp.concatenate(grads, axis=0)
        )
        key_sum[low:high, :] += matmul(
            jnp.concatenate(all_scores, axis=1), jnp.concatenate(queries, axis=0)
        )
        place += size
    joined[:, lanes : 2 * lanes] = key_sum[...].astype(BRAIN)
    joined[:, 2 * lanes :] = value_sum[...].astype(BRAIN)
    weight = jnp.concatenate([wq_ref[...], wk_ref[...], wv_ref[...]], axis=1)
    sums = jnp.zeros((1, 3 * lanes), FLOAT)
    for rows in row_blocks(length):
        part = joined[rows, :]
        total[rows, :] += times_transposed(part, weight)
        sums = sums + jnp.sum(part.astype(FLOAT), axis=0, keepdims=True)
    found = matmul(low_turned[...], joined[...]).astype(BRAIN)
    gq_ref[...] = found[:, :lanes]
    gk_ref[...] = found[:, lanes : 2 * lanes]
    gv_ref[...] = found[:, 2 * lanes :]
    shift_ref[0:1, :] = sums[:, :lanes]
    shift_ref[1:2, :] = sums[:, 2 * lanes :]
    shift_ref[2:8, :] = jnp.zeros((6, lanes), FLOAT)

    @pl.when(pair == HEADS // 2 - 1)
    def _():
        gains = jnp.zeros((1, total.shape[1]), FLOAT)
        moves = jnp.zeros((1, total.shape[1]), FLOAT)
        for rows in row_blocks(length):
            normed, inverse = norm_parts(tokens[rows, :].astype(FLOAT))
            upstream = total[rows, :]
            scaled = upstream * norms[0:1, :]
            centered = scaled - jnp.mean(scaled, axis=-1, keepdims=True)
            inward = centered - normed * jnp.mean(scaled * normed, axis=-1, keepdims=True)
            input_ref[rows, :] = (resid_grad[rows, :] + inverse * inward).astype(BRAIN)
            gains = gains + jnp.sum(upstream * normed, axis=0, keepdims=True)
            moves = moves + jnp.sum(upstream, axis=0, keepdims=True)
        sum_ref[0:1, :] = gains
        sum_ref[1:2, :] = moves
        sum_ref[2:8, :] = jnp.zeros((6, total.shape[1]), FLOAT)

    @pl.when(pair == HEADS // 2 - 1)
    def _():
        beside.rest()
        drain_all(scatters)


def once(shape):
    return pl.BlockSpec(shape, lambda *_: (0,) * len(shape), pipeline_mode=pl.Buffered(1))


def pair_specs(length):
    lanes, width = 2 * HEAD_DIM, HEADS * HEAD_DIM
    pairs = HEADS // 2
    segs = [once((1, length, 1)), once((1, 1, length))]
    plain = pl.BlockSpec((length, lanes), lambda j: (0, j))
    lse = pl.BlockSpec((1, 8, length), lambda j: (j, 0, 0))
    weights = [pl.BlockSpec((width, lanes), lambda j, at=at: (0, at * pairs + j)) for at in range(3)]
    shifts = pl.BlockSpec((8, lanes), lambda j: (0, j))
    bias = pltpu.VMEM((sum(high - low for low, high in windows(length)), QUERY_BLOCK), FLOAT)
    return segs, plain, lse, weights, shifts, bias


def attention_forward(segments, tokens, vectors, full_qkv, shards, counts):
    length, width = tokens.shape
    segs, plain, lse, weights, shifts, bias = pair_specs(length)
    plan = [(False, False)] + [(True, False)] * (len(shards) - 1)
    slots = slot_count(counts, [shard.shape for shard in shards], plan, 0)
    return pl.pallas_call(
        functools.partial(attend_forward, counts, plan),
        grid=(HEADS // 2,),
        in_specs=segs
        + [once((length, width)), once((8, width)), shifts]
        + weights
        + [ANYWHERE] * 3,
        out_specs=[plain] * 4 + [lse] + [ANYWHERE] * 3,
        out_shape=[jax.ShapeDtypeStruct((length, width), BRAIN)] * 4
        + [jax.ShapeDtypeStruct((HEADS // 2, 8, length), FLOAT)]
        + [full_shape(shard, *counts) for shard in shards],
        scratch_shapes=[bias, pltpu.VMEM((length, width), BRAIN)]
        + [pltpu.VMEM(shard.shape, shard.dtype) for shard in shards]
        + [
            pltpu.SemaphoreType.DMA((slots,)),
            pltpu.SemaphoreType.DMA((slots,)),
            pltpu.SemaphoreType.DMA((2 * len(shards),)),
        ],
        name="attend_forward",
        compiler_params=pltpu.CompilerParams(
            collective_id=1, has_side_effects=True, vmem_limit_bytes=48 * 1024 * 1024
        ),
    )(
        segments[:, :, None],
        segments[:, None, :],
        tokens,
        vectors,
        vectors,
        full_qkv,
        full_qkv,
        full_qkv,
        *shards,
    )


def attention_backward(
    segments, heads, context_grad, lse_rows, tokens, vectors, resid_grad, full_qkv, grads, shapes, counts
):
    length, width = tokens.shape
    lanes = 2 * HEAD_DIM
    segs, plain, lse, weights, shifts, bias = pair_specs(length)
    column = pl.BlockSpec((width, lanes), lambda j: (0, j))
    plan = [(True, False)] * (len(shapes) - 1) + [(False, False)]
    slots = slot_count(counts, shapes, plan, 0)
    return pl.pallas_call(
        functools.partial(attend_backward, counts, plan),
        grid=(HEADS // 2,),
        in_specs=segs
        + [plain] * 4
        + [lse, once((length, width)), once((8, width)), once((length, width))]
        + weights
        + [ANYWHERE] * 3,
        out_specs=[column] * 3 + [shifts, once((8, width)), once((length, width))] + [WHOLE] * 3,
        out_shape=[jax.ShapeDtypeStruct((width, width), BRAIN)] * 3
        + [jax.ShapeDtypeStruct((8, width), FLOAT)] * 2
        + [jax.ShapeDtypeStruct((length, width), BRAIN)]
        + [jax.ShapeDtypeStruct(shape, FLOAT) for shape in shapes],
        scratch_shapes=[
            bias,
            pltpu.VMEM((length, lanes), FLOAT),
            pltpu.VMEM((length, lanes), FLOAT),
            pltpu.VMEM((width, length), BRAIN),
            pltpu.VMEM((length, width), FLOAT),
            pltpu.VMEM((length, 3 * lanes), BRAIN),
        ]
        + scatter_buffers(shapes, plan, counts)
        + [
            pltpu.SemaphoreType.DMA((slots,)),
            pltpu.SemaphoreType.DMA((slots,)),
            pltpu.SemaphoreType.DMA((len(shapes),)),
        ],
        name="attend_backward",
        compiler_params=pltpu.CompilerParams(
            collective_id=2, has_side_effects=True, vmem_limit_bytes=62 * 1024 * 1024
        ),
    )(
        segments[:, :, None],
        segments[:, None, :],
        *heads,
        context_grad,
        lse_rows,
        tokens,
        vectors,
        resid_grad,
        full_qkv,
        full_qkv,
        full_qkv,
        *scatter_views(grads, shapes, counts),
    )


MESH = pl.DeviceIdType.MESH
ANYWHERE = pl.BlockSpec(memory_space=pl.ANY)
WHOLE = pl.BlockSpec(memory_space=pltpu.VMEM)


def bits_of(count):
    return count.bit_length() - 1


def flipped(value, bit):
    step = 1 << bit
    return value + step * (1 - 2 * lax.rem(lax.div(value, step), 2))


def rounded_down(value, bit):
    return lax.div(value, 1 << bit) * (1 << bit)


def spread(value, bit, total):
    step = 1 << (bit + 1)
    return [lax.rem(value, step) + step * turn for turn in range(1 << (total - 1 - bit))]


class Here:
    def __init__(self, dp_count, seq_count):
        self.dp_count, self.seq_count = dp_count, seq_count
        self.half_count = dp_count // 2
        self.seq_bits = bits_of(seq_count)
        self.place, self.line = lax.axis_index("dp"), lax.axis_index("seq")
        self.chip, self.core = lax.div(self.place, 2), lax.rem(self.place, 2)

    def core_peer(self):
        return {"dp": flipped(self.place, 0)}

    def line_peer(self, bit):
        return {"seq": flipped(self.line, bit)}

    def other_lines(self):
        return [lax.rem(self.line + turn, self.seq_count) for turn in range(1, self.seq_count)]

    def other_chips(self):
        return [lax.rem(self.chip + turn, self.half_count) for turn in range(1, self.half_count)]

    def chip_peers(self):
        return [{"dp": 2 * chip + self.core} for chip in self.other_chips()]

    def near_peers(self):
        peers = [self.core_peer()] + self.chip_peers()
        return peers + [{"seq": line} for line in self.other_lines()]

    def all_peers(self):
        peers = [{"dp": lax.rem(self.place + turn, self.dp_count)} for turn in range(1, self.dp_count)]
        return peers + [{"seq": line} for line in self.other_lines()]


def greet(peers):
    barrier = pltpu.get_barrier_semaphore()
    for peer in peers:
        pl.semaphore_signal(barrier, inc=1, device_id=peer, device_id_type=MESH)
    pl.semaphore_wait(barrier, len(peers))


class Slots:
    def __init__(self, send_sem, recv_sem):
        self.send_sem, self.recv_sem, self.used = send_sem, recv_sem, 0

    def take(self, count):
        first = self.used
        self.used += count
        return first

    def copy(self, slot, source, target, peer):
        return pltpu.make_async_remote_copy(
            source,
            target,
            self.send_sem.at[slot],
            self.recv_sem.at[slot],
            device_id=peer,
            device_id_type=MESH,
        )


def parts_of(shape, split):
    rows, width = shape
    tiles = width // 128
    if width % 128 or tiles < 2:
        return [[(slice(0, rows), slice(0, width), False)]]
    middle = tiles // 2 * 128
    first, second = (0, middle), (middle, width)
    every = slice(0, rows)
    if split and rows % 32 == 0:
        return [
            [(part, slice(*first), False), (part, slice(*second), True)]
            for part in (slice(0, rows // 2), slice(rows // 2, rows))
        ]
    if split and tiles >= 4:
        lists = [[], []]
        for (low, high), backwards in ((first, False), (second, True)):
            cut = low + (high - low) // 256 * 128
            lists[0].append((every, slice(low, cut), backwards))
            lists[1].append((every, slice(cut, high), backwards))
        return lists
    return [[(every, slice(*first), False), (every, slice(*second), True)]]


class Transfer:
    def start(self, stage):
        for copy in self.copies(stage):
            copy.start()

    def finish(self, stage):
        for copy in self.copies(stage):
            copy.wait_recv()
        self.use(stage)

    def use(self, stage):
        pass

    def drain(self):
        for stage in range(self.stages):
            for copy in self.copies(stage):
                copy.wait_send()


class Gather(Transfer):
    def __init__(self, here, slots, shard, full, pieces, own_done, line_first=False):
        self.here, self.slots, self.shard, self.full = here, slots, shard, full
        self.pieces, self.own_done, self.line_first = pieces, own_done, line_first
        self.stages = here.seq_bits + 2
        self.each = here.half_count + here.seq_count
        self.first = slots.take(self.each * len(pieces))

    def copies(self, stage):
        here, full = self.here, self.full
        chip_stage = here.seq_bits if self.line_first else 0
        chips = here.chip if self.line_first else slice(None)
        found = []
        for index, (rows, columns, backwards) in enumerate(self.pieces):
            slot = self.first + self.each * index
            if stage == chip_stage:
                lines = slice(None) if self.line_first else here.line
                target = full.at[here.chip, here.core, lines, rows, columns]
                source = target if self.line_first else self.shard.at[rows, columns]
                for turn, peer in enumerate(here.chip_peers()):
                    found.append(self.slots.copy(slot + turn, source, target, peer))
                continue
            slot += here.half_count - 1
            if stage == self.stages - 1:
                part = full.at[:, here.core, :, rows, columns]
                slot += here.seq_count - 1
                found.append(self.slots.copy(slot, part, part, here.core_peer()))
                continue
            past = stage if self.line_first else stage - 1
            if backwards:
                bit = here.seq_bits - 1 - past
                slot += (1 << past) - 1
                parts = [
                    full.at[chips, here.core, at, rows, columns]
                    for at in spread(here.line, bit, here.seq_bits)
                ]
            else:
                bit = past
                slot += bit
                block = pl.ds(rounded_down(here.line, bit), 1 << bit)
                parts = [full.at[chips, here.core, block, rows, columns]]
            for turn, part in enumerate(parts):
                found.append(self.slots.copy(slot + turn, part, part, here.line_peer(bit)))
        return found

    def start(self, stage):
        if stage == (0 if self.line_first else 1):
            self.own_done()
        super().start(stage)


class Scatter(Transfer):
    def __init__(
        self, here, slots, grad, own, from_core, from_line, from_chip, share, pieces, load, line_last
    ):
        self.here, self.slots, self.grad, self.own = here, slots, grad, own
        self.from_core, self.from_line, self.from_chip = from_core, from_line, from_chip
        self.share, self.pieces, self.load, self.line_last = share, pieces, load, line_last
        self.stages = here.seq_bits + 2
        self.chip_stage = 1 if line_last else here.seq_bits + 1
        self.each = here.half_count + here.seq_count
        self.first = slots.take(self.each * len(pieces))

    def line_stage(self, stage, backwards):
        here = self.here
        past = stage - 2 if self.line_last else stage - 1
        if backwards:
            bit = past
            away = spread(flipped(here.line, bit), bit, here.seq_bits)
            kept = spread(here.line, bit, here.seq_bits)
        else:
            bit = here.seq_bits - 1 - past
            away = [rounded_down(flipped(here.line, bit), bit) + at for at in range(1 << bit)]
            kept = [rounded_down(here.line, bit) + at for at in range(1 << bit)]
        base = sum(1 << (here.seq_bits - 1 - before) for before in range(past))
        return bit, away, kept, base

    def copies(self, stage):
        here = self.here
        found = []
        for index, (rows, columns, backwards) in enumerate(self.pieces):
            slot = self.first + self.each * index
            if stage == 0:
                found.append(
                    self.slots.copy(
                        slot,
                        self.grad.at[:, 1 - here.core, :, rows, columns],
                        self.from_core.at[:, :, rows, columns],
                        here.core_peer(),
                    )
                )
            elif stage == self.chip_stage:
                slot += here.seq_count
                lines = slice(None) if self.line_last else here.line
                places = slice(None) if self.line_last else 0
                for turn, chip in enumerate(here.other_chips()):
                    found.append(
                        self.slots.copy(
                            slot + turn,
                            self.own.at[chip, lines, rows, columns],
                            self.from_chip.at[turn, places, rows, columns],
                            {"dp": 2 * chip + here.core},
                        )
                    )
            else:
                bit, away, _, base = self.line_stage(stage, backwards)
                chips = here.chip if self.line_last else slice(None)
                places = 0 if self.line_last else slice(None)
                for turn, at in enumerate(away):
                    found.append(
                        self.slots.copy(
                            slot + 1 + base + turn,
                            self.own.at[chips, at, rows, columns],
                            self.from_line.at[base + turn, places, rows, columns],
                            here.line_peer(bit),
                        )
                    )
        return found

    def put(self, rows, columns, values):
        share, offset = self.share
        share[rows, slice(columns.start + offset, columns.stop + offset)] = values

    def use(self, stage):
        here, own = self.here, self.own
        if stage == 0:
            self.load()
        last = stage == self.stages - 1
        for rows, columns, backwards in self.pieces:
            if stage == 0:

                def add(at, carry, rows=rows, columns=columns):
                    one, two = lax.div(at, here.seq_count), lax.rem(at, here.seq_count)
                    own[one, two, rows, columns] = (
                        own[one, two, rows, columns] + self.from_core[one, two, rows, columns]
                    )
                    return carry

                lax.fori_loop(0, here.half_count * here.seq_count, add, 0)
            elif stage == self.chip_stage:

                def total(line, place, rows=rows, columns=columns):
                    found = own[here.chip, line, rows, columns].astype(FLOAT)
                    for turn in range(here.half_count - 1):
                        found = found + self.from_chip[turn, place, rows, columns].astype(FLOAT)
                    return found

                if last:
                    self.put(rows, columns, total(here.line, 0))
                    continue

                def add(line, carry, rows=rows, columns=columns, total=total):
                    own[here.chip, line, rows, columns] = total(line, line).astype(BRAIN)
                    return carry

                lax.fori_loop(0, here.seq_count, add, 0)
            else:
                _, _, kept, base = self.line_stage(stage, backwards)
                for turn, at in enumerate(kept):
                    place = base + turn
                    if last:
                        mine = own[here.chip, at, rows, columns].astype(FLOAT)
                        theirs = self.from_line[place, 0, rows, columns].astype(FLOAT)
                        self.put(rows, columns, mine + theirs)
                    elif self.line_last:
                        own[here.chip, at, rows, columns] = (
                            own[here.chip, at, rows, columns]
                            + self.from_line[place, 0, rows, columns]
                        )
                    else:

                        def add(one, carry, rows=rows, columns=columns, at=at, place=place):
                            own[one, at, rows, columns] = (
                                own[one, at, rows, columns]
                                + self.from_line[place, one, rows, columns]
                            )
                            return carry

                        lax.fori_loop(0, here.half_count, add, 0)


class Exchange(Transfer):
    stages = 1

    def __init__(self, here, slots, source, target, to_rows, bounce, sem):
        self.here, self.slots, self.source, self.target = here, slots, source, target
        self.to_rows, self.bounce, self.sem = to_rows, bounce, sem
        self.first = slots.take(here.seq_count - 1)

    def ends(self, line):
        if self.to_rows:
            count = self.target.shape[0]
            block = self.source.at[pl.ds(line * count, count)]
            return block, self.target.at[:, self.here.line]
        return self.source.at[:, line], self.target.at[self.here.line]

    def copies(self, stage):
        return [
            self.slots.copy(self.first + turn, *self.ends(line), {"seq": line})
            for turn, line in enumerate(self.here.other_lines())
        ]

    def own_in(self):
        return pltpu.make_async_copy(self.ends(self.here.line)[0], self.bounce, self.sem.at[0])

    def own_out(self):
        source, target = self.ends(self.here.line)
        source = source if self.bounce is None else self.bounce
        return pltpu.make_async_copy(source, target, self.sem.at[1])

    def start(self, stage):
        if self.bounce is not None:
            self.own_in().start()
        super().start(stage)
        if self.bounce is not None:
            self.own_in().wait()
        self.own_out().start()

    def use(self, stage):
        self.own_out().wait()


def waves_of(groups):
    def wave(count):
        for index, group in enumerate(groups):
            stage = count - index
            for transfer in group:
                if 1 <= stage <= transfer.stages:
                    transfer.finish(stage - 1)
            for transfer in group:
                if 0 <= stage < transfer.stages:
                    transfer.start(stage)

    total = max(index + transfer.stages for index, group in enumerate(groups) for transfer in group)
    return [functools.partial(wave, count) for count in range(total + 1)]


def drain_all(transfers):
    for transfer in transfers:
        transfer.drain()


def gathers_of(here, slots, shards, fulls, bounces, sem, plan):
    found = []
    for index, (shard, full, bounce) in enumerate(zip(shards, fulls, bounces)):
        inward = lambda shard=shard, bounce=bounce, index=index: pltpu.make_async_copy(
            shard, bounce, sem.at[2 * index]
        )
        outward = lambda full=full, bounce=bounce, index=index: pltpu.make_async_copy(
            bounce, full.at[here.chip, here.core, here.line], sem.at[2 * index + 1]
        )
        split, line_first = plan[index]
        for order, pieces in enumerate(parts_of(shard.shape, split)):

            def own_done(first=order == 0, inward=inward, outward=outward):
                if first:
                    inward().start()
                    inward().wait()
                    outward().start()
                    outward().wait()

            found.append(Gather(here, slots, shard, full, pieces, own_done, line_first))
    return found


def slot_count(here_shape, shapes, plan, exchanges):
    half_count, seq_count = here_shape[0] // 2, here_shape[1]
    each = half_count + seq_count
    pieces = sum(
        len(part) for shape, (split, _) in zip(shapes, plan) for part in parts_of(shape, split)
    )
    return each * pieces + exchanges * (seq_count - 1)


def full_shape(shard, dp_count, seq_count):
    return jax.ShapeDtypeStruct((dp_count // 2, 2, seq_count) + shard.shape, shard.dtype)


def gather_kernel(counts, plan, count, *refs):
    tokens, shards, fulls = refs[0], refs[1 : 1 + count], refs[2 + count : 2 + 2 * count]
    token_rows = refs[1 + count]
    rest = refs[2 + 2 * count :]
    bounces, bounce, send_sem, recv_sem, own_sem, move_sem = rest[:count], *rest[count:]
    here = Here(*counts)
    slots = Slots(send_sem, recv_sem)
    gathers = gathers_of(here, slots, shards, fulls, bounces, own_sem, plan)
    move = Exchange(here, slots, tokens, token_rows, True, bounce, move_sem)
    greet(here.near_peers())
    waves = waves_of([gathers[:2]] + [[each] for each in gathers[2:]])
    waves[0]()
    move.start(0)
    for wave in waves[1:]:
        wave()
    move.finish(0)
    drain_all(gathers + [move])


def gather_first(tokens, shards, counts):
    dp_count, seq_count = counts
    row_count, pos_count, width = tokens.shape
    rows = row_count // seq_count
    plan = [(True, False)] * len(shards)
    slots = slot_count(counts, [shard.shape for shard in shards], plan, 1)
    return pl.pallas_call(
        functools.partial(gather_kernel, counts, plan, len(shards)),
        out_shape=[jax.ShapeDtypeStruct((rows, seq_count, pos_count, width), tokens.dtype)]
        + [full_shape(shard, *counts) for shard in shards],
        in_specs=[ANYWHERE] * (1 + len(shards)),
        out_specs=[ANYWHERE] * (1 + len(shards)),
        scratch_shapes=[pltpu.VMEM(shard.shape, shard.dtype) for shard in shards]
        + [
            pltpu.VMEM((rows, pos_count, width), tokens.dtype),
            pltpu.SemaphoreType.DMA((slots,)),
            pltpu.SemaphoreType.DMA((slots,)),
            pltpu.SemaphoreType.DMA((2 * len(shards),)),
            pltpu.SemaphoreType.DMA((2,)),
        ],
        name="gather_first",
        compiler_params=pltpu.CompilerParams(collective_id=0, has_side_effects=True),
    )(tokens, *shards)


HIDDEN_BLOCK = 512
GELU_SCALE = 0.7978845608028654
GELU_CUBE = 0.044715


def gelu_both(values):
    square = values * values
    turned = jnp.tanh(GELU_SCALE * values * (1.0 + GELU_CUBE * square))
    half = 0.5 + 0.5 * turned
    inner = GELU_SCALE * (1.0 + 3.0 * GELU_CUBE * square)
    return values * half, half + 0.5 * values * (1.0 - turned * turned) * inner


def forward_start(context, tokens, w_out, vectors, resid, low_two, low_turned):
    for rows in row_blocks(resid.shape[0]):
        values = tokens[rows, :].astype(FLOAT) + (matmul(context[rows, :], w_out[...]) + vectors[6:7, :])
        resid[rows, :] = values
        normed, _ = norm_parts(values)
        low = (normed * vectors[2:3, :] + vectors[3:4, :]).astype(BRAIN)
        low_two[rows, :] = low
        low_turned[:, rows] = low.T


def backward_end(
    context, w_out, vectors, resid, total, back, gc_ref, gr_ref, gwo_ref, sum_ref, low_turned
):
    width = resid.shape[1]
    sums = [jnp.zeros((1, width), FLOAT) for _ in range(4)]
    for rows in row_blocks(resid.shape[0]):
        normed, inverse = norm_parts(resid[rows, :])
        upstream = total[rows, :]
        given = back(rows).astype(FLOAT)
        scaled = upstream * vectors[2:3, :]
        centered = scaled - jnp.mean(scaled, axis=-1, keepdims=True)
        inward = centered - normed * jnp.mean(scaled * normed, axis=-1, keepdims=True)
        grad = given + inverse * inward
        low = grad.astype(BRAIN)
        gr_ref[rows, :] = grad
        gc_ref[rows, :] = times_transposed(low, w_out[...]).astype(BRAIN)
        low_turned[:, rows] = context[rows, :].T
        total[rows, :] = low.astype(FLOAT)
        for index, values in enumerate((upstream * normed, upstream, low.astype(FLOAT), given)):
            sums[index] = sums[index] + jnp.sum(values, axis=0, keepdims=True)
    for index in range(4):
        sum_ref[index : index + 1, :] = sums[index]
    sum_ref[4:8, :] = jnp.zeros((4, width), FLOAT)
    gwo_ref[...] = matmul(low_turned[...], total[...].astype(BRAIN)).astype(BRAIN)


def mlp_kernel(counts, *refs):
    context, tokens, w_out, w_up, w_down, vectors, up_shift, cotangent = refs[0:8]
    gup_ref, gdown_ref, gub_ref, gwo_ref, gc_ref, gr_ref, sum_ref, mixed = refs[8:16]
    acts, slopes, low_two, low_turned, resid, total, hidden, back, mixed_rows = refs[16:25]
    send_sem, recv_sem, move_sem = refs[25:28]
    here = Here(*counts)
    slots = Slots(send_sem, recv_sem)
    arrive = Exchange(here, slots, cotangent, back, True, None, move_sem.at[pl.ds(0, 2)])
    leave = Exchange(here, slots, mixed_rows, mixed, False, None, move_sem.at[pl.ds(2, 2)])
    step = pl.program_id(0)
    half = pl.num_programs(0) // 2
    count = resid.shape[0]
    pos_count = back.shape[2]

    def back_rows(rows):
        parts = []
        for first in range(rows.start, rows.stop, pos_count):
            size = min(pos_count, rows.stop - first)
            row, rest = divmod(first, pos_count * counts[1])
            line, offset = divmod(rest, pos_count)
            parts.append(back[row, line, offset : offset + size, :])
        return parts[0] if len(parts) == 1 else jnp.concatenate(parts, axis=0)

    @pl.when(step == 0)
    def _():
        greet(here.near_peers())
        arrive.start(0)
        forward_start(context, tokens, w_out, vectors, resid, low_two, low_turned)
        total[...] = jnp.zeros_like(total)

    @pl.when(step < half)
    def _():
        for rows in row_blocks(count):
            values = matmul(low_two[rows, :], w_up[...]) + up_shift[...]
            act, slope = gelu_both(values)
            low = act.astype(BRAIN)
            acts[step, rows, :] = low
            slopes[step, rows, :] = slope
            total[rows, :] += matmul(low, w_down[...])

    @pl.when(step == half)
    def _():
        for first in range(0, count, pos_count):
            row, line = divmod(first // pos_count, counts[1])
            rows = slice(first, first + pos_count)
            values = resid[rows, :] + (total[rows, :] + vectors[7:8, :])
            mixed_rows[row, line] = values.astype(BRAIN)
        total[...] = jnp.zeros_like(total)
        leave.start(0)
        arrive.finish(0)

    @pl.when(step >= half)
    def _():
        at = step - half
        sums = jnp.zeros((1, hidden.shape[1]), FLOAT)
        for rows in row_blocks(count):
            grad = times_transposed(back_rows(rows), w_down[...]) * slopes[at, rows, :]
            low = grad.astype(BRAIN)
            hidden[rows, :] = low
            sums = sums + jnp.sum(low.astype(FLOAT), axis=0, keepdims=True)
            total[rows, :] += times_transposed(low, w_up[...])
        gub_ref[...] = sums
        gup_ref[...] = matmul(low_turned[...], hidden[...]).astype(BRAIN)
        every = back_rows(slice(0, count))
        gdown_ref[...] = inner_rows(acts[at], every).astype(BRAIN)

    @pl.when(step == 2 * half - 1)
    def _():
        backward_end(
            context, w_out, vectors, resid, total, back_rows, gc_ref, gr_ref, gwo_ref, sum_ref, low_turned
        )
        leave.finish(0)
        drain_all([arrive, leave])


def feed_forward(context, tokens, w_out, w_up, w_down, vectors, up_shift, cotangent, counts):
    count, width = context.shape
    hidden = w_up.shape[1]
    half = hidden // HIDDEN_BLOCK
    seq_count = counts[1]
    row_count, pos_count, _ = cotangent.shape
    rows = row_count // seq_count
    later = lambda j: jnp.maximum(j - half, 0)
    around = lambda j: lax.rem(j, half)
    block = HIDDEN_BLOCK
    slots = 2 * (seq_count - 1)
    return pl.pallas_call(
        functools.partial(mlp_kernel, counts),
        grid=(2 * half,),
        in_specs=[
            once((count, width)),
            once((count, width)),
            once((width, width)),
            pl.BlockSpec((width, block), lambda j: (0, around(j))),
            pl.BlockSpec((block, width), lambda j: (around(j), 0)),
            once((8, width)),
            pl.BlockSpec((1, block), lambda j: (0, around(j))),
            ANYWHERE,
        ],
        out_specs=[
            pl.BlockSpec((width, block), lambda j: (0, later(j))),
            pl.BlockSpec((block, width), lambda j: (later(j), 0)),
            pl.BlockSpec((1, block), lambda j: (0, later(j))),
            once((width, width)),
            once((count, width)),
            once((count, width)),
            once((8, width)),
            ANYWHERE,
        ],
        out_shape=[
            jax.ShapeDtypeStruct((width, hidden), BRAIN),
            jax.ShapeDtypeStruct((hidden, width), BRAIN),
            jax.ShapeDtypeStruct((1, hidden), FLOAT),
            jax.ShapeDtypeStruct((width, width), BRAIN),
            jax.ShapeDtypeStruct((count, width), BRAIN),
            jax.ShapeDtypeStruct((count, width), FLOAT),
            jax.ShapeDtypeStruct((8, width), FLOAT),
            jax.ShapeDtypeStruct((seq_count, rows, pos_count, width), BRAIN),
        ],
        scratch_shapes=[
            pltpu.VMEM((half, count, block), BRAIN),
            pltpu.VMEM((half, count, block), FLOAT),
            pltpu.VMEM((count, width), BRAIN),
            pltpu.VMEM((width, count), BRAIN),
            pltpu.VMEM((count, width), FLOAT),
            pltpu.VMEM((count, width), FLOAT),
            pltpu.VMEM((count, block), BRAIN),
            pltpu.VMEM((rows, seq_count, pos_count, width), BRAIN),
            pltpu.VMEM((rows, seq_count, pos_count, width), BRAIN),
            pltpu.SemaphoreType.DMA((slots,)),
            pltpu.SemaphoreType.DMA((slots,)),
            pltpu.SemaphoreType.DMA((4,)),
        ],
        name="feed_forward",
        compiler_params=pltpu.CompilerParams(
            collective_id=4, has_side_effects=True, vmem_limit_bytes=63 * 1024 * 1024
        ),
    )(context, tokens, w_out, w_up, w_down, vectors, up_shift, cotangent)


def lamb_pieces(weight, first, second, grad, decay):
    first_new = BETA_ONE * first + (1.0 - BETA_ONE) * grad
    second_new = BETA_TWO * second + (1.0 - BETA_TWO) * grad * grad
    spread_out = jnp.sqrt(second_new / CORR_TWO) + ADAM_EPS
    update = first_new / CORR_ONE / spread_out + decay * weight
    return (first_new, second_new, update)


def square_sum(values):
    return jnp.sum(jnp.sum(values * values, axis=1, keepdims=True), axis=0, keepdims=True)


def picked(small, rank, vector_size, bias_size):
    width = small.shape[1]
    row = lax.broadcasted_iota(jnp.int32, (width, 128), 0)
    lane = lax.broadcasted_iota(jnp.int32, (width, 128), 1)
    dot = functools.partial(jnp.dot, precision=lax.Precision.HIGHEST, preferred_element_type=FLOAT)
    chosen = (row == lane + rank * vector_size) & (lane < vector_size)
    vector_grad = dot(small[0:8, :], jnp.where(chosen, 1.0, 0.0))[:, :vector_size]
    start = rank * bias_size
    chosen = (row == lane + lax.rem(start, width)) & (lane < bias_size)
    tail = dot(small[8:16, :], jnp.where(chosen, 1.0, 0.0))
    tail_row = lax.broadcasted_iota(jnp.int32, tail.shape, 0)
    tail = jnp.sum(jnp.where(tail_row == lax.div(start, width), tail, 0.0), axis=0, keepdims=True)
    return vector_grad, tail[:, :bias_size]


def scatters_of(here, slots, grads, buffers, shares, own_sem, plan):
    count = len(grads)
    found, loads = [], []
    for index, grad in enumerate(grads):
        own, *arrivals = buffers[index::count]
        share, offset = shares[index] if isinstance(shares[index], tuple) else (shares[index], 0)
        load = lambda grad=grad, own=own, index=index: pltpu.make_async_copy(
            grad.at[:, here.core], own, own_sem.at[index]
        )
        loads.append(load)
        split, line_last = plan[index]
        for order, pieces in enumerate(parts_of(grad.shape[-2:], split)):
            wait = (lambda load=load: load().wait()) if order == 0 else (lambda: None)
            found.append(
                Scatter(
                    here, slots, grad, own, *arrivals, (share, offset), pieces, wait, line_last
                )
            )
    return found, loads


def scatter_buffers(shapes, plan, counts):
    half_count, seq_count = counts[0] // 2, counts[1]
    found = [pltpu.VMEM((half_count, seq_count) + shape, BRAIN) for shape in shapes * 2]
    for shape, (_, line_last) in zip(shapes, plan):
        found.append(pltpu.VMEM((seq_count - 1, 1 if line_last else half_count) + shape, BRAIN))
    for shape, (_, line_last) in zip(shapes, plan):
        found.append(pltpu.VMEM((half_count - 1, seq_count if line_last else 1) + shape, BRAIN))
    return found


def scatter_views(grads, shapes, counts):
    lead = (counts[0] // 2, 2, counts[1])
    return [grad.reshape(lead + shape) for grad, shape in zip(grads, shapes)]


class SmallSum(Transfer):
    def __init__(self, here, small, sums, arrived, send_sem, recv_sem):
        self.slots = Slots(send_sem, recv_sem)
        self.small, self.sums, self.arrived = small, sums, arrived
        self.peers = [here.core_peer()]
        self.peers += [{"dp": flipped(here.place, bit + 1)} for bit in range(bits_of(here.half_count))]
        self.peers += [here.line_peer(bit) for bit in range(here.seq_bits)]
        self.stages = len(self.peers)

    def copies(self, stage):
        source = self.sums.at[stage - 1] if stage else self.small
        return [self.slots.copy(stage, source, self.arrived.at[stage], self.peers[stage])]

    def use(self, stage):
        before = self.sums[stage - 1] if stage else self.small[...]
        self.sums[stage] = before + self.arrived[stage]


def scatter_kernel(counts, plan, *refs):
    grads, small, input_rows = refs[0:3], refs[3], refs[4]
    ready = refs[5:8]
    weights, firsts, seconds = refs[8:14], refs[14:20], refs[20:26]
    shares, norm_out, input_grad = refs[26:29], refs[29], refs[30]
    buffers, bounce = refs[31:43], refs[43]
    small_sum, small_in, norm_mine, norm_dp, norm_line, norm_seq = refs[44:50]
    send_sem, recv_sem, own_sem, move_sem, small_send, small_recv, norm_send, norm_recv = refs[50:58]
    here = Here(*counts)
    slots = Slots(send_sem, recv_sem)
    thirds = [(shares[0], at * grads[at].shape[-1]) for at in range(3)]
    scatters, loads = scatters_of(here, slots, grads, buffers, thirds, own_sem, plan)
    move = Exchange(here, slots, input_rows, input_grad, False, bounce, move_sem)
    total = SmallSum(here, small, small_sum, small_in, small_send, small_recv)
    for load in loads:
        load().start()
    dp_peers, seq_peers = here.all_peers()[: here.dp_count - 1], here.all_peers()[here.dp_count - 1 :]
    greet(dp_peers + seq_peers)
    waves = waves_of([[each] for each in scatters])
    more = waves_of([[total]])
    for turn in range(max(len(waves), len(more))):
        if turn < len(waves):
            waves[turn]()
        if turn < len(more):
            more[turn]()
        if turn == here.seq_bits + 1:
            move.start(0)

    rank = here.place * here.seq_count + here.line
    vector_grad, bias_grad = picked(
        small_sum[total.stages - 1], rank, shares[1].shape[1], shares[2].shape[1]
    )
    shares[1][...] = vector_grad
    shares[2][...] = bias_grad
    grads_now = [shares[0], *ready, shares[1], shares[2]]

    lane = lax.broadcasted_iota(jnp.int32, (8, 128), 1)
    row = lax.broadcasted_iota(jnp.int32, (8, 128), 0)
    tile = jnp.zeros((8, 128), FLOAT)
    for index in (0, 1, 2, 3, 5):
        decay = DECAY_RATE if index < 4 else 0.0
        weight = weights[index][...]
        update = lamb_pieces(
            weight, firsts[index][...], seconds[index][...], grads_now[index][...], decay
        )[2]
        at = row == (index if index < 4 else 4)
        tile = jnp.where(at & (lane == 0), square_sum(weight), tile)
        tile = jnp.where(at & (lane == 1), square_sum(update), tile)
    norm_mine[0:8, :] = tile
    weight = weights[4][...]
    update = lamb_pieces(weight, firsts[4][...], seconds[4][...], vector_grad, 0.0)[2]
    weight_sq = jnp.sum(weight * weight, axis=1, keepdims=True)
    update_sq = jnp.sum(update * update, axis=1, keepdims=True)
    norm_mine[8:16, :] = jnp.where(lane == 0, weight_sq, jnp.where(lane == 1, update_sq, 0.0))

    norm_slots = Slots(norm_send, norm_recv)

    def exchange(source, held, peers, at):
        base = norm_slots.take(len(peers))
        copies = [
            norm_slots.copy(base + turn, source, held.at[at], peer) for turn, peer in enumerate(peers)
        ]
        for copy in copies:
            copy.start()
        held[at] = source[...]
        for copy in copies:
            copy.wait_recv()
        found = held[0]
        for turn in range(1, held.shape[0]):
            found = found + held[turn]
        return copies, found

    sent, found = exchange(norm_mine, norm_dp, dp_peers, here.place)
    norm_line[...] = found
    also, found = exchange(norm_line, norm_seq, seq_peers, here.line)
    norm_out[...] = found
    move.finish(0)
    for copy in sent + also:
        copy.wait_send()
    drain_all(scatters + [total, move])


def scatter_last(grads, small, input_rows, ready, weights, firsts, seconds, counts):
    dp_count, seq_count = counts
    shapes = [weight.shape for weight in weights]
    thirds = [(shapes[0][0], grad.shape[1]) for grad in grads]
    plan = [(False, False)] * 3
    slots = slot_count(counts, thirds, plan, 1)
    stages = bits_of(dp_count) + bits_of(seq_count)
    return pl.pallas_call(
        functools.partial(scatter_kernel, counts, plan),
        out_shape=[jax.ShapeDtypeStruct(shapes[at], FLOAT) for at in (0, 4, 5)]
        + [
            jax.ShapeDtypeStruct((16, 128), FLOAT),
            jax.ShapeDtypeStruct((seq_count,) + input_rows.shape[0:1] + input_rows.shape[2:], BRAIN),
        ],
        in_specs=[ANYWHERE] * 3 + [WHOLE, ANYWHERE] + [WHOLE] * 21,
        out_specs=[WHOLE] * 4 + [ANYWHERE],
        scratch_shapes=scatter_buffers(thirds, plan, counts)
        + [
            pltpu.VMEM(input_rows.shape[0:1] + input_rows.shape[2:], BRAIN),
            pltpu.VMEM((stages,) + small.shape, FLOAT),
            pltpu.VMEM((stages,) + small.shape, FLOAT),
            pltpu.VMEM((16, 128), FLOAT),
            pltpu.VMEM((dp_count, 16, 128), FLOAT),
            pltpu.VMEM((16, 128), FLOAT),
            pltpu.VMEM((seq_count, 16, 128), FLOAT),
            pltpu.SemaphoreType.DMA((slots,)),
            pltpu.SemaphoreType.DMA((slots,)),
            pltpu.SemaphoreType.DMA((3,)),
            pltpu.SemaphoreType.DMA((2,)),
            pltpu.SemaphoreType.DMA((stages,)),
            pltpu.SemaphoreType.DMA((stages,)),
            pltpu.SemaphoreType.DMA((dp_count + seq_count,)),
            pltpu.SemaphoreType.DMA((dp_count + seq_count,)),
        ],
        name="scatter_last",
        compiler_params=pltpu.CompilerParams(
            collective_id=3, has_side_effects=True, vmem_limit_bytes=56 * 1024 * 1024
        ),
    )(*scatter_views(grads, thirds, counts), small, input_rows, *ready, *weights, *firsts, *seconds)


def lamb_kernel(*refs):
    grads, norms = refs[0:6], refs[6]
    weights, firsts, seconds = refs[7:13], refs[13:19], refs[19:25]
    grad_out, first_out, second_out, new_out = refs[25:31], refs[31:37], refs[37:43], refs[43:49]
    copy_out = refs[49:53]
    weight_norm = jnp.sqrt(norms[:, 0:1])
    scales = weight_norm / (jnp.sqrt(norms[:, 1:2]) + ADAM_EPS)
    for index in range(6):
        grad = grads[index][...]
        weight = weights[index][...]
        decay = DECAY_RATE if index < 4 else 0.0
        first_new, second_new, update = lamb_pieces(
            weight, firsts[index][...], seconds[index][...], grad, decay
        )
        scale = scales[8:16] if index == 4 else scales[min(index, 4) : min(index, 4) + 1]
        new = weight - LEARN_RATE * scale * update
        grad_out[index][...] = grad
        first_out[index][...] = first_new
        second_out[index][...] = second_new
        new_out[index][...] = new
        if index < 4:
            copy_out[index][...] = new.astype(BRAIN)


def lamb_all(grads, norms, weights, firsts, seconds):
    vmem = pl.BlockSpec(memory_space=pltpu.VMEM)
    shapes = [jax.ShapeDtypeStruct(weight.shape, FLOAT) for weight in weights]
    copies = [jax.ShapeDtypeStruct(weight.shape, BRAIN) for weight in weights[:4]]
    return pl.pallas_call(
        lamb_kernel,
        out_shape=shapes * 4 + copies,
        in_specs=[vmem] * 25,
        out_specs=[vmem] * 28,
        name="lamb_update",
        compiler_params=pltpu.CompilerParams(vmem_limit_bytes=48 * 1024 * 1024),
    )(*grads, norms, *weights, *firsts, *seconds)


def body(
    tokens,
    cotangent,
    segment_ids,
    w_qkv,
    m_qkv,
    v_qkv,
    w_out,
    m_out,
    v_out,
    w_up,
    m_up,
    v_up,
    w_down,
    m_down,
    v_down,
    vectors,
    m_vectors,
    v_vectors,
    up_bias,
    m_up_bias,
    v_up_bias,
):
    dp_count, seq_count = lax.axis_size("dp"), lax.axis_size("seq")
    vector_size, bias_size = vectors.shape[1], up_bias.shape[0]
    small = jnp.concatenate(
        [
            jnp.pad(vectors, ((0, 0), (0, 128 - vector_size))),
            jnp.pad(up_bias[None], ((0, 7), (0, 128 - bias_size))),
        ]
    )
    shards = [part.astype(BRAIN) for part in (small, w_qkv, w_out, w_up, w_down)]
    counts = (dp_count, seq_count)
    token_rows, *fulls = gather_first(tokens, shards[:2], counts)
    small = fulls[0].reshape(dp_count * seq_count, 16, 128)
    full_vectors = small[:, :8, :vector_size].transpose(1, 0, 2)
    vector_rows = full_vectors.reshape(8, -1).astype(FLOAT)
    up_shift = small[:, 8, :bias_size].reshape(-1).astype(FLOAT)
    as_matrix = lambda full: full.reshape(-1, full.shape[-1])
    full_qkv = as_matrix(fulls[1])

    width = tokens.shape[2]
    length = segment_ids.shape[1]
    rows = token_rows.shape[0]
    assert rows == 1
    segments = lax.dynamic_slice_in_dim(segment_ids, lax.axis_index("seq"), 1, 0)
    token_rows = token_rows.reshape(length, width)
    *heads, context, lse_rows, full_out, full_up, full_down = attention_forward(
        segments, token_rows, vector_rows, full_qkv, shards[2:], counts
    )
    full_out, full_up, full_down = [as_matrix(full) for full in (full_out, full_up, full_down)]
    grad_up, grad_down, grad_up_bias, grad_out, context_grad, resid_grad, sums, mixed = feed_forward(
        context,
        token_rows,
        full_out,
        full_up,
        full_down,
        vector_rows,
        up_shift[None],
        cotangent,
        counts,
    )
    *qkv_grads, shift_sums, norm_sums, input_rows, share_down, share_up, share_out = attention_backward(
        segments,
        heads,
        context_grad,
        lse_rows,
        token_rows,
        vector_rows,
        resid_grad,
        full_qkv,
        [grad_down, grad_up, grad_out],
        [w_down.shape, w_up.shape, w_out.shape],
        counts,
    )
    grad_vectors = jnp.concatenate([norm_sums[:2], sums[:2], shift_sums[:2], sums[2:4]])
    small_grad = jnp.concatenate([grad_vectors, grad_up_bias.reshape(-1, width)])
    small_grad = jnp.pad(small_grad, ((0, 16 - small_grad.shape[0]), (0, 0)))
    as_row = lambda value: value.reshape(1, -1)
    weights = (w_qkv, w_out, w_up, w_down, vectors, as_row(up_bias))
    firsts = (m_qkv, m_out, m_up, m_down, m_vectors, as_row(m_up_bias))
    seconds = (v_qkv, v_out, v_up, v_down, v_vectors, as_row(v_up_bias))
    share_qkv, share_vectors, share_bias, norms, input_grad = scatter_last(
        qkv_grads,
        small_grad,
        input_rows.reshape(rows, seq_count, length // seq_count, width),
        [share_out, share_up, share_down],
        weights,
        firsts,
        seconds,
        counts,
    )
    shares = [share_qkv, share_out, share_up, share_down, share_vectors, share_bias]
    results = list(lamb_all(shares, norms, weights, firsts, seconds))
    mixed = mixed.reshape(tokens.shape)
    input_grad = input_grad.reshape(tokens.shape).astype(FLOAT)
    for index in (5, 11, 17, 23):
        results[index] = results[index].reshape(-1)
    return (mixed, input_grad, *results)


def solution(mesh):
    matrix = P(("dp", "seq"), None)
    rows = P("dp", "seq", None)
    vector = P(None, ("dp", "seq"))
    bias = P(("dp", "seq"))
    six = (matrix, matrix, matrix, matrix, vector, bias)
    in_specs = (rows, rows, P("dp", None)) + tuple(spec for spec in six for _ in range(3))
    out_specs = (rows, rows) + six * 4 + (matrix,) * 4
    return jax.shard_map(body, mesh=mesh, in_specs=in_specs, out_specs=out_specs, check_vma=False)
```

```python
import functools

import jax
import jax.numpy as jnp
from jax import lax
from jax.experimental import pallas as pl
from jax.experimental.pallas import tpu as pltpu
from jax.sharding import PartitionSpec as P

HEADS = 12
HEAD_DIM = 64
LONGEST = 512
QUERY_BLOCK = 256
ROW_BLOCK = 256


BETA_ONE = 0.9
BETA_TWO = 0.999
ADAM_EPS = 1e-06
DECAY_RATE = 0.01
LEARN_RATE = 0.4
NORM_EPS = 1e-05
STEP_NUMBER = 10.0
CORR_ONE = 1.0 - BETA_ONE**STEP_NUMBER
CORR_TWO = 1.0 - BETA_TWO**STEP_NUMBER

BRAIN = jnp.bfloat16
FLOAT = jnp.float32


def matmul(left_side, right_side):
    return jnp.dot(left_side, right_side, preferred_element_type=FLOAT)


def inner_rows(left_side, right_side):
    return lax.dot_general(
        left_side, right_side, (((0,), (0,)), ((), ())), preferred_element_type=FLOAT
    )


def times_transposed(left_side, right_side):
    return lax.dot_general(
        left_side, right_side, (((1,), (1,)), ((), ())), preferred_element_type=FLOAT
    )


def norm_parts(values):
    center = values - jnp.mean(values, axis=-1, keepdims=True)
    inverse = lax.rsqrt(jnp.mean(center * center, axis=-1, keepdims=True) + NORM_EPS)
    return center * inverse, inverse


def row_blocks(count):
    return [slice(first, first + ROW_BLOCK) for first in range(0, count, ROW_BLOCK)]


def windows(length):
    return [
        (max(0, first - LONGEST), first + QUERY_BLOCK) for first in range(0, length, QUERY_BLOCK)
    ]


def fill_bias(seg_col, seg_row, bias, length):
    place = 0
    for index, (low, high) in enumerate(windows(length)):
        first = index * QUERY_BLOCK
        size = high - low
        keys = seg_col[0, low:high, :]
        queries = seg_row[0, :, first : first + QUERY_BLOCK]
        key_place = low + lax.broadcasted_iota(jnp.int32, (size, QUERY_BLOCK), 0)
        query_place = first + lax.broadcasted_iota(jnp.int32, (size, QUERY_BLOCK), 1)
        allowed = (keys == queries) & (key_place <= query_place)
        bias[place : place + size, :] = jnp.where(allowed, 0.0, -1000000000.0)
        place += size


def split_heads(pair):
    lane = lax.broadcasted_iota(jnp.int32, pair.shape, 1)
    zero = jnp.zeros_like(pair)
    return (jnp.where(lane < HEAD_DIM, pair, zero), jnp.where(lane < HEAD_DIM, zero, pair))


def attend_forward(counts, plan, *refs):
    seg_col, seg_row, tokens, norms, shifts, wq_ref, wk_ref, wv_ref = refs[0:8]
    shards, q_ref, k_ref, v_ref, c_ref, lse_ref = refs[8:11], *refs[11:16]
    fulls, bias, low_one, bounces = refs[16:19], refs[19], refs[20], refs[21:24]
    send_sem, recv_sem, own_sem = refs[24:]
    length = q_ref.shape[0]
    here = Here(*counts)
    slots = Slots(send_sem, recv_sem)
    gathers = gathers_of(here, slots, shards, fulls, bounces, own_sem, plan)
    groups = [gathers[:2]] + [[each] for each in gathers[2:]]
    waves = led_by(lambda: greet(here.near_peers()), waves_of(groups))
    blocks = windows(length)
    beside = Beside(waves, HEADS // 2 * len(blocks))

    @pl.when(pl.program_id(0) == 0)
    def _():
        beside.point(0, len(blocks), first=True)
        fill_bias(seg_col, seg_row, bias, length)
        for rows in row_blocks(length):
            normed, _ = norm_parts(tokens[rows, :].astype(FLOAT))
            low_one[rows, :] = (normed * norms[0:1, :] + norms[1:2, :]).astype(BRAIN)

    lanes = 2 * HEAD_DIM
    joined = jnp.concatenate([wq_ref[...], wk_ref[...], wv_ref[...]], axis=1)
    for rows in row_blocks(length):
        projected = matmul(low_one[rows, :], joined)
        q_ref[rows, :] = (projected[:, :lanes] + shifts[4:5, :]).astype(BRAIN)
        k_ref[rows, :] = projected[:, lanes : 2 * lanes].astype(BRAIN)
        v_ref[rows, :] = (projected[:, 2 * lanes :] + shifts[5:6, :]).astype(BRAIN)
    v_turned = v_ref[...].T
    place = 0
    for index, (low, high) in enumerate(blocks):
        beside.point(index, len(blocks), first=False)
        first = index * QUERY_BLOCK
        size = high - low
        queries = split_heads(q_ref[first : first + QUERY_BLOCK, :] * HEAD_DIM ** (-0.5))
        keys = k_ref[low:high, :]
        blocked = bias[place : place + size, :]
        parts = []
        for head in range(2):
            scores = times_transposed(keys, queries[head]) + blocked
            peak = jnp.max(scores, axis=0, keepdims=True)
            probs = jnp.exp(scores - peak)
            total = jnp.sum(probs, axis=0, keepdims=True)
            probs = (probs * (1.0 / total)).astype(BRAIN)
            lse_ref[0, head : head + 1, first : first + QUERY_BLOCK] = peak + jnp.log(total)
            turned = v_turned[head * HEAD_DIM : (head + 1) * HEAD_DIM, low:high]
            parts.append(matmul(turned, probs))
        context = jnp.concatenate(parts, axis=0).T
        c_ref[first : first + QUERY_BLOCK, :] = context.astype(BRAIN)
        place += size

    @pl.when(pl.program_id(0) == HEADS // 2 - 1)
    def _():
        beside.rest()
        drain_all(gathers)


def led_by(ahead, waves):
    def both():
        ahead()
        waves[0]()

    return [both] + waves[1:]


class Beside:
    def __init__(self, waves, points, ahead=0):
        self.at, self.ahead = {}, ahead
        early = len(waves) - 1
        for index in range(early):
            self.at.setdefault(index * points // early, []).append(waves[index])
        self.late = waves[early:]

    def point(self, index, per_step, first=None):
        for point, calls in self.at.items():
            if point % per_step == index and first in (None, point == 0):

                @pl.when(pl.program_id(0) == self.ahead + point // per_step)
                def _(calls=calls):
                    for call in calls:
                        call()

    def rest(self):
        for call in self.late:
            call()


def attend_backward(counts, plan, *refs):
    seg_col, seg_row, q_ref, k_ref, v_ref, g_ref, lse_ref = refs[0:7]
    tokens, norms, resid_grad, wq_ref, wk_ref, wv_ref = refs[7:13]
    grads, gq_ref, gk_ref, gv_ref, shift_ref, sum_ref, input_ref = refs[13:15], *refs[15:21]
    shares, bias, key_sum, value_sum, low_turned, total, joined = refs[21:23], *refs[23:29]
    buffers, send_sem, recv_sem, own_sem = refs[29:37], *refs[37:]
    length = q_ref.shape[0]
    pair = pl.program_id(0)
    here = Here(*counts)
    slots = Slots(send_sem, recv_sem)
    scatters, loads = scatters_of(here, slots, grads, buffers, shares, own_sem, plan)

    def begin():
        for load in loads:
            load().start()
        greet(here.near_peers())

    groups = [[each] for each in scatters[:-2]] + [scatters[-2:]]
    waves = led_by(begin, waves_of(groups))
    blocks = windows(length)
    beside = Beside(waves, HEADS // 2 * len(blocks))

    @pl.when(pair == 0)
    def _():
        beside.point(0, len(blocks), first=True)
        fill_bias(seg_col, seg_row, bias, length)
        for rows in row_blocks(length):
            normed, _ = norm_parts(tokens[rows, :].astype(FLOAT))
            low_turned[:, rows] = (normed * norms[0:1, :] + norms[1:2, :]).astype(BRAIN).T
        total[...] = jnp.zeros_like(total)

    key_sum[...] = jnp.zeros_like(key_sum)
    value_sum[...] = jnp.zeros_like(value_sum)
    k_turned = k_ref[...].T
    lanes = 2 * HEAD_DIM
    place = 0
    for index, (low, high) in enumerate(blocks):
        beside.point(index, len(blocks), first=False)
        first = index * QUERY_BLOCK
        size = high - low
        rows = slice(first, first + QUERY_BLOCK)
        queries = split_heads(q_ref[rows, :] * HEAD_DIM ** (-0.5))
        grads = split_heads(g_ref[rows, :])
        keys = k_ref[low:high, :]
        values = v_ref[low:high, :]
        blocked = bias[place : place + size, :]
        all_probs = []
        all_scores = []
        parts = []
        for head in range(2):
            scores = times_transposed(keys, queries[head]) + blocked
            probs = jnp.exp(scores - lse_ref[0, head : head + 1, rows])
            prob_grad = times_transposed(values, grads[head])
            row_dot = jnp.sum(probs * prob_grad, axis=0, keepdims=True)
            score_grad = (probs * (prob_grad - row_dot)).astype(BRAIN)
            all_probs.append(probs.astype(BRAIN))
            all_scores.append(score_grad)
            turned = k_turned[head * HEAD_DIM : (head + 1) * HEAD_DIM, low:high]
            parts.append(matmul(turned, score_grad))
        query_grad = jnp.concatenate(parts, axis=0).T * HEAD_DIM ** (-0.5)
        joined[rows, :lanes] = query_grad.astype(BRAIN)
        value_sum[low:high, :] += matmul(
            jnp.concatenate(all_probs, axis=1), jnp.concatenate(grads, axis=0)
        )
        key_sum[low:high, :] += matmul(
            jnp.concatenate(all_scores, axis=1), jnp.concatenate(queries, axis=0)
        )
        place += size
    joined[:, lanes : 2 * lanes] = key_sum[...].astype(BRAIN)
    joined[:, 2 * lanes :] = value_sum[...].astype(BRAIN)
    weight = jnp.concatenate([wq_ref[...], wk_ref[...], wv_ref[...]], axis=1)
    sums = jnp.zeros((1, 3 * lanes), FLOAT)
    for rows in row_blocks(length):
        part = joined[rows, :]
        total[rows, :] += times_transposed(part, weight)
        sums = sums + jnp.sum(part.astype(FLOAT), axis=0, keepdims=True)
    found = matmul(low_turned[...], joined[...]).astype(BRAIN)
    gq_ref[...] = found[:, :lanes]
    gk_ref[...] = found[:, lanes : 2 * lanes]
    gv_ref[...] = found[:, 2 * lanes :]
    shift_ref[0:1, :] = sums[:, :lanes]
    shift_ref[1:2, :] = sums[:, 2 * lanes :]
    shift_ref[2:8, :] = jnp.zeros((6, lanes), FLOAT)

    @pl.when(pair == HEADS // 2 - 1)
    def _():
        gains = jnp.zeros((1, total.shape[1]), FLOAT)
        moves = jnp.zeros((1, total.shape[1]), FLOAT)
        for rows in row_blocks(length):
            normed, inverse = norm_parts(tokens[rows, :].astype(FLOAT))
            upstream = total[rows, :]
            scaled = upstream * norms[0:1, :]
            centered = scaled - jnp.mean(scaled, axis=-1, keepdims=True)
            inward = centered - normed * jnp.mean(scaled * normed, axis=-1, keepdims=True)
            input_ref[rows, :] = (resid_grad[rows, :] + inverse * inward).astype(BRAIN)
            gains = gains + jnp.sum(upstream * normed, axis=0, keepdims=True)
            moves = moves + jnp.sum(upstream, axis=0, keepdims=True)
        sum_ref[0:1, :] = gains
        sum_ref[1:2, :] = moves
        sum_ref[2:8, :] = jnp.zeros((6, total.shape[1]), FLOAT)

    @pl.when(pair == HEADS // 2 - 1)
    def _():
        beside.rest()
        drain_all(scatters)


def once(shape):
    return pl.BlockSpec(shape, lambda *_: (0,) * len(shape), pipeline_mode=pl.Buffered(1))


def pair_specs(length):
    lanes, width = 2 * HEAD_DIM, HEADS * HEAD_DIM
    pairs = HEADS // 2
    segs = [once((1, length, 1)), once((1, 1, length))]
    plain = pl.BlockSpec((length, lanes), lambda j: (0, j))
    lse = pl.BlockSpec((1, 8, length), lambda j: (j, 0, 0))
    weights = [pl.BlockSpec((width, lanes), lambda j, at=at: (0, at * pairs + j)) for at in range(3)]
    shifts = pl.BlockSpec((8, lanes), lambda j: (0, j))
    bias = pltpu.VMEM((sum(high - low for low, high in windows(length)), QUERY_BLOCK), FLOAT)
    return segs, plain, lse, weights, shifts, bias


def attention_forward(segments, tokens, vectors, full_qkv, shards, counts):
    length, width = tokens.shape
    segs, plain, lse, weights, shifts, bias = pair_specs(length)
    plan = [(False, False)] + [(True, False)] * (len(shards) - 1)
    slots = slot_count(counts, [shard.shape for shard in shards], plan, 0)
    return pl.pallas_call(
        functools.partial(attend_forward, counts, plan),
        grid=(HEADS // 2,),
        in_specs=segs
        + [once((length, width)), once((8, width)), shifts]
        + weights
        + [ANYWHERE] * 3,
        out_specs=[plain] * 4 + [lse] + [ANYWHERE] * 3,
        out_shape=[jax.ShapeDtypeStruct((length, width), BRAIN)] * 4
        + [jax.ShapeDtypeStruct((HEADS // 2, 8, length), FLOAT)]
        + [full_shape(shard, *counts) for shard in shards],
        scratch_shapes=[bias, pltpu.VMEM((length, width), BRAIN)]
        + [pltpu.VMEM(shard.shape, shard.dtype) for shard in shards]
        + [
            pltpu.SemaphoreType.DMA((slots,)),
            pltpu.SemaphoreType.DMA((slots,)),
            pltpu.SemaphoreType.DMA((2 * len(shards),)),
        ],
        name="attend_forward",
        compiler_params=pltpu.CompilerParams(
            collective_id=1, has_side_effects=True, vmem_limit_bytes=63 * 1024 * 1024
        ),
    )(
        segments[:, :, None],
        segments[:, None, :],
        tokens,
        vectors,
        vectors,
        full_qkv,
        full_qkv,
        full_qkv,
        *shards,
    )


def attention_backward(
    segments, heads, context_grad, lse_rows, tokens, vectors, resid_grad, full_qkv, grads, shapes, counts
):
    length, width = tokens.shape
    lanes = 2 * HEAD_DIM
    segs, plain, lse, weights, shifts, bias = pair_specs(length)
    column = pl.BlockSpec((width, lanes), lambda j: (0, j))
    plan = [(True, False)] * (len(shapes) - 1) + [(False, False)]
    slots = slot_count(counts, shapes, plan, 0)
    return pl.pallas_call(
        functools.partial(attend_backward, counts, plan),
        grid=(HEADS // 2,),
        in_specs=segs
        + [plain] * 4
        + [lse, once((length, width)), once((8, width)), once((length, width))]
        + weights
        + [ANYWHERE] * len(shapes),
        out_specs=[column] * 3 + [shifts, once((8, width)), once((length, width))] + [WHOLE] * len(shapes),
        out_shape=[jax.ShapeDtypeStruct((width, width), BRAIN)] * 3
        + [jax.ShapeDtypeStruct((8, width), FLOAT)] * 2
        + [jax.ShapeDtypeStruct((length, width), BRAIN)]
        + [jax.ShapeDtypeStruct(shape, FLOAT) for shape in shapes],
        scratch_shapes=[
            bias,
            pltpu.VMEM((length, lanes), FLOAT),
            pltpu.VMEM((length, lanes), FLOAT),
            pltpu.VMEM((width, length), BRAIN),
            pltpu.VMEM((length, width), FLOAT),
            pltpu.VMEM((length, 3 * lanes), BRAIN),
        ]
        + scatter_buffers(shapes, plan, counts)
        + [
            pltpu.SemaphoreType.DMA((slots,)),
            pltpu.SemaphoreType.DMA((slots,)),
            pltpu.SemaphoreType.DMA((len(shapes),)),
        ],
        name="attend_backward",
        compiler_params=pltpu.CompilerParams(
            collective_id=2, has_side_effects=True, vmem_limit_bytes=63 * 1024 * 1024
        ),
    )(
        segments[:, :, None],
        segments[:, None, :],
        *heads,
        context_grad,
        lse_rows,
        tokens,
        vectors,
        resid_grad,
        full_qkv,
        full_qkv,
        full_qkv,
        *scatter_views(grads, shapes, counts),
    )


MESH = pl.DeviceIdType.MESH
ANYWHERE = pl.BlockSpec(memory_space=pl.ANY)
WHOLE = pl.BlockSpec(memory_space=pltpu.VMEM)


def bits_of(count):
    return count.bit_length() - 1


def flipped(value, bit):
    step = 1 << bit
    return value + step * (1 - 2 * lax.rem(lax.div(value, step), 2))


def rounded_down(value, bit):
    return lax.div(value, 1 << bit) * (1 << bit)


def spread(value, bit, total):
    step = 1 << (bit + 1)
    return [lax.rem(value, step) + step * turn for turn in range(1 << (total - 1 - bit))]


class Here:
    def __init__(self, dp_count, seq_count):
        self.dp_count, self.seq_count = dp_count, seq_count
        self.half_count = dp_count // 2
        self.seq_bits = bits_of(seq_count)
        self.place, self.line = lax.axis_index("dp"), lax.axis_index("seq")
        self.chip, self.core = lax.div(self.place, 2), lax.rem(self.place, 2)

    def core_peer(self):
        return {"dp": flipped(self.place, 0)}

    def line_peer(self, bit):
        return {"seq": flipped(self.line, bit)}

    def other_lines(self):
        return [lax.rem(self.line + turn, self.seq_count) for turn in range(1, self.seq_count)]

    def other_chips(self):
        return [lax.rem(self.chip + turn, self.half_count) for turn in range(1, self.half_count)]

    def chip_peers(self):
        return [{"dp": 2 * chip + self.core} for chip in self.other_chips()]

    def near_peers(self):
        peers = [self.core_peer()] + self.chip_peers()
        return peers + [{"seq": line} for line in self.other_lines()]

    def all_peers(self):
        peers = [{"dp": lax.rem(self.place + turn, self.dp_count)} for turn in range(1, self.dp_count)]
        return peers + [{"seq": line} for line in self.other_lines()]


def greet(peers):
    barrier = pltpu.get_barrier_semaphore()
    for peer in peers:
        pl.semaphore_signal(barrier, inc=1, device_id=peer, device_id_type=MESH)
    pl.semaphore_wait(barrier, len(peers))


class Slots:
    def __init__(self, send_sem, recv_sem):
        self.send_sem, self.recv_sem, self.used = send_sem, recv_sem, 0

    def take(self, count):
        first = self.used
        self.used += count
        return first

    def copy(self, slot, source, target, peer):
        return pltpu.make_async_remote_copy(
            source,
            target,
            self.send_sem.at[slot],
            self.recv_sem.at[slot],
            device_id=peer,
            device_id_type=MESH,
        )


def parts_of(shape, split):
    rows, width = shape
    tiles = width // 128
    if width % 128 or tiles < 2:
        return [[(slice(0, rows), slice(0, width), False)]]
    middle = tiles // 2 * 128
    first, second = (0, middle), (middle, width)
    every = slice(0, rows)
    if split and rows % 32 == 0:
        return [
            [(part, slice(*first), False), (part, slice(*second), True)]
            for part in (slice(0, rows // 2), slice(rows // 2, rows))
        ]
    if split and tiles >= 4:
        lists = [[], []]
        for (low, high), backwards in ((first, False), (second, True)):
            cut = low + (high - low) // 256 * 128
            lists[0].append((every, slice(low, cut), backwards))
            lists[1].append((every, slice(cut, high), backwards))
        return lists
    return [[(every, slice(*first), False), (every, slice(*second), True)]]


class Transfer:
    def start(self, stage):
        for copy in self.copies(stage):
            copy.start()

    def finish(self, stage):
        for copy in self.copies(stage):
            copy.wait_recv()
        self.use(stage)

    def use(self, stage):
        pass

    def drain(self):
        for stage in range(self.stages):
            for copy in self.copies(stage):
                copy.wait_send()


class Gather(Transfer):
    def __init__(self, here, slots, shard, full, pieces, own_done, line_first=False):
        self.here, self.slots, self.shard, self.full = here, slots, shard, full
        self.pieces, self.own_done, self.line_first = pieces, own_done, line_first
        self.stages = here.seq_bits + 2
        self.each = here.half_count + here.seq_count
        self.first = slots.take(self.each * len(pieces))

    def copies(self, stage):
        here, full = self.here, self.full
        chip_stage = here.seq_bits if self.line_first else 0
        chips = here.chip if self.line_first else slice(None)
        found = []
        for index, (rows, columns, backwards) in enumerate(self.pieces):
            slot = self.first + self.each * index
            if stage == chip_stage:
                lines = slice(None) if self.line_first else here.line
                target = full.at[here.chip, here.core, lines, rows, columns]
                source = target if self.line_first else self.shard.at[rows, columns]
                for turn, peer in enumerate(here.chip_peers()):
                    found.append(self.slots.copy(slot + turn, source, target, peer))
                continue
            slot += here.half_count - 1
            if stage == self.stages - 1:
                part = full.at[:, here.core, :, rows, columns]
                slot += here.seq_count - 1
                found.append(self.slots.copy(slot, part, part, here.core_peer()))
                continue
            past = stage if self.line_first else stage - 1
            if backwards:
                bit = here.seq_bits - 1 - past
                slot += (1 << past) - 1
                parts = [
                    full.at[chips, here.core, at, rows, columns]
                    for at in spread(here.line, bit, here.seq_bits)
                ]
            else:
                bit = past
                slot += bit
                block = pl.ds(rounded_down(here.line, bit), 1 << bit)
                parts = [full.at[chips, here.core, block, rows, columns]]
            for turn, part in enumerate(parts):
                found.append(self.slots.copy(slot + turn, part, part, here.line_peer(bit)))
        return found

    def start(self, stage):
        if stage == (0 if self.line_first else 1):
            self.own_done()
        super().start(stage)


class Scatter(Transfer):
    def __init__(
        self, here, slots, grad, own, from_core, from_line, from_chip, share, pieces, load, line_last
    ):
        self.here, self.slots, self.grad, self.own = here, slots, grad, own
        self.from_core, self.from_line, self.from_chip = from_core, from_line, from_chip
        self.share, self.pieces, self.load, self.line_last = share, pieces, load, line_last
        self.stages = here.seq_bits + 2
        self.chip_stage = 1 if line_last else here.seq_bits + 1
        self.each = here.half_count + here.seq_count
        self.first = slots.take(self.each * len(pieces))

    def line_stage(self, stage, backwards):
        here = self.here
        past = stage - 2 if self.line_last else stage - 1
        if backwards:
            bit = past
            away = spread(flipped(here.line, bit), bit, here.seq_bits)
            kept = spread(here.line, bit, here.seq_bits)
        else:
            bit = here.seq_bits - 1 - past
            away = [rounded_down(flipped(here.line, bit), bit) + at for at in range(1 << bit)]
            kept = [rounded_down(here.line, bit) + at for at in range(1 << bit)]
        base = sum(1 << (here.seq_bits - 1 - before) for before in range(past))
        return bit, away, kept, base

    def copies(self, stage):
        here = self.here
        found = []
        for index, (rows, columns, backwards) in enumerate(self.pieces):
            slot = self.first + self.each * index
            if stage == 0:
                found.append(
                    self.slots.copy(
                        slot,
                        self.grad.at[:, 1 - here.core, :, rows, columns],
                        self.from_core.at[:, :, rows, columns],
                        here.core_peer(),
                    )
                )
            elif stage == self.chip_stage:
                slot += here.seq_count
                lines = slice(None) if self.line_last else here.line
                places = slice(None) if self.line_last else 0
                for turn, chip in enumerate(here.other_chips()):
                    found.append(
                        self.slots.copy(
                            slot + turn,
                            self.own.at[chip, lines, rows, columns],
                            self.from_chip.at[turn, places, rows, columns],
                            {"dp": 2 * chip + here.core},
                        )
                    )
            else:
                bit, away, _, base = self.line_stage(stage, backwards)
                chips = here.chip if self.line_last else slice(None)
                places = 0 if self.line_last else slice(None)
                for turn, at in enumerate(away):
                    found.append(
                        self.slots.copy(
                            slot + 1 + base + turn,
                            self.own.at[chips, at, rows, columns],
                            self.from_line.at[base + turn, places, rows, columns],
                            here.line_peer(bit),
                        )
                    )
        return found

    def put(self, rows, columns, values):
        share, offset = self.share
        share[rows, slice(columns.start + offset, columns.stop + offset)] = values

    def use(self, stage):
        here, own = self.here, self.own
        if stage == 0:
            self.load()
        last = stage == self.stages - 1
        for rows, columns, backwards in self.pieces:
            if stage == 0:

                def add(at, carry, rows=rows, columns=columns):
                    one, two = lax.div(at, here.seq_count), lax.rem(at, here.seq_count)
                    own[one, two, rows, columns] = (
                        own[one, two, rows, columns] + self.from_core[one, two, rows, columns]
                    )
                    return carry

                lax.fori_loop(0, here.half_count * here.seq_count, add, 0)
            elif stage == self.chip_stage:

                def total(line, place, rows=rows, columns=columns):
                    found = own[here.chip, line, rows, columns].astype(FLOAT)
                    for turn in range(here.half_count - 1):
                        found = found + self.from_chip[turn, place, rows, columns].astype(FLOAT)
                    return found

                if last:
                    self.put(rows, columns, total(here.line, 0))
                    continue

                def add(line, carry, rows=rows, columns=columns, total=total):
                    own[here.chip, line, rows, columns] = total(line, line).astype(BRAIN)
                    return carry

                lax.fori_loop(0, here.seq_count, add, 0)
            else:
                _, _, kept, base = self.line_stage(stage, backwards)
                for turn, at in enumerate(kept):
                    place = base + turn
                    if last:
                        mine = own[here.chip, at, rows, columns].astype(FLOAT)
                        theirs = self.from_line[place, 0, rows, columns].astype(FLOAT)
                        self.put(rows, columns, mine + theirs)
                    elif self.line_last:
                        own[here.chip, at, rows, columns] = (
                            own[here.chip, at, rows, columns]
                            + self.from_line[place, 0, rows, columns]
                        )
                    else:

                        def add(one, carry, rows=rows, columns=columns, at=at, place=place):
                            own[one, at, rows, columns] = (
                                own[one, at, rows, columns]
                                + self.from_line[place, one, rows, columns]
                            )
                            return carry

                        lax.fori_loop(0, here.half_count, add, 0)


class Exchange(Transfer):
    stages = 1

    def __init__(self, here, slots, source, target, to_rows, bounce, sem):
        self.here, self.slots, self.source, self.target = here, slots, source, target
        self.to_rows, self.bounce, self.sem = to_rows, bounce, sem
        self.first = slots.take(here.seq_count - 1)

    def ends(self, line):
        if self.to_rows:
            count = self.target.shape[0]
            block = self.source.at[pl.ds(line * count, count)]
            return block, self.target.at[:, self.here.line]
        return self.source.at[:, line], self.target.at[self.here.line]

    def copies(self, stage):
        return [
            self.slots.copy(self.first + turn, *self.ends(line), {"seq": line})
            for turn, line in enumerate(self.here.other_lines())
        ]

    def own_in(self):
        return pltpu.make_async_copy(self.ends(self.here.line)[0], self.bounce, self.sem.at[0])

    def own_out(self):
        source, target = self.ends(self.here.line)
        source = source if self.bounce is None else self.bounce
        return pltpu.make_async_copy(source, target, self.sem.at[1])

    def start(self, stage):
        if self.bounce is not None:
            self.own_in().start()
        super().start(stage)
        if self.bounce is not None:
            self.own_in().wait()
        self.own_out().start()

    def use(self, stage):
        self.own_out().wait()


def waves_of(groups):
    def wave(count):
        for index, group in enumerate(groups):
            stage = count - index
            for transfer in group:
                if 1 <= stage <= transfer.stages:
                    transfer.finish(stage - 1)
            for transfer in group:
                if 0 <= stage < transfer.stages:
                    transfer.start(stage)

    total = max(index + transfer.stages for index, group in enumerate(groups) for transfer in group)
    return [functools.partial(wave, count) for count in range(total + 1)]


def drain_all(transfers):
    for transfer in transfers:
        transfer.drain()


def gathers_of(here, slots, shards, fulls, bounces, sem, plan):
    found = []
    for index, (shard, full, bounce) in enumerate(zip(shards, fulls, bounces)):
        inward = lambda shard=shard, bounce=bounce, index=index: pltpu.make_async_copy(
            shard, bounce, sem.at[2 * index]
        )
        outward = lambda full=full, bounce=bounce, index=index: pltpu.make_async_copy(
            bounce, full.at[here.chip, here.core, here.line], sem.at[2 * index + 1]
        )
        split, line_first = plan[index]
        for order, pieces in enumerate(parts_of(shard.shape, split)):

            def own_done(first=order == 0, inward=inward, outward=outward):
                if first:
                    inward().start()
                    inward().wait()
                    outward().start()
                    outward().wait()

            found.append(Gather(here, slots, shard, full, pieces, own_done, line_first))
    return found


def slot_count(here_shape, shapes, plan, exchanges):
    half_count, seq_count = here_shape[0] // 2, here_shape[1]
    each = half_count + seq_count
    pieces = sum(
        len(part) for shape, (split, _) in zip(shapes, plan) for part in parts_of(shape, split)
    )
    return each * pieces + exchanges * (seq_count - 1)


def full_shape(shard, dp_count, seq_count):
    return jax.ShapeDtypeStruct((dp_count // 2, 2, seq_count) + shard.shape, shard.dtype)


def gather_kernel(counts, plan, count, *refs):
    tokens, shards, fulls = refs[0], refs[1 : 1 + count], refs[2 + count : 2 + 2 * count]
    token_rows = refs[1 + count]
    rest = refs[2 + 2 * count :]
    bounces, bounce, send_sem, recv_sem, own_sem, move_sem = rest[:count], *rest[count:]
    here = Here(*counts)
    slots = Slots(send_sem, recv_sem)
    gathers = gathers_of(here, slots, shards, fulls, bounces, own_sem, plan)
    move = Exchange(here, slots, tokens, token_rows, True, bounce, move_sem)
    greet(here.near_peers())
    waves = waves_of([gathers[:2]] + [[each] for each in gathers[2:]])
    waves[0]()
    move.start(0)
    for wave in waves[1:]:
        wave()
    move.finish(0)
    drain_all(gathers + [move])


def gather_first(tokens, shards, counts):
    dp_count, seq_count = counts
    row_count, pos_count, width = tokens.shape
    rows = row_count // seq_count
    plan = [(True, False)] * len(shards)
    slots = slot_count(counts, [shard.shape for shard in shards], plan, 1)
    return pl.pallas_call(
        functools.partial(gather_kernel, counts, plan, len(shards)),
        out_shape=[jax.ShapeDtypeStruct((rows, seq_count, pos_count, width), tokens.dtype)]
        + [full_shape(shard, *counts) for shard in shards],
        in_specs=[ANYWHERE] * (1 + len(shards)),
        out_specs=[ANYWHERE] * (1 + len(shards)),
        scratch_shapes=[pltpu.VMEM(shard.shape, shard.dtype) for shard in shards]
        + [
            pltpu.VMEM((rows, pos_count, width), tokens.dtype),
            pltpu.SemaphoreType.DMA((slots,)),
            pltpu.SemaphoreType.DMA((slots,)),
            pltpu.SemaphoreType.DMA((2 * len(shards),)),
            pltpu.SemaphoreType.DMA((2,)),
        ],
        name="gather_first",
        compiler_params=pltpu.CompilerParams(collective_id=0, has_side_effects=True),
    )(tokens, *shards)


HIDDEN_BLOCK = 768
GELU_SCALE = 0.7978845608028654
GELU_CUBE = 0.044715


def gelu_both(values):
    square = values * values
    turned = jnp.tanh(GELU_SCALE * values * (1.0 + GELU_CUBE * square))
    half = 0.5 + 0.5 * turned
    inner = GELU_SCALE * (1.0 + 3.0 * GELU_CUBE * square)
    return values * half, half + 0.5 * values * (1.0 - turned * turned) * inner


def forward_start(context, tokens, w_out, vectors, resid, low_two, low_turned):
    for rows in row_blocks(resid.shape[0]):
        values = tokens[rows, :].astype(FLOAT) + (matmul(context[rows, :], w_out[...]) + vectors[6:7, :])
        resid[rows, :] = values
        normed, _ = norm_parts(values)
        low = (normed * vectors[2:3, :] + vectors[3:4, :]).astype(BRAIN)
        low_two[rows, :] = low
        low_turned[:, rows] = low.T


def backward_end(
    context, w_out, vectors, resid, total, back, gc_ref, gr_ref, gwo_ref, sum_ref, low_turned
):
    width = resid.shape[1]
    sums = [jnp.zeros((1, width), FLOAT) for _ in range(4)]
    for rows in row_blocks(resid.shape[0]):
        normed, inverse = norm_parts(resid[rows, :])
        upstream = total[rows, :]
        given = back(rows).astype(FLOAT)
        scaled = upstream * vectors[2:3, :]
        centered = scaled - jnp.mean(scaled, axis=-1, keepdims=True)
        inward = centered - normed * jnp.mean(scaled * normed, axis=-1, keepdims=True)
        grad = given + inverse * inward
        low = grad.astype(BRAIN)
        gr_ref[rows, :] = grad
        gc_ref[rows, :] = times_transposed(low, w_out[...]).astype(BRAIN)
        low_turned[:, rows] = context[rows, :].T
        total[rows, :] = low.astype(FLOAT)
        for index, values in enumerate((upstream * normed, upstream, low.astype(FLOAT), given)):
            sums[index] = sums[index] + jnp.sum(values, axis=0, keepdims=True)
    for index in range(4):
        sum_ref[index : index + 1, :] = sums[index]
    sum_ref[4:8, :] = jnp.zeros((4, width), FLOAT)
    gwo_ref[...] = matmul(low_turned[...], total[...].astype(BRAIN)).astype(BRAIN)


def mlp_kernel(counts, plan, *refs):
    context, tokens, w_out, w_up, w_down, vectors, up_shift, cotangent = refs[0:8]
    gup_ref, gub_ref, gwo_ref, gc_ref, gr_ref, sum_ref, share, mixed = refs[8:16]
    acts, slopes, low_two, low_turned, resid, total, hidden, back, mixed_rows = refs[16:25]
    grad_down, buffers, send_sem, recv_sem, move_sem, own_sem = refs[25], refs[26:30], *refs[30:]
    here = Here(*counts)
    slots = Slots(send_sem, recv_sem)
    arrive = Exchange(here, slots, cotangent, back, True, None, move_sem.at[pl.ds(0, 2)])
    leave = Exchange(here, slots, mixed_rows, mixed, False, None, move_sem.at[pl.ds(2, 2)])
    scatters, loads = scatters_of(here, slots, [grad_down], buffers, [share], own_sem, plan)
    waves = led_by(lambda: loads[0]().start(), waves_of([[each] for each in scatters]))
    step = pl.program_id(0)
    half = acts.shape[0]
    count = resid.shape[0]
    per_step = len(row_blocks(count))
    beside = Beside(waves, half * per_step, half)
    pos_count = back.shape[2]

    def back_rows(rows):
        parts = []
        for first in range(rows.start, rows.stop, pos_count):
            size = min(pos_count, rows.stop - first)
            row, rest = divmod(first, pos_count * counts[1])
            line, offset = divmod(rest, pos_count)
            parts.append(back[row, line, offset : offset + size, :])
        return parts[0] if len(parts) == 1 else jnp.concatenate(parts, axis=0)

    @pl.when(step == 0)
    def _():
        greet(here.near_peers())
        arrive.start(0)
        forward_start(context, tokens, w_out, vectors, resid, low_two, low_turned)
        total[...] = jnp.zeros_like(total)

    @pl.when(step < half)
    def _():
        for rows in row_blocks(count):
            values = matmul(low_two[rows, :], w_up[...]) + up_shift[...]
            act, slope = gelu_both(values)
            low = act.astype(BRAIN)
            acts[step, rows, :] = low
            slopes[step, rows, :] = slope.astype(BRAIN)
            total[rows, :] += matmul(low, w_down[...])

    @pl.when(step == half)
    def _():
        for first in range(0, count, pos_count):
            row, line = divmod(first // pos_count, counts[1])
            rows = slice(first, first + pos_count)
            values = resid[rows, :] + (total[rows, :] + vectors[7:8, :])
            mixed_rows[row, line] = values.astype(BRAIN)
        total[...] = jnp.zeros_like(total)
        leave.start(0)
        arrive.finish(0)
        every = back_rows(slice(0, count))
        granule = grad_down.shape[3]
        for block in range(half):
            values = inner_rows(acts[block], every).astype(BRAIN)
            each = values.shape[0] // granule
            for order in range(each):
                pair, line = divmod(block * each + order, counts[1])
                part = values[order * granule : (order + 1) * granule, :]
                grad_down[pair // 2, pair % 2, line] = part

    @pl.when(step >= half)
    def _():
        at = step - half
        sums = jnp.zeros((1, hidden.shape[1]), FLOAT)
        for index, rows in enumerate(row_blocks(count)):
            beside.point(index, per_step)
            grad = times_transposed(back_rows(rows), w_down[...]) * slopes[at, rows, :].astype(FLOAT)
            low = grad.astype(BRAIN)
            hidden[rows, :] = low
            sums = sums + jnp.sum(low.astype(FLOAT), axis=0, keepdims=True)
            total[rows, :] += times_transposed(low, w_up[...])
        gub_ref[...] = sums
        gup_ref[...] = matmul(low_turned[...], hidden[...]).astype(BRAIN)

    @pl.when(step == 2 * half - 1)
    def _():
        backward_end(
            context, w_out, vectors, resid, total, back_rows, gc_ref, gr_ref, gwo_ref, sum_ref, low_turned
        )
        beside.rest()
        leave.finish(0)
        drain_all([arrive, leave] + scatters)


def feed_forward(context, tokens, w_out, w_up, w_down, vectors, up_shift, cotangent, shape, counts):
    count, width = context.shape
    hidden = w_up.shape[1]
    half = hidden // HIDDEN_BLOCK
    seq_count = counts[1]
    row_count, pos_count, _ = cotangent.shape
    rows = row_count // seq_count
    later = lambda j: jnp.maximum(j - half, 0)
    around = lambda j: lax.rem(j, half)
    block = HIDDEN_BLOCK
    plan = [(True, False)]
    slots = slot_count(counts, [shape], plan, 2)
    return pl.pallas_call(
        functools.partial(mlp_kernel, counts, plan),
        grid=(2 * half,),
        in_specs=[
            once((count, width)),
            once((count, width)),
            once((width, width)),
            pl.BlockSpec((width, block), lambda j: (0, around(j))),
            pl.BlockSpec((block, width), lambda j: (around(j), 0)),
            once((8, width)),
            pl.BlockSpec((1, block), lambda j: (0, around(j))),
            ANYWHERE,
        ],
        out_specs=[
            pl.BlockSpec((width, block), lambda j: (0, later(j))),
            pl.BlockSpec((1, block), lambda j: (0, later(j))),
            once((width, width)),
            once((count, width)),
            once((count, width)),
            once((8, width)),
            once(shape),
            ANYWHERE,
        ],
        out_shape=[
            jax.ShapeDtypeStruct((width, hidden), BRAIN),
            jax.ShapeDtypeStruct((1, hidden), FLOAT),
            jax.ShapeDtypeStruct((width, width), BRAIN),
            jax.ShapeDtypeStruct((count, width), BRAIN),
            jax.ShapeDtypeStruct((count, width), FLOAT),
            jax.ShapeDtypeStruct((8, width), FLOAT),
            jax.ShapeDtypeStruct(shape, FLOAT),
            jax.ShapeDtypeStruct((seq_count, rows, pos_count, width), BRAIN),
        ],
        scratch_shapes=[
            pltpu.VMEM((half, count, block), BRAIN),
            pltpu.VMEM((half, count, block), BRAIN),
            pltpu.VMEM((count, width), BRAIN),
            pltpu.VMEM((width, count), BRAIN),
            pltpu.VMEM((count, width), FLOAT),
            pltpu.VMEM((count, width), FLOAT),
            pltpu.VMEM((count, block), BRAIN),
            pltpu.VMEM((rows, seq_count, pos_count, width), BRAIN),
            pltpu.VMEM((rows, seq_count, pos_count, width), BRAIN),
            pltpu.VMEM((counts[0] // 2, 2, seq_count) + shape, BRAIN),
        ]
        + scatter_buffers([shape], plan, counts)
        + [
            pltpu.SemaphoreType.DMA((slots,)),
            pltpu.SemaphoreType.DMA((slots,)),
            pltpu.SemaphoreType.DMA((4,)),
            pltpu.SemaphoreType.DMA((1,)),
        ],
        name="feed_forward",
        compiler_params=pltpu.CompilerParams(
            collective_id=4, has_side_effects=True, vmem_limit_bytes=63 * 1024 * 1024
        ),
    )(context, tokens, w_out, w_up, w_down, vectors, up_shift, cotangent)


def lamb_pieces(weight, first, second, grad, decay):
    first_new = BETA_ONE * first + (1.0 - BETA_ONE) * grad
    second_new = BETA_TWO * second + (1.0 - BETA_TWO) * grad * grad
    spread_out = jnp.sqrt(second_new / CORR_TWO) + ADAM_EPS
    update = first_new / CORR_ONE / spread_out + decay * weight
    return (first_new, second_new, update)


def square_sum(values):
    return jnp.sum(jnp.sum(values * values, axis=1, keepdims=True), axis=0, keepdims=True)


def picked(small, rank, vector_size, bias_size):
    width = small.shape[1]
    row = lax.broadcasted_iota(jnp.int32, (width, 128), 0)
    lane = lax.broadcasted_iota(jnp.int32, (width, 128), 1)
    dot = functools.partial(jnp.dot, precision=lax.Precision.HIGHEST, preferred_element_type=FLOAT)
    chosen = (row == lane + rank * vector_size) & (lane < vector_size)
    vector_grad = dot(small[0:8, :], jnp.where(chosen, 1.0, 0.0))[:, :vector_size]
    start = rank * bias_size
    chosen = (row == lane + lax.rem(start, width)) & (lane < bias_size)
    tail = dot(small[8:16, :], jnp.where(chosen, 1.0, 0.0))
    tail_row = lax.broadcasted_iota(jnp.int32, tail.shape, 0)
    tail = jnp.sum(jnp.where(tail_row == lax.div(start, width), tail, 0.0), axis=0, keepdims=True)
    return vector_grad, tail[:, :bias_size]


def scatters_of(here, slots, grads, buffers, shares, own_sem, plan):
    count = len(grads)
    found, loads = [], []
    for index, grad in enumerate(grads):
        own, *arrivals = buffers[index::count]
        share, offset = shares[index] if isinstance(shares[index], tuple) else (shares[index], 0)
        load = lambda grad=grad, own=own, index=index: pltpu.make_async_copy(
            grad.at[:, here.core], own, own_sem.at[index]
        )
        loads.append(load)
        split, line_last = plan[index]
        for order, pieces in enumerate(parts_of(grad.shape[-2:], split)):
            wait = (lambda load=load: load().wait()) if order == 0 else (lambda: None)
            found.append(
                Scatter(
                    here, slots, grad, own, *arrivals, (share, offset), pieces, wait, line_last
                )
            )
    return found, loads


def scatter_buffers(shapes, plan, counts):
    half_count, seq_count = counts[0] // 2, counts[1]
    found = [pltpu.VMEM((half_count, seq_count) + shape, BRAIN) for shape in shapes * 2]
    for shape, (_, line_last) in zip(shapes, plan):
        found.append(pltpu.VMEM((seq_count - 1, 1 if line_last else half_count) + shape, BRAIN))
    for shape, (_, line_last) in zip(shapes, plan):
        found.append(pltpu.VMEM((half_count - 1, seq_count if line_last else 1) + shape, BRAIN))
    return found


def scatter_views(grads, shapes, counts):
    lead = (counts[0] // 2, 2, counts[1])
    return [grad.reshape(lead + shape) for grad, shape in zip(grads, shapes)]


class SmallSum(Transfer):
    def __init__(self, here, small, sums, arrived, send_sem, recv_sem):
        self.slots = Slots(send_sem, recv_sem)
        self.small, self.sums, self.arrived = small, sums, arrived
        self.peers = [here.core_peer()]
        self.peers += [{"dp": flipped(here.place, bit + 1)} for bit in range(bits_of(here.half_count))]
        self.peers += [here.line_peer(bit) for bit in range(here.seq_bits)]
        self.stages = len(self.peers)

    def copies(self, stage):
        source = self.sums.at[stage - 1] if stage else self.small
        return [self.slots.copy(stage, source, self.arrived.at[stage], self.peers[stage])]

    def use(self, stage):
        before = self.sums[stage - 1] if stage else self.small[...]
        self.sums[stage] = before + self.arrived[stage]


def scatter_kernel(counts, plan, *refs):
    grads, small, input_rows = refs[0:3], refs[3], refs[4]
    ready = refs[5:8]
    weights, firsts, seconds = refs[8:14], refs[14:20], refs[20:26]
    shares, norm_out, input_grad = refs[26:29], refs[29], refs[30]
    buffers, bounce = refs[31:43], refs[43]
    small_sum, small_in, norm_mine, norm_dp, norm_line, norm_seq = refs[44:50]
    send_sem, recv_sem, own_sem, move_sem, small_send, small_recv, norm_send, norm_recv = refs[50:58]
    here = Here(*counts)
    slots = Slots(send_sem, recv_sem)
    thirds = [(shares[0], at * grads[at].shape[-1]) for at in range(3)]
    scatters, loads = scatters_of(here, slots, grads, buffers, thirds, own_sem, plan)
    move = Exchange(here, slots, input_rows, input_grad, False, bounce, move_sem)
    total = SmallSum(here, small, small_sum, small_in, small_send, small_recv)
    for load in loads:
        load().start()
    dp_peers, seq_peers = here.all_peers()[: here.dp_count - 1], here.all_peers()[here.dp_count - 1 :]
    greet(dp_peers + seq_peers)
    groups = [scatters[:1], scatters[1:]]
    waves = waves_of(groups)
    more = waves_of([[total]])
    lane = lax.broadcasted_iota(jnp.int32, (8, 128), 1)
    row = lax.broadcasted_iota(jnp.int32, (8, 128), 0)

    def with_norms(tile, index, grad):
        decay = DECAY_RATE if index < 4 else 0.0
        weight = weights[index][...]
        update = lamb_pieces(weight, firsts[index][...], seconds[index][...], grad, decay)[2]
        at = row == min(index, 4)
        tile = jnp.where(at & (lane == 0), square_sum(weight), tile)
        return jnp.where(at & (lane == 1), square_sum(update), tile)

    for turn in range(max(len(waves), len(more))):
        if turn < len(waves):
            waves[turn]()
        if turn < len(more):
            more[turn]()
        if turn == 1:
            tile = jnp.zeros((8, 128), FLOAT)
            for index in (1, 2, 3):
                tile = with_norms(tile, index, ready[index - 1][...])
        if turn == len(groups) - 1 + here.seq_bits:
            move.start(0)

    rank = here.place * here.seq_count + here.line
    vector_grad, bias_grad = picked(
        small_sum[total.stages - 1], rank, shares[1].shape[1], shares[2].shape[1]
    )
    shares[1][...] = vector_grad
    shares[2][...] = bias_grad
    tile = with_norms(tile, 0, shares[0][...])
    norm_mine[0:8, :] = with_norms(tile, 5, bias_grad)
    weight = weights[4][...]
    update = lamb_pieces(weight, firsts[4][...], seconds[4][...], vector_grad, 0.0)[2]
    weight_sq = jnp.sum(weight * weight, axis=1, keepdims=True)
    update_sq = jnp.sum(update * update, axis=1, keepdims=True)
    norm_mine[8:16, :] = jnp.where(lane == 0, weight_sq, jnp.where(lane == 1, update_sq, 0.0))

    norm_slots = Slots(norm_send, norm_recv)

    def exchange(source, held, peers, at):
        base = norm_slots.take(len(peers))
        copies = [
            norm_slots.copy(base + turn, source, held.at[at], peer) for turn, peer in enumerate(peers)
        ]
        for copy in copies:
            copy.start()
        held[at] = source[...]
        for copy in copies:
            copy.wait_recv()
        found = held[0]
        for turn in range(1, held.shape[0]):
            found = found + held[turn]
        return copies, found

    sent, found = exchange(norm_mine, norm_dp, dp_peers, here.place)
    norm_line[...] = found
    also, found = exchange(norm_line, norm_seq, seq_peers, here.line)
    norm_out[...] = found
    move.finish(0)
    for copy in sent + also:
        copy.wait_send()
    drain_all(scatters + [total, move])


def scatter_last(grads, small, input_rows, ready, weights, firsts, seconds, counts):
    dp_count, seq_count = counts
    shapes = [weight.shape for weight in weights]
    thirds = [(shapes[0][0], grad.shape[1]) for grad in grads]
    plan = [(False, False)] * 3
    slots = slot_count(counts, thirds, plan, 1)
    stages = bits_of(dp_count) + bits_of(seq_count)
    return pl.pallas_call(
        functools.partial(scatter_kernel, counts, plan),
        out_shape=[jax.ShapeDtypeStruct(shapes[at], FLOAT) for at in (0, 4, 5)]
        + [
            jax.ShapeDtypeStruct((16, 128), FLOAT),
            jax.ShapeDtypeStruct((seq_count,) + input_rows.shape[0:1] + input_rows.shape[2:], BRAIN),
        ],
        in_specs=[ANYWHERE] * 3 + [WHOLE, ANYWHERE] + [WHOLE] * 21,
        out_specs=[WHOLE] * 4 + [ANYWHERE],
        scratch_shapes=scatter_buffers(thirds, plan, counts)
        + [
            pltpu.VMEM(input_rows.shape[0:1] + input_rows.shape[2:], BRAIN),
            pltpu.VMEM((stages,) + small.shape, FLOAT),
            pltpu.VMEM((stages,) + small.shape, FLOAT),
            pltpu.VMEM((16, 128), FLOAT),
            pltpu.VMEM((dp_count, 16, 128), FLOAT),
            pltpu.VMEM((16, 128), FLOAT),
            pltpu.VMEM((seq_count, 16, 128), FLOAT),
            pltpu.SemaphoreType.DMA((slots,)),
            pltpu.SemaphoreType.DMA((slots,)),
            pltpu.SemaphoreType.DMA((3,)),
            pltpu.SemaphoreType.DMA((2,)),
            pltpu.SemaphoreType.DMA((stages,)),
            pltpu.SemaphoreType.DMA((stages,)),
            pltpu.SemaphoreType.DMA((dp_count + seq_count,)),
            pltpu.SemaphoreType.DMA((dp_count + seq_count,)),
        ],
        name="scatter_last",
        compiler_params=pltpu.CompilerParams(
            collective_id=3, has_side_effects=True, vmem_limit_bytes=56 * 1024 * 1024
        ),
    )(*scatter_views(grads, thirds, counts), small, input_rows, *ready, *weights, *firsts, *seconds)


def lamb_kernel(*refs):
    grads, norms = refs[0:6], refs[6]
    weights, firsts, seconds = refs[7:13], refs[13:19], refs[19:25]
    grad_out, first_out, second_out, new_out = refs[25:31], refs[31:37], refs[37:43], refs[43:49]
    copy_out = refs[49:53]
    weight_norm = jnp.sqrt(norms[:, 0:1])
    scales = weight_norm / (jnp.sqrt(norms[:, 1:2]) + ADAM_EPS)
    for index in range(6):
        grad = grads[index][...]
        weight = weights[index][...]
        decay = DECAY_RATE if index < 4 else 0.0
        first_new, second_new, update = lamb_pieces(
            weight, firsts[index][...], seconds[index][...], grad, decay
        )
        scale = scales[8:16] if index == 4 else scales[min(index, 4) : min(index, 4) + 1]
        new = weight - LEARN_RATE * scale * update
        grad_out[index][...] = grad
        first_out[index][...] = first_new
        second_out[index][...] = second_new
        new_out[index][...] = new
        if index < 4:
            copy_out[index][...] = new.astype(BRAIN)


def lamb_all(grads, norms, weights, firsts, seconds):
    vmem = pl.BlockSpec(memory_space=pltpu.VMEM)
    shapes = [jax.ShapeDtypeStruct(weight.shape, FLOAT) for weight in weights]
    copies = [jax.ShapeDtypeStruct(weight.shape, BRAIN) for weight in weights[:4]]
    return pl.pallas_call(
        lamb_kernel,
        out_shape=shapes * 4 + copies,
        in_specs=[vmem] * 25,
        out_specs=[vmem] * 28,
        name="lamb_update",
        compiler_params=pltpu.CompilerParams(vmem_limit_bytes=48 * 1024 * 1024),
    )(*grads, norms, *weights, *firsts, *seconds)


def body(
    tokens,
    cotangent,
    segment_ids,
    w_qkv,
    m_qkv,
    v_qkv,
    w_out,
    m_out,
    v_out,
    w_up,
    m_up,
    v_up,
    w_down,
    m_down,
    v_down,
    vectors,
    m_vectors,
    v_vectors,
    up_bias,
    m_up_bias,
    v_up_bias,
):
    dp_count, seq_count = lax.axis_size("dp"), lax.axis_size("seq")
    vector_size, bias_size = vectors.shape[1], up_bias.shape[0]
    small = jnp.concatenate(
        [
            jnp.pad(vectors, ((0, 0), (0, 128 - vector_size))),
            jnp.pad(up_bias[None], ((0, 7), (0, 128 - bias_size))),
        ]
    )
    shards = [part.astype(BRAIN) for part in (small, w_qkv, w_out, w_up, w_down)]
    counts = (dp_count, seq_count)
    token_rows, *fulls = gather_first(tokens, shards[:2], counts)
    small = fulls[0].reshape(dp_count * seq_count, 16, 128)
    full_vectors = small[:, :8, :vector_size].transpose(1, 0, 2)
    vector_rows = full_vectors.reshape(8, -1).astype(FLOAT)
    up_shift = small[:, 8, :bias_size].reshape(-1).astype(FLOAT)
    as_matrix = lambda full: full.reshape(-1, full.shape[-1])
    full_qkv = as_matrix(fulls[1])

    width = tokens.shape[2]
    length = segment_ids.shape[1]
    rows = token_rows.shape[0]
    assert rows == 1
    segments = lax.dynamic_slice_in_dim(segment_ids, lax.axis_index("seq"), 1, 0)
    token_rows = token_rows.reshape(length, width)
    *heads, context, lse_rows, full_out, full_up, full_down = attention_forward(
        segments, token_rows, vector_rows, full_qkv, shards[2:], counts
    )
    full_out, full_up, full_down = [as_matrix(full) for full in (full_out, full_up, full_down)]
    grad_up, grad_up_bias, grad_out, context_grad, resid_grad, sums, share_down, mixed = feed_forward(
        context,
        token_rows,
        full_out,
        full_up,
        full_down,
        vector_rows,
        up_shift[None],
        cotangent,
        w_down.shape,
        counts,
    )
    *qkv_grads, shift_sums, norm_sums, input_rows, share_up, share_out = attention_backward(
        segments,
        heads,
        context_grad,
        lse_rows,
        token_rows,
        vector_rows,
        resid_grad,
        full_qkv,
        [grad_up, grad_out],
        [w_up.shape, w_out.shape],
        counts,
    )
    grad_vectors = jnp.concatenate([norm_sums[:2], sums[:2], shift_sums[:2], sums[2:4]])
    small_grad = jnp.concatenate([grad_vectors, grad_up_bias.reshape(-1, width)])
    small_grad = jnp.pad(small_grad, ((0, 16 - small_grad.shape[0]), (0, 0)))
    as_row = lambda value: value.reshape(1, -1)
    weights = (w_qkv, w_out, w_up, w_down, vectors, as_row(up_bias))
    firsts = (m_qkv, m_out, m_up, m_down, m_vectors, as_row(m_up_bias))
    seconds = (v_qkv, v_out, v_up, v_down, v_vectors, as_row(v_up_bias))
    share_qkv, share_vectors, share_bias, norms, input_grad = scatter_last(
        qkv_grads,
        small_grad,
        input_rows.reshape(rows, seq_count, length // seq_count, width),
        [share_out, share_up, share_down],
        weights,
        firsts,
        seconds,
        counts,
    )
    shares = [share_qkv, share_out, share_up, share_down, share_vectors, share_bias]
    results = list(lamb_all(shares, norms, weights, firsts, seconds))
    mixed = mixed.reshape(tokens.shape)
    input_grad = input_grad.reshape(tokens.shape).astype(FLOAT)
    for index in (5, 11, 17, 23):
        results[index] = results[index].reshape(-1)
    return (mixed, input_grad, *results)


def solution(mesh):
    matrix = P(("dp", "seq"), None)
    rows = P("dp", "seq", None)
    vector = P(None, ("dp", "seq"))
    bias = P(("dp", "seq"))
    six = (matrix, matrix, matrix, matrix, vector, bias)
    in_specs = (rows, rows, P("dp", None)) + tuple(spec for spec in six for _ in range(3))
    out_specs = (rows, rows) + six * 4 + (matrix,) * 4
    return jax.shard_map(body, mesh=mesh, in_specs=in_specs, out_specs=out_specs, check_vma=False)
```

```python
import functools

import jax
import jax.numpy as jnp
from jax import lax
from jax.experimental import pallas as pl
from jax.experimental.pallas import tpu as pltpu
from jax.sharding import PartitionSpec as P

HEADS = 12
HEAD_DIM = 64
LONGEST = 512
QUERY_BLOCK = 256
ROW_BLOCK = 256


BETA_ONE = 0.9
BETA_TWO = 0.999
ADAM_EPS = 1e-06
DECAY_RATE = 0.01
LEARN_RATE = 0.4
NORM_EPS = 1e-05
STEP_NUMBER = 10.0
CORR_ONE = 1.0 - BETA_ONE**STEP_NUMBER
CORR_TWO = 1.0 - BETA_TWO**STEP_NUMBER

BRAIN = jnp.bfloat16
FLOAT = jnp.float32


def matmul(left_side, right_side):
    return jnp.dot(left_side, right_side, preferred_element_type=FLOAT)


def inner_rows(left_side, right_side):
    return lax.dot_general(
        left_side, right_side, (((0,), (0,)), ((), ())), preferred_element_type=FLOAT
    )


def times_transposed(left_side, right_side):
    return lax.dot_general(
        left_side, right_side, (((1,), (1,)), ((), ())), preferred_element_type=FLOAT
    )


def norm_parts(values):
    center = values - jnp.mean(values, axis=-1, keepdims=True)
    inverse = lax.rsqrt(jnp.mean(center * center, axis=-1, keepdims=True) + NORM_EPS)
    return center * inverse, inverse


def row_blocks(count):
    return [slice(first, first + ROW_BLOCK) for first in range(0, count, ROW_BLOCK)]


def windows(length):
    return [
        (max(0, first - LONGEST), first + QUERY_BLOCK) for first in range(0, length, QUERY_BLOCK)
    ]


def fill_bias(seg_col, seg_row, bias, length):
    place = 0
    for index, (low, high) in enumerate(windows(length)):
        first = index * QUERY_BLOCK
        size = high - low
        keys = seg_col[0, low:high, :]
        queries = seg_row[0, :, first : first + QUERY_BLOCK]
        key_place = low + lax.broadcasted_iota(jnp.int32, (size, QUERY_BLOCK), 0)
        query_place = first + lax.broadcasted_iota(jnp.int32, (size, QUERY_BLOCK), 1)
        allowed = (keys == queries) & (key_place <= query_place)
        bias[place : place + size, :] = jnp.where(allowed, 0.0, -1000000000.0)
        place += size


def split_heads(pair):
    lane = lax.broadcasted_iota(jnp.int32, pair.shape, 1)
    zero = jnp.zeros_like(pair)
    return (jnp.where(lane < HEAD_DIM, pair, zero), jnp.where(lane < HEAD_DIM, zero, pair))


def attend_forward(counts, splits, *refs):
    seg_col, seg_row, tokens, norms, shifts, wq_ref, wk_ref, wv_ref = refs[0:8]
    q_ref, k_ref, v_ref, c_ref, lse_ref = refs[11:16]
    fulls, bias, low_one, send_sem, recv_sem = refs[16:19], *refs[19:]
    length = q_ref.shape[0]
    here = Here(*counts)
    slots = Slots(send_sem, recv_sem)
    gathers = gathers_of(here, slots, fulls, splits)
    waves = led_by(lambda: greet(here.near_peers()), flow_of(gathers))
    blocks = windows(length)
    beside = Beside(waves, HEADS // 2 * len(blocks))

    @pl.when(pl.program_id(0) == 0)
    def _():
        beside.point(0, len(blocks), first=True)
        fill_bias(seg_col, seg_row, bias, length)
        for rows in row_blocks(length):
            normed, _ = norm_parts(tokens[rows, :].astype(FLOAT))
            low_one[rows, :] = (normed * norms[0:1, :] + norms[1:2, :]).astype(BRAIN)

    lanes = 2 * HEAD_DIM
    joined = jnp.concatenate([wq_ref[...], wk_ref[...], wv_ref[...]], axis=1)
    for rows in row_blocks(length):
        projected = matmul(low_one[rows, :], joined)
        q_ref[rows, :] = (projected[:, :lanes] + shifts[4:5, :]).astype(BRAIN)
        k_ref[rows, :] = projected[:, lanes : 2 * lanes].astype(BRAIN)
        v_ref[rows, :] = (projected[:, 2 * lanes :] + shifts[5:6, :]).astype(BRAIN)
    v_turned = v_ref[...].T
    place = 0
    for index, (low, high) in enumerate(blocks):
        beside.point(index, len(blocks), first=False)
        first = index * QUERY_BLOCK
        size = high - low
        queries = split_heads(q_ref[first : first + QUERY_BLOCK, :] * HEAD_DIM ** (-0.5))
        keys = k_ref[low:high, :]
        blocked = bias[place : place + size, :]
        parts = []
        for head in range(2):
            scores = times_transposed(keys, queries[head]) + blocked
            peak = jnp.max(scores, axis=0, keepdims=True)
            probs = jnp.exp(scores - peak)
            total = jnp.sum(probs, axis=0, keepdims=True)
            probs = (probs * (1.0 / total)).astype(BRAIN)
            lse_ref[0, head : head + 1, first : first + QUERY_BLOCK] = peak + jnp.log(total)
            turned = v_turned[head * HEAD_DIM : (head + 1) * HEAD_DIM, low:high]
            parts.append(matmul(turned, probs))
        context = jnp.concatenate(parts, axis=0).T
        c_ref[first : first + QUERY_BLOCK, :] = context.astype(BRAIN)
        place += size

    @pl.when(pl.program_id(0) == HEADS // 2 - 1)
    def _():
        beside.rest()
        drain_all(gathers)


def led_by(ahead, waves):
    def both():
        ahead()
        waves[0]()

    return [both] + waves[1:]


class Beside:
    def __init__(self, waves, points):
        self.at = {}
        early = len(waves) - 1
        for index in range(early):
            self.at.setdefault(index * points // early, []).append(waves[index])
        self.late = waves[early:]

    def point(self, index, per_step, first):
        for point, calls in self.at.items():
            if point % per_step == index and first == (point == 0):

                @pl.when(pl.program_id(0) == point // per_step)
                def _(calls=calls):
                    for call in calls:
                        call()

    def rest(self):
        for call in self.late:
            call()


def attend_backward(counts, splits, *refs):
    seg_col, seg_row, q_ref, k_ref, v_ref, g_ref, lse_ref = refs[0:7]
    tokens, norms, resid_grad, wq_ref, wk_ref, wv_ref = refs[7:13]
    grads, gq_ref, gk_ref, gv_ref, shift_ref, sum_ref, input_ref = refs[13:16], *refs[16:22]
    partials, bias, key_sum, value_sum, low_turned, total, joined = refs[22:25], *refs[25:31]
    buffers, send_sem, recv_sem, own_sem = refs[31:40], *refs[40:]
    length = q_ref.shape[0]
    pair = pl.program_id(0)
    here = Here(*counts)
    slots = Slots(send_sem, recv_sem)
    scatters, loads = scatters_of(here, slots, grads, buffers, partials, own_sem, splits)

    def begin():
        for load in loads:
            load().start()
        greet(here.near_peers())

    waves = led_by(begin, flow_of(scatters))
    blocks = windows(length)
    beside = Beside(waves, HEADS // 2 * len(blocks))

    @pl.when(pair == 0)
    def _():
        beside.point(0, len(blocks), first=True)
        fill_bias(seg_col, seg_row, bias, length)
        for rows in row_blocks(length):
            normed, _ = norm_parts(tokens[rows, :].astype(FLOAT))
            low_turned[:, rows] = (normed * norms[0:1, :] + norms[1:2, :]).astype(BRAIN).T
        total[...] = jnp.zeros_like(total)

    key_sum[...] = jnp.zeros_like(key_sum)
    value_sum[...] = jnp.zeros_like(value_sum)
    k_turned = k_ref[...].T
    lanes = 2 * HEAD_DIM
    place = 0
    for index, (low, high) in enumerate(blocks):
        beside.point(index, len(blocks), first=False)
        first = index * QUERY_BLOCK
        size = high - low
        rows = slice(first, first + QUERY_BLOCK)
        queries = split_heads(q_ref[rows, :] * HEAD_DIM ** (-0.5))
        grads = split_heads(g_ref[rows, :])
        keys = k_ref[low:high, :]
        values = v_ref[low:high, :]
        blocked = bias[place : place + size, :]
        all_probs = []
        all_scores = []
        parts = []
        for head in range(2):
            scores = times_transposed(keys, queries[head]) + blocked
            probs = jnp.exp(scores - lse_ref[0, head : head + 1, rows])
            prob_grad = times_transposed(values, grads[head])
            row_dot = jnp.sum(probs * prob_grad, axis=0, keepdims=True)
            score_grad = (probs * (prob_grad - row_dot)).astype(BRAIN)
            all_probs.append(probs.astype(BRAIN))
            all_scores.append(score_grad)
            turned = k_turned[head * HEAD_DIM : (head + 1) * HEAD_DIM, low:high]
            parts.append(matmul(turned, score_grad))
        query_grad = jnp.concatenate(parts, axis=0).T * HEAD_DIM ** (-0.5)
        joined[rows, :lanes] = query_grad.astype(BRAIN)
        value_sum[low:high, :] += matmul(
            jnp.concatenate(all_probs, axis=1), jnp.concatenate(grads, axis=0)
        )
        key_sum[low:high, :] += matmul(
            jnp.concatenate(all_scores, axis=1), jnp.concatenate(queries, axis=0)
        )
        place += size
    joined[:, lanes : 2 * lanes] = key_sum[...].astype(BRAIN)
    joined[:, 2 * lanes :] = value_sum[...].astype(BRAIN)
    weight = jnp.concatenate([wq_ref[...], wk_ref[...], wv_ref[...]], axis=1)
    sums = jnp.zeros((1, 3 * lanes), FLOAT)
    for rows in row_blocks(length):
        part = joined[rows, :]
        total[rows, :] += times_transposed(part, weight)
        sums = sums + jnp.sum(part.astype(FLOAT), axis=0, keepdims=True)
    found = matmul(low_turned[...], joined[...]).astype(BRAIN)
    gq_ref[...] = found[:, :lanes]
    gk_ref[...] = found[:, lanes : 2 * lanes]
    gv_ref[...] = found[:, 2 * lanes :]
    shift_ref[0:1, :] = sums[:, :lanes]
    shift_ref[1:2, :] = sums[:, 2 * lanes :]
    shift_ref[2:8, :] = jnp.zeros((6, lanes), FLOAT)

    @pl.when(pair == HEADS // 2 - 1)
    def _():
        gains = jnp.zeros((1, total.shape[1]), FLOAT)
        moves = jnp.zeros((1, total.shape[1]), FLOAT)
        for rows in row_blocks(length):
            normed, inverse = norm_parts(tokens[rows, :].astype(FLOAT))
            upstream = total[rows, :]
            scaled = upstream * norms[0:1, :]
            centered = scaled - jnp.mean(scaled, axis=-1, keepdims=True)
            inward = centered - normed * jnp.mean(scaled * normed, axis=-1, keepdims=True)
            input_ref[rows, :] = (resid_grad[rows, :] + inverse * inward).astype(BRAIN)
            gains = gains + jnp.sum(upstream * normed, axis=0, keepdims=True)
            moves = moves + jnp.sum(upstream, axis=0, keepdims=True)
        sum_ref[0:1, :] = gains
        sum_ref[1:2, :] = moves
        sum_ref[2:8, :] = jnp.zeros((6, total.shape[1]), FLOAT)

    @pl.when(pair == HEADS // 2 - 1)
    def _():
        beside.rest()
        drain_all(scatters)


def once(shape):
    return pl.BlockSpec(shape, lambda *_: (0,) * len(shape), pipeline_mode=pl.Buffered(1))


def pair_specs(length):
    lanes, width = 2 * HEAD_DIM, HEADS * HEAD_DIM
    pairs = HEADS // 2
    segs = [once((1, length, 1)), once((1, 1, length))]
    plain = pl.BlockSpec((length, lanes), lambda j: (0, j))
    lse = pl.BlockSpec((1, 8, length), lambda j: (j, 0, 0))
    weights = [pl.BlockSpec((width, lanes), lambda j, at=at: (0, at * pairs + j)) for at in range(3)]
    shifts = pl.BlockSpec((8, lanes), lambda j: (0, j))
    bias = pltpu.VMEM((sum(high - low for low, high in windows(length)), QUERY_BLOCK), FLOAT)
    return segs, plain, lse, weights, shifts, bias


def attention_forward(segments, tokens, vectors, full_qkv, fulls, counts):
    length, width = tokens.shape
    segs, plain, lse, weights, shifts, bias = pair_specs(length)
    splits = [False] + [True] * (len(fulls) - 1)
    slots = piece_count([full.shape[-2:] for full in fulls], splits) * counts[1]
    return pl.pallas_call(
        functools.partial(attend_forward, counts, splits),
        grid=(HEADS // 2,),
        in_specs=segs
        + [once((length, width)), once((8, width)), shifts]
        + weights
        + [ANYWHERE] * 3,
        out_specs=[plain] * 4 + [lse] + [ANYWHERE] * 3,
        out_shape=[jax.ShapeDtypeStruct((length, width), BRAIN)] * 4
        + [jax.ShapeDtypeStruct((HEADS // 2, 8, length), FLOAT)]
        + [jax.ShapeDtypeStruct(full.shape, full.dtype) for full in fulls],
        input_output_aliases={8 + index: 5 + index for index in range(len(fulls))},
        scratch_shapes=[
            bias,
            pltpu.VMEM((length, width), BRAIN),
            pltpu.SemaphoreType.DMA((slots,)),
            pltpu.SemaphoreType.DMA((slots,)),
        ],
        name="attend_forward",
        compiler_params=pltpu.CompilerParams(
            collective_id=1, has_side_effects=True, vmem_limit_bytes=63 * 1024 * 1024
        ),
    )(
        segments[:, :, None],
        segments[:, None, :],
        tokens,
        vectors,
        vectors,
        full_qkv,
        full_qkv,
        full_qkv,
        *fulls,
    )


def attention_backward(
    segments, heads, context_grad, lse_rows, tokens, vectors, resid_grad, full_qkv, grads, shapes, counts
):
    length, width = tokens.shape
    lanes = 2 * HEAD_DIM
    segs, plain, lse, weights, shifts, bias = pair_specs(length)
    column = pl.BlockSpec((width, lanes), lambda j: (0, j))
    splits = [True] * (len(shapes) - 1) + [False]
    slots = piece_count(shapes, splits) * counts[1]
    partials = [jax.ShapeDtypeStruct((counts[0] // 2,) + shape, BRAIN) for shape in shapes]
    return pl.pallas_call(
        functools.partial(attend_backward, counts, splits),
        grid=(HEADS // 2,),
        in_specs=segs
        + [plain] * 4
        + [lse, once((length, width)), once((8, width)), once((length, width))]
        + weights
        + [ANYWHERE] * 3,
        out_specs=[column] * 3 + [shifts, once((8, width)), once((length, width))] + [WHOLE] * 3,
        out_shape=[jax.ShapeDtypeStruct((width, width), BRAIN)] * 3
        + [jax.ShapeDtypeStruct((8, width), FLOAT)] * 2
        + [jax.ShapeDtypeStruct((length, width), BRAIN)]
        + partials,
        scratch_shapes=[
            bias,
            pltpu.VMEM((length, lanes), FLOAT),
            pltpu.VMEM((length, lanes), FLOAT),
            pltpu.VMEM((width, length), BRAIN),
            pltpu.VMEM((length, width), FLOAT),
            pltpu.VMEM((length, 3 * lanes), BRAIN),
        ]
        + scatter_buffers(shapes, counts)
        + [
            pltpu.SemaphoreType.DMA((slots,)),
            pltpu.SemaphoreType.DMA((slots,)),
            pltpu.SemaphoreType.DMA((len(shapes),)),
        ],
        name="attend_backward",
        compiler_params=pltpu.CompilerParams(
            collective_id=2, has_side_effects=True, vmem_limit_bytes=63 * 1024 * 1024
        ),
    )(
        segments[:, :, None],
        segments[:, None, :],
        *heads,
        context_grad,
        lse_rows,
        tokens,
        vectors,
        resid_grad,
        full_qkv,
        full_qkv,
        full_qkv,
        *scatter_views(grads, shapes, counts),
    )


MESH = pl.DeviceIdType.MESH
ANYWHERE = pl.BlockSpec(memory_space=pl.ANY)
WHOLE = pl.BlockSpec(memory_space=pltpu.VMEM)


def bits_of(count):
    return count.bit_length() - 1


def flipped(value, bit):
    step = 1 << bit
    return value + step * (1 - 2 * lax.rem(lax.div(value, step), 2))


def rounded_down(value, bit):
    return lax.div(value, 1 << bit) * (1 << bit)


def spread(value, bit, total):
    step = 1 << (bit + 1)
    return [lax.rem(value, step) + step * turn for turn in range(1 << (total - 1 - bit))]


class Here:
    def __init__(self, dp_count, seq_count):
        self.dp_count, self.seq_count = dp_count, seq_count
        self.half_count = dp_count // 2
        self.seq_bits = bits_of(seq_count)
        self.place, self.line = lax.axis_index("dp"), lax.axis_index("seq")
        self.chip, self.core = lax.div(self.place, 2), lax.rem(self.place, 2)

    def core_peer(self):
        return {"dp": flipped(self.place, 0)}

    def line_peer(self, bit):
        return {"seq": flipped(self.line, bit)}

    def other_lines(self):
        return [lax.rem(self.line + turn, self.seq_count) for turn in range(1, self.seq_count)]

    def other_chips(self):
        return [lax.rem(self.chip + turn, self.half_count) for turn in range(1, self.half_count)]

    def chip_peers(self):
        return [{"dp": 2 * chip + self.core} for chip in self.other_chips()]

    def near_peers(self):
        peers = [self.core_peer()] + self.chip_peers()
        return peers + [{"seq": line} for line in self.other_lines()]

    def all_peers(self):
        peers = [{"dp": lax.rem(self.place + turn, self.dp_count)} for turn in range(1, self.dp_count)]
        return peers + [{"seq": line} for line in self.other_lines()]


def greet(peers):
    barrier = pltpu.get_barrier_semaphore()
    for peer in peers:
        pl.semaphore_signal(barrier, inc=1, device_id=peer, device_id_type=MESH)
    pl.semaphore_wait(barrier, len(peers))


class Slots:
    def __init__(self, send_sem, recv_sem):
        self.send_sem, self.recv_sem, self.used = send_sem, recv_sem, 0

    def take(self, count):
        first = self.used
        self.used += count
        return first

    def copy(self, slot, source, target, peer):
        return pltpu.make_async_remote_copy(
            source,
            target,
            self.send_sem.at[slot],
            self.recv_sem.at[slot],
            device_id=peer,
            device_id_type=MESH,
        )


def parts_of(shape, split):
    rows, width = shape
    tiles = width // 128
    if width % 128 or tiles < 2:
        return [[(slice(0, rows), slice(0, width), False)]]
    middle = tiles // 2 * 128
    first, second = (0, middle), (middle, width)
    every = slice(0, rows)
    if split and rows % 32 == 0:
        return [
            [(part, slice(*first), False), (part, slice(*second), True)]
            for part in (slice(0, rows // 2), slice(rows // 2, rows))
        ]
    if split and tiles >= 4:
        lists = [[], []]
        for (low, high), backwards in ((first, False), (second, True)):
            cut = low + (high - low) // 256 * 128
            lists[0].append((every, slice(low, cut), backwards))
            lists[1].append((every, slice(cut, high), backwards))
        return lists
    return [[(every, slice(*first), False), (every, slice(*second), True)]]


class Transfer:
    def start(self, stage):
        for copy in self.copies(stage):
            copy.start()

    def finish(self, stage):
        for copy in self.copies(stage):
            copy.wait_recv()
        self.use(stage)

    def use(self, stage):
        pass

    def drain(self):
        for stage in range(self.stages):
            for copy in self.copies(stage):
                copy.wait_send()


class ChipGather(Transfer):
    stages = 1

    def __init__(self, here, slots, shard, full, bounce, inward, outward):
        self.here, self.slots, self.shard = here, slots, shard
        self.target = full.at[here.chip, here.core, here.line]
        self.moves = [
            pltpu.make_async_copy(shard, bounce, inward),
            pltpu.make_async_copy(bounce, self.target, outward),
        ]
        self.first = slots.take(here.half_count - 1)

    def copies(self, stage):
        return [
            self.slots.copy(self.first + turn, self.shard, self.target, peer)
            for turn, peer in enumerate(self.here.chip_peers())
        ]

    def own(self):
        for move in self.moves:
            move.start()
            move.wait()


class Gather(Transfer):
    def __init__(self, here, slots, full, pieces):
        self.here, self.slots, self.full, self.pieces = here, slots, full, pieces
        self.stages = here.seq_bits + 1
        self.each = here.seq_count
        self.first = slots.take(self.each * len(pieces))

    def copies(self, stage):
        here, full = self.here, self.full
        found = []
        for index, (rows, columns, backwards) in enumerate(self.pieces):
            slot = self.first + self.each * index
            if stage == self.stages - 1:
                part = full.at[:, here.core, :, rows, columns]
                found.append(self.slots.copy(slot, part, part, here.core_peer()))
                continue
            if backwards:
                bit = here.seq_bits - 1 - stage
                slot += 1 << stage
                parts = [
                    full.at[:, here.core, at, rows, columns]
                    for at in spread(here.line, bit, here.seq_bits)
                ]
            else:
                bit = stage
                slot += 1 + bit
                block = pl.ds(rounded_down(here.line, bit), 1 << bit)
                parts = [full.at[:, here.core, block, rows, columns]]
            for turn, part in enumerate(parts):
                found.append(self.slots.copy(slot + turn, part, part, here.line_peer(bit)))
        return found


class ChipSum(Transfer):
    stages = 1

    def __init__(self, here, slots, partial, arrived, share, offset):
        self.here, self.slots, self.partial, self.arrived = here, slots, partial, arrived
        self.share, self.offset = share, offset
        self.first = slots.take(here.half_count - 1)

    def copies(self, stage):
        return [
            self.slots.copy(
                self.first + turn,
                self.partial.at[chip],
                self.arrived.at[turn],
                {"dp": 2 * chip + self.here.core},
            )
            for turn, chip in enumerate(self.here.other_chips())
        ]

    def use(self, stage):
        total = self.partial[self.here.chip].astype(FLOAT)
        for turn in range(self.here.half_count - 1):
            total = total + self.arrived[turn].astype(FLOAT)
        self.share[:, self.offset : self.offset + total.shape[1]] = total


class Scatter(Transfer):
    def __init__(self, here, slots, grad, own, from_core, from_line, partial, pieces, load):
        self.here, self.slots, self.grad, self.own = here, slots, grad, own
        self.from_core, self.from_line, self.partial = from_core, from_line, partial
        self.pieces, self.load = pieces, load
        self.stages = here.seq_bits + 1
        self.each = here.seq_count
        self.first = slots.take(self.each * len(pieces))

    def line_stage(self, stage, backwards):
        here = self.here
        if backwards:
            bit = stage - 1
            away = spread(flipped(here.line, bit), bit, here.seq_bits)
            kept = spread(here.line, bit, here.seq_bits)
        else:
            bit = here.seq_bits - stage
            away = [rounded_down(flipped(here.line, bit), bit) + at for at in range(1 << bit)]
            kept = [rounded_down(here.line, bit) + at for at in range(1 << bit)]
        base = sum(1 << (here.seq_bits - past) for past in range(1, stage))
        return bit, away, kept, base

    def copies(self, stage):
        here = self.here
        found = []
        for index, (rows, columns, backwards) in enumerate(self.pieces):
            slot = self.first + self.each * index
            if stage == 0:
                found.append(
                    self.slots.copy(
                        slot,
                        self.grad.at[:, 1 - here.core, :, rows, columns],
                        self.from_core.at[:, :, rows, columns],
                        here.core_peer(),
                    )
                )
                continue
            bit, away, _, base = self.line_stage(stage, backwards)
            for turn, at in enumerate(away):
                found.append(
                    self.slots.copy(
                        slot + 1 + base + turn,
                        self.own.at[:, at, rows, columns],
                        self.from_line.at[base + turn, :, rows, columns],
                        here.line_peer(bit),
                    )
                )
        return found

    def use(self, stage):
        here, own = self.here, self.own
        if stage == 0:
            self.load()
        for rows, columns, backwards in self.pieces:
            if stage == 0:

                def add(at, carry, rows=rows, columns=columns):
                    one, two = lax.div(at, here.seq_count), lax.rem(at, here.seq_count)
                    own[one, two, rows, columns] = (
                        own[one, two, rows, columns] + self.from_core[one, two, rows, columns]
                    )
                    return carry

                lax.fori_loop(0, here.half_count * here.seq_count, add, 0)
                continue
            _, _, kept, base = self.line_stage(stage, backwards)
            for turn, at in enumerate(kept):
                last = stage == self.stages - 1

                def add(one, carry, rows=rows, columns=columns, at=at, place=base + turn, last=last):
                    found = own[one, at, rows, columns] + self.from_line[place, one, rows, columns]
                    if last:
                        self.partial[one, rows, columns] = found
                    else:
                        own[one, at, rows, columns] = found
                    return carry

                lax.fori_loop(0, here.half_count, add, 0)


class Exchange(Transfer):
    stages = 1

    def __init__(self, here, slots, source, target, to_rows, bounce, sem):
        self.here, self.slots, self.source, self.target = here, slots, source, target
        self.to_rows, self.bounce, self.sem = to_rows, bounce, sem
        self.first = slots.take(here.seq_count - 1)

    def ends(self, line):
        if self.to_rows:
            count = self.target.shape[0]
            block = self.source.at[pl.ds(line * count, count)]
            return block, self.target.at[:, self.here.line]
        return self.source.at[:, line], self.target.at[self.here.line]

    def copies(self, stage):
        return [
            self.slots.copy(self.first + turn, *self.ends(line), {"seq": line})
            for turn, line in enumerate(self.here.other_lines())
        ]

    def own_in(self):
        return pltpu.make_async_copy(self.ends(self.here.line)[0], self.bounce, self.sem.at[0])

    def own_out(self):
        source, target = self.ends(self.here.line)
        source = source if self.bounce is None else self.bounce
        return pltpu.make_async_copy(source, target, self.sem.at[1])

    def start(self, stage):
        if self.bounce is not None:
            self.own_in().start()
        super().start(stage)
        if self.bounce is not None:
            self.own_in().wait()
        self.own_out().start()

    def use(self, stage):
        self.own_out().wait()


def flow_of(transfers):
    def begin():
        for transfer in transfers:
            transfer.start(0)

    def follow(transfer, stage):
        transfer.finish(stage - 1)
        if stage < transfer.stages:
            transfer.start(stage)

    calls = [begin]
    for stage in range(1, max(transfer.stages for transfer in transfers) + 1):
        for transfer in transfers:
            if stage <= transfer.stages:
                calls.append(functools.partial(follow, transfer, stage))
    return calls


def drain_all(transfers):
    for transfer in transfers:
        transfer.drain()


def chip_gathers_of(here, slots, shards, fulls, bounces, sem):
    return [
        ChipGather(here, slots, shard, full, bounce, sem.at[2 * index], sem.at[2 * index + 1])
        for index, (shard, full, bounce) in enumerate(zip(shards, fulls, bounces))
    ]


def gathers_of(here, slots, fulls, splits):
    return [
        Gather(here, slots, full, pieces)
        for full, split in zip(fulls, splits)
        for pieces in parts_of(full.shape[-2:], split)
    ]


def piece_count(shapes, splits):
    return sum(len(part) for shape, split in zip(shapes, splits) for part in parts_of(shape, split))


def full_shape(shard, dp_count, seq_count):
    return jax.ShapeDtypeStruct((dp_count // 2, 2, seq_count) + shard.shape, shard.dtype)


def gather_kernel(counts, first, count, *refs):
    tokens, shards = refs[0], refs[1 : 1 + count]
    token_rows, fulls = refs[1 + count], refs[2 + count : 2 + 2 * count]
    rest = refs[2 + 2 * count :]
    bounces, bounce, send_sem, recv_sem, own_sem, move_sem = rest[:count], *rest[count:]
    here = Here(*counts)
    slots = Slots(send_sem, recv_sem)
    chips = chip_gathers_of(here, slots, shards, fulls, bounces, own_sem)
    move = Exchange(here, slots, tokens, token_rows, True, bounce, move_sem)
    gathers = gathers_of(here, slots, fulls[:first], [False] + [True] * (first - 1))
    flow = flow_of(gathers)
    greet(here.near_peers())
    for chip in chips[:first]:
        chip.start(0)
    move.start(0)
    for chip in chips[first:]:
        chip.start(0)
    for chip in chips:
        chip.own()
    for chip in chips[:first]:
        chip.finish(0)
    for call in flow:
        call()
    move.finish(0)
    for chip in chips[first:]:
        chip.finish(0)
    drain_all(chips + gathers + [move])


def gather_first(tokens, shards, first, counts):
    dp_count, seq_count = counts
    row_count, pos_count, width = tokens.shape
    rows = row_count // seq_count
    pieces = piece_count([shard.shape for shard in shards[:first]], [False] + [True] * (first - 1))
    slots = len(shards) * (dp_count // 2 - 1) + pieces * seq_count + seq_count - 1
    return pl.pallas_call(
        functools.partial(gather_kernel, counts, first, len(shards)),
        out_shape=[jax.ShapeDtypeStruct((rows, seq_count, pos_count, width), tokens.dtype)]
        + [full_shape(shard, *counts) for shard in shards],
        in_specs=[ANYWHERE] * (1 + len(shards)),
        out_specs=[ANYWHERE] * (1 + len(shards)),
        scratch_shapes=[pltpu.VMEM(shard.shape, shard.dtype) for shard in shards]
        + [
            pltpu.VMEM((rows, pos_count, width), tokens.dtype),
            pltpu.SemaphoreType.DMA((slots,)),
            pltpu.SemaphoreType.DMA((slots,)),
            pltpu.SemaphoreType.DMA((2 * len(shards),)),
            pltpu.SemaphoreType.DMA((2,)),
        ],
        name="gather_first",
        compiler_params=pltpu.CompilerParams(
            collective_id=0, has_side_effects=True, vmem_limit_bytes=63 * 1024 * 1024
        ),
    )(tokens, *shards)


HIDDEN_BLOCK = 512
GELU_SCALE = 0.7978845608028654
GELU_CUBE = 0.044715


def gelu_both(values):
    square = values * values
    turned = jnp.tanh(GELU_SCALE * values * (1.0 + GELU_CUBE * square))
    half = 0.5 + 0.5 * turned
    inner = GELU_SCALE * (1.0 + 3.0 * GELU_CUBE * square)
    return values * half, half + 0.5 * values * (1.0 - turned * turned) * inner


def forward_start(context, tokens, w_out, vectors, resid, low_two, low_turned):
    for rows in row_blocks(resid.shape[0]):
        values = tokens[rows, :].astype(FLOAT) + (matmul(context[rows, :], w_out[...]) + vectors[6:7, :])
        resid[rows, :] = values
        normed, _ = norm_parts(values)
        low = (normed * vectors[2:3, :] + vectors[3:4, :]).astype(BRAIN)
        low_two[rows, :] = low
        low_turned[:, rows] = low.T


def backward_end(
    context, w_out, vectors, resid, total, back, gc_ref, gr_ref, gwo_ref, sum_ref, low_turned
):
    width = resid.shape[1]
    sums = [jnp.zeros((1, width), FLOAT) for _ in range(4)]
    for rows in row_blocks(resid.shape[0]):
        normed, inverse = norm_parts(resid[rows, :])
        upstream = total[rows, :]
        given = back(rows).astype(FLOAT)
        scaled = upstream * vectors[2:3, :]
        centered = scaled - jnp.mean(scaled, axis=-1, keepdims=True)
        inward = centered - normed * jnp.mean(scaled * normed, axis=-1, keepdims=True)
        grad = given + inverse * inward
        low = grad.astype(BRAIN)
        gr_ref[rows, :] = grad
        gc_ref[rows, :] = times_transposed(low, w_out[...]).astype(BRAIN)
        low_turned[:, rows] = context[rows, :].T
        total[rows, :] = low.astype(FLOAT)
        for index, values in enumerate((upstream * normed, upstream, low.astype(FLOAT), given)):
            sums[index] = sums[index] + jnp.sum(values, axis=0, keepdims=True)
    for index in range(4):
        sum_ref[index : index + 1, :] = sums[index]
    sum_ref[4:8, :] = jnp.zeros((4, width), FLOAT)
    gwo_ref[...] = matmul(low_turned[...], total[...].astype(BRAIN)).astype(BRAIN)


def mlp_kernel(counts, *refs):
    context, tokens, w_out, w_up, w_down, vectors, up_shift, cotangent = refs[0:8]
    gup_ref, gdown_ref, gub_ref, gwo_ref, gc_ref, gr_ref, sum_ref, mixed = refs[8:16]
    acts, slopes, low_two, low_turned, resid, total, hidden, back, mixed_rows = refs[16:25]
    send_sem, recv_sem, move_sem = refs[25:28]
    here = Here(*counts)
    slots = Slots(send_sem, recv_sem)
    arrive = Exchange(here, slots, cotangent, back, True, None, move_sem.at[pl.ds(0, 2)])
    leave = Exchange(here, slots, mixed_rows, mixed, False, None, move_sem.at[pl.ds(2, 2)])
    step = pl.program_id(0)
    half = pl.num_programs(0) // 2
    count = resid.shape[0]
    pos_count = back.shape[2]

    def back_rows(rows):
        parts = []
        for first in range(rows.start, rows.stop, pos_count):
            size = min(pos_count, rows.stop - first)
            row, rest = divmod(first, pos_count * counts[1])
            line, offset = divmod(rest, pos_count)
            parts.append(back[row, line, offset : offset + size, :])
        return parts[0] if len(parts) == 1 else jnp.concatenate(parts, axis=0)

    @pl.when(step == 0)
    def _():
        greet(here.near_peers())
        arrive.start(0)
        forward_start(context, tokens, w_out, vectors, resid, low_two, low_turned)
        total[...] = jnp.zeros_like(total)

    @pl.when(step < half)
    def _():
        for rows in row_blocks(count):
            values = matmul(low_two[rows, :], w_up[...]) + up_shift[...]
            act, slope = gelu_both(values)
            low = act.astype(BRAIN)
            acts[step, rows, :] = low
            slopes[step, rows, :] = slope
            total[rows, :] += matmul(low, w_down[...])

    @pl.when(step == half)
    def _():
        for first in range(0, count, pos_count):
            row, line = divmod(first // pos_count, counts[1])
            rows = slice(first, first + pos_count)
            values = resid[rows, :] + (total[rows, :] + vectors[7:8, :])
            mixed_rows[row, line] = values.astype(BRAIN)
        total[...] = jnp.zeros_like(total)
        leave.start(0)
        arrive.finish(0)

    @pl.when(step >= half)
    def _():
        at = step - half
        sums = jnp.zeros((1, hidden.shape[1]), FLOAT)
        for rows in row_blocks(count):
            grad = times_transposed(back_rows(rows), w_down[...]) * slopes[at, rows, :]
            low = grad.astype(BRAIN)
            hidden[rows, :] = low
            sums = sums + jnp.sum(low.astype(FLOAT), axis=0, keepdims=True)
            total[rows, :] += times_transposed(low, w_up[...])
        gub_ref[...] = sums
        gup_ref[...] = matmul(low_turned[...], hidden[...]).astype(BRAIN)
        every = back_rows(slice(0, count))
        gdown_ref[...] = inner_rows(acts[at], every).astype(BRAIN)

    @pl.when(step == 2 * half - 1)
    def _():
        backward_end(
            context, w_out, vectors, resid, total, back_rows, gc_ref, gr_ref, gwo_ref, sum_ref, low_turned
        )
        leave.finish(0)
        drain_all([arrive, leave])


def feed_forward(context, tokens, w_out, w_up, w_down, vectors, up_shift, cotangent, counts):
    count, width = context.shape
    hidden = w_up.shape[1]
    half = hidden // HIDDEN_BLOCK
    seq_count = counts[1]
    row_count, pos_count, _ = cotangent.shape
    rows = row_count // seq_count
    later = lambda j: jnp.maximum(j - half, 0)
    around = lambda j: lax.rem(j, half)
    block = HIDDEN_BLOCK
    slots = 2 * (seq_count - 1)
    return pl.pallas_call(
        functools.partial(mlp_kernel, counts),
        grid=(2 * half,),
        in_specs=[
            once((count, width)),
            once((count, width)),
            once((width, width)),
            pl.BlockSpec((width, block), lambda j: (0, around(j))),
            pl.BlockSpec((block, width), lambda j: (around(j), 0)),
            once((8, width)),
            pl.BlockSpec((1, block), lambda j: (0, around(j))),
            ANYWHERE,
        ],
        out_specs=[
            pl.BlockSpec((width, block), lambda j: (0, later(j))),
            pl.BlockSpec((block, width), lambda j: (later(j), 0)),
            pl.BlockSpec((1, block), lambda j: (0, later(j))),
            once((width, width)),
            once((count, width)),
            once((count, width)),
            once((8, width)),
            ANYWHERE,
        ],
        out_shape=[
            jax.ShapeDtypeStruct((width, hidden), BRAIN),
            jax.ShapeDtypeStruct((hidden, width), BRAIN),
            jax.ShapeDtypeStruct((1, hidden), FLOAT),
            jax.ShapeDtypeStruct((width, width), BRAIN),
            jax.ShapeDtypeStruct((count, width), BRAIN),
            jax.ShapeDtypeStruct((count, width), FLOAT),
            jax.ShapeDtypeStruct((8, width), FLOAT),
            jax.ShapeDtypeStruct((seq_count, rows, pos_count, width), BRAIN),
        ],
        scratch_shapes=[
            pltpu.VMEM((half, count, block), BRAIN),
            pltpu.VMEM((half, count, block), FLOAT),
            pltpu.VMEM((count, width), BRAIN),
            pltpu.VMEM((width, count), BRAIN),
            pltpu.VMEM((count, width), FLOAT),
            pltpu.VMEM((count, width), FLOAT),
            pltpu.VMEM((count, block), BRAIN),
            pltpu.VMEM((rows, seq_count, pos_count, width), BRAIN),
            pltpu.VMEM((rows, seq_count, pos_count, width), BRAIN),
            pltpu.SemaphoreType.DMA((slots,)),
            pltpu.SemaphoreType.DMA((slots,)),
            pltpu.SemaphoreType.DMA((4,)),
        ],
        name="feed_forward",
        compiler_params=pltpu.CompilerParams(
            collective_id=4, has_side_effects=True, vmem_limit_bytes=63 * 1024 * 1024
        ),
    )(context, tokens, w_out, w_up, w_down, vectors, up_shift, cotangent)


def lamb_pieces(weight, first, second, grad, decay):
    first_new = BETA_ONE * first + (1.0 - BETA_ONE) * grad
    second_new = BETA_TWO * second + (1.0 - BETA_TWO) * grad * grad
    spread_out = jnp.sqrt(second_new / CORR_TWO) + ADAM_EPS
    update = first_new / CORR_ONE / spread_out + decay * weight
    return (first_new, second_new, update)


def square_sum(values):
    return jnp.sum(jnp.sum(values * values, axis=1, keepdims=True), axis=0, keepdims=True)


def picked(small, rank, vector_size, bias_size):
    width = small.shape[1]
    row = lax.broadcasted_iota(jnp.int32, (width, 128), 0)
    lane = lax.broadcasted_iota(jnp.int32, (width, 128), 1)
    dot = functools.partial(jnp.dot, precision=lax.Precision.HIGHEST, preferred_element_type=FLOAT)
    chosen = (row == lane + rank * vector_size) & (lane < vector_size)
    vector_grad = dot(small[0:8, :], jnp.where(chosen, 1.0, 0.0))[:, :vector_size]
    start = rank * bias_size
    chosen = (row == lane + lax.rem(start, width)) & (lane < bias_size)
    tail = dot(small[8:16, :], jnp.where(chosen, 1.0, 0.0))
    tail_row = lax.broadcasted_iota(jnp.int32, tail.shape, 0)
    tail = jnp.sum(jnp.where(tail_row == lax.div(start, width), tail, 0.0), axis=0, keepdims=True)
    return vector_grad, tail[:, :bias_size]


def scatters_of(here, slots, grads, buffers, partials, own_sem, splits):
    count = len(grads)
    found, loads = [], []
    for index, (grad, partial) in enumerate(zip(grads, partials)):
        own, *arrivals = buffers[index::count]
        load = lambda grad=grad, own=own, index=index: pltpu.make_async_copy(
            grad.at[:, here.core], own, own_sem.at[index]
        )
        loads.append(load)
        for order, pieces in enumerate(parts_of(grad.shape[-2:], splits[index])):
            wait = (lambda load=load: load().wait()) if order == 0 else (lambda: None)
            found.append(Scatter(here, slots, grad, own, *arrivals, partial, pieces, wait))
    return found, loads


def scatter_buffers(shapes, counts):
    half_count, seq_count = counts[0] // 2, counts[1]
    leads = [(half_count, seq_count)] * 2 + [(seq_count - 1, half_count)]
    return [pltpu.VMEM(lead + shape, BRAIN) for lead in leads for shape in shapes]


def scatter_views(grads, shapes, counts):
    lead = (counts[0] // 2, 2, counts[1])
    return [grad.reshape(lead + shape) for grad, shape in zip(grads, shapes)]


class SmallSum(Transfer):
    def __init__(self, here, small, sums, arrived, send_sem, recv_sem):
        self.slots = Slots(send_sem, recv_sem)
        self.small, self.sums, self.arrived = small, sums, arrived
        self.peers = [here.core_peer()]
        self.peers += [{"dp": flipped(here.place, bit + 1)} for bit in range(bits_of(here.half_count))]
        self.peers += [here.line_peer(bit) for bit in range(here.seq_bits)]
        self.stages = len(self.peers)

    def copies(self, stage):
        source = self.sums.at[stage - 1] if stage else self.small
        return [self.slots.copy(stage, source, self.arrived.at[stage], self.peers[stage])]

    def use(self, stage):
        before = self.sums[stage - 1] if stage else self.small[...]
        self.sums[stage] = before + self.arrived[stage]


def scatter_kernel(counts, *refs):
    grads, small, input_rows, partials = refs[0:3], refs[3], refs[4], refs[5:8]
    weights, firsts, seconds = refs[8:14], refs[14:20], refs[20:26]
    shares, norm_out, input_grad = refs[26:32], refs[32], refs[33]
    buffers, mine, arrived, bounce = refs[34:43], refs[43:46], refs[46:52], refs[52]
    small_sum, small_in, norm_mine, norm_dp, norm_line, norm_seq = refs[53:59]
    send_sem, recv_sem, own_sem, move_sem, small_send, small_recv, norm_send, norm_recv = refs[59:67]
    here = Here(*counts)
    slots = Slots(send_sem, recv_sem)
    scatters, loads = scatters_of(here, slots, grads, buffers, mine, own_sem, [False] * 3)
    early = [
        ChipSum(here, slots, partial, arrived[index], shares[index + 1], 0)
        for index, partial in enumerate(partials)
    ]
    late = [
        ChipSum(here, slots, mine[at], arrived[3 + at], shares[0], at * grads[at].shape[-1])
        for at in range(3)
    ]
    move = Exchange(here, slots, input_rows, input_grad, False, bounce, move_sem)
    total = SmallSum(here, small, small_sum, small_in, small_send, small_recv)
    for load in loads:
        load().start()
    dp_peers, seq_peers = here.all_peers()[: here.dp_count - 1], here.all_peers()[here.dp_count - 1 :]
    greet(dp_peers + seq_peers)
    lane = lax.broadcasted_iota(jnp.int32, (8, 128), 1)
    row = lax.broadcasted_iota(jnp.int32, (8, 128), 0)

    def with_norms(tile, index, grad):
        decay = DECAY_RATE if index < 4 else 0.0
        weight = weights[index][...]
        update = lamb_pieces(weight, firsts[index][...], seconds[index][...], grad, decay)[2]
        at = row == min(index, 4)
        tile = jnp.where(at & (lane == 0), square_sum(weight), tile)
        return jnp.where(at & (lane == 1), square_sum(update), tile)

    for chip in early:
        chip.start(0)
    total.start(0)
    for stage in range(scatters[0].stages + 1):
        for index, scatter in enumerate(scatters):
            if stage:
                scatter.finish(stage - 1)
            if stage < scatter.stages:
                scatter.start(stage)
            else:
                late[index].start(0)
        if stage == scatters[0].stages - 1:
            move.start(0)
        if stage < total.stages:
            total.finish(stage)
            if stage + 1 < total.stages:
                total.start(stage + 1)
    for stage in range(scatters[0].stages + 1, total.stages):
        total.finish(stage)
        if stage + 1 < total.stages:
            total.start(stage + 1)
    tile = jnp.zeros((8, 128), FLOAT)
    for index, chip in enumerate(early):
        chip.finish(0)
        tile = with_norms(tile, index + 1, shares[index + 1][...])

    rank = here.place * here.seq_count + here.line
    vector_grad, bias_grad = picked(
        small_sum[total.stages - 1], rank, shares[4].shape[1], shares[5].shape[1]
    )
    shares[4][...] = vector_grad
    shares[5][...] = bias_grad
    tile = with_norms(tile, 5, bias_grad)
    for chip in late:
        chip.finish(0)
    norm_mine[0:8, :] = with_norms(tile, 0, shares[0][...])
    weight = weights[4][...]
    update = lamb_pieces(weight, firsts[4][...], seconds[4][...], vector_grad, 0.0)[2]
    weight_sq = jnp.sum(weight * weight, axis=1, keepdims=True)
    update_sq = jnp.sum(update * update, axis=1, keepdims=True)
    norm_mine[8:16, :] = jnp.where(lane == 0, weight_sq, jnp.where(lane == 1, update_sq, 0.0))

    norm_slots = Slots(norm_send, norm_recv)

    def exchange(source, held, peers, at):
        base = norm_slots.take(len(peers))
        copies = [
            norm_slots.copy(base + turn, source, held.at[at], peer) for turn, peer in enumerate(peers)
        ]
        for copy in copies:
            copy.start()
        held[at] = source[...]
        for copy in copies:
            copy.wait_recv()
        found = held[0]
        for turn in range(1, held.shape[0]):
            found = found + held[turn]
        return copies, found

    sent, found = exchange(norm_mine, norm_dp, dp_peers, here.place)
    norm_line[...] = found
    also, found = exchange(norm_line, norm_seq, seq_peers, here.line)
    norm_out[...] = found
    move.finish(0)
    for copy in sent + also:
        copy.wait_send()
    drain_all(scatters + early + late + [total, move])


def scatter_last(grads, small, input_rows, partials, weights, firsts, seconds, counts):
    dp_count, seq_count = counts
    shapes = [weight.shape for weight in weights]
    thirds = [(shapes[0][0], grad.shape[1]) for grad in grads]
    lead = (dp_count // 2,)
    pieces = piece_count(thirds, [False] * 3)
    slots = pieces * seq_count + 6 * (dp_count // 2 - 1) + seq_count - 1
    stages = bits_of(dp_count) + bits_of(seq_count)
    return pl.pallas_call(
        functools.partial(scatter_kernel, counts),
        out_shape=[jax.ShapeDtypeStruct(shape, FLOAT) for shape in shapes]
        + [
            jax.ShapeDtypeStruct((16, 128), FLOAT),
            jax.ShapeDtypeStruct((seq_count,) + input_rows.shape[0:1] + input_rows.shape[2:], BRAIN),
        ],
        in_specs=[ANYWHERE] * 3 + [WHOLE, ANYWHERE] + [WHOLE] * 21,
        out_specs=[WHOLE] * 7 + [ANYWHERE],
        scratch_shapes=scatter_buffers(thirds, counts)
        + [pltpu.VMEM(lead + shape, BRAIN) for shape in thirds]
        + [pltpu.VMEM((lead[0] - 1,) + shape, BRAIN) for shape in shapes[1:4] + thirds]
        + [
            pltpu.VMEM(input_rows.shape[0:1] + input_rows.shape[2:], BRAIN),
            pltpu.VMEM((stages,) + small.shape, FLOAT),
            pltpu.VMEM((stages,) + small.shape, FLOAT),
            pltpu.VMEM((16, 128), FLOAT),
            pltpu.VMEM((dp_count, 16, 128), FLOAT),
            pltpu.VMEM((16, 128), FLOAT),
            pltpu.VMEM((seq_count, 16, 128), FLOAT),
            pltpu.SemaphoreType.DMA((slots,)),
            pltpu.SemaphoreType.DMA((slots,)),
            pltpu.SemaphoreType.DMA((3,)),
            pltpu.SemaphoreType.DMA((2,)),
            pltpu.SemaphoreType.DMA((stages,)),
            pltpu.SemaphoreType.DMA((stages,)),
            pltpu.SemaphoreType.DMA((dp_count + seq_count,)),
            pltpu.SemaphoreType.DMA((dp_count + seq_count,)),
        ],
        name="scatter_last",
        compiler_params=pltpu.CompilerParams(
            collective_id=3, has_side_effects=True, vmem_limit_bytes=60 * 1024 * 1024
        ),
    )(
        *scatter_views(grads, thirds, counts),
        small,
        input_rows,
        *partials,
        *weights,
        *firsts,
        *seconds,
    )


def lamb_kernel(*refs):
    grads, norms = refs[0:6], refs[6]
    weights, firsts, seconds = refs[7:13], refs[13:19], refs[19:25]
    grad_out, first_out, second_out, new_out = refs[25:31], refs[31:37], refs[37:43], refs[43:49]
    copy_out = refs[49:53]
    weight_norm = jnp.sqrt(norms[:, 0:1])
    scales = weight_norm / (jnp.sqrt(norms[:, 1:2]) + ADAM_EPS)
    for index in range(6):
        grad = grads[index][...]
        weight = weights[index][...]
        decay = DECAY_RATE if index < 4 else 0.0
        first_new, second_new, update = lamb_pieces(
            weight, firsts[index][...], seconds[index][...], grad, decay
        )
        scale = scales[8:16] if index == 4 else scales[min(index, 4) : min(index, 4) + 1]
        new = weight - LEARN_RATE * scale * update
        grad_out[index][...] = grad
        first_out[index][...] = first_new
        second_out[index][...] = second_new
        new_out[index][...] = new
        if index < 4:
            copy_out[index][...] = new.astype(BRAIN)


def lamb_all(grads, norms, weights, firsts, seconds):
    vmem = pl.BlockSpec(memory_space=pltpu.VMEM)
    shapes = [jax.ShapeDtypeStruct(weight.shape, FLOAT) for weight in weights]
    copies = [jax.ShapeDtypeStruct(weight.shape, BRAIN) for weight in weights[:4]]
    return pl.pallas_call(
        lamb_kernel,
        out_shape=shapes * 4 + copies,
        in_specs=[vmem] * 25,
        out_specs=[vmem] * 28,
        name="lamb_update",
        compiler_params=pltpu.CompilerParams(vmem_limit_bytes=48 * 1024 * 1024),
    )(*grads, norms, *weights, *firsts, *seconds)


def body(
    tokens,
    cotangent,
    segment_ids,
    w_qkv,
    m_qkv,
    v_qkv,
    w_out,
    m_out,
    v_out,
    w_up,
    m_up,
    v_up,
    w_down,
    m_down,
    v_down,
    vectors,
    m_vectors,
    v_vectors,
    up_bias,
    m_up_bias,
    v_up_bias,
):
    dp_count, seq_count = lax.axis_size("dp"), lax.axis_size("seq")
    vector_size, bias_size = vectors.shape[1], up_bias.shape[0]
    small = jnp.concatenate(
        [
            jnp.pad(vectors, ((0, 0), (0, 128 - vector_size))),
            jnp.pad(up_bias[None], ((0, 7), (0, 128 - bias_size))),
        ]
    )
    shards = [part.astype(BRAIN) for part in (small, w_qkv, w_out, w_up, w_down)]
    counts = (dp_count, seq_count)
    token_rows, *fulls = gather_first(tokens, shards, 2, counts)
    small = fulls[0].reshape(dp_count * seq_count, 16, 128)
    full_vectors = small[:, :8, :vector_size].transpose(1, 0, 2)
    vector_rows = full_vectors.reshape(8, -1).astype(FLOAT)
    up_shift = small[:, 8, :bias_size].reshape(-1).astype(FLOAT)
    as_matrix = lambda full: full.reshape(-1, full.shape[-1])
    full_qkv = as_matrix(fulls[1])

    width = tokens.shape[2]
    length = segment_ids.shape[1]
    rows = token_rows.shape[0]
    assert rows == 1
    segments = lax.dynamic_slice_in_dim(segment_ids, lax.axis_index("seq"), 1, 0)
    token_rows = token_rows.reshape(length, width)
    *heads, context, lse_rows, full_out, full_up, full_down = attention_forward(
        segments, token_rows, vector_rows, full_qkv, fulls[2:], counts
    )
    full_out, full_up, full_down = [as_matrix(full) for full in (full_out, full_up, full_down)]
    grad_up, grad_down, grad_up_bias, grad_out, context_grad, resid_grad, sums, mixed = feed_forward(
        context,
        token_rows,
        full_out,
        full_up,
        full_down,
        vector_rows,
        up_shift[None],
        cotangent,
        counts,
    )
    *qkv_grads, shift_sums, norm_sums, input_rows, sum_down, sum_up, sum_out = attention_backward(
        segments,
        heads,
        context_grad,
        lse_rows,
        token_rows,
        vector_rows,
        resid_grad,
        full_qkv,
        [grad_down, grad_up, grad_out],
        [w_down.shape, w_up.shape, w_out.shape],
        counts,
    )
    grad_vectors = jnp.concatenate([norm_sums[:2], sums[:2], shift_sums[:2], sums[2:4]])
    small_grad = jnp.concatenate([grad_vectors, grad_up_bias.reshape(-1, width)])
    small_grad = jnp.pad(small_grad, ((0, 16 - small_grad.shape[0]), (0, 0)))
    as_row = lambda value: value.reshape(1, -1)
    weights = (w_qkv, w_out, w_up, w_down, vectors, as_row(up_bias))
    firsts = (m_qkv, m_out, m_up, m_down, m_vectors, as_row(m_up_bias))
    seconds = (v_qkv, v_out, v_up, v_down, v_vectors, as_row(v_up_bias))
    *shares, norms, input_grad = scatter_last(
        qkv_grads,
        small_grad,
        input_rows.reshape(rows, seq_count, length // seq_count, width),
        [sum_out, sum_up, sum_down],
        weights,
        firsts,
        seconds,
        counts,
    )
    results = list(lamb_all(shares, norms, weights, firsts, seconds))
    mixed = mixed.reshape(tokens.shape)
    input_grad = input_grad.reshape(tokens.shape).astype(FLOAT)
    for index in (5, 11, 17, 23):
        results[index] = results[index].reshape(-1)
    return (mixed, input_grad, *results)


def solution(mesh):
    matrix = P(("dp", "seq"), None)
    rows = P("dp", "seq", None)
    vector = P(None, ("dp", "seq"))
    bias = P(("dp", "seq"))
    six = (matrix, matrix, matrix, matrix, vector, bias)
    in_specs = (rows, rows, P("dp", None)) + tuple(spec for spec in six for _ in range(3))
    out_specs = (rows, rows) + six * 4 + (matrix,) * 4
    return jax.shard_map(body, mesh=mesh, in_specs=in_specs, out_specs=out_specs, check_vma=False)
```

```python
import functools

import jax
import jax.numpy as jnp
from jax import lax
from jax.experimental import pallas as pl
from jax.experimental.pallas import tpu as pltpu
from jax.sharding import PartitionSpec as P

HEADS = 12
HEAD_DIM = 64
LONGEST = 512
QUERY_BLOCK = 256
ROW_BLOCK = 256


BETA_ONE = 0.9
BETA_TWO = 0.999
ADAM_EPS = 1e-06
DECAY_RATE = 0.01
LEARN_RATE = 0.4
NORM_EPS = 1e-05
STEP_NUMBER = 10.0
CORR_ONE = 1.0 - BETA_ONE**STEP_NUMBER
CORR_TWO = 1.0 - BETA_TWO**STEP_NUMBER

BRAIN = jnp.bfloat16
FLOAT = jnp.float32


def matmul(left_side, right_side):
    return jnp.dot(left_side, right_side, preferred_element_type=FLOAT)


def inner_rows(left_side, right_side):
    return lax.dot_general(
        left_side, right_side, (((0,), (0,)), ((), ())), preferred_element_type=FLOAT
    )


def times_transposed(left_side, right_side):
    return lax.dot_general(
        left_side, right_side, (((1,), (1,)), ((), ())), preferred_element_type=FLOAT
    )


def norm_parts(values):
    center = values - jnp.mean(values, axis=-1, keepdims=True)
    inverse = lax.rsqrt(jnp.mean(center * center, axis=-1, keepdims=True) + NORM_EPS)
    return center * inverse, inverse


def row_blocks(count):
    return [slice(first, first + ROW_BLOCK) for first in range(0, count, ROW_BLOCK)]


def windows(length):
    return [
        (max(0, first - LONGEST), first + QUERY_BLOCK) for first in range(0, length, QUERY_BLOCK)
    ]


def fill_bias(segments, bias, length):
    own = segments[pl.ds(lax.axis_index("seq"), 1), :].astype(FLOAT)
    turned = jnp.broadcast_to(own, (8, length)).T
    place = 0
    for index, (low, high) in enumerate(windows(length)):
        first = index * QUERY_BLOCK
        size = high - low
        keys = turned[low:high, 0:1]
        queries = own[:, first : first + QUERY_BLOCK]
        key_place = low + lax.broadcasted_iota(jnp.int32, (size, QUERY_BLOCK), 0)
        query_place = first + lax.broadcasted_iota(jnp.int32, (size, QUERY_BLOCK), 1)
        allowed = (keys == queries) & (key_place <= query_place)
        bias[place : place + size, :] = jnp.where(allowed, 0.0, -1000000000.0)
        place += size


def split_heads(pair):
    lane = lax.broadcasted_iota(jnp.int32, pair.shape, 1)
    zero = jnp.zeros_like(pair)
    return (jnp.where(lane < HEAD_DIM, pair, zero), jnp.where(lane < HEAD_DIM, zero, pair))


def attend_forward(counts, splits, *refs):
    segments, tokens, norms, shifts, wq_ref, wk_ref, wv_ref = refs[0:7]
    q_ref, k_ref, v_ref, c_ref, lse_ref = refs[10:15]
    fulls, bias, low_one, send_sem, recv_sem = refs[15:18], *refs[18:]
    length = q_ref.shape[0]
    here = Here(*counts)
    slots = Slots(send_sem, recv_sem)
    gathers = gathers_of(here, slots, fulls, splits)
    waves = led_by(lambda: greet(here.near_peers()), flow_of(gathers))
    blocks = windows(length)
    beside = Beside(waves, HEADS // 2 * len(blocks))

    @pl.when(pl.program_id(0) == 0)
    def _():
        beside.point(0, len(blocks), first=True)
        fill_bias(segments, bias, length)
        for rows in row_blocks(length):
            normed, _ = norm_parts(tokens[rows, :].astype(FLOAT))
            low_one[rows, :] = (normed * norms[0:1, :] + norms[1:2, :]).astype(BRAIN)

    lanes = 2 * HEAD_DIM
    joined = jnp.concatenate([wq_ref[...], wk_ref[...], wv_ref[...]], axis=1)
    for rows in row_blocks(length):
        projected = matmul(low_one[rows, :], joined)
        q_ref[rows, :] = (projected[:, :lanes] + shifts[4:5, :]).astype(BRAIN)
        k_ref[rows, :] = projected[:, lanes : 2 * lanes].astype(BRAIN)
        v_ref[rows, :] = (projected[:, 2 * lanes :] + shifts[5:6, :]).astype(BRAIN)
    v_turned = v_ref[...].T
    place = 0
    for index, (low, high) in enumerate(blocks):
        beside.point(index, len(blocks), first=False)
        first = index * QUERY_BLOCK
        size = high - low
        queries = split_heads(q_ref[first : first + QUERY_BLOCK, :] * HEAD_DIM ** (-0.5))
        keys = k_ref[low:high, :]
        blocked = bias[place : place + size, :]
        parts = []
        for head in range(2):
            scores = times_transposed(keys, queries[head]) + blocked
            peak = jnp.max(scores, axis=0, keepdims=True)
            probs = jnp.exp(scores - peak)
            total = jnp.sum(probs, axis=0, keepdims=True)
            probs = (probs * (1.0 / total)).astype(BRAIN)
            lse_ref[0, head : head + 1, first : first + QUERY_BLOCK] = peak + jnp.log(total)
            turned = v_turned[head * HEAD_DIM : (head + 1) * HEAD_DIM, low:high]
            parts.append(matmul(turned, probs))
        context = jnp.concatenate(parts, axis=0).T
        c_ref[first : first + QUERY_BLOCK, :] = context.astype(BRAIN)
        place += size

    @pl.when(pl.program_id(0) == HEADS // 2 - 1)
    def _():
        beside.rest()
        drain_all(gathers)


def led_by(ahead, waves):
    def both():
        ahead()
        waves[0]()

    return [both] + waves[1:]


class Beside:
    def __init__(self, waves, points):
        self.at = {}
        early = len(waves) - 1
        for index in range(early):
            self.at.setdefault(index * points // early, []).append(waves[index])
        self.late = waves[early:]

    def point(self, index, per_step, first):
        for point, calls in self.at.items():
            if point % per_step == index and first == (point == 0):

                @pl.when(pl.program_id(0) == point // per_step)
                def _(calls=calls):
                    for call in calls:
                        call()

    def rest(self):
        for call in self.late:
            call()


def attend_backward(counts, splits, *refs):
    refs = (None, *refs)
    segments, q_ref, k_ref, v_ref, g_ref, lse_ref = refs[1:7]
    tokens, norms, resid_grad, wq_ref, wk_ref, wv_ref = refs[7:13]
    grads, gq_ref, gk_ref, gv_ref, shift_ref, sum_ref, input_ref = refs[13:16], *refs[16:22]
    share, partials, bias, key_sum, value_sum = refs[22], refs[23:25], *refs[25:28]
    low_turned, total, joined, buffers = *refs[28:31], refs[31:40]
    first_partial, arrived, send_sem, recv_sem, own_sem = refs[40:]
    partials = (first_partial, *partials)
    length = q_ref.shape[0]
    pair = pl.program_id(0)
    here = Here(*counts)
    slots = Slots(send_sem, recv_sem)
    scatters, loads = scatters_of(here, slots, grads, buffers, partials, own_sem, splits)

    def begin():
        for load in loads:
            load().start()
        greet(here.near_peers())

    last = ChipSum(here, slots, first_partial, arrived, share, 0)
    early = len(parts_of(share.shape, splits[0]))
    flow = flow_of(scatters)
    flow.insert(len(flow) - len(scatters) + early, lambda: last.start(0))
    waves = led_by(begin, flow + [lambda: last.finish(0)])
    blocks = windows(length)
    beside = Beside(waves, HEADS // 2 * len(blocks))

    @pl.when(pair == 0)
    def _():
        beside.point(0, len(blocks), first=True)
        fill_bias(segments, bias, length)
        for rows in row_blocks(length):
            normed, _ = norm_parts(tokens[rows, :].astype(FLOAT))
            low_turned[:, rows] = (normed * norms[0:1, :] + norms[1:2, :]).astype(BRAIN).T
        total[...] = jnp.zeros_like(total)

    key_sum[...] = jnp.zeros_like(key_sum)
    value_sum[...] = jnp.zeros_like(value_sum)
    k_turned = k_ref[...].T
    lanes = 2 * HEAD_DIM
    place = 0
    for index, (low, high) in enumerate(blocks):
        beside.point(index, len(blocks), first=False)
        first = index * QUERY_BLOCK
        size = high - low
        rows = slice(first, first + QUERY_BLOCK)
        queries = split_heads(q_ref[rows, :] * HEAD_DIM ** (-0.5))
        grads = split_heads(g_ref[rows, :])
        keys = k_ref[low:high, :]
        values = v_ref[low:high, :]
        blocked = bias[place : place + size, :]
        all_probs = []
        all_scores = []
        parts = []
        for head in range(2):
            scores = times_transposed(keys, queries[head]) + blocked
            probs = jnp.exp(scores - lse_ref[0, head : head + 1, rows])
            prob_grad = times_transposed(values, grads[head])
            row_dot = jnp.sum(probs * prob_grad, axis=0, keepdims=True)
            score_grad = (probs * (prob_grad - row_dot)).astype(BRAIN)
            all_probs.append(probs.astype(BRAIN))
            all_scores.append(score_grad)
            turned = k_turned[head * HEAD_DIM : (head + 1) * HEAD_DIM, low:high]
            parts.append(matmul(turned, score_grad))
        query_grad = jnp.concatenate(parts, axis=0).T * HEAD_DIM ** (-0.5)
        joined[rows, :lanes] = query_grad.astype(BRAIN)
        value_sum[low:high, :] += matmul(
            jnp.concatenate(all_probs, axis=1), jnp.concatenate(grads, axis=0)
        )
        key_sum[low:high, :] += matmul(
            jnp.concatenate(all_scores, axis=1), jnp.concatenate(queries, axis=0)
        )
        place += size
    joined[:, lanes : 2 * lanes] = key_sum[...].astype(BRAIN)
    joined[:, 2 * lanes :] = value_sum[...].astype(BRAIN)
    weight = jnp.concatenate([wq_ref[...], wk_ref[...], wv_ref[...]], axis=1)
    sums = jnp.zeros((1, 3 * lanes), FLOAT)
    for rows in row_blocks(length):
        part = joined[rows, :]
        total[rows, :] += times_transposed(part, weight)
        sums = sums + jnp.sum(part.astype(FLOAT), axis=0, keepdims=True)
    found = matmul(low_turned[...], joined[...]).astype(BRAIN)
    gq_ref[...] = found[:, :lanes]
    gk_ref[...] = found[:, lanes : 2 * lanes]
    gv_ref[...] = found[:, 2 * lanes :]
    shift_ref[0:1, :] = sums[:, :lanes]
    shift_ref[1:2, :] = sums[:, 2 * lanes :]
    shift_ref[2:8, :] = jnp.zeros((6, lanes), FLOAT)

    @pl.when(pair == HEADS // 2 - 1)
    def _():
        gains = jnp.zeros((1, total.shape[1]), FLOAT)
        moves = jnp.zeros((1, total.shape[1]), FLOAT)
        for rows in row_blocks(length):
            normed, inverse = norm_parts(tokens[rows, :].astype(FLOAT))
            upstream = total[rows, :]
            scaled = upstream * norms[0:1, :]
            centered = scaled - jnp.mean(scaled, axis=-1, keepdims=True)
            inward = centered - normed * jnp.mean(scaled * normed, axis=-1, keepdims=True)
            input_ref[rows, :] = (resid_grad[rows, :] + inverse * inward).astype(BRAIN)
            gains = gains + jnp.sum(upstream * normed, axis=0, keepdims=True)
            moves = moves + jnp.sum(upstream, axis=0, keepdims=True)
        sum_ref[0:1, :] = gains
        sum_ref[1:2, :] = moves
        sum_ref[2:8, :] = jnp.zeros((6, total.shape[1]), FLOAT)

    @pl.when(pair == HEADS // 2 - 1)
    def _():
        beside.rest()
        drain_all(scatters + [last])


def once(shape):
    return pl.BlockSpec(shape, lambda *_: (0,) * len(shape), pipeline_mode=pl.Buffered(1))


def pair_specs(rows, length):
    lanes, width = 2 * HEAD_DIM, HEADS * HEAD_DIM
    pairs = HEADS // 2
    segs = [once((rows, length))]
    plain = pl.BlockSpec((length, lanes), lambda j: (0, j))
    lse = pl.BlockSpec((1, 8, length), lambda j: (j, 0, 0))
    weights = [pl.BlockSpec((width, lanes), lambda j, at=at: (0, at * pairs + j)) for at in range(3)]
    shifts = pl.BlockSpec((8, lanes), lambda j: (0, j))
    bias = pltpu.VMEM((sum(high - low for low, high in windows(length)), QUERY_BLOCK), FLOAT)
    return segs, plain, lse, weights, shifts, bias


def attention_forward(segments, tokens, vectors, full_qkv, fulls, counts):
    length, width = tokens.shape
    segs, plain, lse, weights, shifts, bias = pair_specs(segments.shape[0], length)
    splits = [False] + [True] * (len(fulls) - 1)
    slots = piece_count([full.shape[-2:] for full in fulls], splits) * counts[1]
    return pl.pallas_call(
        functools.partial(attend_forward, counts, splits),
        grid=(HEADS // 2,),
        in_specs=segs
        + [once((length, width)), once((8, width)), shifts]
        + weights
        + [ANYWHERE] * 3,
        out_specs=[plain] * 4 + [lse] + [ANYWHERE] * 3,
        out_shape=[jax.ShapeDtypeStruct((length, width), BRAIN)] * 4
        + [jax.ShapeDtypeStruct((HEADS // 2, 8, length), FLOAT)]
        + [jax.ShapeDtypeStruct(full.shape, full.dtype) for full in fulls],
        input_output_aliases={7 + index: 5 + index for index in range(len(fulls))},
        scratch_shapes=[
            bias,
            pltpu.VMEM((length, width), BRAIN),
            pltpu.SemaphoreType.DMA((slots,)),
            pltpu.SemaphoreType.DMA((slots,)),
        ],
        name="attend_forward",
        compiler_params=pltpu.CompilerParams(
            collective_id=1, has_side_effects=True, vmem_limit_bytes=63 * 1024 * 1024
        ),
    )(
        segments,
        tokens,
        vectors,
        vectors,
        full_qkv,
        full_qkv,
        full_qkv,
        *fulls,
    )


def attention_backward(
    segments, heads, context_grad, lse_rows, tokens, vectors, resid_grad, full_qkv, grads, shapes, counts
):
    length, width = tokens.shape
    lanes = 2 * HEAD_DIM
    segs, plain, lse, weights, shifts, bias = pair_specs(segments.shape[0], length)
    column = pl.BlockSpec((width, lanes), lambda j: (0, j))
    splits = [True] * (len(shapes) - 1) + [False]
    half_count = counts[0] // 2
    slots = piece_count(shapes, splits) * counts[1] + half_count - 1
    partials = [jax.ShapeDtypeStruct((half_count,) + shape, BRAIN) for shape in shapes[1:]]
    return pl.pallas_call(
        functools.partial(attend_backward, counts, splits),
        grid=(HEADS // 2,),
        in_specs=segs
        + [plain] * 4
        + [lse, once((length, width)), once((8, width)), once((length, width))]
        + weights
        + [ANYWHERE] * 3,
        out_specs=[column] * 3 + [shifts, once((8, width)), once((length, width))] + [WHOLE] * 3,
        out_shape=[jax.ShapeDtypeStruct((width, width), BRAIN)] * 3
        + [jax.ShapeDtypeStruct((8, width), FLOAT)] * 2
        + [jax.ShapeDtypeStruct((length, width), BRAIN), jax.ShapeDtypeStruct(shapes[0], FLOAT)]
        + partials,
        scratch_shapes=[
            bias,
            pltpu.VMEM((length, lanes), FLOAT),
            pltpu.VMEM((length, lanes), FLOAT),
            pltpu.VMEM((width, length), BRAIN),
            pltpu.VMEM((length, width), FLOAT),
            pltpu.VMEM((length, 3 * lanes), BRAIN),
        ]
        + scatter_buffers(shapes, counts)
        + [
            pltpu.VMEM((half_count,) + shapes[0], BRAIN),
            pltpu.VMEM((half_count - 1,) + shapes[0], BRAIN),
            pltpu.SemaphoreType.DMA((slots,)),
            pltpu.SemaphoreType.DMA((slots,)),
            pltpu.SemaphoreType.DMA((len(shapes),)),
        ],
        name="attend_backward",
        compiler_params=pltpu.CompilerParams(
            collective_id=2, has_side_effects=True, vmem_limit_bytes=63 * 1024 * 1024
        ),
    )(
        segments,
        *heads,
        context_grad,
        lse_rows,
        tokens,
        vectors,
        resid_grad,
        full_qkv,
        full_qkv,
        full_qkv,
        *scatter_views(grads, shapes, counts),
    )


MESH = pl.DeviceIdType.MESH
ANYWHERE = pl.BlockSpec(memory_space=pl.ANY)
WHOLE = pl.BlockSpec(memory_space=pltpu.VMEM)


def bits_of(count):
    return count.bit_length() - 1


def flipped(value, bit):
    step = 1 << bit
    return value + step * (1 - 2 * lax.rem(lax.div(value, step), 2))


def rounded_down(value, bit):
    return lax.div(value, 1 << bit) * (1 << bit)


def spread(value, bit, total):
    step = 1 << (bit + 1)
    return [lax.rem(value, step) + step * turn for turn in range(1 << (total - 1 - bit))]


class Here:
    def __init__(self, dp_count, seq_count):
        self.dp_count, self.seq_count = dp_count, seq_count
        self.half_count = dp_count // 2
        self.seq_bits = bits_of(seq_count)
        self.place, self.line = lax.axis_index("dp"), lax.axis_index("seq")
        self.chip, self.core = lax.div(self.place, 2), lax.rem(self.place, 2)

    def core_peer(self):
        return {"dp": flipped(self.place, 0)}

    def line_peer(self, bit):
        return {"seq": flipped(self.line, bit)}

    def other_lines(self):
        return [lax.rem(self.line + turn, self.seq_count) for turn in range(1, self.seq_count)]

    def other_chips(self):
        return [lax.rem(self.chip + turn, self.half_count) for turn in range(1, self.half_count)]

    def chip_peers(self):
        return [{"dp": 2 * chip + self.core} for chip in self.other_chips()]

    def near_peers(self):
        peers = [self.core_peer()] + self.chip_peers()
        return peers + [{"seq": line} for line in self.other_lines()]

    def all_peers(self):
        peers = [{"dp": lax.rem(self.place + turn, self.dp_count)} for turn in range(1, self.dp_count)]
        return peers + [{"seq": line} for line in self.other_lines()]


def greet(peers):
    barrier = pltpu.get_barrier_semaphore()
    for peer in peers:
        pl.semaphore_signal(barrier, inc=1, device_id=peer, device_id_type=MESH)
    pl.semaphore_wait(barrier, len(peers))


class Slots:
    def __init__(self, send_sem, recv_sem):
        self.send_sem, self.recv_sem, self.used = send_sem, recv_sem, 0

    def take(self, count):
        first = self.used
        self.used += count
        return first

    def copy(self, slot, source, target, peer):
        return pltpu.make_async_remote_copy(
            source,
            target,
            self.send_sem.at[slot],
            self.recv_sem.at[slot],
            device_id=peer,
            device_id_type=MESH,
        )


def parts_of(shape, split):
    rows, width = shape
    tiles = width // 128
    if width % 128 or tiles < 2:
        return [[(slice(0, rows), slice(0, width), False)]]
    middle = tiles // 2 * 128
    first, second = (0, middle), (middle, width)
    every = slice(0, rows)
    if split and rows % 32 == 0:
        return [
            [(part, slice(*first), False), (part, slice(*second), True)]
            for part in (slice(0, rows // 2), slice(rows // 2, rows))
        ]
    if split and tiles >= 4:
        lists = [[], []]
        for (low, high), backwards in ((first, False), (second, True)):
            cut = low + (high - low) // 256 * 128
            lists[0].append((every, slice(low, cut), backwards))
            lists[1].append((every, slice(cut, high), backwards))
        return lists
    return [[(every, slice(*first), False), (every, slice(*second), True)]]


class Transfer:
    def start(self, stage):
        for copy in self.copies(stage):
            copy.start()

    def finish(self, stage):
        for copy in self.copies(stage):
            copy.wait_recv()
        self.use(stage)

    def use(self, stage):
        pass

    def drain(self):
        for stage in range(self.stages):
            for copy in self.copies(stage):
                copy.wait_send()


class ChipGather(Transfer):
    stages = 1

    def __init__(self, here, slots, shard, full, sem):
        self.here, self.slots, self.shard = here, slots, shard
        self.target = full.at[here.chip, here.core, here.line]
        self.own = pltpu.make_async_copy(shard, self.target, sem)
        self.first = slots.take(here.half_count - 1)

    def copies(self, stage):
        return [
            self.slots.copy(self.first + turn, self.shard, self.target, peer)
            for turn, peer in enumerate(self.here.chip_peers())
        ]


class Gather(Transfer):
    def __init__(self, here, slots, full, pieces):
        self.here, self.slots, self.full, self.pieces = here, slots, full, pieces
        self.stages = here.seq_bits + 1
        self.each = here.seq_count
        self.first = slots.take(self.each * len(pieces))

    def copies(self, stage):
        here, full = self.here, self.full
        found = []
        for index, (rows, columns, backwards) in enumerate(self.pieces):
            slot = self.first + self.each * index
            if stage == self.stages - 1:
                part = full.at[:, here.core, :, rows, columns]
                found.append(self.slots.copy(slot, part, part, here.core_peer()))
                continue
            if backwards:
                bit = here.seq_bits - 1 - stage
                slot += 1 << stage
                parts = [
                    full.at[:, here.core, at, rows, columns]
                    for at in spread(here.line, bit, here.seq_bits)
                ]
            else:
                bit = stage
                slot += 1 + bit
                block = pl.ds(rounded_down(here.line, bit), 1 << bit)
                parts = [full.at[:, here.core, block, rows, columns]]
            for turn, part in enumerate(parts):
                found.append(self.slots.copy(slot + turn, part, part, here.line_peer(bit)))
        return found


class ChipSum(Transfer):
    stages = 1

    def __init__(self, here, slots, partial, arrived, share, offset):
        self.here, self.slots, self.partial, self.arrived = here, slots, partial, arrived
        self.share, self.offset = share, offset
        self.first = slots.take(here.half_count - 1)

    def copies(self, stage):
        return [
            self.slots.copy(
                self.first + turn,
                self.partial.at[chip],
                self.arrived.at[turn],
                {"dp": 2 * chip + self.here.core},
            )
            for turn, chip in enumerate(self.here.other_chips())
        ]

    def use(self, stage):
        total = self.partial[self.here.chip].astype(FLOAT)
        for turn in range(self.here.half_count - 1):
            total = total + self.arrived[turn].astype(FLOAT)
        self.share[:, self.offset : self.offset + total.shape[1]] = total


class Scatter(Transfer):
    def __init__(self, here, slots, grad, own, from_core, from_line, partial, pieces, load):
        self.here, self.slots, self.grad, self.own = here, slots, grad, own
        self.from_core, self.from_line, self.partial = from_core, from_line, partial
        self.pieces, self.load = pieces, load
        self.stages = here.seq_bits + 1
        self.each = here.seq_count
        self.first = slots.take(self.each * len(pieces))

    def line_stage(self, stage, backwards):
        here = self.here
        if backwards:
            bit = stage - 1
            away = spread(flipped(here.line, bit), bit, here.seq_bits)
            kept = spread(here.line, bit, here.seq_bits)
        else:
            bit = here.seq_bits - stage
            away = [rounded_down(flipped(here.line, bit), bit) + at for at in range(1 << bit)]
            kept = [rounded_down(here.line, bit) + at for at in range(1 << bit)]
        base = sum(1 << (here.seq_bits - past) for past in range(1, stage))
        return bit, away, kept, base

    def copies(self, stage):
        here = self.here
        found = []
        for index, (rows, columns, backwards) in enumerate(self.pieces):
            slot = self.first + self.each * index
            if stage == 0:
                found.append(
                    self.slots.copy(
                        slot,
                        self.grad.at[:, 1 - here.core, :, rows, columns],
                        self.from_core.at[:, :, rows, columns],
                        here.core_peer(),
                    )
                )
                continue
            bit, away, _, base = self.line_stage(stage, backwards)
            for turn, at in enumerate(away):
                found.append(
                    self.slots.copy(
                        slot + 1 + base + turn,
                        self.own.at[:, at, rows, columns],
                        self.from_line.at[base + turn, :, rows, columns],
                        here.line_peer(bit),
                    )
                )
        return found

    def use(self, stage):
        here, own = self.here, self.own
        if stage == 0:
            self.load()
        for rows, columns, backwards in self.pieces:
            if stage == 0:

                def add(at, carry, rows=rows, columns=columns):
                    one, two = lax.div(at, here.seq_count), lax.rem(at, here.seq_count)
                    own[one, two, rows, columns] = (
                        own[one, two, rows, columns] + self.from_core[one, two, rows, columns]
                    )
                    return carry

                lax.fori_loop(0, here.half_count * here.seq_count, add, 0)
                continue
            _, _, kept, base = self.line_stage(stage, backwards)
            for turn, at in enumerate(kept):
                last = stage == self.stages - 1

                def add(one, carry, rows=rows, columns=columns, at=at, place=base + turn, last=last):
                    found = own[one, at, rows, columns] + self.from_line[place, one, rows, columns]
                    if last:
                        self.partial[one, rows, columns] = found
                    else:
                        own[one, at, rows, columns] = found
                    return carry

                lax.fori_loop(0, here.half_count, add, 0)


class Exchange(Transfer):
    stages = 1

    def __init__(self, here, slots, source, target, to_rows, bounce, sem):
        self.here, self.slots, self.source, self.target = here, slots, source, target
        self.to_rows, self.bounce, self.sem = to_rows, bounce, sem
        self.first = slots.take(here.seq_count - 1)

    def ends(self, line):
        if self.to_rows:
            count = self.target.shape[0]
            block = self.source.at[pl.ds(line * count, count)]
            return block, self.target.at[:, self.here.line]
        return self.source.at[:, line], self.target.at[self.here.line]

    def copies(self, stage):
        return [
            self.slots.copy(self.first + turn, *self.ends(line), {"seq": line})
            for turn, line in enumerate(self.here.other_lines())
        ]

    def own_in(self):
        return pltpu.make_async_copy(self.ends(self.here.line)[0], self.bounce, self.sem.at[0])

    def own_out(self):
        source, target = self.ends(self.here.line)
        source = source if self.bounce is None else self.bounce
        return pltpu.make_async_copy(source, target, self.sem.at[1])

    def start(self, stage):
        if self.bounce is not None:
            self.own_in().start()
        super().start(stage)
        if self.bounce is not None:
            self.own_in().wait()
        self.own_out().start()

    def use(self, stage):
        self.own_out().wait()


def flow_of(transfers):
    def begin():
        for transfer in transfers:
            transfer.start(0)

    def follow(transfer, stage):
        transfer.finish(stage - 1)
        if stage < transfer.stages:
            transfer.start(stage)

    calls = [begin]
    for stage in range(1, max(transfer.stages for transfer in transfers) + 1):
        for transfer in transfers:
            if stage <= transfer.stages:
                calls.append(functools.partial(follow, transfer, stage))
    return calls


def drain_all(transfers):
    for transfer in transfers:
        transfer.drain()


def chip_gathers_of(here, slots, shards, fulls, sem):
    return [
        ChipGather(here, slots, shard, full, sem.at[index])
        for index, (shard, full) in enumerate(zip(shards, fulls))
    ]


def gathers_of(here, slots, fulls, splits):
    return [
        Gather(here, slots, full, pieces)
        for full, split in zip(fulls, splits)
        for pieces in parts_of(full.shape[-2:], split)
    ]


def piece_count(shapes, splits):
    return sum(len(part) for shape, split in zip(shapes, splits) for part in parts_of(shape, split))


def full_shape(shard, dp_count, seq_count):
    return jax.ShapeDtypeStruct((dp_count // 2, 2, seq_count) + shard.shape, shard.dtype)


def gather_kernel(counts, first, count, *refs):
    tokens, vectors, up_bias, weights = refs[0], refs[1], refs[2], refs[3 : 2 + count]
    token_rows, fulls = refs[2 + count], refs[3 + count : 3 + 2 * count]
    rest = refs[3 + 2 * count :]
    shards, small, bounce, send_sem, recv_sem, own_sem, move_sem = rest[:count], *rest[count:]
    small[...] = jnp.zeros_like(small)
    small[0:8, : vectors.shape[1]] = vectors[...]
    small[8:9, : up_bias.shape[1]] = up_bias[...]
    shards[0][...] = small[...].astype(BRAIN)
    for shard, weight in zip(shards[1:], weights):
        shard[...] = weight[...].astype(BRAIN)
    here = Here(*counts)
    slots = Slots(send_sem, recv_sem)
    chips = chip_gathers_of(here, slots, shards, fulls, own_sem)
    move = Exchange(here, slots, tokens, token_rows, True, bounce, move_sem)
    gathers = gathers_of(here, slots, fulls[:first], [False] + [True] * (first - 1))
    flow = flow_of(gathers)
    greet(here.near_peers())
    for chip in chips[:first]:
        chip.start(0)
    move.start(0)
    for chip in chips[first:]:
        chip.start(0)
    for chip in chips:
        chip.own.start()
    for chip in chips[:first]:
        chip.own.wait()
        chip.finish(0)
    for call in flow:
        call()
    move.finish(0)
    for chip in chips[first:]:
        chip.own.wait()
        chip.finish(0)
    drain_all(chips + gathers + [move])


def gather_first(tokens, vectors, up_bias, weights, first, counts):
    dp_count, seq_count = counts
    row_count, pos_count, width = tokens.shape
    rows = row_count // seq_count
    shards = [jax.ShapeDtypeStruct(shape, BRAIN) for shape in [(16, 128)] + [w.shape for w in weights]]
    pieces = piece_count([shard.shape for shard in shards[:first]], [False] + [True] * (first - 1))
    slots = len(shards) * (dp_count // 2 - 1) + pieces * seq_count + seq_count - 1
    return pl.pallas_call(
        functools.partial(gather_kernel, counts, first, len(shards)),
        out_shape=[jax.ShapeDtypeStruct((rows, seq_count, pos_count, width), tokens.dtype)]
        + [full_shape(shard, *counts) for shard in shards],
        in_specs=[ANYWHERE] + [WHOLE] * (2 + len(weights)),
        out_specs=[ANYWHERE] * (1 + len(shards)),
        scratch_shapes=[pltpu.VMEM(shard.shape, BRAIN) for shard in shards]
        + [
            pltpu.VMEM((16, 128), FLOAT),
            pltpu.VMEM((rows, pos_count, width), tokens.dtype),
            pltpu.SemaphoreType.DMA((slots,)),
            pltpu.SemaphoreType.DMA((slots,)),
            pltpu.SemaphoreType.DMA((len(shards),)),
            pltpu.SemaphoreType.DMA((2,)),
        ],
        name="gather_first",
        compiler_params=pltpu.CompilerParams(
            collective_id=0, has_side_effects=True, vmem_limit_bytes=63 * 1024 * 1024
        ),
    )(tokens, vectors, up_bias, *weights)


HIDDEN_BLOCK = 512
GELU_SCALE = 0.7978845608028654
GELU_CUBE = 0.044715


def gelu_both(values):
    square = values * values
    turned = jnp.tanh(GELU_SCALE * values * (1.0 + GELU_CUBE * square))
    half = 0.5 + 0.5 * turned
    inner = GELU_SCALE * (1.0 + 3.0 * GELU_CUBE * square)
    return values * half, half + 0.5 * values * (1.0 - turned * turned) * inner


def forward_start(context, tokens, w_out, vectors, resid, low_two, low_turned):
    for rows in row_blocks(resid.shape[0]):
        values = tokens[rows, :].astype(FLOAT) + (matmul(context[rows, :], w_out[...]) + vectors[6:7, :])
        resid[rows, :] = values
        normed, _ = norm_parts(values)
        low = (normed * vectors[2:3, :] + vectors[3:4, :]).astype(BRAIN)
        low_two[rows, :] = low
        low_turned[:, rows] = low.T


def backward_end(
    context, w_out, vectors, resid, total, back, gc_ref, gr_ref, gwo_ref, sum_ref, low_turned
):
    width = resid.shape[1]
    sums = [jnp.zeros((1, width), FLOAT) for _ in range(4)]
    for rows in row_blocks(resid.shape[0]):
        normed, inverse = norm_parts(resid[rows, :])
        upstream = total[rows, :]
        given = back(rows).astype(FLOAT)
        scaled = upstream * vectors[2:3, :]
        centered = scaled - jnp.mean(scaled, axis=-1, keepdims=True)
        inward = centered - normed * jnp.mean(scaled * normed, axis=-1, keepdims=True)
        grad = given + inverse * inward
        low = grad.astype(BRAIN)
        gr_ref[rows, :] = grad
        gc_ref[rows, :] = times_transposed(low, w_out[...]).astype(BRAIN)
        low_turned[:, rows] = context[rows, :].T
        total[rows, :] = low.astype(FLOAT)
        for index, values in enumerate((upstream * normed, upstream, low.astype(FLOAT), given)):
            sums[index] = sums[index] + jnp.sum(values, axis=0, keepdims=True)
    for index in range(4):
        sum_ref[index : index + 1, :] = sums[index]
    sum_ref[4:8, :] = jnp.zeros((4, width), FLOAT)
    gwo_ref[...] = matmul(low_turned[...], total[...].astype(BRAIN)).astype(BRAIN)


def mlp_kernel(counts, *refs):
    context, tokens, w_out, w_up, w_down, vectors, up_shift, cotangent = refs[0:8]
    gup_ref, gdown_ref, gub_ref, gwo_ref, gc_ref, gr_ref, sum_ref, mixed = refs[8:16]
    acts, slopes, low_two, low_turned, resid, total, hidden, back, mixed_rows = refs[16:25]
    send_sem, recv_sem, move_sem = refs[25:28]
    here = Here(*counts)
    slots = Slots(send_sem, recv_sem)
    arrive = Exchange(here, slots, cotangent, back, True, None, move_sem.at[pl.ds(0, 2)])
    leave = Exchange(here, slots, mixed_rows, mixed, False, None, move_sem.at[pl.ds(2, 2)])
    step = pl.program_id(0)
    half = pl.num_programs(0) // 2
    count = resid.shape[0]
    pos_count = back.shape[2]

    def back_rows(rows):
        parts = []
        for first in range(rows.start, rows.stop, pos_count):
            size = min(pos_count, rows.stop - first)
            row, rest = divmod(first, pos_count * counts[1])
            line, offset = divmod(rest, pos_count)
            parts.append(back[row, line, offset : offset + size, :])
        return parts[0] if len(parts) == 1 else jnp.concatenate(parts, axis=0)

    @pl.when(step == 0)
    def _():
        greet(here.near_peers())
        arrive.start(0)
        forward_start(context, tokens, w_out, vectors, resid, low_two, low_turned)
        total[...] = jnp.zeros_like(total)

    @pl.when(step < half)
    def _():
        for rows in row_blocks(count):
            values = matmul(low_two[rows, :], w_up[...]) + up_shift[...]
            act, slope = gelu_both(values)
            low = act.astype(BRAIN)
            acts[step, rows, :] = low
            slopes[step, rows, :] = slope
            total[rows, :] += matmul(low, w_down[...])

    @pl.when(step == half)
    def _():
        for first in range(0, count, pos_count):
            row, line = divmod(first // pos_count, counts[1])
            rows = slice(first, first + pos_count)
            values = resid[rows, :] + (total[rows, :] + vectors[7:8, :])
            mixed_rows[row, line] = values.astype(BRAIN)
        total[...] = jnp.zeros_like(total)
        leave.start(0)
        arrive.finish(0)

    @pl.when(step >= half)
    def _():
        at = step - half
        sums = jnp.zeros((1, hidden.shape[1]), FLOAT)
        for rows in row_blocks(count):
            grad = times_transposed(back_rows(rows), w_down[...]) * slopes[at, rows, :]
            low = grad.astype(BRAIN)
            hidden[rows, :] = low
            sums = sums + jnp.sum(low.astype(FLOAT), axis=0, keepdims=True)
            total[rows, :] += times_transposed(low, w_up[...])
        gub_ref[...] = sums
        gup_ref[...] = matmul(low_turned[...], hidden[...]).astype(BRAIN)
        every = back_rows(slice(0, count))
        gdown_ref[...] = inner_rows(acts[at], every).astype(BRAIN)

    @pl.when(step == 2 * half - 1)
    def _():
        backward_end(
            context, w_out, vectors, resid, total, back_rows, gc_ref, gr_ref, gwo_ref, sum_ref, low_turned
        )
        leave.finish(0)
        drain_all([arrive, leave])


def feed_forward(context, tokens, w_out, w_up, w_down, vectors, up_shift, cotangent, counts):
    count, width = context.shape
    hidden = w_up.shape[1]
    half = hidden // HIDDEN_BLOCK
    seq_count = counts[1]
    row_count, pos_count, _ = cotangent.shape
    rows = row_count // seq_count
    later = lambda j: jnp.maximum(j - half, 0)
    around = lambda j: lax.rem(j, half)
    block = HIDDEN_BLOCK
    slots = 2 * (seq_count - 1)
    return pl.pallas_call(
        functools.partial(mlp_kernel, counts),
        grid=(2 * half,),
        in_specs=[
            once((count, width)),
            once((count, width)),
            once((width, width)),
            pl.BlockSpec((width, block), lambda j: (0, around(j))),
            pl.BlockSpec((block, width), lambda j: (around(j), 0)),
            once((8, width)),
            pl.BlockSpec((1, block), lambda j: (0, around(j))),
            ANYWHERE,
        ],
        out_specs=[
            pl.BlockSpec((width, block), lambda j: (0, later(j))),
            pl.BlockSpec((block, width), lambda j: (later(j), 0)),
            pl.BlockSpec((1, block), lambda j: (0, later(j))),
            once((width, width)),
            once((count, width)),
            once((count, width)),
            once((8, width)),
            ANYWHERE,
        ],
        out_shape=[
            jax.ShapeDtypeStruct((width, hidden), BRAIN),
            jax.ShapeDtypeStruct((hidden, width), BRAIN),
            jax.ShapeDtypeStruct((1, hidden), FLOAT),
            jax.ShapeDtypeStruct((width, width), BRAIN),
            jax.ShapeDtypeStruct((count, width), BRAIN),
            jax.ShapeDtypeStruct((count, width), FLOAT),
            jax.ShapeDtypeStruct((8, width), FLOAT),
            jax.ShapeDtypeStruct((seq_count, rows, pos_count, width), BRAIN),
        ],
        scratch_shapes=[
            pltpu.VMEM((half, count, block), BRAIN),
            pltpu.VMEM((half, count, block), FLOAT),
            pltpu.VMEM((count, width), BRAIN),
            pltpu.VMEM((width, count), BRAIN),
            pltpu.VMEM((count, width), FLOAT),
            pltpu.VMEM((count, width), FLOAT),
            pltpu.VMEM((count, block), BRAIN),
            pltpu.VMEM((rows, seq_count, pos_count, width), BRAIN),
            pltpu.VMEM((rows, seq_count, pos_count, width), BRAIN),
            pltpu.SemaphoreType.DMA((slots,)),
            pltpu.SemaphoreType.DMA((slots,)),
            pltpu.SemaphoreType.DMA((4,)),
        ],
        name="feed_forward",
        compiler_params=pltpu.CompilerParams(
            collective_id=4, has_side_effects=True, vmem_limit_bytes=63 * 1024 * 1024
        ),
    )(context, tokens, w_out, w_up, w_down, vectors, up_shift, cotangent)


def lamb_pieces(weight, first, second, grad, decay):
    first_new = BETA_ONE * first + (1.0 - BETA_ONE) * grad
    second_new = BETA_TWO * second + (1.0 - BETA_TWO) * grad * grad
    spread_out = jnp.sqrt(second_new / CORR_TWO) + ADAM_EPS
    update = first_new / CORR_ONE / spread_out + decay * weight
    return (first_new, second_new, update)


def square_sum(values):
    return jnp.sum(jnp.sum(values * values, axis=1, keepdims=True), axis=0, keepdims=True)


def picked(small, rank, vector_size, bias_size):
    width = small.shape[1]
    row = lax.broadcasted_iota(jnp.int32, (width, 128), 0)
    lane = lax.broadcasted_iota(jnp.int32, (width, 128), 1)
    dot = functools.partial(jnp.dot, precision=lax.Precision.HIGHEST, preferred_element_type=FLOAT)
    chosen = (row == lane + rank * vector_size) & (lane < vector_size)
    vector_grad = dot(small[0:8, :], jnp.where(chosen, 1.0, 0.0))[:, :vector_size]
    start = rank * bias_size
    chosen = (row == lane + lax.rem(start, width)) & (lane < bias_size)
    tail = dot(small[8:16, :], jnp.where(chosen, 1.0, 0.0))
    tail_row = lax.broadcasted_iota(jnp.int32, tail.shape, 0)
    tail = jnp.sum(jnp.where(tail_row == lax.div(start, width), tail, 0.0), axis=0, keepdims=True)
    return vector_grad, tail[:, :bias_size]


def scatters_of(here, slots, grads, buffers, partials, own_sem, splits):
    count = len(grads)
    found, loads = [], []
    for index, (grad, partial) in enumerate(zip(grads, partials)):
        own, *arrivals = buffers[index::count]
        load = lambda grad=grad, own=own, index=index: pltpu.make_async_copy(
            grad.at[:, here.core], own, own_sem.at[index]
        )
        loads.append(load)
        for order, pieces in enumerate(parts_of(grad.shape[-2:], splits[index])):
            wait = (lambda load=load: load().wait()) if order == 0 else (lambda: None)
            found.append(Scatter(here, slots, grad, own, *arrivals, partial, pieces, wait))
    return found, loads


def scatter_buffers(shapes, counts):
    half_count, seq_count = counts[0] // 2, counts[1]
    leads = [(half_count, seq_count)] * 2 + [(seq_count - 1, half_count)]
    return [pltpu.VMEM(lead + shape, BRAIN) for lead in leads for shape in shapes]


def scatter_views(grads, shapes, counts):
    lead = (counts[0] // 2, 2, counts[1])
    return [grad.reshape(lead + shape) for grad, shape in zip(grads, shapes)]


class SmallSum(Transfer):
    def __init__(self, here, small, sums, arrived, send_sem, recv_sem):
        self.slots = Slots(send_sem, recv_sem)
        self.small, self.sums, self.arrived = small, sums, arrived
        self.peers = [here.core_peer()]
        self.peers += [{"dp": flipped(here.place, bit + 1)} for bit in range(bits_of(here.half_count))]
        self.peers += [here.line_peer(bit) for bit in range(here.seq_bits)]
        self.stages = len(self.peers)

    def copies(self, stage):
        source = self.sums.at[stage - 1] if stage else self.small
        return [self.slots.copy(stage, source, self.arrived.at[stage], self.peers[stage])]

    def use(self, stage):
        before = self.sums[stage - 1] if stage else self.small[...]
        self.sums[stage] = before + self.arrived[stage]


def scatter_kernel(counts, *refs):
    grads, small, input_rows, partials, ready = refs[0:3], refs[3], refs[4], refs[5:7], refs[7]
    weights, firsts, seconds = refs[8:14], refs[14:20], refs[20:26]
    shares, norm_out, input_grad = refs[26:32], refs[32], refs[33]
    buffers, mine, arrived, bounce = refs[34:43], refs[43:46], refs[46:51], refs[51]
    small_sum, small_in, norm_mine, norm_dp, norm_line, norm_seq = refs[52:58]
    send_sem, recv_sem, own_sem, move_sem, small_send, small_recv, norm_send, norm_recv = refs[58:66]
    here = Here(*counts)
    slots = Slots(send_sem, recv_sem)
    scatters, loads = scatters_of(here, slots, grads, buffers, mine, own_sem, [False] * 3)
    early = [
        ChipSum(here, slots, partial, arrived[index], shares[index + 1], 0)
        for index, partial in enumerate(partials)
    ]
    late = [
        ChipSum(here, slots, mine[at], arrived[2 + at], shares[0], at * grads[at].shape[-1])
        for at in range(3)
    ]
    move = Exchange(here, slots, input_rows, input_grad, False, bounce, move_sem)
    total = SmallSum(here, small, small_sum, small_in, small_send, small_recv)
    for load in loads:
        load().start()
    dp_peers, seq_peers = here.all_peers()[: here.dp_count - 1], here.all_peers()[here.dp_count - 1 :]
    greet(dp_peers + seq_peers)
    lane = lax.broadcasted_iota(jnp.int32, (8, 128), 1)
    row = lax.broadcasted_iota(jnp.int32, (8, 128), 0)

    def with_norms(tile, index, grad):
        decay = DECAY_RATE if index < 4 else 0.0
        weight = weights[index][...]
        update = lamb_pieces(weight, firsts[index][...], seconds[index][...], grad, decay)[2]
        at = row == min(index, 4)
        tile = jnp.where(at & (lane == 0), square_sum(weight), tile)
        return jnp.where(at & (lane == 1), square_sum(update), tile)

    for chip in early:
        chip.start(0)
    total.start(0)
    tile = jnp.zeros((8, 128), FLOAT)
    for stage in range(scatters[0].stages + 1):
        for index, scatter in enumerate(scatters):
            if stage:
                scatter.finish(stage - 1)
            if stage < scatter.stages:
                scatter.start(stage)
            else:
                late[index].start(0)
        if stage == 0:
            shares[3][...] = ready[...]
            tile = with_norms(tile, 3, ready[...])
        if stage == scatters[0].stages - 1:
            move.start(0)
        if stage < total.stages:
            total.finish(stage)
            if stage + 1 < total.stages:
                total.start(stage + 1)
    for stage in range(scatters[0].stages + 1, total.stages):
        total.finish(stage)
        if stage + 1 < total.stages:
            total.start(stage + 1)
    for index, chip in enumerate(early):
        chip.finish(0)
        tile = with_norms(tile, index + 1, shares[index + 1][...])

    rank = here.place * here.seq_count + here.line
    vector_grad, bias_grad = picked(
        small_sum[total.stages - 1], rank, shares[4].shape[1], shares[5].shape[1]
    )
    shares[4][...] = vector_grad
    shares[5][...] = bias_grad
    tile = with_norms(tile, 5, bias_grad)
    for chip in late:
        chip.finish(0)
    norm_mine[0:8, :] = with_norms(tile, 0, shares[0][...])
    weight = weights[4][...]
    update = lamb_pieces(weight, firsts[4][...], seconds[4][...], vector_grad, 0.0)[2]
    weight_sq = jnp.sum(weight * weight, axis=1, keepdims=True)
    update_sq = jnp.sum(update * update, axis=1, keepdims=True)
    norm_mine[8:16, :] = jnp.where(lane == 0, weight_sq, jnp.where(lane == 1, update_sq, 0.0))

    norm_slots = Slots(norm_send, norm_recv)

    def exchange(source, held, peers, at):
        base = norm_slots.take(len(peers))
        copies = [
            norm_slots.copy(base + turn, source, held.at[at], peer) for turn, peer in enumerate(peers)
        ]
        for copy in copies:
            copy.start()
        held[at] = source[...]
        for copy in copies:
            copy.wait_recv()
        found = held[0]
        for turn in range(1, held.shape[0]):
            found = found + held[turn]
        return copies, found

    sent, found = exchange(norm_mine, norm_dp, dp_peers, here.place)
    norm_line[...] = found
    also, found = exchange(norm_line, norm_seq, seq_peers, here.line)
    norm_out[...] = found
    move.finish(0)
    for copy in sent + also:
        copy.wait_send()
    drain_all(scatters + early + late + [total, move])


def scatter_last(grads, small, input_rows, partials, ready, weights, firsts, seconds, counts):
    dp_count, seq_count = counts
    shapes = [weight.shape for weight in weights]
    thirds = [(shapes[0][0], grad.shape[1]) for grad in grads]
    lead = (dp_count // 2,)
    pieces = piece_count(thirds, [False] * 3)
    slots = pieces * seq_count + 5 * (dp_count // 2 - 1) + seq_count - 1
    stages = bits_of(dp_count) + bits_of(seq_count)
    return pl.pallas_call(
        functools.partial(scatter_kernel, counts),
        out_shape=[jax.ShapeDtypeStruct(shape, FLOAT) for shape in shapes]
        + [
            jax.ShapeDtypeStruct((16, 128), FLOAT),
            jax.ShapeDtypeStruct((seq_count,) + input_rows.shape[0:1] + input_rows.shape[2:], BRAIN),
        ],
        in_specs=[ANYWHERE] * 3 + [WHOLE, ANYWHERE] + [WHOLE] * 21,
        out_specs=[WHOLE] * 7 + [ANYWHERE],
        scratch_shapes=scatter_buffers(thirds, counts)
        + [pltpu.VMEM(lead + shape, BRAIN) for shape in thirds]
        + [pltpu.VMEM((lead[0] - 1,) + shape, BRAIN) for shape in shapes[1:3] + thirds]
        + [
            pltpu.VMEM(input_rows.shape[0:1] + input_rows.shape[2:], BRAIN),
            pltpu.VMEM((stages,) + small.shape, FLOAT),
            pltpu.VMEM((stages,) + small.shape, FLOAT),
            pltpu.VMEM((16, 128), FLOAT),
            pltpu.VMEM((dp_count, 16, 128), FLOAT),
            pltpu.VMEM((16, 128), FLOAT),
            pltpu.VMEM((seq_count, 16, 128), FLOAT),
            pltpu.SemaphoreType.DMA((slots,)),
            pltpu.SemaphoreType.DMA((slots,)),
            pltpu.SemaphoreType.DMA((3,)),
            pltpu.SemaphoreType.DMA((2,)),
            pltpu.SemaphoreType.DMA((stages,)),
            pltpu.SemaphoreType.DMA((stages,)),
            pltpu.SemaphoreType.DMA((dp_count + seq_count,)),
            pltpu.SemaphoreType.DMA((dp_count + seq_count,)),
        ],
        name="scatter_last",
        compiler_params=pltpu.CompilerParams(
            collective_id=3, has_side_effects=True, vmem_limit_bytes=60 * 1024 * 1024
        ),
    )(
        *scatter_views(grads, thirds, counts),
        small,
        input_rows,
        *partials,
        ready,
        *weights,
        *firsts,
        *seconds,
    )


def lamb_kernel(*refs):
    grads, norms = refs[0:6], refs[6]
    weights, firsts, seconds = refs[7:13], refs[13:19], refs[19:25]
    grad_out, first_out, second_out, new_out = refs[25:31], refs[31:37], refs[37:43], refs[43:49]
    copy_out = refs[49:53]
    weight_norm = jnp.sqrt(norms[:, 0:1])
    scales = weight_norm / (jnp.sqrt(norms[:, 1:2]) + ADAM_EPS)
    for index in range(6):
        grad = grads[index][...]
        weight = weights[index][...]
        decay = DECAY_RATE if index < 4 else 0.0
        first_new, second_new, update = lamb_pieces(
            weight, firsts[index][...], seconds[index][...], grad, decay
        )
        scale = scales[8:16] if index == 4 else scales[min(index, 4) : min(index, 4) + 1]
        new = weight - LEARN_RATE * scale * update
        grad_out[index][...] = grad
        first_out[index][...] = first_new
        second_out[index][...] = second_new
        new_out[index][...] = new
        if index < 4:
            copy_out[index][...] = new.astype(BRAIN)


def lamb_all(grads, norms, weights, firsts, seconds):
    vmem = pl.BlockSpec(memory_space=pltpu.VMEM)
    shapes = [jax.ShapeDtypeStruct(weight.shape, FLOAT) for weight in weights]
    copies = [jax.ShapeDtypeStruct(weight.shape, BRAIN) for weight in weights[:4]]
    return pl.pallas_call(
        lamb_kernel,
        out_shape=shapes * 4 + copies,
        in_specs=[vmem] * 25,
        out_specs=[vmem] * 28,
        name="lamb_update",
        compiler_params=pltpu.CompilerParams(vmem_limit_bytes=63 * 1024 * 1024),
    )(*grads, norms, *weights, *firsts, *seconds)


def body(
    tokens,
    cotangent,
    segment_ids,
    w_qkv,
    m_qkv,
    v_qkv,
    w_out,
    m_out,
    v_out,
    w_up,
    m_up,
    v_up,
    w_down,
    m_down,
    v_down,
    vectors,
    m_vectors,
    v_vectors,
    up_bias,
    m_up_bias,
    v_up_bias,
):
    dp_count, seq_count = lax.axis_size("dp"), lax.axis_size("seq")
    vector_size, bias_size = vectors.shape[1], up_bias.shape[0]
    counts = (dp_count, seq_count)
    token_rows, *fulls = gather_first(
        tokens, vectors, up_bias[None], [w_qkv, w_out, w_up, w_down], 2, counts
    )
    small = fulls[0].reshape(dp_count * seq_count, 16, 128)
    full_vectors = small[:, :8, :vector_size].transpose(1, 0, 2)
    vector_rows = full_vectors.reshape(8, -1).astype(FLOAT)
    up_shift = small[:, 8, :bias_size].reshape(-1).astype(FLOAT)
    as_matrix = lambda full: full.reshape(-1, full.shape[-1])
    full_qkv = as_matrix(fulls[1])

    width = tokens.shape[2]
    length = segment_ids.shape[1]
    rows = token_rows.shape[0]
    assert rows == 1
    token_rows = token_rows.reshape(length, width)
    *heads, context, lse_rows, full_out, full_up, full_down = attention_forward(
        segment_ids, token_rows, vector_rows, full_qkv, fulls[2:], counts
    )
    full_out, full_up, full_down = [as_matrix(full) for full in (full_out, full_up, full_down)]
    grad_up, grad_down, grad_up_bias, grad_out, context_grad, resid_grad, sums, mixed = feed_forward(
        context,
        token_rows,
        full_out,
        full_up,
        full_down,
        vector_rows,
        up_shift[None],
        cotangent,
        counts,
    )
    *qkv_grads, shift_sums, norm_sums, input_rows, share_down, sum_up, sum_out = attention_backward(
        segment_ids,
        heads,
        context_grad,
        lse_rows,
        token_rows,
        vector_rows,
        resid_grad,
        full_qkv,
        [grad_down, grad_up, grad_out],
        [w_down.shape, w_up.shape, w_out.shape],
        counts,
    )
    grad_vectors = jnp.concatenate([norm_sums[:2], sums[:2], shift_sums[:2], sums[2:4]])
    small_grad = jnp.concatenate([grad_vectors, grad_up_bias.reshape(-1, width)])
    small_grad = jnp.pad(small_grad, ((0, 16 - small_grad.shape[0]), (0, 0)))
    as_row = lambda value: value.reshape(1, -1)
    weights = (w_qkv, w_out, w_up, w_down, vectors, as_row(up_bias))
    firsts = (m_qkv, m_out, m_up, m_down, m_vectors, as_row(m_up_bias))
    seconds = (v_qkv, v_out, v_up, v_down, v_vectors, as_row(v_up_bias))
    *shares, norms, input_grad = scatter_last(
        qkv_grads,
        small_grad,
        input_rows.reshape(rows, seq_count, length // seq_count, width),
        [sum_out, sum_up],
        share_down,
        weights,
        firsts,
        seconds,
        counts,
    )
    results = list(lamb_all(shares, norms, weights, firsts, seconds))
    mixed = mixed.reshape(tokens.shape)
    input_grad = input_grad.reshape(tokens.shape).astype(FLOAT)
    for index in (5, 11, 17, 23):
        results[index] = results[index].reshape(-1)
    return (mixed, input_grad, *results)


def solution(mesh):
    matrix = P(("dp", "seq"), None)
    rows = P("dp", "seq", None)
    vector = P(None, ("dp", "seq"))
    bias = P(("dp", "seq"))
    six = (matrix, matrix, matrix, matrix, vector, bias)
    in_specs = (rows, rows, P("dp", None)) + tuple(spec for spec in six for _ in range(3))
    out_specs = (rows, rows) + six * 4 + (matrix,) * 4
    return jax.shard_map(body, mesh=mesh, in_specs=in_specs, out_specs=out_specs, check_vma=False)
```

```python
import functools

import jax
import jax.numpy as jnp
from jax import lax
from jax.experimental import pallas as pl
from jax.experimental.pallas import tpu as pltpu
from jax.sharding import PartitionSpec as P

HEADS = 12
HEAD_DIM = 64
LONGEST = 512
QUERY_BLOCK = 256
ROW_BLOCK = 256


BETA_ONE = 0.9
BETA_TWO = 0.999
ADAM_EPS = 1e-06
DECAY_RATE = 0.01
LEARN_RATE = 0.4
NORM_EPS = 1e-05
STEP_NUMBER = 10.0
CORR_ONE = 1.0 - BETA_ONE**STEP_NUMBER
CORR_TWO = 1.0 - BETA_TWO**STEP_NUMBER

BRAIN = jnp.bfloat16
FLOAT = jnp.float32


def matmul(left_side, right_side):
    return jnp.dot(left_side, right_side, preferred_element_type=FLOAT)


def inner_rows(left_side, right_side):
    return lax.dot_general(
        left_side, right_side, (((0,), (0,)), ((), ())), preferred_element_type=FLOAT
    )


def times_transposed(left_side, right_side):
    return lax.dot_general(
        left_side, right_side, (((1,), (1,)), ((), ())), preferred_element_type=FLOAT
    )


def norm_parts(values):
    center = values - jnp.mean(values, axis=-1, keepdims=True)
    inverse = lax.rsqrt(jnp.mean(center * center, axis=-1, keepdims=True) + NORM_EPS)
    return center * inverse, inverse


def row_blocks(count):
    return [slice(first, first + ROW_BLOCK) for first in range(0, count, ROW_BLOCK)]


def windows(length):
    return [
        (max(0, first - LONGEST), first + QUERY_BLOCK) for first in range(0, length, QUERY_BLOCK)
    ]


def fill_bias(segments, bias, length):
    own = segments[pl.ds(lax.axis_index("seq"), 1), :].astype(FLOAT)
    turned = jnp.broadcast_to(own, (8, length)).T
    place = 0
    for index, (low, high) in enumerate(windows(length)):
        first = index * QUERY_BLOCK
        size = high - low
        keys = turned[low:high, 0:1]
        queries = own[:, first : first + QUERY_BLOCK]
        key_place = low + lax.broadcasted_iota(jnp.int32, (size, QUERY_BLOCK), 0)
        query_place = first + lax.broadcasted_iota(jnp.int32, (size, QUERY_BLOCK), 1)
        allowed = (keys == queries) & (key_place <= query_place)
        bias[place : place + size, :] = jnp.where(allowed, 0.0, -1000000000.0)
        place += size


def split_heads(pair):
    lane = lax.broadcasted_iota(jnp.int32, pair.shape, 1)
    zero = jnp.zeros_like(pair)
    return (jnp.where(lane < HEAD_DIM, pair, zero), jnp.where(lane < HEAD_DIM, zero, pair))


def attend_forward(counts, splits, *refs):
    segments, tokens, norms, shifts, wq_ref, wk_ref, wv_ref = refs[0:7]
    q_ref, k_ref, v_ref, c_ref, lse_ref = refs[10:15]
    fulls, bias, low_one, send_sem, recv_sem = refs[15:18], *refs[18:]
    length = q_ref.shape[0]
    here = Here(*counts)
    slots = Slots(send_sem, recv_sem)
    gathers = gathers_of(here, slots, fulls, splits)

    def begin():
        greet(here.near_peers())
        begin_all(gathers)

    timed, late = [(0, begin)], []
    weight = (1 << here.seq_bits) - 1
    for stage in range(1, here.seq_bits + 1):
        low, high = (1 << stage - 1) - 1, (1 << stage) - 1
        timed += evenly(follows(gathers, stage), 22 * low / weight + 2 + stage, 22 * high / weight + 1.5)
    late += follows(gathers, here.seq_bits + 1)
    blocks = windows(length)
    beside = Beside(timed, late, HEADS // 2 * len(blocks))

    @pl.when(pl.program_id(0) == 0)
    def _():
        beside.point(0, len(blocks), first=True)
        fill_bias(segments, bias, length)
        for rows in row_blocks(length):
            normed, _ = norm_parts(tokens[rows, :].astype(FLOAT))
            low_one[rows, :] = (normed * norms[0:1, :] + norms[1:2, :]).astype(BRAIN)

    lanes = 2 * HEAD_DIM
    joined = jnp.concatenate([wq_ref[...], wk_ref[...], wv_ref[...]], axis=1)
    for rows in row_blocks(length):
        projected = matmul(low_one[rows, :], joined)
        q_ref[rows, :] = (projected[:, :lanes] + shifts[4:5, :]).astype(BRAIN)
        k_ref[rows, :] = projected[:, lanes : 2 * lanes].astype(BRAIN)
        v_ref[rows, :] = (projected[:, 2 * lanes :] + shifts[5:6, :]).astype(BRAIN)
    v_turned = v_ref[...].T
    place = 0
    for index, (low, high) in enumerate(blocks):
        beside.point(index, len(blocks), first=False)
        first = index * QUERY_BLOCK
        size = high - low
        queries = split_heads(q_ref[first : first + QUERY_BLOCK, :] * HEAD_DIM ** (-0.5))
        keys = k_ref[low:high, :]
        blocked = bias[place : place + size, :]
        parts = []
        for head in range(2):
            scores = times_transposed(keys, queries[head]) + blocked
            peak = jnp.max(scores, axis=0, keepdims=True)
            probs = jnp.exp(scores - peak)
            total = jnp.sum(probs, axis=0, keepdims=True)
            probs = (probs * (1.0 / total)).astype(BRAIN)
            lse_ref[0, head : head + 1, first : first + QUERY_BLOCK] = peak + jnp.log(total)
            turned = v_turned[head * HEAD_DIM : (head + 1) * HEAD_DIM, low:high]
            parts.append(matmul(turned, probs))
        context = jnp.concatenate(parts, axis=0).T
        c_ref[first : first + QUERY_BLOCK, :] = context.astype(BRAIN)
        place += size

    @pl.when(pl.program_id(0) == HEADS // 2 - 1)
    def _():
        beside.rest()
        drain_all(gathers)


class Beside:
    def __init__(self, timed, late, points):
        self.at, self.late = {}, late
        for time, call in timed:
            self.at.setdefault(int(time * points / 24), []).append(call)

    def point(self, index, per_step, first):
        for point, calls in self.at.items():
            if point % per_step == index and first == (point == 0):

                @pl.when(pl.program_id(0) == point // per_step)
                def _(calls=calls):
                    for call in calls:
                        call()

    def rest(self):
        for call in self.late:
            call()


def attend_backward(counts, splits, *refs):
    refs = (None, *refs)
    segments, q_ref, k_ref, v_ref, g_ref, lse_ref = refs[1:7]
    tokens, norms, resid_grad, wq_ref, wk_ref, wv_ref = refs[7:13]
    grads, gq_ref, gk_ref, gv_ref, shift_ref, sum_ref, input_ref = refs[13:16], *refs[16:22]
    share, partials, bias, key_sum, value_sum = refs[22], refs[23:25], *refs[25:28]
    low_turned, total, joined, buffers = *refs[28:31], refs[31:40]
    first_partial, arrived, send_sem, recv_sem, own_sem = refs[40:]
    partials = (first_partial, *partials)
    length = q_ref.shape[0]
    pair = pl.program_id(0)
    here = Here(*counts)
    slots = Slots(send_sem, recv_sem)
    scatters, loads = scatters_of(here, slots, grads, buffers, partials, own_sem, splits)

    def begin():
        for load in loads:
            load().start()
        greet(here.near_peers())
        begin_all(scatters)

    last = ChipSum(here, slots, first_partial, arrived, share, 0)
    early = len(parts_of(share.shape, splits[0]))
    ahead, behind = scatters[:early], scatters[early:]
    stages = scatters[0].stages
    calls = []
    for stage in range(1, stages + 2):
        if stage <= stages:
            calls += follows(ahead, stage)
        if stage == stages:
            calls.append(lambda: last.start(0))
        if stage > 1:
            calls += follows(behind, stage - 1)
    timed = evenly(calls, 1, 21)
    if len(calls) == 16:
        times = (1, 2, 4, 7, 6, 8, 9, 10, 12, 12, 13, 15, 16, 18, 20, 21)
        timed = list(zip(times, calls))
    blocks = windows(length)
    beside = Beside([(0, begin)] + timed, [lambda: last.finish(0)], HEADS // 2 * len(blocks))

    @pl.when(pair == 0)
    def _():
        beside.point(0, len(blocks), first=True)
        fill_bias(segments, bias, length)
        for rows in row_blocks(length):
            normed, _ = norm_parts(tokens[rows, :].astype(FLOAT))
            low_turned[:, rows] = (normed * norms[0:1, :] + norms[1:2, :]).astype(BRAIN).T
        total[...] = jnp.zeros_like(total)

    key_sum[...] = jnp.zeros_like(key_sum)
    value_sum[...] = jnp.zeros_like(value_sum)
    k_turned = k_ref[...].T
    lanes = 2 * HEAD_DIM
    place = 0
    for index, (low, high) in enumerate(blocks):
        beside.point(index, len(blocks), first=False)
        first = index * QUERY_BLOCK
        size = high - low
        rows = slice(first, first + QUERY_BLOCK)
        queries = split_heads(q_ref[rows, :] * HEAD_DIM ** (-0.5))
        grads = split_heads(g_ref[rows, :])
        keys = k_ref[low:high, :]
        values = v_ref[low:high, :]
        blocked = bias[place : place + size, :]
        all_probs = []
        all_scores = []
        parts = []
        for head in range(2):
            scores = times_transposed(keys, queries[head]) + blocked
            probs = jnp.exp(scores - lse_ref[0, head : head + 1, rows])
            prob_grad = times_transposed(values, grads[head])
            row_dot = jnp.sum(probs * prob_grad, axis=0, keepdims=True)
            score_grad = (probs * (prob_grad - row_dot)).astype(BRAIN)
            all_probs.append(probs.astype(BRAIN))
            all_scores.append(score_grad)
            turned = k_turned[head * HEAD_DIM : (head + 1) * HEAD_DIM, low:high]
            parts.append(matmul(turned, score_grad))
        query_grad = jnp.concatenate(parts, axis=0).T * HEAD_DIM ** (-0.5)
        joined[rows, :lanes] = query_grad.astype(BRAIN)
        value_sum[low:high, :] += matmul(
            jnp.concatenate(all_probs, axis=1), jnp.concatenate(grads, axis=0)
        )
        key_sum[low:high, :] += matmul(
            jnp.concatenate(all_scores, axis=1), jnp.concatenate(queries, axis=0)
        )
        place += size
    joined[:, lanes : 2 * lanes] = key_sum[...].astype(BRAIN)
    joined[:, 2 * lanes :] = value_sum[...].astype(BRAIN)
    weight = jnp.concatenate([wq_ref[...], wk_ref[...], wv_ref[...]], axis=1)
    sums = jnp.zeros((1, 3 * lanes), FLOAT)
    for rows in row_blocks(length):
        part = joined[rows, :]
        total[rows, :] += times_transposed(part, weight)
        sums = sums + jnp.sum(part.astype(FLOAT), axis=0, keepdims=True)
    found = matmul(low_turned[...], joined[...]).astype(BRAIN)
    gq_ref[...] = found[:, :lanes]
    gk_ref[...] = found[:, lanes : 2 * lanes]
    gv_ref[...] = found[:, 2 * lanes :]
    shift_ref[0:1, :] = sums[:, :lanes]
    shift_ref[1:2, :] = sums[:, 2 * lanes :]
    shift_ref[2:8, :] = jnp.zeros((6, lanes), FLOAT)

    @pl.when(pair == HEADS // 2 - 1)
    def _():
        gains = jnp.zeros((1, total.shape[1]), FLOAT)
        moves = jnp.zeros((1, total.shape[1]), FLOAT)
        for rows in row_blocks(length):
            normed, inverse = norm_parts(tokens[rows, :].astype(FLOAT))
            upstream = total[rows, :]
            scaled = upstream * norms[0:1, :]
            centered = scaled - jnp.mean(scaled, axis=-1, keepdims=True)
            inward = centered - normed * jnp.mean(scaled * normed, axis=-1, keepdims=True)
            input_ref[rows, :] = (resid_grad[rows, :] + inverse * inward).astype(BRAIN)
            gains = gains + jnp.sum(upstream * normed, axis=0, keepdims=True)
            moves = moves + jnp.sum(upstream, axis=0, keepdims=True)
        sum_ref[0:1, :] = gains
        sum_ref[1:2, :] = moves
        sum_ref[2:8, :] = jnp.zeros((6, total.shape[1]), FLOAT)

    @pl.when(pair == HEADS // 2 - 1)
    def _():
        beside.rest()
        drain_all(scatters + [last])


def once(shape):
    return pl.BlockSpec(shape, lambda *_: (0,) * len(shape), pipeline_mode=pl.Buffered(1))


def pair_specs(rows, length):
    lanes, width = 2 * HEAD_DIM, HEADS * HEAD_DIM
    pairs = HEADS // 2
    segs = [once((rows, length))]
    plain = pl.BlockSpec((length, lanes), lambda j: (0, j))
    lse = pl.BlockSpec((1, 8, length), lambda j: (j, 0, 0))
    weights = [pl.BlockSpec((width, lanes), lambda j, at=at: (0, at * pairs + j)) for at in range(3)]
    shifts = pl.BlockSpec((8, lanes), lambda j: (0, j))
    bias = pltpu.VMEM((sum(high - low for low, high in windows(length)), QUERY_BLOCK), FLOAT)
    return segs, plain, lse, weights, shifts, bias


def attention_forward(segments, tokens, vectors, full_qkv, fulls, counts):
    length, width = tokens.shape
    segs, plain, lse, weights, shifts, bias = pair_specs(segments.shape[0], length)
    splits = [False] + [True] * (len(fulls) - 1)
    slots = piece_count([full.shape[-2:] for full in fulls], splits) * counts[1]
    return pl.pallas_call(
        functools.partial(attend_forward, counts, splits),
        grid=(HEADS // 2,),
        in_specs=segs
        + [once((length, width)), once((8, width)), shifts]
        + weights
        + [ANYWHERE] * 3,
        out_specs=[plain] * 4 + [lse] + [ANYWHERE] * 3,
        out_shape=[jax.ShapeDtypeStruct((length, width), BRAIN)] * 4
        + [jax.ShapeDtypeStruct((HEADS // 2, 8, length), FLOAT)]
        + [jax.ShapeDtypeStruct(full.shape, full.dtype) for full in fulls],
        input_output_aliases={7 + index: 5 + index for index in range(len(fulls))},
        scratch_shapes=[
            bias,
            pltpu.VMEM((length, width), BRAIN),
            pltpu.SemaphoreType.DMA((slots,)),
            pltpu.SemaphoreType.DMA((slots,)),
        ],
        name="attend_forward",
        compiler_params=pltpu.CompilerParams(
            collective_id=1, has_side_effects=True, vmem_limit_bytes=63 * 1024 * 1024
        ),
    )(
        segments,
        tokens,
        vectors,
        vectors,
        full_qkv,
        full_qkv,
        full_qkv,
        *fulls,
    )


def attention_backward(
    segments, heads, context_grad, lse_rows, tokens, vectors, resid_grad, full_qkv, grads, shapes, counts
):
    length, width = tokens.shape
    lanes = 2 * HEAD_DIM
    segs, plain, lse, weights, shifts, bias = pair_specs(segments.shape[0], length)
    column = pl.BlockSpec((width, lanes), lambda j: (0, j))
    splits = [True] * (len(shapes) - 1) + [False]
    half_count = counts[0] // 2
    slots = piece_count(shapes, splits) * counts[1] + half_count - 1
    partials = [jax.ShapeDtypeStruct((half_count,) + shape, BRAIN) for shape in shapes[1:]]
    return pl.pallas_call(
        functools.partial(attend_backward, counts, splits),
        grid=(HEADS // 2,),
        in_specs=segs
        + [plain] * 4
        + [lse, once((length, width)), once((8, width)), once((length, width))]
        + weights
        + [ANYWHERE] * 3,
        out_specs=[column] * 3 + [shifts, once((8, width)), once((length, width))] + [WHOLE] * 3,
        out_shape=[jax.ShapeDtypeStruct((width, width), BRAIN)] * 3
        + [jax.ShapeDtypeStruct((8, width), FLOAT)] * 2
        + [jax.ShapeDtypeStruct((length, width), BRAIN), jax.ShapeDtypeStruct(shapes[0], FLOAT)]
        + partials,
        scratch_shapes=[
            bias,
            pltpu.VMEM((length, lanes), FLOAT),
            pltpu.VMEM((length, lanes), FLOAT),
            pltpu.VMEM((width, length), BRAIN),
            pltpu.VMEM((length, width), FLOAT),
            pltpu.VMEM((length, 3 * lanes), BRAIN),
        ]
        + scatter_buffers(shapes, counts)
        + [
            pltpu.VMEM((half_count,) + shapes[0], BRAIN),
            pltpu.VMEM((half_count - 1,) + shapes[0], BRAIN),
            pltpu.SemaphoreType.DMA((slots,)),
            pltpu.SemaphoreType.DMA((slots,)),
            pltpu.SemaphoreType.DMA((len(shapes),)),
        ],
        name="attend_backward",
        compiler_params=pltpu.CompilerParams(
            collective_id=2, has_side_effects=True, vmem_limit_bytes=63 * 1024 * 1024
        ),
    )(
        segments,
        *heads,
        context_grad,
        lse_rows,
        tokens,
        vectors,
        resid_grad,
        full_qkv,
        full_qkv,
        full_qkv,
        *scatter_views(grads, shapes, counts),
    )


MESH = pl.DeviceIdType.MESH
ANYWHERE = pl.BlockSpec(memory_space=pl.ANY)
WHOLE = pl.BlockSpec(memory_space=pltpu.VMEM)


def bits_of(count):
    return count.bit_length() - 1


def flipped(value, bit):
    step = 1 << bit
    return value + step * (1 - 2 * lax.rem(lax.div(value, step), 2))


def rounded_down(value, bit):
    return lax.div(value, 1 << bit) * (1 << bit)


def spread(value, bit, total):
    step = 1 << (bit + 1)
    return [lax.rem(value, step) + step * turn for turn in range(1 << (total - 1 - bit))]


class Here:
    def __init__(self, dp_count, seq_count):
        self.dp_count, self.seq_count = dp_count, seq_count
        self.half_count = dp_count // 2
        self.seq_bits = bits_of(seq_count)
        self.place, self.line = lax.axis_index("dp"), lax.axis_index("seq")
        self.chip, self.core = lax.div(self.place, 2), lax.rem(self.place, 2)

    def core_peer(self):
        return {"dp": flipped(self.place, 0)}

    def line_peer(self, bit):
        return {"seq": flipped(self.line, bit)}

    def other_lines(self):
        return [lax.rem(self.line + turn, self.seq_count) for turn in range(1, self.seq_count)]

    def other_chips(self):
        return [lax.rem(self.chip + turn, self.half_count) for turn in range(1, self.half_count)]

    def chip_peers(self):
        return [{"dp": 2 * chip + self.core} for chip in self.other_chips()]

    def near_peers(self):
        peers = [self.core_peer()] + self.chip_peers()
        return peers + [{"seq": line} for line in self.other_lines()]

    def all_peers(self):
        peers = [{"dp": lax.rem(self.place + turn, self.dp_count)} for turn in range(1, self.dp_count)]
        return peers + [{"seq": line} for line in self.other_lines()]


def greet(peers):
    barrier = pltpu.get_barrier_semaphore()
    for peer in peers:
        pl.semaphore_signal(barrier, inc=1, device_id=peer, device_id_type=MESH)
    pl.semaphore_wait(barrier, len(peers))


class Slots:
    def __init__(self, send_sem, recv_sem):
        self.send_sem, self.recv_sem, self.used = send_sem, recv_sem, 0

    def take(self, count):
        first = self.used
        self.used += count
        return first

    def copy(self, slot, source, target, peer):
        return pltpu.make_async_remote_copy(
            source,
            target,
            self.send_sem.at[slot],
            self.recv_sem.at[slot],
            device_id=peer,
            device_id_type=MESH,
        )


def parts_of(shape, split):
    rows, width = shape
    tiles = width // 128
    if width % 128 or tiles < 2:
        return [[(slice(0, rows), slice(0, width), False)]]
    middle = tiles // 2 * 128
    first, second = (0, middle), (middle, width)
    every = slice(0, rows)
    if split and rows % 32 == 0:
        return [
            [(part, slice(*first), False), (part, slice(*second), True)]
            for part in (slice(0, rows // 2), slice(rows // 2, rows))
        ]
    if split and tiles >= 4:
        lists = [[], []]
        for (low, high), backwards in ((first, False), (second, True)):
            cut = low + (high - low) // 256 * 128
            lists[0].append((every, slice(low, cut), backwards))
            lists[1].append((every, slice(cut, high), backwards))
        return lists
    return [[(every, slice(*first), False), (every, slice(*second), True)]]


class Transfer:
    def start(self, stage):
        for copy in self.copies(stage):
            copy.start()

    def finish(self, stage):
        for copy in self.copies(stage):
            copy.wait_recv()
        self.use(stage)

    def use(self, stage):
        pass

    def drain(self):
        for stage in range(self.stages):
            for copy in self.copies(stage):
                copy.wait_send()


class ChipGather(Transfer):
    stages = 1

    def __init__(self, here, slots, shard, full, sem):
        self.here, self.slots, self.shard = here, slots, shard
        self.target = full.at[here.chip, here.core, here.line]
        self.own = pltpu.make_async_copy(shard, self.target, sem)
        self.first = slots.take(here.half_count - 1)

    def copies(self, stage):
        return [
            self.slots.copy(self.first + turn, self.shard, self.target, peer)
            for turn, peer in enumerate(self.here.chip_peers())
        ]


class Gather(Transfer):
    def __init__(self, here, slots, full, pieces):
        self.here, self.slots, self.full, self.pieces = here, slots, full, pieces
        self.stages = here.seq_bits + 1
        self.each = here.seq_count
        self.first = slots.take(self.each * len(pieces))

    def copies(self, stage):
        here, full = self.here, self.full
        found = []
        for index, (rows, columns, backwards) in enumerate(self.pieces):
            slot = self.first + self.each * index
            if stage == self.stages - 1:
                part = full.at[:, here.core, :, rows, columns]
                found.append(self.slots.copy(slot, part, part, here.core_peer()))
                continue
            if backwards:
                bit = here.seq_bits - 1 - stage
                slot += 1 << stage
                parts = [
                    full.at[:, here.core, at, rows, columns]
                    for at in spread(here.line, bit, here.seq_bits)
                ]
            else:
                bit = stage
                slot += 1 + bit
                block = pl.ds(rounded_down(here.line, bit), 1 << bit)
                parts = [full.at[:, here.core, block, rows, columns]]
            for turn, part in enumerate(parts):
                found.append(self.slots.copy(slot + turn, part, part, here.line_peer(bit)))
        return found


class ChipSum(Transfer):
    stages = 1

    def __init__(self, here, slots, partial, arrived, share, offset):
        self.here, self.slots, self.partial, self.arrived = here, slots, partial, arrived
        self.share, self.offset = share, offset
        self.first = slots.take(here.half_count - 1)

    def copies(self, stage):
        return [
            self.slots.copy(
                self.first + turn,
                self.partial.at[chip],
                self.arrived.at[turn],
                {"dp": 2 * chip + self.here.core},
            )
            for turn, chip in enumerate(self.here.other_chips())
        ]

    def use(self, stage):
        total = self.partial[self.here.chip].astype(FLOAT)
        for turn in range(self.here.half_count - 1):
            total = total + self.arrived[turn].astype(FLOAT)
        self.share[:, self.offset : self.offset + total.shape[1]] = total


class Scatter(Transfer):
    def __init__(self, here, slots, grad, own, from_core, from_line, partial, pieces, load):
        self.here, self.slots, self.grad, self.own = here, slots, grad, own
        self.from_core, self.from_line, self.partial = from_core, from_line, partial
        self.pieces, self.load = pieces, load
        self.stages = here.seq_bits + 1
        self.each = here.seq_count
        self.first = slots.take(self.each * len(pieces))

    def line_stage(self, stage, backwards):
        here = self.here
        if backwards:
            bit = stage - 1
            away = spread(flipped(here.line, bit), bit, here.seq_bits)
            kept = spread(here.line, bit, here.seq_bits)
        else:
            bit = here.seq_bits - stage
            away = [rounded_down(flipped(here.line, bit), bit) + at for at in range(1 << bit)]
            kept = [rounded_down(here.line, bit) + at for at in range(1 << bit)]
        base = sum(1 << (here.seq_bits - past) for past in range(1, stage))
        return bit, away, kept, base

    def copies(self, stage):
        here = self.here
        found = []
        for index, (rows, columns, backwards) in enumerate(self.pieces):
            slot = self.first + self.each * index
            if stage == 0:
                found.append(
                    self.slots.copy(
                        slot,
                        self.grad.at[:, 1 - here.core, :, rows, columns],
                        self.from_core.at[:, :, rows, columns],
                        here.core_peer(),
                    )
                )
                continue
            bit, away, _, base = self.line_stage(stage, backwards)
            for turn, at in enumerate(away):
                found.append(
                    self.slots.copy(
                        slot + 1 + base + turn,
                        self.own.at[:, at, rows, columns],
                        self.from_line.at[base + turn, :, rows, columns],
                        here.line_peer(bit),
                    )
                )
        return found

    def use(self, stage):
        here, own = self.here, self.own
        if stage == 0:
            self.load()
        for rows, columns, backwards in self.pieces:
            if stage == 0:

                def add(at, carry, rows=rows, columns=columns):
                    one, two = lax.div(at, here.seq_count), lax.rem(at, here.seq_count)
                    own[one, two, rows, columns] = (
                        own[one, two, rows, columns] + self.from_core[one, two, rows, columns]
                    )
                    return carry

                lax.fori_loop(0, here.half_count * here.seq_count, add, 0)
                continue
            _, _, kept, base = self.line_stage(stage, backwards)
            for turn, at in enumerate(kept):
                last = stage == self.stages - 1

                def add(one, carry, rows=rows, columns=columns, at=at, place=base + turn, last=last):
                    found = own[one, at, rows, columns] + self.from_line[place, one, rows, columns]
                    if last:
                        self.partial[one, rows, columns] = found
                    else:
                        own[one, at, rows, columns] = found
                    return carry

                lax.fori_loop(0, here.half_count, add, 0)


class Exchange(Transfer):
    stages = 1

    def __init__(self, here, slots, source, target, to_rows, bounce, sem):
        self.here, self.slots, self.source, self.target = here, slots, source, target
        self.to_rows, self.bounce, self.sem = to_rows, bounce, sem
        self.first = slots.take(here.seq_count - 1)

    def ends(self, line):
        if self.to_rows:
            count = self.target.shape[0]
            block = self.source.at[pl.ds(line * count, count)]
            return block, self.target.at[:, self.here.line]
        return self.source.at[:, line], self.target.at[self.here.line]

    def copies(self, stage):
        return [
            self.slots.copy(self.first + turn, *self.ends(line), {"seq": line})
            for turn, line in enumerate(self.here.other_lines())
        ]

    def own_in(self):
        return pltpu.make_async_copy(self.ends(self.here.line)[0], self.bounce, self.sem.at[0])

    def own_out(self):
        source, target = self.ends(self.here.line)
        source = source if self.bounce is None else self.bounce
        return pltpu.make_async_copy(source, target, self.sem.at[1])

    def start(self, stage):
        if self.bounce is not None:
            self.own_in().start()
        super().start(stage)
        if self.bounce is not None:
            self.own_in().wait()
        self.own_out().start()

    def use(self, stage):
        self.own_out().wait()


def begin_all(transfers):
    for transfer in transfers:
        transfer.start(0)


def follow(transfer, stage):
    transfer.finish(stage - 1)
    if stage < transfer.stages:
        transfer.start(stage)


def follows(transfers, stage):
    return [functools.partial(follow, transfer, stage) for transfer in transfers]


def flow_of(transfers):
    calls = [functools.partial(begin_all, transfers)]
    for stage in range(1, transfers[0].stages + 1):
        calls += follows(transfers, stage)
    return calls


def evenly(calls, low, high):
    gap = (high - low) / max(len(calls) - 1, 1)
    return [(low + gap * turn, call) for turn, call in enumerate(calls)]


def drain_all(transfers):
    for transfer in transfers:
        transfer.drain()


def chip_gathers_of(here, slots, shards, fulls, sem):
    return [
        ChipGather(here, slots, shard, full, sem.at[index])
        for index, (shard, full) in enumerate(zip(shards, fulls))
    ]


def gathers_of(here, slots, fulls, splits):
    return [
        Gather(here, slots, full, pieces)
        for full, split in zip(fulls, splits)
        for pieces in parts_of(full.shape[-2:], split)
    ]


def piece_count(shapes, splits):
    return sum(len(part) for shape, split in zip(shapes, splits) for part in parts_of(shape, split))


def full_shape(shard, dp_count, seq_count):
    return jax.ShapeDtypeStruct((dp_count // 2, 2, seq_count) + shard.shape, shard.dtype)


def gather_kernel(counts, first, count, *refs):
    tokens, vectors, up_bias, weights = refs[0], refs[1], refs[2], refs[3 : 2 + count]
    token_rows, fulls = refs[2 + count], refs[3 + count : 3 + 2 * count]
    rest = refs[3 + 2 * count :]
    shards, small, bounce, send_sem, recv_sem, own_sem, move_sem = rest[:count], *rest[count:]
    small[...] = jnp.zeros_like(small)
    small[0:8, : vectors.shape[1]] = vectors[...]
    small[8:9, : up_bias.shape[1]] = up_bias[...]
    shards[0][...] = small[...].astype(BRAIN)
    for shard, weight in zip(shards[1:], weights):
        shard[...] = weight[...].astype(BRAIN)
    here = Here(*counts)
    slots = Slots(send_sem, recv_sem)
    chips = chip_gathers_of(here, slots, shards, fulls, own_sem)
    move = Exchange(here, slots, tokens, token_rows, True, bounce, move_sem)
    gathers = gathers_of(here, slots, fulls[:first], [False] + [True] * (first - 1))
    flow = flow_of(gathers)
    greet(here.near_peers())
    for chip in chips[:first]:
        chip.start(0)
    move.start(0)
    for chip in chips[first:]:
        chip.start(0)
    for chip in chips:
        chip.own.start()
    for chip in chips[:first]:
        chip.own.wait()
        chip.finish(0)
    for call in flow:
        call()
    move.finish(0)
    for chip in chips[first:]:
        chip.own.wait()
        chip.finish(0)
    drain_all(chips + gathers + [move])


def gather_first(tokens, vectors, up_bias, weights, first, counts):
    dp_count, seq_count = counts
    row_count, pos_count, width = tokens.shape
    rows = row_count // seq_count
    shards = [jax.ShapeDtypeStruct(shape, BRAIN) for shape in [(16, 128)] + [w.shape for w in weights]]
    pieces = piece_count([shard.shape for shard in shards[:first]], [False] + [True] * (first - 1))
    slots = len(shards) * (dp_count // 2 - 1) + pieces * seq_count + seq_count - 1
    return pl.pallas_call(
        functools.partial(gather_kernel, counts, first, len(shards)),
        out_shape=[jax.ShapeDtypeStruct((rows, seq_count, pos_count, width), tokens.dtype)]
        + [full_shape(shard, *counts) for shard in shards],
        in_specs=[ANYWHERE] + [WHOLE] * (2 + len(weights)),
        out_specs=[ANYWHERE] * (1 + len(shards)),
        scratch_shapes=[pltpu.VMEM(shard.shape, BRAIN) for shard in shards]
        + [
            pltpu.VMEM((16, 128), FLOAT),
            pltpu.VMEM((rows, pos_count, width), tokens.dtype),
            pltpu.SemaphoreType.DMA((slots,)),
            pltpu.SemaphoreType.DMA((slots,)),
            pltpu.SemaphoreType.DMA((len(shards),)),
            pltpu.SemaphoreType.DMA((2,)),
        ],
        name="gather_first",
        compiler_params=pltpu.CompilerParams(
            collective_id=0, has_side_effects=True, vmem_limit_bytes=63 * 1024 * 1024
        ),
    )(tokens, vectors, up_bias, *weights)


HIDDEN_BLOCK = 512
GELU_SCALE = 0.7978845608028654
GELU_CUBE = 0.044715


def gelu_both(values):
    square = values * values
    turned = jnp.tanh(GELU_SCALE * values * (1.0 + GELU_CUBE * square))
    half = 0.5 + 0.5 * turned
    inner = GELU_SCALE * (1.0 + 3.0 * GELU_CUBE * square)
    return values * half, half + 0.5 * values * (1.0 - turned * turned) * inner


def forward_start(context, tokens, w_out, vectors, resid, low_two, low_turned):
    for rows in row_blocks(resid.shape[0]):
        values = tokens[rows, :].astype(FLOAT) + (matmul(context[rows, :], w_out[...]) + vectors[6:7, :])
        resid[rows, :] = values
        normed, _ = norm_parts(values)
        low = (normed * vectors[2:3, :] + vectors[3:4, :]).astype(BRAIN)
        low_two[rows, :] = low
        low_turned[:, rows] = low.T


def backward_end(
    context, w_out, vectors, resid, total, back, gc_ref, gr_ref, gwo_ref, sum_ref, low_turned
):
    width = resid.shape[1]
    sums = [jnp.zeros((1, width), FLOAT) for _ in range(4)]
    for rows in row_blocks(resid.shape[0]):
        normed, inverse = norm_parts(resid[rows, :])
        upstream = total[rows, :]
        given = back(rows).astype(FLOAT)
        scaled = upstream * vectors[2:3, :]
        centered = scaled - jnp.mean(scaled, axis=-1, keepdims=True)
        inward = centered - normed * jnp.mean(scaled * normed, axis=-1, keepdims=True)
        grad = given + inverse * inward
        low = grad.astype(BRAIN)
        gr_ref[rows, :] = grad
        gc_ref[rows, :] = times_transposed(low, w_out[...]).astype(BRAIN)
        low_turned[:, rows] = context[rows, :].T
        total[rows, :] = low.astype(FLOAT)
        for index, values in enumerate((upstream * normed, upstream, low.astype(FLOAT), given)):
            sums[index] = sums[index] + jnp.sum(values, axis=0, keepdims=True)
    for index in range(4):
        sum_ref[index : index + 1, :] = sums[index]
    sum_ref[4:8, :] = jnp.zeros((4, width), FLOAT)
    gwo_ref[...] = matmul(low_turned[...], total[...].astype(BRAIN)).astype(BRAIN)


def mlp_kernel(counts, *refs):
    context, tokens, w_out, w_up, w_down, vectors, up_shift, cotangent = refs[0:8]
    gup_ref, gdown_ref, gub_ref, gwo_ref, gc_ref, gr_ref, sum_ref, mixed = refs[8:16]
    acts, slopes, low_two, low_turned, resid, total, hidden, back, mixed_rows = refs[16:25]
    send_sem, recv_sem, move_sem = refs[25:28]
    here = Here(*counts)
    slots = Slots(send_sem, recv_sem)
    arrive = Exchange(here, slots, cotangent, back, True, None, move_sem.at[pl.ds(0, 2)])
    leave = Exchange(here, slots, mixed_rows, mixed, False, None, move_sem.at[pl.ds(2, 2)])
    step = pl.program_id(0)
    half = pl.num_programs(0) // 2
    count = resid.shape[0]
    pos_count = back.shape[2]

    def back_rows(rows):
        parts = []
        for first in range(rows.start, rows.stop, pos_count):
            size = min(pos_count, rows.stop - first)
            row, rest = divmod(first, pos_count * counts[1])
            line, offset = divmod(rest, pos_count)
            parts.append(back[row, line, offset : offset + size, :])
        return parts[0] if len(parts) == 1 else jnp.concatenate(parts, axis=0)

    @pl.when(step == 0)
    def _():
        greet(here.near_peers())
        arrive.start(0)
        forward_start(context, tokens, w_out, vectors, resid, low_two, low_turned)
        total[...] = jnp.zeros_like(total)

    @pl.when(step < half)
    def _():
        for rows in row_blocks(count):
            values = matmul(low_two[rows, :], w_up[...]) + up_shift[...]
            act, slope = gelu_both(values)
            low = act.astype(BRAIN)
            acts[step, rows, :] = low
            slopes[step, rows, :] = slope
            total[rows, :] += matmul(low, w_down[...])

    @pl.when(step == half)
    def _():
        for first in range(0, count, pos_count):
            row, line = divmod(first // pos_count, counts[1])
            rows = slice(first, first + pos_count)
            values = resid[rows, :] + (total[rows, :] + vectors[7:8, :])
            mixed_rows[row, line] = values.astype(BRAIN)
        total[...] = jnp.zeros_like(total)
        leave.start(0)
        arrive.finish(0)

    @pl.when(step >= half)
    def _():
        at = step - half
        sums = jnp.zeros((1, hidden.shape[1]), FLOAT)
        for rows in row_blocks(count):
            grad = times_transposed(back_rows(rows), w_down[...]) * slopes[at, rows, :]
            low = grad.astype(BRAIN)
            hidden[rows, :] = low
            sums = sums + jnp.sum(low.astype(FLOAT), axis=0, keepdims=True)
            total[rows, :] += times_transposed(low, w_up[...])
        gub_ref[...] = sums
        gup_ref[...] = matmul(low_turned[...], hidden[...]).astype(BRAIN)
        every = back_rows(slice(0, count))
        gdown_ref[...] = inner_rows(acts[at], every).astype(BRAIN)

    @pl.when(step == 2 * half - 1)
    def _():
        backward_end(
            context, w_out, vectors, resid, total, back_rows, gc_ref, gr_ref, gwo_ref, sum_ref, low_turned
        )
        leave.finish(0)
        drain_all([arrive, leave])


def feed_forward(context, tokens, w_out, w_up, w_down, vectors, up_shift, cotangent, counts):
    count, width = context.shape
    hidden = w_up.shape[1]
    half = hidden // HIDDEN_BLOCK
    seq_count = counts[1]
    row_count, pos_count, _ = cotangent.shape
    rows = row_count // seq_count
    later = lambda j: jnp.maximum(j - half, 0)
    around = lambda j: lax.rem(j, half)
    block = HIDDEN_BLOCK
    slots = 2 * (seq_count - 1)
    return pl.pallas_call(
        functools.partial(mlp_kernel, counts),
        grid=(2 * half,),
        in_specs=[
            once((count, width)),
            once((count, width)),
            once((width, width)),
            pl.BlockSpec((width, block), lambda j: (0, around(j))),
            pl.BlockSpec((block, width), lambda j: (around(j), 0)),
            once((8, width)),
            pl.BlockSpec((1, block), lambda j: (0, around(j))),
            ANYWHERE,
        ],
        out_specs=[
            pl.BlockSpec((width, block), lambda j: (0, later(j))),
            pl.BlockSpec((block, width), lambda j: (later(j), 0)),
            pl.BlockSpec((1, block), lambda j: (0, later(j))),
            once((width, width)),
            once((count, width)),
            once((count, width)),
            once((8, width)),
            ANYWHERE,
        ],
        out_shape=[
            jax.ShapeDtypeStruct((width, hidden), BRAIN),
            jax.ShapeDtypeStruct((hidden, width), BRAIN),
            jax.ShapeDtypeStruct((1, hidden), FLOAT),
            jax.ShapeDtypeStruct((width, width), BRAIN),
            jax.ShapeDtypeStruct((count, width), BRAIN),
            jax.ShapeDtypeStruct((count, width), FLOAT),
            jax.ShapeDtypeStruct((8, width), FLOAT),
            jax.ShapeDtypeStruct((seq_count, rows, pos_count, width), BRAIN),
        ],
        scratch_shapes=[
            pltpu.VMEM((half, count, block), BRAIN),
            pltpu.VMEM((half, count, block), FLOAT),
            pltpu.VMEM((count, width), BRAIN),
            pltpu.VMEM((width, count), BRAIN),
            pltpu.VMEM((count, width), FLOAT),
            pltpu.VMEM((count, width), FLOAT),
            pltpu.VMEM((count, block), BRAIN),
            pltpu.VMEM((rows, seq_count, pos_count, width), BRAIN),
            pltpu.VMEM((rows, seq_count, pos_count, width), BRAIN),
            pltpu.SemaphoreType.DMA((slots,)),
            pltpu.SemaphoreType.DMA((slots,)),
            pltpu.SemaphoreType.DMA((4,)),
        ],
        name="feed_forward",
        compiler_params=pltpu.CompilerParams(
            collective_id=4, has_side_effects=True, vmem_limit_bytes=63 * 1024 * 1024
        ),
    )(context, tokens, w_out, w_up, w_down, vectors, up_shift, cotangent)


def lamb_pieces(weight, first, second, grad, decay):
    first_new = BETA_ONE * first + (1.0 - BETA_ONE) * grad
    second_new = BETA_TWO * second + (1.0 - BETA_TWO) * grad * grad
    spread_out = jnp.sqrt(second_new / CORR_TWO) + ADAM_EPS
    update = first_new / CORR_ONE / spread_out + decay * weight
    return (first_new, second_new, update)


def square_sum(values):
    return jnp.sum(jnp.sum(values * values, axis=1, keepdims=True), axis=0, keepdims=True)


def picked(small, rank, vector_size, bias_size):
    width = small.shape[1]
    row = lax.broadcasted_iota(jnp.int32, (width, 128), 0)
    lane = lax.broadcasted_iota(jnp.int32, (width, 128), 1)
    dot = functools.partial(jnp.dot, precision=lax.Precision.HIGHEST, preferred_element_type=FLOAT)
    chosen = (row == lane + rank * vector_size) & (lane < vector_size)
    vector_grad = dot(small[0:8, :], jnp.where(chosen, 1.0, 0.0))[:, :vector_size]
    start = rank * bias_size
    chosen = (row == lane + lax.rem(start, width)) & (lane < bias_size)
    tail = dot(small[8:16, :], jnp.where(chosen, 1.0, 0.0))
    tail_row = lax.broadcasted_iota(jnp.int32, tail.shape, 0)
    tail = jnp.sum(jnp.where(tail_row == lax.div(start, width), tail, 0.0), axis=0, keepdims=True)
    return vector_grad, tail[:, :bias_size]


def scatters_of(here, slots, grads, buffers, partials, own_sem, splits):
    count = len(grads)
    found, loads = [], []
    for index, (grad, partial) in enumerate(zip(grads, partials)):
        own, *arrivals = buffers[index::count]
        load = lambda grad=grad, own=own, index=index: pltpu.make_async_copy(
            grad.at[:, here.core], own, own_sem.at[index]
        )
        loads.append(load)
        for order, pieces in enumerate(parts_of(grad.shape[-2:], splits[index])):
            wait = (lambda load=load: load().wait()) if order == 0 else (lambda: None)
            found.append(Scatter(here, slots, grad, own, *arrivals, partial, pieces, wait))
    return found, loads


def scatter_buffers(shapes, counts):
    half_count, seq_count = counts[0] // 2, counts[1]
    leads = [(half_count, seq_count)] * 2 + [(seq_count - 1, half_count)]
    return [pltpu.VMEM(lead + shape, BRAIN) for lead in leads for shape in shapes]


def scatter_views(grads, shapes, counts):
    lead = (counts[0] // 2, 2, counts[1])
    return [grad.reshape(lead + shape) for grad, shape in zip(grads, shapes)]


class SmallSum(Transfer):
    def __init__(self, here, small, sums, arrived, send_sem, recv_sem):
        self.slots = Slots(send_sem, recv_sem)
        self.small, self.sums, self.arrived = small, sums, arrived
        self.peers = [here.core_peer()]
        self.peers += [here.line_peer(bit) for bit in range(here.seq_bits)]
        self.peers += [{"dp": flipped(here.place, bit + 1)} for bit in range(bits_of(here.half_count))]
        self.stages = len(self.peers)

    def copies(self, stage):
        source = self.sums.at[stage - 1] if stage else self.small
        return [self.slots.copy(stage, source, self.arrived.at[stage], self.peers[stage])]

    def use(self, stage):
        before = self.sums[stage - 1] if stage else self.small[...]
        self.sums[stage] = before + self.arrived[stage]


def scatter_kernel(counts, *refs):
    grads, small, input_rows, partials, ready = refs[0:3], refs[3], refs[4], refs[5:7], refs[7]
    weights, firsts, seconds = refs[8:14], refs[14:20], refs[20:26]
    shares, norm_out, input_grad = refs[26:32], refs[32], refs[33]
    buffers, mine, arrived, bounce = refs[34:43], refs[43:46], refs[46:51], refs[51]
    small_sum, small_in, norm_mine, norm_dp, norm_line, norm_seq = refs[52:58]
    send_sem, recv_sem, own_sem, move_sem, small_send, small_recv, norm_send, norm_recv = refs[58:66]
    here = Here(*counts)
    slots = Slots(send_sem, recv_sem)
    scatters, loads = scatters_of(here, slots, grads, buffers, mine, own_sem, [False] * 3)
    early = [
        ChipSum(here, slots, partial, arrived[index], shares[index + 1], 0)
        for index, partial in enumerate(partials)
    ]
    late = [
        ChipSum(here, slots, mine[at], arrived[2 + at], shares[0], at * grads[at].shape[-1])
        for at in range(3)
    ]
    move = Exchange(here, slots, input_rows, input_grad, False, bounce, move_sem)
    total = SmallSum(here, small, small_sum, small_in, small_send, small_recv)
    for load in loads:
        load().start()
    dp_peers, seq_peers = here.all_peers()[: here.dp_count - 1], here.all_peers()[here.dp_count - 1 :]
    greet(dp_peers + seq_peers)
    lane = lax.broadcasted_iota(jnp.int32, (8, 128), 1)
    row = lax.broadcasted_iota(jnp.int32, (8, 128), 0)

    def with_norms(tile, index, grad):
        decay = DECAY_RATE if index < 4 else 0.0
        weight = weights[index][...]
        update = lamb_pieces(weight, firsts[index][...], seconds[index][...], grad, decay)[2]
        at = row == min(index, 4)
        tile = jnp.where(at & (lane == 0), square_sum(weight), tile)
        return jnp.where(at & (lane == 1), square_sum(update), tile)

    total.start(0)
    begin_all(scatters + early)
    tile = jnp.zeros((8, 128), FLOAT)
    follow(total, 1)
    shares[3][...] = ready[...]
    tile = with_norms(tile, 3, ready[...])
    for stage in range(2, here.seq_bits + 1):
        follow(total, stage)
    stages = scatters[0].stages
    done = here.seq_bits
    for stage in range(1, stages + 1):
        if stage == stages:
            move.start(0)
        for index, scatter in enumerate(scatters):
            follow(scatter, stage)
            if stage == stages:
                late[index].start(0)
        if done < total.stages and stage < stages:
            done += 1
            follow(total, done)
    for stage in range(done + 1, total.stages + 1):
        follow(total, stage)
    for index, chip in enumerate(early):
        chip.finish(0)
        tile = with_norms(tile, index + 1, shares[index + 1][...])

    rank = here.place * here.seq_count + here.line
    vector_grad, bias_grad = picked(
        small_sum[total.stages - 1], rank, shares[4].shape[1], shares[5].shape[1]
    )
    shares[4][...] = vector_grad
    shares[5][...] = bias_grad
    tile = with_norms(tile, 5, bias_grad)
    for chip in late:
        chip.finish(0)
    norm_mine[0:8, :] = with_norms(tile, 0, shares[0][...])
    weight = weights[4][...]
    update = lamb_pieces(weight, firsts[4][...], seconds[4][...], vector_grad, 0.0)[2]
    weight_sq = jnp.sum(weight * weight, axis=1, keepdims=True)
    update_sq = jnp.sum(update * update, axis=1, keepdims=True)
    norm_mine[8:16, :] = jnp.where(lane == 0, weight_sq, jnp.where(lane == 1, update_sq, 0.0))

    norm_slots = Slots(norm_send, norm_recv)

    def exchange(source, held, peers, at):
        base = norm_slots.take(len(peers))
        copies = [
            norm_slots.copy(base + turn, source, held.at[at], peer) for turn, peer in enumerate(peers)
        ]
        for copy in copies:
            copy.start()
        held[at] = source[...]
        for copy in copies:
            copy.wait_recv()
        found = held[0]
        for turn in range(1, held.shape[0]):
            found = found + held[turn]
        return copies, found

    sent, found = exchange(norm_mine, norm_dp, dp_peers, here.place)
    norm_line[...] = found
    also, found = exchange(norm_line, norm_seq, seq_peers, here.line)
    norm_out[...] = found
    move.finish(0)
    for copy in sent + also:
        copy.wait_send()
    drain_all(scatters + early + late + [total, move])


def scatter_last(grads, small, input_rows, partials, ready, weights, firsts, seconds, counts):
    dp_count, seq_count = counts
    shapes = [weight.shape for weight in weights]
    thirds = [(shapes[0][0], grad.shape[1]) for grad in grads]
    lead = (dp_count // 2,)
    pieces = piece_count(thirds, [False] * 3)
    slots = pieces * seq_count + 5 * (dp_count // 2 - 1) + seq_count - 1
    stages = bits_of(dp_count) + bits_of(seq_count)
    return pl.pallas_call(
        functools.partial(scatter_kernel, counts),
        out_shape=[jax.ShapeDtypeStruct(shape, FLOAT) for shape in shapes]
        + [
            jax.ShapeDtypeStruct((16, 128), FLOAT),
            jax.ShapeDtypeStruct((seq_count,) + input_rows.shape[0:1] + input_rows.shape[2:], BRAIN),
        ],
        in_specs=[ANYWHERE] * 3 + [WHOLE, ANYWHERE] + [WHOLE] * 21,
        out_specs=[WHOLE] * 7 + [ANYWHERE],
        scratch_shapes=scatter_buffers(thirds, counts)
        + [pltpu.VMEM(lead + shape, BRAIN) for shape in thirds]
        + [pltpu.VMEM((lead[0] - 1,) + shape, BRAIN) for shape in shapes[1:3] + thirds]
        + [
            pltpu.VMEM(input_rows.shape[0:1] + input_rows.shape[2:], BRAIN),
            pltpu.VMEM((stages,) + small.shape, FLOAT),
            pltpu.VMEM((stages,) + small.shape, FLOAT),
            pltpu.VMEM((16, 128), FLOAT),
            pltpu.VMEM((dp_count, 16, 128), FLOAT),
            pltpu.VMEM((16, 128), FLOAT),
            pltpu.VMEM((seq_count, 16, 128), FLOAT),
            pltpu.SemaphoreType.DMA((slots,)),
            pltpu.SemaphoreType.DMA((slots,)),
            pltpu.SemaphoreType.DMA((3,)),
            pltpu.SemaphoreType.DMA((2,)),
            pltpu.SemaphoreType.DMA((stages,)),
            pltpu.SemaphoreType.DMA((stages,)),
            pltpu.SemaphoreType.DMA((dp_count + seq_count,)),
            pltpu.SemaphoreType.DMA((dp_count + seq_count,)),
        ],
        name="scatter_last",
        compiler_params=pltpu.CompilerParams(
            collective_id=3, has_side_effects=True, vmem_limit_bytes=60 * 1024 * 1024
        ),
    )(
        *scatter_views(grads, thirds, counts),
        small,
        input_rows,
        *partials,
        ready,
        *weights,
        *firsts,
        *seconds,
    )


def lamb_kernel(*refs):
    grads, norms = refs[0:6], refs[6]
    weights, firsts, seconds = refs[7:13], refs[13:19], refs[19:25]
    grad_out, first_out, second_out, new_out = refs[25:31], refs[31:37], refs[37:43], refs[43:49]
    copy_out = refs[49:53]
    weight_norm = jnp.sqrt(norms[:, 0:1])
    scales = weight_norm / (jnp.sqrt(norms[:, 1:2]) + ADAM_EPS)
    for index in range(6):
        grad = grads[index][...]
        weight = weights[index][...]
        decay = DECAY_RATE if index < 4 else 0.0
        first_new, second_new, update = lamb_pieces(
            weight, firsts[index][...], seconds[index][...], grad, decay
        )
        scale = scales[8:16] if index == 4 else scales[min(index, 4) : min(index, 4) + 1]
        new = weight - LEARN_RATE * scale * update
        grad_out[index][...] = grad
        first_out[index][...] = first_new
        second_out[index][...] = second_new
        new_out[index][...] = new
        if index < 4:
            copy_out[index][...] = new.astype(BRAIN)


def lamb_all(grads, norms, weights, firsts, seconds):
    vmem = pl.BlockSpec(memory_space=pltpu.VMEM)
    shapes = [jax.ShapeDtypeStruct(weight.shape, FLOAT) for weight in weights]
    copies = [jax.ShapeDtypeStruct(weight.shape, BRAIN) for weight in weights[:4]]
    return pl.pallas_call(
        lamb_kernel,
        out_shape=shapes * 4 + copies,
        in_specs=[vmem] * 25,
        out_specs=[vmem] * 28,
        name="lamb_update",
        compiler_params=pltpu.CompilerParams(vmem_limit_bytes=63 * 1024 * 1024),
    )(*grads, norms, *weights, *firsts, *seconds)


def body(
    tokens,
    cotangent,
    segment_ids,
    w_qkv,
    m_qkv,
    v_qkv,
    w_out,
    m_out,
    v_out,
    w_up,
    m_up,
    v_up,
    w_down,
    m_down,
    v_down,
    vectors,
    m_vectors,
    v_vectors,
    up_bias,
    m_up_bias,
    v_up_bias,
):
    dp_count, seq_count = lax.axis_size("dp"), lax.axis_size("seq")
    vector_size, bias_size = vectors.shape[1], up_bias.shape[0]
    counts = (dp_count, seq_count)
    token_rows, *fulls = gather_first(
        tokens, vectors, up_bias[None], [w_qkv, w_out, w_up, w_down], 2, counts
    )
    small = fulls[0].reshape(dp_count * seq_count, 16, 128)
    full_vectors = small[:, :8, :vector_size].transpose(1, 0, 2)
    vector_rows = full_vectors.reshape(8, -1).astype(FLOAT)
    up_shift = small[:, 8, :bias_size].reshape(-1).astype(FLOAT)
    as_matrix = lambda full: full.reshape(-1, full.shape[-1])
    full_qkv = as_matrix(fulls[1])

    width = tokens.shape[2]
    length = segment_ids.shape[1]
    rows = token_rows.shape[0]
    assert rows == 1
    token_rows = token_rows.reshape(length, width)
    *heads, context, lse_rows, full_out, full_up, full_down = attention_forward(
        segment_ids, token_rows, vector_rows, full_qkv, fulls[2:], counts
    )
    full_out, full_up, full_down = [as_matrix(full) for full in (full_out, full_up, full_down)]
    grad_up, grad_down, grad_up_bias, grad_out, context_grad, resid_grad, sums, mixed = feed_forward(
        context,
        token_rows,
        full_out,
        full_up,
        full_down,
        vector_rows,
        up_shift[None],
        cotangent,
        counts,
    )
    *qkv_grads, shift_sums, norm_sums, input_rows, share_down, sum_up, sum_out = attention_backward(
        segment_ids,
        heads,
        context_grad,
        lse_rows,
        token_rows,
        vector_rows,
        resid_grad,
        full_qkv,
        [grad_down, grad_up, grad_out],
        [w_down.shape, w_up.shape, w_out.shape],
        counts,
    )
    grad_vectors = jnp.concatenate([norm_sums[:2], sums[:2], shift_sums[:2], sums[2:4]])
    small_grad = jnp.concatenate([grad_vectors, grad_up_bias.reshape(-1, width)])
    small_grad = jnp.pad(small_grad, ((0, 16 - small_grad.shape[0]), (0, 0)))
    as_row = lambda value: value.reshape(1, -1)
    weights = (w_qkv, w_out, w_up, w_down, vectors, as_row(up_bias))
    firsts = (m_qkv, m_out, m_up, m_down, m_vectors, as_row(m_up_bias))
    seconds = (v_qkv, v_out, v_up, v_down, v_vectors, as_row(v_up_bias))
    *shares, norms, input_grad = scatter_last(
        qkv_grads,
        small_grad,
        input_rows.reshape(rows, seq_count, length // seq_count, width),
        [sum_out, sum_up],
        share_down,
        weights,
        firsts,
        seconds,
        counts,
    )
    results = list(lamb_all(shares, norms, weights, firsts, seconds))
    mixed = mixed.reshape(tokens.shape)
    input_grad = input_grad.reshape(tokens.shape).astype(FLOAT)
    for index in (5, 11, 17, 23):
        results[index] = results[index].reshape(-1)
    return (mixed, input_grad, *results)


def solution(mesh):
    matrix = P(("dp", "seq"), None)
    rows = P("dp", "seq", None)
    vector = P(None, ("dp", "seq"))
    bias = P(("dp", "seq"))
    six = (matrix, matrix, matrix, matrix, vector, bias)
    in_specs = (rows, rows, P("dp", None)) + tuple(spec for spec in six for _ in range(3))
    out_specs = (rows, rows) + six * 4 + (matrix,) * 4
    return jax.shard_map(body, mesh=mesh, in_specs=in_specs, out_specs=out_specs, check_vma=False)
```

```python
import functools

import jax
import jax.numpy as jnp
from jax import lax
from jax.experimental import pallas as pl
from jax.experimental.pallas import tpu as pltpu
from jax.sharding import PartitionSpec as P

HEADS = 12
HEAD_DIM = 64
LONGEST = 512
QUERY_BLOCK = 256
ROW_BLOCK = 256


BETA_ONE = 0.9
BETA_TWO = 0.999
ADAM_EPS = 1e-06
DECAY_RATE = 0.01
LEARN_RATE = 0.4
NORM_EPS = 1e-05
STEP_NUMBER = 10.0
CORR_ONE = 1.0 - BETA_ONE**STEP_NUMBER
CORR_TWO = 1.0 - BETA_TWO**STEP_NUMBER

BRAIN = jnp.bfloat16
FLOAT = jnp.float32


def matmul(left_side, right_side):
    return jnp.dot(left_side, right_side, preferred_element_type=FLOAT)


def inner_rows(left_side, right_side):
    return lax.dot_general(
        left_side, right_side, (((0,), (0,)), ((), ())), preferred_element_type=FLOAT
    )


def times_transposed(left_side, right_side):
    return lax.dot_general(
        left_side, right_side, (((1,), (1,)), ((), ())), preferred_element_type=FLOAT
    )


def norm_parts(values):
    center = values - jnp.mean(values, axis=-1, keepdims=True)
    inverse = lax.rsqrt(jnp.mean(center * center, axis=-1, keepdims=True) + NORM_EPS)
    return center * inverse, inverse


def row_blocks(count):
    return [slice(first, first + ROW_BLOCK) for first in range(0, count, ROW_BLOCK)]


def windows(length):
    return [
        (max(0, first - LONGEST), first + QUERY_BLOCK) for first in range(0, length, QUERY_BLOCK)
    ]


def fill_bias(segments, bias, length):
    own = segments[pl.ds(lax.axis_index("seq"), 1), :].astype(FLOAT)
    turned = jnp.broadcast_to(own, (8, length)).T
    place = 0
    for index, (low, high) in enumerate(windows(length)):
        first = index * QUERY_BLOCK
        size = high - low
        keys = turned[low:high, 0:1]
        queries = own[:, first : first + QUERY_BLOCK]
        key_place = low + lax.broadcasted_iota(jnp.int32, (size, QUERY_BLOCK), 0)
        query_place = first + lax.broadcasted_iota(jnp.int32, (size, QUERY_BLOCK), 1)
        allowed = (keys == queries) & (key_place <= query_place)
        bias[place : place + size, :] = jnp.where(allowed, 0.0, -1000000000.0)
        place += size


def split_heads(pair):
    lane = lax.broadcasted_iota(jnp.int32, pair.shape, 1)
    zero = jnp.zeros_like(pair)
    return (jnp.where(lane < HEAD_DIM, pair, zero), jnp.where(lane < HEAD_DIM, zero, pair))


def attend_forward(counts, splits, *refs):
    segments, tokens, norms, shifts, wq_ref, wk_ref, wv_ref = refs[0:7]
    q_ref, k_ref, v_ref, c_ref, lse_ref = refs[10:15]
    fulls, bias, low_one, send_sem, recv_sem = refs[15:18], *refs[18:]
    length = q_ref.shape[0]
    here = Here(*counts)
    slots = Slots(send_sem, recv_sem)
    gathers = gathers_of(here, slots, fulls, splits)

    def begin():
        greet(here.near_peers())
        begin_all(gathers)

    timed, late = [(0, begin)], []
    weight = (1 << here.seq_bits) - 1
    for stage in range(1, here.seq_bits + 1):
        low, high = (1 << stage - 1) - 1, (1 << stage) - 1
        timed += evenly(follows(gathers, stage), 22 * low / weight + 2 + stage, 22 * high / weight + 1.5)
    late += follows(gathers, here.seq_bits + 1)
    blocks = windows(length)
    beside = Beside(timed, late, HEADS // 2 * len(blocks))

    @pl.when(pl.program_id(0) == 0)
    def _():
        beside.point(0, len(blocks), first=True)
        fill_bias(segments, bias, length)
        for rows in row_blocks(length):
            normed, _ = norm_parts(tokens[rows, :].astype(FLOAT))
            low_one[rows, :] = (normed * norms[0:1, :] + norms[1:2, :]).astype(BRAIN)

    lanes = 2 * HEAD_DIM
    joined = jnp.concatenate([wq_ref[...], wk_ref[...], wv_ref[...]], axis=1)
    for rows in row_blocks(length):
        projected = matmul(low_one[rows, :], joined)
        q_ref[rows, :] = (projected[:, :lanes] + shifts[4:5, :]).astype(BRAIN)
        k_ref[rows, :] = projected[:, lanes : 2 * lanes].astype(BRAIN)
        v_ref[rows, :] = (projected[:, 2 * lanes :] + shifts[5:6, :]).astype(BRAIN)
    v_turned = v_ref[...].T
    place = 0
    for index, (low, high) in enumerate(blocks):
        beside.point(index, len(blocks), first=False)
        first = index * QUERY_BLOCK
        size = high - low
        queries = split_heads(q_ref[first : first + QUERY_BLOCK, :] * HEAD_DIM ** (-0.5))
        keys = k_ref[low:high, :]
        blocked = bias[place : place + size, :]
        parts = []
        for head in range(2):
            scores = times_transposed(keys, queries[head]) + blocked
            peak = jnp.max(scores, axis=0, keepdims=True)
            probs = jnp.exp(scores - peak)
            total = jnp.sum(probs, axis=0, keepdims=True)
            probs = (probs * (1.0 / total)).astype(BRAIN)
            lse_ref[0, head : head + 1, first : first + QUERY_BLOCK] = peak + jnp.log(total)
            turned = v_turned[head * HEAD_DIM : (head + 1) * HEAD_DIM, low:high]
            parts.append(matmul(turned, probs))
        context = jnp.concatenate(parts, axis=0).T
        c_ref[first : first + QUERY_BLOCK, :] = context.astype(BRAIN)
        place += size

    @pl.when(pl.program_id(0) == HEADS // 2 - 1)
    def _():
        beside.rest()
        drain_all(gathers)


class Beside:
    def __init__(self, timed, late, points):
        self.at, self.late = {}, late
        for time, call in timed:
            self.at.setdefault(int(time * points / 24), []).append(call)

    def point(self, index, per_step, first):
        for point, calls in self.at.items():
            if point % per_step == index and first == (point == 0):

                @pl.when(pl.program_id(0) == point // per_step)
                def _(calls=calls):
                    for call in calls:
                        call()

    def rest(self):
        for call in self.late:
            call()


def attend_backward(counts, splits, *refs):
    refs = (None, *refs)
    segments, q_ref, k_ref, v_ref, g_ref, lse_ref = refs[1:7]
    tokens, norms, resid_grad, wq_ref, wk_ref, wv_ref = refs[7:13]
    grads, gq_ref, gk_ref, gv_ref, shift_ref, sum_ref, input_ref = refs[13:16], *refs[16:22]
    share, partials, bias, key_sum, value_sum = refs[22], refs[23:25], *refs[25:28]
    low_turned, total, joined, buffers = *refs[28:31], refs[31:40]
    first_partial, arrived, send_sem, recv_sem, own_sem = refs[40:]
    partials = (first_partial, *partials)
    length = q_ref.shape[0]
    pair = pl.program_id(0)
    here = Here(*counts)
    slots = Slots(send_sem, recv_sem)
    scatters, loads = scatters_of(here, slots, grads, buffers, partials, own_sem, splits)

    def begin():
        for load in loads:
            load().start()
        greet(here.near_peers())
        begin_all(scatters)

    last = ChipSum(here, slots, first_partial, arrived, share, 0)
    early = len(parts_of(share.shape, splits[0]))
    ahead, behind = scatters[:early], scatters[early:]
    stages = scatters[0].stages
    calls = []
    for stage in range(1, stages + 2):
        if stage <= stages:
            calls += follows(ahead, stage)
        if stage == stages:
            calls.append(lambda: last.start(0))
        if stage > 1:
            calls += follows(behind, stage - 1)
    timed = evenly(calls, 1, 21)
    if len(calls) == 16:
        times = (1, 2, 4, 7, 6, 8, 9, 10, 12, 12, 13, 15, 16, 18, 20, 21)
        timed = list(zip(times, calls))
    blocks = windows(length)
    beside = Beside([(0, begin)] + timed, [lambda: last.finish(0)], HEADS // 2 * len(blocks))

    @pl.when(pair == 0)
    def _():
        beside.point(0, len(blocks), first=True)
        fill_bias(segments, bias, length)
        for rows in row_blocks(length):
            normed, _ = norm_parts(tokens[rows, :].astype(FLOAT))
            low_turned[:, rows] = (normed * norms[0:1, :] + norms[1:2, :]).astype(BRAIN).T
        total[...] = jnp.zeros_like(total)

    key_sum[...] = jnp.zeros_like(key_sum)
    value_sum[...] = jnp.zeros_like(value_sum)
    k_turned = k_ref[...].T
    lanes = 2 * HEAD_DIM
    place = 0
    for index, (low, high) in enumerate(blocks):
        beside.point(index, len(blocks), first=False)
        first = index * QUERY_BLOCK
        size = high - low
        rows = slice(first, first + QUERY_BLOCK)
        queries = split_heads(q_ref[rows, :] * HEAD_DIM ** (-0.5))
        grads = split_heads(g_ref[rows, :])
        keys = k_ref[low:high, :]
        values = v_ref[low:high, :]
        blocked = bias[place : place + size, :]
        all_probs = []
        all_scores = []
        parts = []
        for head in range(2):
            scores = times_transposed(keys, queries[head]) + blocked
            probs = jnp.exp(scores - lse_ref[0, head : head + 1, rows])
            prob_grad = times_transposed(values, grads[head])
            row_dot = jnp.sum(probs * prob_grad, axis=0, keepdims=True)
            score_grad = (probs * (prob_grad - row_dot)).astype(BRAIN)
            all_probs.append(probs.astype(BRAIN))
            all_scores.append(score_grad)
            turned = k_turned[head * HEAD_DIM : (head + 1) * HEAD_DIM, low:high]
            parts.append(matmul(turned, score_grad))
        query_grad = jnp.concatenate(parts, axis=0).T * HEAD_DIM ** (-0.5)
        joined[rows, :lanes] = query_grad.astype(BRAIN)
        value_sum[low:high, :] += matmul(
            jnp.concatenate(all_probs, axis=1), jnp.concatenate(grads, axis=0)
        )
        key_sum[low:high, :] += matmul(
            jnp.concatenate(all_scores, axis=1), jnp.concatenate(queries, axis=0)
        )
        place += size
    joined[:, lanes : 2 * lanes] = key_sum[...].astype(BRAIN)
    joined[:, 2 * lanes :] = value_sum[...].astype(BRAIN)
    weight = jnp.concatenate([wq_ref[...], wk_ref[...], wv_ref[...]], axis=1)
    sums = jnp.zeros((1, 3 * lanes), FLOAT)
    for rows in row_blocks(length):
        part = joined[rows, :]
        total[rows, :] += times_transposed(part, weight)
        sums = sums + jnp.sum(part.astype(FLOAT), axis=0, keepdims=True)
    found = matmul(low_turned[...], joined[...]).astype(BRAIN)
    gq_ref[...] = found[:, :lanes]
    gk_ref[...] = found[:, lanes : 2 * lanes]
    gv_ref[...] = found[:, 2 * lanes :]
    shift_ref[0:1, :] = sums[:, :lanes]
    shift_ref[1:2, :] = sums[:, 2 * lanes :]
    shift_ref[2:8, :] = jnp.zeros((6, lanes), FLOAT)

    @pl.when(pair == HEADS // 2 - 1)
    def _():
        gains = jnp.zeros((1, total.shape[1]), FLOAT)
        moves = jnp.zeros((1, total.shape[1]), FLOAT)
        for rows in row_blocks(length):
            normed, inverse = norm_parts(tokens[rows, :].astype(FLOAT))
            upstream = total[rows, :]
            scaled = upstream * norms[0:1, :]
            centered = scaled - jnp.mean(scaled, axis=-1, keepdims=True)
            inward = centered - normed * jnp.mean(scaled * normed, axis=-1, keepdims=True)
            input_ref[rows, :] = (resid_grad[rows, :] + inverse * inward).astype(BRAIN)
            gains = gains + jnp.sum(upstream * normed, axis=0, keepdims=True)
            moves = moves + jnp.sum(upstream, axis=0, keepdims=True)
        sum_ref[0:1, :] = gains
        sum_ref[1:2, :] = moves
        sum_ref[2:8, :] = jnp.zeros((6, total.shape[1]), FLOAT)

    @pl.when(pair == HEADS // 2 - 1)
    def _():
        beside.rest()
        drain_all(scatters + [last])


def once(shape):
    return pl.BlockSpec(shape, lambda *_: (0,) * len(shape), pipeline_mode=pl.Buffered(1))


def pair_specs(rows, length):
    lanes, width = 2 * HEAD_DIM, HEADS * HEAD_DIM
    pairs = HEADS // 2
    segs = [once((rows, length))]
    plain = pl.BlockSpec((length, lanes), lambda j: (0, j))
    lse = pl.BlockSpec((1, 8, length), lambda j: (j, 0, 0))
    weights = [pl.BlockSpec((width, lanes), lambda j, at=at: (0, at * pairs + j)) for at in range(3)]
    shifts = pl.BlockSpec((8, lanes), lambda j: (0, j))
    bias = pltpu.VMEM((sum(high - low for low, high in windows(length)), QUERY_BLOCK), FLOAT)
    return segs, plain, lse, weights, shifts, bias


def attention_forward(segments, tokens, vectors, full_qkv, fulls, counts):
    length, width = tokens.shape
    segs, plain, lse, weights, shifts, bias = pair_specs(segments.shape[0], length)
    splits = [False] + [True] * (len(fulls) - 1)
    slots = piece_count([full.shape[-2:] for full in fulls], splits) * counts[1]
    return pl.pallas_call(
        functools.partial(attend_forward, counts, splits),
        grid=(HEADS // 2,),
        in_specs=segs
        + [once((length, width)), once((8, width)), shifts]
        + weights
        + [ANYWHERE] * 3,
        out_specs=[plain] * 4 + [lse] + [ANYWHERE] * 3,
        out_shape=[jax.ShapeDtypeStruct((length, width), BRAIN)] * 4
        + [jax.ShapeDtypeStruct((HEADS // 2, 8, length), FLOAT)]
        + [jax.ShapeDtypeStruct(full.shape, full.dtype) for full in fulls],
        input_output_aliases={7 + index: 5 + index for index in range(len(fulls))},
        scratch_shapes=[
            bias,
            pltpu.VMEM((length, width), BRAIN),
            pltpu.SemaphoreType.DMA((slots,)),
            pltpu.SemaphoreType.DMA((slots,)),
        ],
        name="attend_forward",
        compiler_params=pltpu.CompilerParams(
            collective_id=1, has_side_effects=True, vmem_limit_bytes=63 * 1024 * 1024
        ),
    )(
        segments,
        tokens,
        vectors,
        vectors,
        full_qkv,
        full_qkv,
        full_qkv,
        *fulls,
    )


def attention_backward(
    segments, heads, context_grad, lse_rows, tokens, vectors, resid_grad, full_qkv, grads, shapes, counts
):
    length, width = tokens.shape
    lanes = 2 * HEAD_DIM
    segs, plain, lse, weights, shifts, bias = pair_specs(segments.shape[0], length)
    column = pl.BlockSpec((width, lanes), lambda j: (0, j))
    splits = [True] * (len(shapes) - 1) + [False]
    half_count = counts[0] // 2
    slots = piece_count(shapes, splits) * counts[1] + half_count - 1
    partials = [jax.ShapeDtypeStruct((half_count,) + shape, BRAIN) for shape in shapes[1:]]
    return pl.pallas_call(
        functools.partial(attend_backward, counts, splits),
        grid=(HEADS // 2,),
        in_specs=segs
        + [plain] * 4
        + [lse, once((length, width)), once((8, width)), once((length, width))]
        + weights
        + [ANYWHERE] * 3,
        out_specs=[column] * 3 + [shifts, once((8, width)), once((length, width))] + [WHOLE] * 3,
        out_shape=[jax.ShapeDtypeStruct((width, width), BRAIN)] * 3
        + [jax.ShapeDtypeStruct((8, width), FLOAT)] * 2
        + [jax.ShapeDtypeStruct((length, width), BRAIN), jax.ShapeDtypeStruct(shapes[0], FLOAT)]
        + partials,
        scratch_shapes=[
            bias,
            pltpu.VMEM((length, lanes), FLOAT),
            pltpu.VMEM((length, lanes), FLOAT),
            pltpu.VMEM((width, length), BRAIN),
            pltpu.VMEM((length, width), FLOAT),
            pltpu.VMEM((length, 3 * lanes), BRAIN),
        ]
        + scatter_buffers(shapes, counts)
        + [
            pltpu.VMEM((half_count,) + shapes[0], BRAIN),
            pltpu.VMEM((half_count - 1,) + shapes[0], BRAIN),
            pltpu.SemaphoreType.DMA((slots,)),
            pltpu.SemaphoreType.DMA((slots,)),
            pltpu.SemaphoreType.DMA((len(shapes),)),
        ],
        name="attend_backward",
        compiler_params=pltpu.CompilerParams(
            collective_id=2, has_side_effects=True, vmem_limit_bytes=63 * 1024 * 1024
        ),
    )(
        segments,
        *heads,
        context_grad,
        lse_rows,
        tokens,
        vectors,
        resid_grad,
        full_qkv,
        full_qkv,
        full_qkv,
        *scatter_views(grads, shapes, counts),
    )


MESH = pl.DeviceIdType.MESH
ANYWHERE = pl.BlockSpec(memory_space=pl.ANY)
WHOLE = pl.BlockSpec(memory_space=pltpu.VMEM)


def bits_of(count):
    return count.bit_length() - 1


def flipped(value, bit):
    step = 1 << bit
    return value + step * (1 - 2 * lax.rem(lax.div(value, step), 2))


def rounded_down(value, bit):
    return lax.div(value, 1 << bit) * (1 << bit)


def spread(value, bit, total):
    step = 1 << (bit + 1)
    return [lax.rem(value, step) + step * turn for turn in range(1 << (total - 1 - bit))]


class Here:
    def __init__(self, dp_count, seq_count):
        self.dp_count, self.seq_count = dp_count, seq_count
        self.half_count = dp_count // 2
        self.seq_bits = bits_of(seq_count)
        self.place, self.line = lax.axis_index("dp"), lax.axis_index("seq")
        self.chip, self.core = lax.div(self.place, 2), lax.rem(self.place, 2)

    def core_peer(self):
        return {"dp": flipped(self.place, 0)}

    def line_peer(self, bit):
        return {"seq": flipped(self.line, bit)}

    def other_lines(self):
        return [lax.rem(self.line + turn, self.seq_count) for turn in range(1, self.seq_count)]

    def other_chips(self):
        return [lax.rem(self.chip + turn, self.half_count) for turn in range(1, self.half_count)]

    def chip_peers(self):
        return [{"dp": 2 * chip + self.core} for chip in self.other_chips()]

    def near_peers(self):
        peers = [self.core_peer()] + self.chip_peers()
        return peers + [{"seq": line} for line in self.other_lines()]

    def all_peers(self):
        peers = [{"dp": lax.rem(self.place + turn, self.dp_count)} for turn in range(1, self.dp_count)]
        return peers + [{"seq": line} for line in self.other_lines()]


def greet(peers):
    barrier = pltpu.get_barrier_semaphore()
    for peer in peers:
        pl.semaphore_signal(barrier, inc=1, device_id=peer, device_id_type=MESH)
    pl.semaphore_wait(barrier, len(peers))


class Slots:
    def __init__(self, send_sem, recv_sem):
        self.send_sem, self.recv_sem, self.used = send_sem, recv_sem, 0

    def take(self, count):
        first = self.used
        self.used += count
        return first

    def copy(self, slot, source, target, peer):
        return pltpu.make_async_remote_copy(
            source,
            target,
            self.send_sem.at[slot],
            self.recv_sem.at[slot],
            device_id=peer,
            device_id_type=MESH,
        )


def parts_of(shape, split):
    rows, width = shape
    tiles = width // 128
    if width % 128 or tiles < 2:
        return [[(slice(0, rows), slice(0, width), False)]]
    middle = tiles // 2 * 128
    first, second = (0, middle), (middle, width)
    every = slice(0, rows)
    if split and rows % 32 == 0:
        return [
            [(part, slice(*first), False), (part, slice(*second), True)]
            for part in (slice(0, rows // 2), slice(rows // 2, rows))
        ]
    if split and tiles >= 4:
        lists = [[], []]
        for (low, high), backwards in ((first, False), (second, True)):
            cut = low + (high - low) // 256 * 128
            lists[0].append((every, slice(low, cut), backwards))
            lists[1].append((every, slice(cut, high), backwards))
        return lists
    return [[(every, slice(*first), False), (every, slice(*second), True)]]


class Transfer:
    def start(self, stage):
        for copy in self.copies(stage):
            copy.start()

    def finish(self, stage):
        for copy in self.copies(stage):
            copy.wait_recv()
        self.use(stage)

    def use(self, stage):
        pass

    def drain(self):
        for stage in range(self.stages):
            for copy in self.copies(stage):
                copy.wait_send()


class ChipGather(Transfer):
    stages = 1

    def __init__(self, here, slots, shard, full, sem):
        self.here, self.slots, self.shard = here, slots, shard
        self.target = full.at[here.chip, here.core, here.line]
        self.own = pltpu.make_async_copy(shard, self.target, sem)
        self.first = slots.take(here.half_count - 1)

    def copies(self, stage):
        return [
            self.slots.copy(self.first + turn, self.shard, self.target, peer)
            for turn, peer in enumerate(self.here.chip_peers())
        ]


class Gather(Transfer):
    def __init__(self, here, slots, full, pieces):
        self.here, self.slots, self.full, self.pieces = here, slots, full, pieces
        self.stages = here.seq_bits + 1
        self.each = here.seq_count
        self.first = slots.take(self.each * len(pieces))

    def copies(self, stage):
        here, full = self.here, self.full
        found = []
        for index, (rows, columns, backwards) in enumerate(self.pieces):
            slot = self.first + self.each * index
            if stage == self.stages - 1:
                part = full.at[:, here.core, :, rows, columns]
                found.append(self.slots.copy(slot, part, part, here.core_peer()))
                continue
            if backwards:
                bit = here.seq_bits - 1 - stage
                slot += 1 << stage
                parts = [
                    full.at[:, here.core, at, rows, columns]
                    for at in spread(here.line, bit, here.seq_bits)
                ]
            else:
                bit = stage
                slot += 1 + bit
                block = pl.ds(rounded_down(here.line, bit), 1 << bit)
                parts = [full.at[:, here.core, block, rows, columns]]
            for turn, part in enumerate(parts):
                found.append(self.slots.copy(slot + turn, part, part, here.line_peer(bit)))
        return found


class ChipSum(Transfer):
    stages = 1

    def __init__(self, here, slots, partial, arrived, share, offset):
        self.here, self.slots, self.partial, self.arrived = here, slots, partial, arrived
        self.share, self.offset = share, offset
        self.first = slots.take(here.half_count - 1)

    def copies(self, stage):
        return [
            self.slots.copy(
                self.first + turn,
                self.partial.at[chip],
                self.arrived.at[turn],
                {"dp": 2 * chip + self.here.core},
            )
            for turn, chip in enumerate(self.here.other_chips())
        ]

    def use(self, stage):
        total = self.partial[self.here.chip].astype(FLOAT)
        for turn in range(self.here.half_count - 1):
            total = total + self.arrived[turn].astype(FLOAT)
        self.share[:, self.offset : self.offset + total.shape[1]] = total


class Scatter(Transfer):
    def __init__(self, here, slots, grad, own, from_core, from_line, partial, pieces, load):
        self.here, self.slots, self.grad, self.own = here, slots, grad, own
        self.from_core, self.from_line, self.partial = from_core, from_line, partial
        self.pieces, self.load = pieces, load
        self.stages = here.seq_bits + 1
        self.each = here.seq_count
        self.first = slots.take(self.each * len(pieces))

    def line_stage(self, stage, backwards):
        here = self.here
        if backwards:
            bit = stage - 1
            away = spread(flipped(here.line, bit), bit, here.seq_bits)
            kept = spread(here.line, bit, here.seq_bits)
        else:
            bit = here.seq_bits - stage
            away = [rounded_down(flipped(here.line, bit), bit) + at for at in range(1 << bit)]
            kept = [rounded_down(here.line, bit) + at for at in range(1 << bit)]
        base = sum(1 << (here.seq_bits - past) for past in range(1, stage))
        return bit, away, kept, base

    def copies(self, stage):
        here = self.here
        found = []
        for index, (rows, columns, backwards) in enumerate(self.pieces):
            slot = self.first + self.each * index
            if stage == 0:
                found.append(
                    self.slots.copy(
                        slot,
                        self.grad.at[:, 1 - here.core, :, rows, columns],
                        self.from_core.at[:, :, rows, columns],
                        here.core_peer(),
                    )
                )
                continue
            bit, away, _, base = self.line_stage(stage, backwards)
            for turn, at in enumerate(away):
                found.append(
                    self.slots.copy(
                        slot + 1 + base + turn,
                        self.own.at[:, at, rows, columns],
                        self.from_line.at[base + turn, :, rows, columns],
                        here.line_peer(bit),
                    )
                )
        return found

    def use(self, stage):
        here, own = self.here, self.own
        if stage == 0:
            self.load()
        for rows, columns, backwards in self.pieces:
            if stage == 0:

                def add(one, carry, rows=rows, columns=columns):
                    own[one, :, rows, columns] = (
                        own[one, :, rows, columns] + self.from_core[one, :, rows, columns]
                    )
                    return carry

                lax.fori_loop(0, here.half_count, add, 0)
                continue
            _, _, kept, base = self.line_stage(stage, backwards)
            for turn, at in enumerate(kept):
                total = own[:, at, rows, columns] + self.from_line[base + turn, :, rows, columns]
                if stage == self.stages - 1:
                    self.partial[:, rows, columns] = total
                else:
                    own[:, at, rows, columns] = total


class Exchange(Transfer):
    stages = 1

    def __init__(self, here, slots, source, target, to_rows, bounce, sem):
        self.here, self.slots, self.source, self.target = here, slots, source, target
        self.to_rows, self.bounce, self.sem = to_rows, bounce, sem
        self.first = slots.take(here.seq_count - 1)

    def ends(self, line):
        if self.to_rows:
            count = self.target.shape[0]
            block = self.source.at[pl.ds(line * count, count)]
            return block, self.target.at[:, self.here.line]
        return self.source.at[:, line], self.target.at[self.here.line]

    def copies(self, stage):
        return [
            self.slots.copy(self.first + turn, *self.ends(line), {"seq": line})
            for turn, line in enumerate(self.here.other_lines())
        ]

    def own_in(self):
        return pltpu.make_async_copy(self.ends(self.here.line)[0], self.bounce, self.sem.at[0])

    def own_out(self):
        source, target = self.ends(self.here.line)
        source = source if self.bounce is None else self.bounce
        return pltpu.make_async_copy(source, target, self.sem.at[1])

    def start(self, stage):
        if self.bounce is not None:
            self.own_in().start()
        super().start(stage)
        if self.bounce is not None:
            self.own_in().wait()
        self.own_out().start()

    def use(self, stage):
        self.own_out().wait()


def begin_all(transfers):
    for transfer in transfers:
        transfer.start(0)


def follow(transfer, stage):
    transfer.finish(stage - 1)
    if stage < transfer.stages:
        transfer.start(stage)


def follows(transfers, stage):
    return [functools.partial(follow, transfer, stage) for transfer in transfers]


def flow_of(transfers):
    calls = [functools.partial(begin_all, transfers)]
    for stage in range(1, transfers[0].stages + 1):
        calls += follows(transfers, stage)
    return calls


def evenly(calls, low, high):
    gap = (high - low) / max(len(calls) - 1, 1)
    return [(low + gap * turn, call) for turn, call in enumerate(calls)]


def drain_all(transfers):
    for transfer in transfers:
        transfer.drain()


def chip_gathers_of(here, slots, shards, fulls, sem):
    return [
        ChipGather(here, slots, shard, full, sem.at[index])
        for index, (shard, full) in enumerate(zip(shards, fulls))
    ]


def gathers_of(here, slots, fulls, splits):
    return [
        Gather(here, slots, full, pieces)
        for full, split in zip(fulls, splits)
        for pieces in parts_of(full.shape[-2:], split)
    ]


def piece_count(shapes, splits):
    return sum(len(part) for shape, split in zip(shapes, splits) for part in parts_of(shape, split))


def full_shape(shard, dp_count, seq_count):
    return jax.ShapeDtypeStruct((dp_count // 2, 2, seq_count) + shard.shape, shard.dtype)


def gather_kernel(counts, first, count, *refs):
    tokens, vectors, up_bias, weights = refs[0], refs[1], refs[2], refs[3 : 2 + count]
    token_rows, fulls = refs[2 + count], refs[3 + count : 3 + 2 * count]
    rest = refs[3 + 2 * count :]
    shards, small, bounce, send_sem, recv_sem, own_sem, move_sem = rest[:count], *rest[count:]
    small[...] = jnp.zeros_like(small)
    small[0:8, : vectors.shape[1]] = vectors[...]
    small[8:9, : up_bias.shape[1]] = up_bias[...]
    shards[0][...] = small[...].astype(BRAIN)
    for shard, weight in zip(shards[1:], weights):
        shard[...] = weight[...].astype(BRAIN)
    here = Here(*counts)
    slots = Slots(send_sem, recv_sem)
    chips = chip_gathers_of(here, slots, shards, fulls, own_sem)
    move = Exchange(here, slots, tokens, token_rows, True, bounce, move_sem)
    gathers = gathers_of(here, slots, fulls[:first], [False] + [True] * (first - 1))
    flow = flow_of(gathers)
    greet(here.near_peers())
    for chip in chips[:first]:
        chip.start(0)
    move.start(0)
    for chip in chips[first:]:
        chip.start(0)
    for chip in chips:
        chip.own.start()
    for chip in chips[:first]:
        chip.own.wait()
        chip.finish(0)
    for call in flow:
        call()
    move.finish(0)
    for chip in chips[first:]:
        chip.own.wait()
        chip.finish(0)
    drain_all(chips + gathers + [move])


def gather_first(tokens, vectors, up_bias, weights, first, counts):
    dp_count, seq_count = counts
    row_count, pos_count, width = tokens.shape
    rows = row_count // seq_count
    shards = [jax.ShapeDtypeStruct(shape, BRAIN) for shape in [(16, 128)] + [w.shape for w in weights]]
    pieces = piece_count([shard.shape for shard in shards[:first]], [False] + [True] * (first - 1))
    slots = len(shards) * (dp_count // 2 - 1) + pieces * seq_count + seq_count - 1
    return pl.pallas_call(
        functools.partial(gather_kernel, counts, first, len(shards)),
        out_shape=[jax.ShapeDtypeStruct((rows, seq_count, pos_count, width), tokens.dtype)]
        + [full_shape(shard, *counts) for shard in shards],
        in_specs=[ANYWHERE] + [WHOLE] * (2 + len(weights)),
        out_specs=[ANYWHERE] * (1 + len(shards)),
        scratch_shapes=[pltpu.VMEM(shard.shape, BRAIN) for shard in shards]
        + [
            pltpu.VMEM((16, 128), FLOAT),
            pltpu.VMEM((rows, pos_count, width), tokens.dtype),
            pltpu.SemaphoreType.DMA((slots,)),
            pltpu.SemaphoreType.DMA((slots,)),
            pltpu.SemaphoreType.DMA((len(shards),)),
            pltpu.SemaphoreType.DMA((2,)),
        ],
        name="gather_first",
        compiler_params=pltpu.CompilerParams(
            collective_id=0, has_side_effects=True, vmem_limit_bytes=63 * 1024 * 1024
        ),
    )(tokens, vectors, up_bias, *weights)


HIDDEN_BLOCK = 512
GELU_SCALE = 0.7978845608028654
GELU_CUBE = 0.044715


def gelu_both(values):
    square = values * values
    turned = jnp.tanh(GELU_SCALE * values * (1.0 + GELU_CUBE * square))
    half = 0.5 + 0.5 * turned
    inner = GELU_SCALE * (1.0 + 3.0 * GELU_CUBE * square)
    return values * half, half + 0.5 * values * (1.0 - turned * turned) * inner


def forward_start(context, tokens, w_out, vectors, resid, low_two, low_turned):
    for rows in row_blocks(resid.shape[0]):
        values = tokens[rows, :].astype(FLOAT) + (matmul(context[rows, :], w_out[...]) + vectors[6:7, :])
        resid[rows, :] = values
        normed, _ = norm_parts(values)
        low = (normed * vectors[2:3, :] + vectors[3:4, :]).astype(BRAIN)
        low_two[rows, :] = low
        low_turned[:, rows] = low.T


def backward_end(
    context, w_out, vectors, resid, total, back, gc_ref, gr_ref, gwo_ref, sum_ref, low_turned
):
    width = resid.shape[1]
    sums = [jnp.zeros((1, width), FLOAT) for _ in range(4)]
    for rows in row_blocks(resid.shape[0]):
        normed, inverse = norm_parts(resid[rows, :])
        upstream = total[rows, :]
        given = back(rows).astype(FLOAT)
        scaled = upstream * vectors[2:3, :]
        centered = scaled - jnp.mean(scaled, axis=-1, keepdims=True)
        inward = centered - normed * jnp.mean(scaled * normed, axis=-1, keepdims=True)
        grad = given + inverse * inward
        low = grad.astype(BRAIN)
        gr_ref[rows, :] = grad
        gc_ref[rows, :] = times_transposed(low, w_out[...]).astype(BRAIN)
        low_turned[:, rows] = context[rows, :].T
        total[rows, :] = low.astype(FLOAT)
        for index, values in enumerate((upstream * normed, upstream, low.astype(FLOAT), given)):
            sums[index] = sums[index] + jnp.sum(values, axis=0, keepdims=True)
    for index in range(4):
        sum_ref[index : index + 1, :] = sums[index]
    sum_ref[4:8, :] = jnp.zeros((4, width), FLOAT)
    gwo_ref[...] = matmul(low_turned[...], total[...].astype(BRAIN)).astype(BRAIN)


def mlp_kernel(counts, *refs):
    context, tokens, w_out, w_up, w_down, vectors, up_shift, cotangent = refs[0:8]
    gup_ref, gdown_ref, gub_ref, gwo_ref, gc_ref, gr_ref, sum_ref, mixed = refs[8:16]
    acts, slopes, low_two, low_turned, resid, total, hidden, back, mixed_rows = refs[16:25]
    send_sem, recv_sem, move_sem = refs[25:28]
    here = Here(*counts)
    slots = Slots(send_sem, recv_sem)
    arrive = Exchange(here, slots, cotangent, back, True, None, move_sem.at[pl.ds(0, 2)])
    leave = Exchange(here, slots, mixed_rows, mixed, False, None, move_sem.at[pl.ds(2, 2)])
    step = pl.program_id(0)
    half = pl.num_programs(0) // 2
    count = resid.shape[0]
    pos_count = back.shape[2]

    def back_rows(rows):
        parts = []
        for first in range(rows.start, rows.stop, pos_count):
            size = min(pos_count, rows.stop - first)
            row, rest = divmod(first, pos_count * counts[1])
            line, offset = divmod(rest, pos_count)
            parts.append(back[row, line, offset : offset + size, :])
        return parts[0] if len(parts) == 1 else jnp.concatenate(parts, axis=0)

    @pl.when(step == 0)
    def _():
        greet(here.near_peers())
        arrive.start(0)
        forward_start(context, tokens, w_out, vectors, resid, low_two, low_turned)
        total[...] = jnp.zeros_like(total)

    @pl.when(step < half)
    def _():
        for rows in row_blocks(count):
            values = matmul(low_two[rows, :], w_up[...]) + up_shift[...]
            act, slope = gelu_both(values)
            low = act.astype(BRAIN)
            acts[step, rows, :] = low
            slopes[step, rows, :] = slope
            total[rows, :] += matmul(low, w_down[...])

    @pl.when(step == half)
    def _():
        for first in range(0, count, pos_count):
            row, line = divmod(first // pos_count, counts[1])
            rows = slice(first, first + pos_count)
            values = resid[rows, :] + (total[rows, :] + vectors[7:8, :])
            mixed_rows[row, line] = values.astype(BRAIN)
        total[...] = jnp.zeros_like(total)
        leave.start(0)
        arrive.finish(0)

    @pl.when(step >= half)
    def _():
        at = step - half
        sums = jnp.zeros((1, hidden.shape[1]), FLOAT)
        for rows in row_blocks(count):
            grad = times_transposed(back_rows(rows), w_down[...]) * slopes[at, rows, :]
            low = grad.astype(BRAIN)
            hidden[rows, :] = low
            sums = sums + jnp.sum(low.astype(FLOAT), axis=0, keepdims=True)
            total[rows, :] += times_transposed(low, w_up[...])
        gub_ref[...] = sums
        gup_ref[...] = matmul(low_turned[...], hidden[...]).astype(BRAIN)
        every = back_rows(slice(0, count))
        gdown_ref[...] = inner_rows(acts[at], every).astype(BRAIN)

    @pl.when(step == 2 * half - 1)
    def _():
        backward_end(
            context, w_out, vectors, resid, total, back_rows, gc_ref, gr_ref, gwo_ref, sum_ref, low_turned
        )
        leave.finish(0)
        drain_all([arrive, leave])


def feed_forward(context, tokens, w_out, w_up, w_down, vectors, up_shift, cotangent, counts):
    count, width = context.shape
    hidden = w_up.shape[1]
    half = hidden // HIDDEN_BLOCK
    seq_count = counts[1]
    row_count, pos_count, _ = cotangent.shape
    rows = row_count // seq_count
    later = lambda j: jnp.maximum(j - half, 0)
    around = lambda j: lax.rem(j, half)
    block = HIDDEN_BLOCK
    slots = 2 * (seq_count - 1)
    return pl.pallas_call(
        functools.partial(mlp_kernel, counts),
        grid=(2 * half,),
        in_specs=[
            once((count, width)),
            once((count, width)),
            once((width, width)),
            pl.BlockSpec((width, block), lambda j: (0, around(j))),
            pl.BlockSpec((block, width), lambda j: (around(j), 0)),
            once((8, width)),
            pl.BlockSpec((1, block), lambda j: (0, around(j))),
            ANYWHERE,
        ],
        out_specs=[
            pl.BlockSpec((width, block), lambda j: (0, later(j))),
            pl.BlockSpec((block, width), lambda j: (later(j), 0)),
            pl.BlockSpec((1, block), lambda j: (0, later(j))),
            once((width, width)),
            once((count, width)),
            once((count, width)),
            once((8, width)),
            ANYWHERE,
        ],
        out_shape=[
            jax.ShapeDtypeStruct((width, hidden), BRAIN),
            jax.ShapeDtypeStruct((hidden, width), BRAIN),
            jax.ShapeDtypeStruct((1, hidden), FLOAT),
            jax.ShapeDtypeStruct((width, width), BRAIN),
            jax.ShapeDtypeStruct((count, width), BRAIN),
            jax.ShapeDtypeStruct((count, width), FLOAT),
            jax.ShapeDtypeStruct((8, width), FLOAT),
            jax.ShapeDtypeStruct((seq_count, rows, pos_count, width), BRAIN),
        ],
        scratch_shapes=[
            pltpu.VMEM((half, count, block), BRAIN),
            pltpu.VMEM((half, count, block), FLOAT),
            pltpu.VMEM((count, width), BRAIN),
            pltpu.VMEM((width, count), BRAIN),
            pltpu.VMEM((count, width), FLOAT),
            pltpu.VMEM((count, width), FLOAT),
            pltpu.VMEM((count, block), BRAIN),
            pltpu.VMEM((rows, seq_count, pos_count, width), BRAIN),
            pltpu.VMEM((rows, seq_count, pos_count, width), BRAIN),
            pltpu.SemaphoreType.DMA((slots,)),
            pltpu.SemaphoreType.DMA((slots,)),
            pltpu.SemaphoreType.DMA((4,)),
        ],
        name="feed_forward",
        compiler_params=pltpu.CompilerParams(
            collective_id=4, has_side_effects=True, vmem_limit_bytes=63 * 1024 * 1024
        ),
    )(context, tokens, w_out, w_up, w_down, vectors, up_shift, cotangent)


def lamb_pieces(weight, first, second, grad, decay):
    first_new = BETA_ONE * first + (1.0 - BETA_ONE) * grad
    second_new = BETA_TWO * second + (1.0 - BETA_TWO) * grad * grad
    spread_out = jnp.sqrt(second_new / CORR_TWO) + ADAM_EPS
    update = first_new / CORR_ONE / spread_out + decay * weight
    return (first_new, second_new, update)


def square_sum(values):
    return jnp.sum(jnp.sum(values * values, axis=1, keepdims=True), axis=0, keepdims=True)


def picked(small, rank, vector_size, bias_size):
    width = small.shape[1]
    row = lax.broadcasted_iota(jnp.int32, (width, 128), 0)
    lane = lax.broadcasted_iota(jnp.int32, (width, 128), 1)
    dot = functools.partial(jnp.dot, precision=lax.Precision.HIGHEST, preferred_element_type=FLOAT)
    chosen = (row == lane + rank * vector_size) & (lane < vector_size)
    vector_grad = dot(small[0:8, :], jnp.where(chosen, 1.0, 0.0))[:, :vector_size]
    start = rank * bias_size
    chosen = (row == lane + lax.rem(start, width)) & (lane < bias_size)
    tail = dot(small[8:16, :], jnp.where(chosen, 1.0, 0.0))
    tail_row = lax.broadcasted_iota(jnp.int32, tail.shape, 0)
    tail = jnp.sum(jnp.where(tail_row == lax.div(start, width), tail, 0.0), axis=0, keepdims=True)
    return vector_grad, tail[:, :bias_size]


def scatters_of(here, slots, grads, buffers, partials, own_sem, splits):
    count = len(grads)
    found, loads = [], []
    for index, (grad, partial) in enumerate(zip(grads, partials)):
        own, *arrivals = buffers[index::count]
        load = lambda grad=grad, own=own, index=index: pltpu.make_async_copy(
            grad.at[:, here.core], own, own_sem.at[index]
        )
        loads.append(load)
        for order, pieces in enumerate(parts_of(grad.shape[-2:], splits[index])):
            wait = (lambda load=load: load().wait()) if order == 0 else (lambda: None)
            found.append(Scatter(here, slots, grad, own, *arrivals, partial, pieces, wait))
    return found, loads


def scatter_buffers(shapes, counts):
    half_count, seq_count = counts[0] // 2, counts[1]
    leads = [(half_count, seq_count)] * 2 + [(seq_count - 1, half_count)]
    return [pltpu.VMEM(lead + shape, BRAIN) for lead in leads for shape in shapes]


def scatter_views(grads, shapes, counts):
    lead = (counts[0] // 2, 2, counts[1])
    return [grad.reshape(lead + shape) for grad, shape in zip(grads, shapes)]


class SmallSum(Transfer):
    def __init__(self, here, small, sums, arrived, send_sem, recv_sem):
        self.slots = Slots(send_sem, recv_sem)
        self.small, self.sums, self.arrived = small, sums, arrived
        self.peers = [here.core_peer()]
        self.peers += [here.line_peer(bit) for bit in range(here.seq_bits)]
        self.peers += [{"dp": flipped(here.place, bit + 1)} for bit in range(bits_of(here.half_count))]
        self.stages = len(self.peers)

    def copies(self, stage):
        source = self.sums.at[stage - 1] if stage else self.small
        return [self.slots.copy(stage, source, self.arrived.at[stage], self.peers[stage])]

    def use(self, stage):
        before = self.sums[stage - 1] if stage else self.small[...]
        self.sums[stage] = before + self.arrived[stage]


def scatter_kernel(counts, *refs):
    parts, refs = refs[3:7], (*refs[:3], refs[-1], *refs[7:-1])
    grads, small, input_rows, partials, ready = refs[0:3], refs[3], refs[4], refs[5:7], refs[7]
    norm_sums, shift_sums, sums, hidden_sums = parts
    small[0:2, :] = norm_sums[0:2, :]
    small[2:4, :] = sums[0:2, :]
    small[4:6, :] = shift_sums[0:2, :]
    small[6:8, :] = sums[2:4, :]
    small[8:16, :] = jnp.zeros((8, small.shape[1]), FLOAT)
    for row in range(hidden_sums.shape[1] // small.shape[1]):
        columns = slice(row * small.shape[1], (row + 1) * small.shape[1])
        small[8 + row : 9 + row, :] = hidden_sums[0:1, columns]
    weights, firsts, seconds = refs[8:14], refs[14:20], refs[20:26]
    shares, norm_out, input_grad = refs[26:32], refs[32], refs[33]
    buffers, mine, arrived, bounce = refs[34:43], refs[43:46], refs[46:51], refs[51]
    small_sum, small_in, norm_mine, norm_dp, norm_line, norm_seq = refs[52:58]
    send_sem, recv_sem, own_sem, move_sem, small_send, small_recv, norm_send, norm_recv = refs[58:66]
    here = Here(*counts)
    slots = Slots(send_sem, recv_sem)
    scatters, loads = scatters_of(here, slots, grads, buffers, mine, own_sem, [False] * 3)
    early = [
        ChipSum(here, slots, partial, arrived[index], shares[index + 1], 0)
        for index, partial in enumerate(partials)
    ]
    late = [
        ChipSum(here, slots, mine[at], arrived[2 + at], shares[0], at * grads[at].shape[-1])
        for at in range(3)
    ]
    move = Exchange(here, slots, input_rows, input_grad, False, bounce, move_sem)
    total = SmallSum(here, small, small_sum, small_in, small_send, small_recv)
    for load in loads:
        load().start()
    dp_peers, seq_peers = here.all_peers()[: here.dp_count - 1], here.all_peers()[here.dp_count - 1 :]
    greet(dp_peers + seq_peers)
    lane = lax.broadcasted_iota(jnp.int32, (8, 128), 1)
    row = lax.broadcasted_iota(jnp.int32, (8, 128), 0)

    def with_norms(tile, index, grad):
        decay = DECAY_RATE if index < 4 else 0.0
        weight = weights[index][...]
        update = lamb_pieces(weight, firsts[index][...], seconds[index][...], grad, decay)[2]
        at = row == min(index, 4)
        tile = jnp.where(at & (lane == 0), square_sum(weight), tile)
        return jnp.where(at & (lane == 1), square_sum(update), tile)

    total.start(0)
    begin_all(scatters + early)
    tile = jnp.zeros((8, 128), FLOAT)
    follow(total, 1)
    shares[3][...] = ready[...]
    tile = with_norms(tile, 3, ready[...])
    for stage in range(2, here.seq_bits + 1):
        follow(total, stage)
    stages = scatters[0].stages
    done = here.seq_bits
    for stage in range(1, stages + 1):
        if stage == stages:
            move.start(0)
        for index, scatter in enumerate(scatters):
            follow(scatter, stage)
            if stage == stages:
                late[index].start(0)
        if done < total.stages and stage < stages:
            done += 1
            follow(total, done)
    for stage in range(done + 1, total.stages + 1):
        follow(total, stage)
    for index, chip in enumerate(early):
        chip.finish(0)
        tile = with_norms(tile, index + 1, shares[index + 1][...])

    rank = here.place * here.seq_count + here.line
    vector_grad, bias_grad = picked(
        small_sum[total.stages - 1], rank, shares[4].shape[1], shares[5].shape[1]
    )
    shares[4][...] = vector_grad
    shares[5][...] = bias_grad
    tile = with_norms(tile, 5, bias_grad)
    for chip in late:
        chip.finish(0)
    norm_mine[0:8, :] = with_norms(tile, 0, shares[0][...])
    weight = weights[4][...]
    update = lamb_pieces(weight, firsts[4][...], seconds[4][...], vector_grad, 0.0)[2]
    weight_sq = jnp.sum(weight * weight, axis=1, keepdims=True)
    update_sq = jnp.sum(update * update, axis=1, keepdims=True)
    norm_mine[8:16, :] = jnp.where(lane == 0, weight_sq, jnp.where(lane == 1, update_sq, 0.0))

    norm_slots = Slots(norm_send, norm_recv)

    def exchange(source, held, peers, at):
        base = norm_slots.take(len(peers))
        copies = [
            norm_slots.copy(base + turn, source, held.at[at], peer) for turn, peer in enumerate(peers)
        ]
        for copy in copies:
            copy.start()
        held[at] = source[...]
        for copy in copies:
            copy.wait_recv()
        found = held[0]
        for turn in range(1, held.shape[0]):
            found = found + held[turn]
        return copies, found

    sent, found = exchange(norm_mine, norm_dp, dp_peers, here.place)
    norm_line[...] = found
    also, found = exchange(norm_line, norm_seq, seq_peers, here.line)
    norm_out[...] = found
    move.finish(0)
    for copy in sent + also:
        copy.wait_send()
    drain_all(scatters + early + late + [total, move])


def scatter_last(grads, sums, input_rows, partials, ready, weights, firsts, seconds, counts):
    dp_count, seq_count = counts
    shapes = [weight.shape for weight in weights]
    thirds = [(shapes[0][0], grad.shape[1]) for grad in grads]
    lead, small = (dp_count // 2,), (16, sums[0].shape[1])
    pieces = piece_count(thirds, [False] * 3)
    slots = pieces * seq_count + 5 * (dp_count // 2 - 1) + seq_count - 1
    stages = bits_of(dp_count) + bits_of(seq_count)
    return pl.pallas_call(
        functools.partial(scatter_kernel, counts),
        out_shape=[jax.ShapeDtypeStruct(shape, FLOAT) for shape in shapes]
        + [
            jax.ShapeDtypeStruct((16, 128), FLOAT),
            jax.ShapeDtypeStruct((seq_count,) + input_rows.shape[0:1] + input_rows.shape[2:], BRAIN),
        ],
        in_specs=[ANYWHERE] * 3 + [WHOLE] * 4 + [ANYWHERE] + [WHOLE] * 21,
        out_specs=[WHOLE] * 7 + [ANYWHERE],
        scratch_shapes=scatter_buffers(thirds, counts)
        + [pltpu.VMEM(lead + shape, BRAIN) for shape in thirds]
        + [pltpu.VMEM((lead[0] - 1,) + shape, BRAIN) for shape in shapes[1:3] + thirds]
        + [
            pltpu.VMEM(input_rows.shape[0:1] + input_rows.shape[2:], BRAIN),
            pltpu.VMEM((stages,) + small, FLOAT),
            pltpu.VMEM((stages,) + small, FLOAT),
            pltpu.VMEM((16, 128), FLOAT),
            pltpu.VMEM((dp_count, 16, 128), FLOAT),
            pltpu.VMEM((16, 128), FLOAT),
            pltpu.VMEM((seq_count, 16, 128), FLOAT),
            pltpu.SemaphoreType.DMA((slots,)),
            pltpu.SemaphoreType.DMA((slots,)),
            pltpu.SemaphoreType.DMA((3,)),
            pltpu.SemaphoreType.DMA((2,)),
            pltpu.SemaphoreType.DMA((stages,)),
            pltpu.SemaphoreType.DMA((stages,)),
            pltpu.SemaphoreType.DMA((dp_count + seq_count,)),
            pltpu.SemaphoreType.DMA((dp_count + seq_count,)),
            pltpu.VMEM(small, FLOAT),
        ],
        name="scatter_last",
        compiler_params=pltpu.CompilerParams(
            collective_id=3, has_side_effects=True, vmem_limit_bytes=60 * 1024 * 1024
        ),
    )(
        *scatter_views(grads, thirds, counts),
        *sums,
        input_rows,
        *partials,
        ready,
        *weights,
        *firsts,
        *seconds,
    )


def lamb_kernel(*refs):
    grads, norms = refs[0:6], refs[6]
    weights, firsts, seconds = refs[7:13], refs[13:19], refs[19:25]
    input_rows, refs = refs[25], refs[26:]
    grad_out, first_out, second_out, new_out = refs[0:6], refs[6:12], refs[12:18], refs[18:24]
    copy_out, input_out = refs[24:28], refs[28]
    for row in range(input_rows.shape[0]):
        input_out[row] = input_rows[row].astype(FLOAT)
    weight_norm = jnp.sqrt(norms[:, 0:1])
    scales = weight_norm / (jnp.sqrt(norms[:, 1:2]) + ADAM_EPS)
    for index in range(6):
        grad = grads[index][...]
        weight = weights[index][...]
        decay = DECAY_RATE if index < 4 else 0.0
        first_new, second_new, update = lamb_pieces(
            weight, firsts[index][...], seconds[index][...], grad, decay
        )
        scale = scales[8:16] if index == 4 else scales[min(index, 4) : min(index, 4) + 1]
        new = weight - LEARN_RATE * scale * update
        grad_out[index][...] = grad
        first_out[index][...] = first_new
        second_out[index][...] = second_new
        new_out[index][...] = new
        if index < 4:
            copy_out[index][...] = new.astype(BRAIN)


def lamb_all(grads, norms, weights, firsts, seconds, input_rows):
    vmem = pl.BlockSpec(memory_space=pltpu.VMEM)
    shapes = [jax.ShapeDtypeStruct(weight.shape, FLOAT) for weight in weights]
    copies = [jax.ShapeDtypeStruct(weight.shape, BRAIN) for weight in weights[:4]]
    return pl.pallas_call(
        lamb_kernel,
        out_shape=shapes * 4 + copies + [jax.ShapeDtypeStruct(input_rows.shape, FLOAT)],
        in_specs=[vmem] * 26,
        out_specs=[vmem] * 29,
        name="lamb_update",
        compiler_params=pltpu.CompilerParams(vmem_limit_bytes=63 * 1024 * 1024),
    )(*grads, norms, *weights, *firsts, *seconds, input_rows)


def body(
    tokens,
    cotangent,
    segment_ids,
    w_qkv,
    m_qkv,
    v_qkv,
    w_out,
    m_out,
    v_out,
    w_up,
    m_up,
    v_up,
    w_down,
    m_down,
    v_down,
    vectors,
    m_vectors,
    v_vectors,
    up_bias,
    m_up_bias,
    v_up_bias,
):
    dp_count, seq_count = lax.axis_size("dp"), lax.axis_size("seq")
    vector_size, bias_size = vectors.shape[1], up_bias.shape[0]
    counts = (dp_count, seq_count)
    token_rows, *fulls = gather_first(
        tokens, vectors, up_bias[None], [w_qkv, w_out, w_up, w_down], 2, counts
    )
    small = fulls[0].reshape(dp_count * seq_count, 16, 128)
    full_vectors = small[:, :8, :vector_size].transpose(1, 0, 2)
    vector_rows = full_vectors.reshape(8, -1).astype(FLOAT)
    up_shift = small[:, 8, :bias_size].reshape(-1).astype(FLOAT)
    as_matrix = lambda full: full.reshape(-1, full.shape[-1])
    full_qkv = as_matrix(fulls[1])

    width = tokens.shape[2]
    length = segment_ids.shape[1]
    rows = token_rows.shape[0]
    assert rows == 1
    token_rows = token_rows.reshape(length, width)
    *heads, context, lse_rows, full_out, full_up, full_down = attention_forward(
        segment_ids, token_rows, vector_rows, full_qkv, fulls[2:], counts
    )
    full_out, full_up, full_down = [as_matrix(full) for full in (full_out, full_up, full_down)]
    grad_up, grad_down, grad_up_bias, grad_out, context_grad, resid_grad, sums, mixed = feed_forward(
        context,
        token_rows,
        full_out,
        full_up,
        full_down,
        vector_rows,
        up_shift[None],
        cotangent,
        counts,
    )
    *qkv_grads, shift_sums, norm_sums, input_rows, share_down, sum_up, sum_out = attention_backward(
        segment_ids,
        heads,
        context_grad,
        lse_rows,
        token_rows,
        vector_rows,
        resid_grad,
        full_qkv,
        [grad_down, grad_up, grad_out],
        [w_down.shape, w_up.shape, w_out.shape],
        counts,
    )
    as_row = lambda value: value.reshape(1, -1)
    weights = (w_qkv, w_out, w_up, w_down, vectors, as_row(up_bias))
    firsts = (m_qkv, m_out, m_up, m_down, m_vectors, as_row(m_up_bias))
    seconds = (v_qkv, v_out, v_up, v_down, v_vectors, as_row(v_up_bias))
    *shares, norms, input_grad = scatter_last(
        qkv_grads,
        [norm_sums, shift_sums, sums, grad_up_bias],
        input_rows.reshape(rows, seq_count, length // seq_count, width),
        [sum_out, sum_up],
        share_down,
        weights,
        firsts,
        seconds,
        counts,
    )
    *results, input_grad = lamb_all(
        shares, norms, weights, firsts, seconds, input_grad.reshape(tokens.shape)
    )
    mixed = mixed.reshape(tokens.shape)
    for index in (5, 11, 17, 23):
        results[index] = results[index].reshape(-1)
    return (mixed, input_grad, *results)


def solution(mesh):
    matrix = P(("dp", "seq"), None)
    rows = P("dp", "seq", None)
    vector = P(None, ("dp", "seq"))
    bias = P(("dp", "seq"))
    six = (matrix, matrix, matrix, matrix, vector, bias)
    in_specs = (rows, rows, P("dp", None)) + tuple(spec for spec in six for _ in range(3))
    out_specs = (rows, rows) + six * 4 + (matrix,) * 4
    return jax.shard_map(body, mesh=mesh, in_specs=in_specs, out_specs=out_specs, check_vma=False)
```

```python
import functools

import jax
import jax.numpy as jnp
from jax import lax
from jax.experimental import pallas as pl
from jax.experimental.pallas import tpu as pltpu
from jax.sharding import PartitionSpec as P

HEADS = 12
HEAD_DIM = 64
LONGEST = 512
QUERY_BLOCK = 256
ROW_BLOCK = 256


BETA_ONE = 0.9
BETA_TWO = 0.999
ADAM_EPS = 1e-06
DECAY_RATE = 0.01
LEARN_RATE = 0.4
NORM_EPS = 1e-05
STEP_NUMBER = 10.0
CORR_ONE = 1.0 - BETA_ONE**STEP_NUMBER
CORR_TWO = 1.0 - BETA_TWO**STEP_NUMBER

BRAIN = jnp.bfloat16
FLOAT = jnp.float32


def matmul(left_side, right_side):
    return jnp.dot(left_side, right_side, preferred_element_type=FLOAT)


def inner_rows(left_side, right_side):
    return lax.dot_general(
        left_side, right_side, (((0,), (0,)), ((), ())), preferred_element_type=FLOAT
    )


def times_transposed(left_side, right_side):
    return lax.dot_general(
        left_side, right_side, (((1,), (1,)), ((), ())), preferred_element_type=FLOAT
    )


def norm_parts(values):
    center = values - jnp.mean(values, axis=-1, keepdims=True)
    inverse = lax.rsqrt(jnp.mean(center * center, axis=-1, keepdims=True) + NORM_EPS)
    return center * inverse, inverse


def row_blocks(count):
    return [slice(first, first + ROW_BLOCK) for first in range(0, count, ROW_BLOCK)]


def windows(length):
    return [
        (max(0, first - LONGEST), first + QUERY_BLOCK) for first in range(0, length, QUERY_BLOCK)
    ]


def fill_bias(segments, bias, length):
    own = segments[pl.ds(lax.axis_index("seq"), 1), :].astype(FLOAT)
    turned = jnp.broadcast_to(own, (8, length)).T
    place = 0
    for index, (low, high) in enumerate(windows(length)):
        first = index * QUERY_BLOCK
        size = high - low
        keys = turned[low:high, 0:1]
        queries = own[:, first : first + QUERY_BLOCK]
        key_place = low + lax.broadcasted_iota(jnp.int32, (size, QUERY_BLOCK), 0)
        query_place = first + lax.broadcasted_iota(jnp.int32, (size, QUERY_BLOCK), 1)
        allowed = (keys == queries) & (key_place <= query_place)
        bias[place : place + size, :] = jnp.where(allowed, 0.0, -1000000000.0)
        place += size


def split_heads(pair):
    lane = lax.broadcasted_iota(jnp.int32, pair.shape, 1)
    zero = jnp.zeros_like(pair)
    return (jnp.where(lane < HEAD_DIM, pair, zero), jnp.where(lane < HEAD_DIM, zero, pair))


def attend_forward(counts, splits, *refs):
    segments, tokens, norms, shifts, wq_ref, wk_ref, wv_ref = refs[0:7]
    q_ref, k_ref, v_ref, c_ref, lse_ref = refs[10:15]
    fulls, bias, low_one, send_sem, recv_sem = refs[15:18], *refs[18:]
    length = q_ref.shape[0]
    here = Here(*counts)
    slots = Slots(send_sem, recv_sem)
    gathers = gathers_of(here, slots, fulls, splits)

    def begin():
        greet(here.near_peers())
        begin_all(gathers)

    timed, late = [(0, begin)], []
    weight = (1 << here.seq_bits) - 1
    for stage in range(1, here.seq_bits + 1):
        low, high = (1 << stage - 1) - 1, (1 << stage) - 1
        timed += evenly(follows(gathers, stage), 22 * low / weight + 2 + stage, 22 * high / weight + 1.5)
    late += follows(gathers, here.seq_bits + 1)
    blocks = windows(length)
    beside = Beside(timed, late, HEADS // 2 * len(blocks))

    @pl.when(pl.program_id(0) == 0)
    def _():
        beside.point(0, len(blocks), first=True)
        fill_bias(segments, bias, length)
        for rows in row_blocks(length):
            normed, _ = norm_parts(tokens[rows, :].astype(FLOAT))
            low_one[rows, :] = (normed * norms[0:1, :] + norms[1:2, :]).astype(BRAIN)

    lanes = 2 * HEAD_DIM
    joined = jnp.concatenate([wq_ref[...], wk_ref[...], wv_ref[...]], axis=1)
    for rows in row_blocks(length):
        projected = matmul(low_one[rows, :], joined)
        q_ref[rows, :] = (projected[:, :lanes] + shifts[4:5, :]).astype(BRAIN)
        k_ref[rows, :] = projected[:, lanes : 2 * lanes].astype(BRAIN)
        v_ref[rows, :] = (projected[:, 2 * lanes :] + shifts[5:6, :]).astype(BRAIN)
    v_turned = v_ref[...].T
    place = 0
    for index, (low, high) in enumerate(blocks):
        beside.point(index, len(blocks), first=False)
        first = index * QUERY_BLOCK
        size = high - low
        queries = split_heads(q_ref[first : first + QUERY_BLOCK, :] * HEAD_DIM ** (-0.5))
        keys = k_ref[low:high, :]
        blocked = bias[place : place + size, :]
        parts = []
        for head in range(2):
            scores = times_transposed(keys, queries[head]) + blocked
            peak = jnp.max(scores, axis=0, keepdims=True)
            probs = jnp.exp(scores - peak)
            total = jnp.sum(probs, axis=0, keepdims=True)
            probs = (probs * (1.0 / total)).astype(BRAIN)
            lse_ref[0, head : head + 1, first : first + QUERY_BLOCK] = peak + jnp.log(total)
            turned = v_turned[head * HEAD_DIM : (head + 1) * HEAD_DIM, low:high]
            parts.append(matmul(turned, probs))
        context = jnp.concatenate(parts, axis=0).T
        c_ref[first : first + QUERY_BLOCK, :] = context.astype(BRAIN)
        place += size

    @pl.when(pl.program_id(0) == HEADS // 2 - 1)
    def _():
        beside.rest()
        drain_all(gathers)


class Beside:
    def __init__(self, timed, late, points):
        self.at, self.late = {}, late
        for time, call in timed:
            self.at.setdefault(int(time * points / 24), []).append(call)

    def point(self, index, per_step, first):
        for point, calls in self.at.items():
            if point % per_step == index and first == (point == 0):

                @pl.when(pl.program_id(0) == point // per_step)
                def _(calls=calls):
                    for call in calls:
                        call()

    def rest(self):
        for call in self.late:
            call()


def attend_backward(counts, splits, *refs):
    refs = (None, *refs)
    segments, q_ref, k_ref, v_ref, g_ref, lse_ref = refs[1:7]
    tokens, norms, resid_grad, wq_ref, wk_ref, wv_ref = refs[7:13]
    grads, gq_ref, gk_ref, gv_ref, shift_ref, sum_ref, input_ref = refs[13:16], *refs[16:22]
    share, partials, bias, key_sum, value_sum = refs[22], refs[23:25], *refs[25:28]
    low_turned, total, joined, buffers = *refs[28:31], refs[31:40]
    first_partial, arrived, send_sem, recv_sem, own_sem = refs[40:]
    partials = (first_partial, *partials)
    length = q_ref.shape[0]
    pair = pl.program_id(0)
    here = Here(*counts)
    slots = Slots(send_sem, recv_sem)
    scatters, loads = scatters_of(here, slots, grads, buffers, partials, own_sem, splits)

    def begin():
        for load in loads:
            load().start()
        greet(here.near_peers())
        begin_all(scatters)

    last = ChipSum(here, slots, first_partial, arrived, share, 0)
    early = len(parts_of(share.shape, splits[0]))
    ahead, behind = scatters[:early], scatters[early:]
    stages = scatters[0].stages
    calls = []
    for stage in range(1, stages + 2):
        if stage <= stages:
            calls += follows(ahead, stage)
        if stage == stages:
            calls.append(lambda: last.start(0))
        if stage > 1:
            calls += follows(behind, stage - 1)
    timed = evenly(calls, 1, 21)
    if len(calls) == 16:
        times = (2, 3, 6, 8, 5, 9, 10, 11, 13, 13, 14, 16, 17, 18, 20, 21)
        timed = list(zip(times, calls))
    blocks = windows(length)
    beside = Beside([(0, begin)] + timed, [lambda: last.finish(0)], HEADS // 2 * len(blocks))

    @pl.when(pair == 0)
    def _():
        beside.point(0, len(blocks), first=True)
        fill_bias(segments, bias, length)
        for rows in row_blocks(length):
            normed, _ = norm_parts(tokens[rows, :].astype(FLOAT))
            low_turned[:, rows] = (normed * norms[0:1, :] + norms[1:2, :]).astype(BRAIN).T
        total[...] = jnp.zeros_like(total)

    key_sum[...] = jnp.zeros_like(key_sum)
    value_sum[...] = jnp.zeros_like(value_sum)
    k_turned = k_ref[...].T
    lanes = 2 * HEAD_DIM
    place = 0
    for index, (low, high) in enumerate(blocks):
        beside.point(index, len(blocks), first=False)
        first = index * QUERY_BLOCK
        size = high - low
        rows = slice(first, first + QUERY_BLOCK)
        queries = split_heads(q_ref[rows, :] * HEAD_DIM ** (-0.5))
        grads = split_heads(g_ref[rows, :])
        keys = k_ref[low:high, :]
        values = v_ref[low:high, :]
        blocked = bias[place : place + size, :]
        all_probs = []
        all_scores = []
        parts = []
        for head in range(2):
            scores = times_transposed(keys, queries[head]) + blocked
            probs = jnp.exp(scores - lse_ref[0, head : head + 1, rows])
            prob_grad = times_transposed(values, grads[head])
            row_dot = jnp.sum(probs * prob_grad, axis=0, keepdims=True)
            score_grad = (probs * (prob_grad - row_dot)).astype(BRAIN)
            all_probs.append(probs.astype(BRAIN))
            all_scores.append(score_grad)
            turned = k_turned[head * HEAD_DIM : (head + 1) * HEAD_DIM, low:high]
            parts.append(matmul(turned, score_grad))
        query_grad = jnp.concatenate(parts, axis=0).T * HEAD_DIM ** (-0.5)
        joined[rows, :lanes] = query_grad.astype(BRAIN)
        value_sum[low:high, :] += matmul(
            jnp.concatenate(all_probs, axis=1), jnp.concatenate(grads, axis=0)
        )
        key_sum[low:high, :] += matmul(
            jnp.concatenate(all_scores, axis=1), jnp.concatenate(queries, axis=0)
        )
        place += size
    joined[:, lanes : 2 * lanes] = key_sum[...].astype(BRAIN)
    joined[:, 2 * lanes :] = value_sum[...].astype(BRAIN)
    weight = jnp.concatenate([wq_ref[...], wk_ref[...], wv_ref[...]], axis=1)
    sums = jnp.zeros((1, 3 * lanes), FLOAT)
    for rows in row_blocks(length):
        part = joined[rows, :]
        total[rows, :] += times_transposed(part, weight)
        sums = sums + jnp.sum(part.astype(FLOAT), axis=0, keepdims=True)
    found = matmul(low_turned[...], joined[...]).astype(BRAIN)
    gq_ref[...] = found[:, :lanes]
    gk_ref[...] = found[:, lanes : 2 * lanes]
    gv_ref[...] = found[:, 2 * lanes :]
    shift_ref[0:1, :] = sums[:, :lanes]
    shift_ref[1:2, :] = sums[:, 2 * lanes :]
    shift_ref[2:8, :] = jnp.zeros((6, lanes), FLOAT)

    @pl.when(pair == HEADS // 2 - 1)
    def _():
        gains = jnp.zeros((1, total.shape[1]), FLOAT)
        moves = jnp.zeros((1, total.shape[1]), FLOAT)
        for rows in row_blocks(length):
            normed, inverse = norm_parts(tokens[rows, :].astype(FLOAT))
            upstream = total[rows, :]
            scaled = upstream * norms[0:1, :]
            centered = scaled - jnp.mean(scaled, axis=-1, keepdims=True)
            inward = centered - normed * jnp.mean(scaled * normed, axis=-1, keepdims=True)
            input_ref[rows, :] = (resid_grad[rows, :] + inverse * inward).astype(BRAIN)
            gains = gains + jnp.sum(upstream * normed, axis=0, keepdims=True)
            moves = moves + jnp.sum(upstream, axis=0, keepdims=True)
        sum_ref[0:1, :] = gains
        sum_ref[1:2, :] = moves
        sum_ref[2:8, :] = jnp.zeros((6, total.shape[1]), FLOAT)

    @pl.when(pair == HEADS // 2 - 1)
    def _():
        beside.rest()
        drain_all(scatters + [last])


def once(shape):
    return pl.BlockSpec(shape, lambda *_: (0,) * len(shape), pipeline_mode=pl.Buffered(1))


def pair_specs(rows, length):
    lanes, width = 2 * HEAD_DIM, HEADS * HEAD_DIM
    pairs = HEADS // 2
    segs = [once((rows, length))]
    plain = pl.BlockSpec((length, lanes), lambda j: (0, j))
    lse = pl.BlockSpec((1, 8, length), lambda j: (j, 0, 0))
    weights = [pl.BlockSpec((width, lanes), lambda j, at=at: (0, at * pairs + j)) for at in range(3)]
    shifts = pl.BlockSpec((8, lanes), lambda j: (0, j))
    bias = pltpu.VMEM((sum(high - low for low, high in windows(length)), QUERY_BLOCK), FLOAT)
    return segs, plain, lse, weights, shifts, bias


def attention_forward(segments, tokens, vectors, full_qkv, fulls, counts):
    length, width = tokens.shape
    segs, plain, lse, weights, shifts, bias = pair_specs(segments.shape[0], length)
    splits = [False] + [True] * (len(fulls) - 1)
    slots = piece_count([full.shape[-2:] for full in fulls], splits) * counts[1]
    return pl.pallas_call(
        functools.partial(attend_forward, counts, splits),
        grid=(HEADS // 2,),
        in_specs=segs
        + [once((length, width)), once((8, width)), shifts]
        + weights
        + [ANYWHERE] * 3,
        out_specs=[plain] * 4 + [lse] + [ANYWHERE] * 3,
        out_shape=[jax.ShapeDtypeStruct((length, width), BRAIN)] * 4
        + [jax.ShapeDtypeStruct((HEADS // 2, 8, length), FLOAT)]
        + [jax.ShapeDtypeStruct(full.shape, full.dtype) for full in fulls],
        input_output_aliases={7 + index: 5 + index for index in range(len(fulls))},
        scratch_shapes=[
            bias,
            pltpu.VMEM((length, width), BRAIN),
            pltpu.SemaphoreType.DMA((slots,)),
            pltpu.SemaphoreType.DMA((slots,)),
        ],
        name="attend_forward",
        compiler_params=pltpu.CompilerParams(
            collective_id=1, has_side_effects=True, vmem_limit_bytes=63 * 1024 * 1024
        ),
    )(
        segments,
        tokens,
        vectors,
        vectors,
        full_qkv,
        full_qkv,
        full_qkv,
        *fulls,
    )


def attention_backward(
    segments, heads, context_grad, lse_rows, tokens, vectors, resid_grad, full_qkv, grads, shapes, counts
):
    length, width = tokens.shape
    lanes = 2 * HEAD_DIM
    segs, plain, lse, weights, shifts, bias = pair_specs(segments.shape[0], length)
    column = pl.BlockSpec((width, lanes), lambda j: (0, j))
    splits = [True] * (len(shapes) - 1) + [False]
    half_count = counts[0] // 2
    slots = piece_count(shapes, splits) * counts[1] + half_count - 1
    partials = [jax.ShapeDtypeStruct((half_count,) + shape, BRAIN) for shape in shapes[1:]]
    return pl.pallas_call(
        functools.partial(attend_backward, counts, splits),
        grid=(HEADS // 2,),
        in_specs=segs
        + [plain] * 4
        + [lse, once((length, width)), once((8, width)), once((length, width))]
        + weights
        + [ANYWHERE] * 3,
        out_specs=[column] * 3 + [shifts, once((8, width)), once((length, width))] + [WHOLE] * 3,
        out_shape=[jax.ShapeDtypeStruct((width, width), BRAIN)] * 3
        + [jax.ShapeDtypeStruct((8, width), FLOAT)] * 2
        + [jax.ShapeDtypeStruct((length, width), BRAIN), jax.ShapeDtypeStruct(shapes[0], FLOAT)]
        + partials,
        scratch_shapes=[
            bias,
            pltpu.VMEM((length, lanes), FLOAT),
            pltpu.VMEM((length, lanes), FLOAT),
            pltpu.VMEM((width, length), BRAIN),
            pltpu.VMEM((length, width), FLOAT),
            pltpu.VMEM((length, 3 * lanes), BRAIN),
        ]
        + scatter_buffers(shapes, counts)
        + [
            pltpu.VMEM((half_count,) + shapes[0], BRAIN),
            pltpu.VMEM((half_count - 1,) + shapes[0], BRAIN),
            pltpu.SemaphoreType.DMA((slots,)),
            pltpu.SemaphoreType.DMA((slots,)),
            pltpu.SemaphoreType.DMA((len(shapes),)),
        ],
        name="attend_backward",
        compiler_params=pltpu.CompilerParams(
            collective_id=2, has_side_effects=True, vmem_limit_bytes=63 * 1024 * 1024
        ),
    )(
        segments,
        *heads,
        context_grad,
        lse_rows,
        tokens,
        vectors,
        resid_grad,
        full_qkv,
        full_qkv,
        full_qkv,
        *scatter_views(grads, shapes, counts),
    )


MESH = pl.DeviceIdType.MESH
ANYWHERE = pl.BlockSpec(memory_space=pl.ANY)
WHOLE = pl.BlockSpec(memory_space=pltpu.VMEM)


def bits_of(count):
    return count.bit_length() - 1


def flipped(value, bit):
    step = 1 << bit
    return value + step * (1 - 2 * lax.rem(lax.div(value, step), 2))


def rounded_down(value, bit):
    return lax.div(value, 1 << bit) * (1 << bit)


def spread(value, bit, total):
    step = 1 << (bit + 1)
    return [lax.rem(value, step) + step * turn for turn in range(1 << (total - 1 - bit))]


class Here:
    def __init__(self, dp_count, seq_count):
        self.dp_count, self.seq_count = dp_count, seq_count
        self.half_count = dp_count // 2
        self.seq_bits = bits_of(seq_count)
        self.place, self.line = lax.axis_index("dp"), lax.axis_index("seq")
        self.chip, self.core = lax.div(self.place, 2), lax.rem(self.place, 2)

    def core_peer(self):
        return {"dp": flipped(self.place, 0)}

    def line_peer(self, bit):
        return {"seq": flipped(self.line, bit)}

    def other_lines(self):
        return [lax.rem(self.line + turn, self.seq_count) for turn in range(1, self.seq_count)]

    def other_chips(self):
        return [lax.rem(self.chip + turn, self.half_count) for turn in range(1, self.half_count)]

    def chip_peers(self):
        return [{"dp": 2 * chip + self.core} for chip in self.other_chips()]

    def near_peers(self):
        peers = [self.core_peer()] + self.chip_peers()
        return peers + [{"seq": line} for line in self.other_lines()]

    def all_peers(self):
        peers = [{"dp": lax.rem(self.place + turn, self.dp_count)} for turn in range(1, self.dp_count)]
        return peers + [{"seq": line} for line in self.other_lines()]


def greet(peers):
    barrier = pltpu.get_barrier_semaphore()
    for peer in peers:
        pl.semaphore_signal(barrier, inc=1, device_id=peer, device_id_type=MESH)
    pl.semaphore_wait(barrier, len(peers))


class Slots:
    def __init__(self, send_sem, recv_sem):
        self.send_sem, self.recv_sem, self.used = send_sem, recv_sem, 0

    def take(self, count):
        first = self.used
        self.used += count
        return first

    def copy(self, slot, source, target, peer):
        return pltpu.make_async_remote_copy(
            source,
            target,
            self.send_sem.at[slot],
            self.recv_sem.at[slot],
            device_id=peer,
            device_id_type=MESH,
        )


def parts_of(shape, split):
    rows, width = shape
    tiles = width // 128
    if width % 128 or tiles < 2:
        return [[(slice(0, rows), slice(0, width), False)]]
    middle = tiles // 2 * 128
    first, second = (0, middle), (middle, width)
    every = slice(0, rows)
    if split and rows % 32 == 0:
        return [
            [(part, slice(*first), False), (part, slice(*second), True)]
            for part in (slice(0, rows // 2), slice(rows // 2, rows))
        ]
    if split and tiles >= 4:
        lists = [[], []]
        for (low, high), backwards in ((first, False), (second, True)):
            cut = low + (high - low) // 256 * 128
            lists[0].append((every, slice(low, cut), backwards))
            lists[1].append((every, slice(cut, high), backwards))
        return lists
    return [[(every, slice(*first), False), (every, slice(*second), True)]]


class Transfer:
    def start(self, stage):
        for copy in self.copies(stage):
            copy.start()

    def finish(self, stage):
        for copy in self.copies(stage):
            copy.wait_recv()
        self.use(stage)

    def use(self, stage):
        pass

    def drain(self):
        for stage in range(self.stages):
            for copy in self.copies(stage):
                copy.wait_send()


class ChipGather(Transfer):
    stages = 1

    def __init__(self, here, slots, shard, full, sem):
        self.here, self.slots, self.shard = here, slots, shard
        self.target = full.at[here.chip, here.core, here.line]
        self.own = pltpu.make_async_copy(shard, self.target, sem)
        self.first = slots.take(here.half_count - 1)

    def copies(self, stage):
        return [
            self.slots.copy(self.first + turn, self.shard, self.target, peer)
            for turn, peer in enumerate(self.here.chip_peers())
        ]


class Gather(Transfer):
    def __init__(self, here, slots, full, pieces):
        self.here, self.slots, self.full, self.pieces = here, slots, full, pieces
        self.stages = here.seq_bits + 1
        self.each = here.seq_count
        self.first = slots.take(self.each * len(pieces))

    def copies(self, stage):
        here, full = self.here, self.full
        found = []
        for index, (rows, columns, backwards) in enumerate(self.pieces):
            slot = self.first + self.each * index
            if stage == self.stages - 1:
                part = full.at[:, here.core, :, rows, columns]
                found.append(self.slots.copy(slot, part, part, here.core_peer()))
                continue
            if backwards:
                bit = here.seq_bits - 1 - stage
                slot += 1 << stage
                parts = [
                    full.at[:, here.core, at, rows, columns]
                    for at in spread(here.line, bit, here.seq_bits)
                ]
            else:
                bit = stage
                slot += 1 + bit
                block = pl.ds(rounded_down(here.line, bit), 1 << bit)
                parts = [full.at[:, here.core, block, rows, columns]]
            for turn, part in enumerate(parts):
                found.append(self.slots.copy(slot + turn, part, part, here.line_peer(bit)))
        return found


class ChipSum(Transfer):
    stages = 1

    def __init__(self, here, slots, partial, arrived, share, offset):
        self.here, self.slots, self.partial, self.arrived = here, slots, partial, arrived
        self.share, self.offset = share, offset
        self.first = slots.take(here.half_count - 1)

    def copies(self, stage):
        return [
            self.slots.copy(
                self.first + turn,
                self.partial.at[chip],
                self.arrived.at[turn],
                {"dp": 2 * chip + self.here.core},
            )
            for turn, chip in enumerate(self.here.other_chips())
        ]

    def use(self, stage):
        total = self.partial[self.here.chip].astype(FLOAT)
        for turn in range(self.here.half_count - 1):
            total = total + self.arrived[turn].astype(FLOAT)
        self.share[:, self.offset : self.offset + total.shape[1]] = total


class Scatter(Transfer):
    def __init__(self, here, slots, grad, own, from_core, from_line, partial, pieces, load):
        self.here, self.slots, self.grad, self.own = here, slots, grad, own
        self.from_core, self.from_line, self.partial = from_core, from_line, partial
        self.pieces, self.load = pieces, load
        self.stages = here.seq_bits + 1
        self.each = here.seq_count
        self.first = slots.take(self.each * len(pieces))

    def line_stage(self, stage, backwards):
        here = self.here
        if backwards:
            bit = stage - 1
            away = spread(flipped(here.line, bit), bit, here.seq_bits)
            kept = spread(here.line, bit, here.seq_bits)
        else:
            bit = here.seq_bits - stage
            away = [rounded_down(flipped(here.line, bit), bit) + at for at in range(1 << bit)]
            kept = [rounded_down(here.line, bit) + at for at in range(1 << bit)]
        base = sum(1 << (here.seq_bits - past) for past in range(1, stage))
        return bit, away, kept, base

    def copies(self, stage):
        here = self.here
        found = []
        for index, (rows, columns, backwards) in enumerate(self.pieces):
            slot = self.first + self.each * index
            if stage == 0:
                found.append(
                    self.slots.copy(
                        slot,
                        self.grad.at[:, 1 - here.core, :, rows, columns],
                        self.from_core.at[:, :, rows, columns],
                        here.core_peer(),
                    )
                )
                continue
            bit, away, _, base = self.line_stage(stage, backwards)
            for turn, at in enumerate(away):
                found.append(
                    self.slots.copy(
                        slot + 1 + base + turn,
                        self.own.at[:, at, rows, columns],
                        self.from_line.at[base + turn, :, rows, columns],
                        here.line_peer(bit),
                    )
                )
        return found

    def use(self, stage):
        here, own = self.here, self.own
        if stage == 0:
            self.load()
        for rows, columns, backwards in self.pieces:
            if stage == 0:

                def add(one, carry, rows=rows, columns=columns):
                    own[one, :, rows, columns] = (
                        own[one, :, rows, columns] + self.from_core[one, :, rows, columns]
                    )
                    return carry

                lax.fori_loop(0, here.half_count, add, 0)
                continue
            _, _, kept, base = self.line_stage(stage, backwards)
            for turn, at in enumerate(kept):
                total = own[:, at, rows, columns] + self.from_line[base + turn, :, rows, columns]
                if stage == self.stages - 1:
                    self.partial[:, rows, columns] = total
                else:
                    own[:, at, rows, columns] = total


class Exchange(Transfer):
    stages = 1

    def __init__(self, here, slots, source, target, to_rows, bounce, sem):
        self.here, self.slots, self.source, self.target = here, slots, source, target
        self.to_rows, self.bounce, self.sem = to_rows, bounce, sem
        self.first = slots.take(here.seq_count - 1)

    def ends(self, line):
        if self.to_rows:
            count = self.target.shape[0]
            block = self.source.at[pl.ds(line * count, count)]
            return block, self.target.at[:, self.here.line]
        return self.source.at[:, line], self.target.at[self.here.line]

    def copies(self, stage):
        return [
            self.slots.copy(self.first + turn, *self.ends(line), {"seq": line})
            for turn, line in enumerate(self.here.other_lines())
        ]

    def own_in(self):
        return pltpu.make_async_copy(self.ends(self.here.line)[0], self.bounce, self.sem.at[0])

    def own_out(self):
        source, target = self.ends(self.here.line)
        source = source if self.bounce is None else self.bounce
        return pltpu.make_async_copy(source, target, self.sem.at[1])

    def start(self, stage):
        if self.bounce is not None:
            self.own_in().start()
        super().start(stage)
        if self.bounce is not None:
            self.own_in().wait()
        self.own_out().start()

    def use(self, stage):
        self.own_out().wait()


def begin_all(transfers):
    for transfer in transfers:
        transfer.start(0)


def follow(transfer, stage):
    transfer.finish(stage - 1)
    if stage < transfer.stages:
        transfer.start(stage)


def follows(transfers, stage):
    return [functools.partial(follow, transfer, stage) for transfer in transfers]


def flow_of(transfers):
    calls = [functools.partial(begin_all, transfers)]
    for stage in range(1, transfers[0].stages + 1):
        calls += follows(transfers, stage)
    return calls


def evenly(calls, low, high):
    gap = (high - low) / max(len(calls) - 1, 1)
    return [(low + gap * turn, call) for turn, call in enumerate(calls)]


def drain_all(transfers):
    for transfer in transfers:
        transfer.drain()


def chip_gathers_of(here, slots, shards, fulls, sem):
    return [
        ChipGather(here, slots, shard, full, sem.at[index])
        for index, (shard, full) in enumerate(zip(shards, fulls))
    ]


def gathers_of(here, slots, fulls, splits):
    return [
        Gather(here, slots, full, pieces)
        for full, split in zip(fulls, splits)
        for pieces in parts_of(full.shape[-2:], split)
    ]


def piece_count(shapes, splits):
    return sum(len(part) for shape, split in zip(shapes, splits) for part in parts_of(shape, split))


def full_shape(shard, dp_count, seq_count):
    return jax.ShapeDtypeStruct((dp_count // 2, 2, seq_count) + shard.shape, shard.dtype)


def gather_kernel(counts, first, count, *refs):
    tokens, vectors, up_bias, weights = refs[0], refs[1], refs[2], refs[3 : 2 + count]
    token_rows, fulls = refs[2 + count], refs[3 + count : 3 + 2 * count]
    rest = refs[3 + 2 * count :]
    shards, small, bounce, send_sem, recv_sem, own_sem, move_sem = rest[:count], *rest[count:]
    small[...] = jnp.zeros_like(small)
    small[0:8, : vectors.shape[1]] = vectors[...]
    small[8:9, : up_bias.shape[1]] = up_bias[...]
    shards[0][...] = small[...].astype(BRAIN)
    for shard, weight in zip(shards[1:], weights):
        shard[...] = weight[...].astype(BRAIN)
    here = Here(*counts)
    slots = Slots(send_sem, recv_sem)
    chips = chip_gathers_of(here, slots, shards, fulls, own_sem)
    move = Exchange(here, slots, tokens, token_rows, True, bounce, move_sem)
    gathers = gathers_of(here, slots, fulls[:first], [False] + [True] * (first - 1))
    flow = flow_of(gathers)
    greet(here.near_peers())
    for chip in chips[:first]:
        chip.start(0)
    move.start(0)
    for chip in chips[first:]:
        chip.start(0)
    for chip in chips:
        chip.own.start()
    for chip in chips[:first]:
        chip.own.wait()
        chip.finish(0)
    for call in flow:
        call()
    move.finish(0)
    for chip in chips[first:]:
        chip.own.wait()
        chip.finish(0)
    drain_all(chips + gathers + [move])


def gather_first(tokens, vectors, up_bias, weights, first, counts):
    dp_count, seq_count = counts
    row_count, pos_count, width = tokens.shape
    rows = row_count // seq_count
    shards = [jax.ShapeDtypeStruct(shape, BRAIN) for shape in [(16, 128)] + [w.shape for w in weights]]
    pieces = piece_count([shard.shape for shard in shards[:first]], [False] + [True] * (first - 1))
    slots = len(shards) * (dp_count // 2 - 1) + pieces * seq_count + seq_count - 1
    return pl.pallas_call(
        functools.partial(gather_kernel, counts, first, len(shards)),
        out_shape=[jax.ShapeDtypeStruct((rows, seq_count, pos_count, width), tokens.dtype)]
        + [full_shape(shard, *counts) for shard in shards],
        in_specs=[ANYWHERE] + [WHOLE] * (2 + len(weights)),
        out_specs=[ANYWHERE] * (1 + len(shards)),
        scratch_shapes=[pltpu.VMEM(shard.shape, BRAIN) for shard in shards]
        + [
            pltpu.VMEM((16, 128), FLOAT),
            pltpu.VMEM((rows, pos_count, width), tokens.dtype),
            pltpu.SemaphoreType.DMA((slots,)),
            pltpu.SemaphoreType.DMA((slots,)),
            pltpu.SemaphoreType.DMA((len(shards),)),
            pltpu.SemaphoreType.DMA((2,)),
        ],
        name="gather_first",
        compiler_params=pltpu.CompilerParams(
            collective_id=0, has_side_effects=True, vmem_limit_bytes=63 * 1024 * 1024
        ),
    )(tokens, vectors, up_bias, *weights)


HIDDEN_BLOCK = 512
GELU_SCALE = 0.7978845608028654
GELU_CUBE = 0.044715


def gelu_both(values):
    square = values * values
    turned = jnp.tanh(GELU_SCALE * values * (1.0 + GELU_CUBE * square))
    half = 0.5 + 0.5 * turned
    inner = GELU_SCALE * (1.0 + 3.0 * GELU_CUBE * square)
    return values * half, half + 0.5 * values * (1.0 - turned * turned) * inner


def forward_start(context, tokens, w_out, vectors, resid, low_two, low_turned):
    for rows in row_blocks(resid.shape[0]):
        values = tokens[rows, :].astype(FLOAT) + (matmul(context[rows, :], w_out[...]) + vectors[6:7, :])
        resid[rows, :] = values
        normed, _ = norm_parts(values)
        low = (normed * vectors[2:3, :] + vectors[3:4, :]).astype(BRAIN)
        low_two[rows, :] = low
        low_turned[:, rows] = low.T


def backward_end(
    context, w_out, vectors, resid, total, back, gc_ref, gr_ref, gwo_ref, sum_ref, low_turned
):
    width = resid.shape[1]
    sums = [jnp.zeros((1, width), FLOAT) for _ in range(4)]
    for rows in row_blocks(resid.shape[0]):
        normed, inverse = norm_parts(resid[rows, :])
        upstream = total[rows, :]
        given = back(rows).astype(FLOAT)
        scaled = upstream * vectors[2:3, :]
        centered = scaled - jnp.mean(scaled, axis=-1, keepdims=True)
        inward = centered - normed * jnp.mean(scaled * normed, axis=-1, keepdims=True)
        grad = given + inverse * inward
        low = grad.astype(BRAIN)
        gr_ref[rows, :] = grad
        gc_ref[rows, :] = times_transposed(low, w_out[...]).astype(BRAIN)
        low_turned[:, rows] = context[rows, :].T
        total[rows, :] = low.astype(FLOAT)
        for index, values in enumerate((upstream * normed, upstream, low.astype(FLOAT), given)):
            sums[index] = sums[index] + jnp.sum(values, axis=0, keepdims=True)
    for index in range(4):
        sum_ref[index : index + 1, :] = sums[index]
    sum_ref[4:8, :] = jnp.zeros((4, width), FLOAT)
    gwo_ref[...] = matmul(low_turned[...], total[...].astype(BRAIN)).astype(BRAIN)


def mlp_kernel(counts, *refs):
    context, tokens, w_out, w_up, w_down, vectors, up_shift, cotangent = refs[0:8]
    gup_ref, gdown_ref, gub_ref, gwo_ref, gc_ref, gr_ref, sum_ref, mixed = refs[8:16]
    acts, slopes, low_two, low_turned, resid, total, hidden, back, mixed_rows = refs[16:25]
    send_sem, recv_sem, move_sem = refs[25:28]
    here = Here(*counts)
    slots = Slots(send_sem, recv_sem)
    arrive = Exchange(here, slots, cotangent, back, True, None, move_sem.at[pl.ds(0, 2)])
    leave = Exchange(here, slots, mixed_rows, mixed, False, None, move_sem.at[pl.ds(2, 2)])
    step = pl.program_id(0)
    half = pl.num_programs(0) // 2
    count = resid.shape[0]
    pos_count = back.shape[2]

    def back_rows(rows):
        parts = []
        for first in range(rows.start, rows.stop, pos_count):
            size = min(pos_count, rows.stop - first)
            row, rest = divmod(first, pos_count * counts[1])
            line, offset = divmod(rest, pos_count)
            parts.append(back[row, line, offset : offset + size, :])
        return parts[0] if len(parts) == 1 else jnp.concatenate(parts, axis=0)

    @pl.when(step == 0)
    def _():
        greet(here.near_peers())
        arrive.start(0)
        forward_start(context, tokens, w_out, vectors, resid, low_two, low_turned)
        total[...] = jnp.zeros_like(total)

    @pl.when(step < half)
    def _():
        for rows in row_blocks(count):
            values = matmul(low_two[rows, :], w_up[...]) + up_shift[...]
            act, slope = gelu_both(values)
            low = act.astype(BRAIN)
            acts[step, rows, :] = low
            slopes[step, rows, :] = slope
            total[rows, :] += matmul(low, w_down[...])

    @pl.when(step == half)
    def _():
        for first in range(0, count, pos_count):
            row, line = divmod(first // pos_count, counts[1])
            rows = slice(first, first + pos_count)
            values = resid[rows, :] + (total[rows, :] + vectors[7:8, :])
            mixed_rows[row, line] = values.astype(BRAIN)
        total[...] = jnp.zeros_like(total)
        leave.start(0)
        arrive.finish(0)

    @pl.when(step >= half)
    def _():
        at = step - half
        sums = jnp.zeros((1, hidden.shape[1]), FLOAT)
        for rows in row_blocks(count):
            grad = times_transposed(back_rows(rows), w_down[...]) * slopes[at, rows, :]
            low = grad.astype(BRAIN)
            hidden[rows, :] = low
            sums = sums + jnp.sum(low.astype(FLOAT), axis=0, keepdims=True)
            total[rows, :] += times_transposed(low, w_up[...])
        gub_ref[...] = sums
        gup_ref[...] = matmul(low_turned[...], hidden[...]).astype(BRAIN)
        every = back_rows(slice(0, count))
        gdown_ref[...] = inner_rows(acts[at], every).astype(BRAIN)

    @pl.when(step == 2 * half - 1)
    def _():
        backward_end(
            context, w_out, vectors, resid, total, back_rows, gc_ref, gr_ref, gwo_ref, sum_ref, low_turned
        )
        leave.finish(0)
        drain_all([arrive, leave])


def feed_forward(context, tokens, w_out, w_up, w_down, vectors, up_shift, cotangent, counts):
    count, width = context.shape
    hidden = w_up.shape[1]
    half = hidden // HIDDEN_BLOCK
    seq_count = counts[1]
    row_count, pos_count, _ = cotangent.shape
    rows = row_count // seq_count
    later = lambda j: jnp.maximum(j - half, 0)
    around = lambda j: lax.rem(j, half)
    block = HIDDEN_BLOCK
    slots = 2 * (seq_count - 1)
    return pl.pallas_call(
        functools.partial(mlp_kernel, counts),
        grid=(2 * half,),
        in_specs=[
            once((count, width)),
            once((count, width)),
            once((width, width)),
            pl.BlockSpec((width, block), lambda j: (0, around(j))),
            pl.BlockSpec((block, width), lambda j: (around(j), 0)),
            once((8, width)),
            pl.BlockSpec((1, block), lambda j: (0, around(j))),
            ANYWHERE,
        ],
        out_specs=[
            pl.BlockSpec((width, block), lambda j: (0, later(j))),
            pl.BlockSpec((block, width), lambda j: (later(j), 0)),
            pl.BlockSpec((1, block), lambda j: (0, later(j))),
            once((width, width)),
            once((count, width)),
            once((count, width)),
            once((8, width)),
            ANYWHERE,
        ],
        out_shape=[
            jax.ShapeDtypeStruct((width, hidden), BRAIN),
            jax.ShapeDtypeStruct((hidden, width), BRAIN),
            jax.ShapeDtypeStruct((1, hidden), FLOAT),
            jax.ShapeDtypeStruct((width, width), BRAIN),
            jax.ShapeDtypeStruct((count, width), BRAIN),
            jax.ShapeDtypeStruct((count, width), FLOAT),
            jax.ShapeDtypeStruct((8, width), FLOAT),
            jax.ShapeDtypeStruct((seq_count, rows, pos_count, width), BRAIN),
        ],
        scratch_shapes=[
            pltpu.VMEM((half, count, block), BRAIN),
            pltpu.VMEM((half, count, block), FLOAT),
            pltpu.VMEM((count, width), BRAIN),
            pltpu.VMEM((width, count), BRAIN),
            pltpu.VMEM((count, width), FLOAT),
            pltpu.VMEM((count, width), FLOAT),
            pltpu.VMEM((count, block), BRAIN),
            pltpu.VMEM((rows, seq_count, pos_count, width), BRAIN),
            pltpu.VMEM((rows, seq_count, pos_count, width), BRAIN),
            pltpu.SemaphoreType.DMA((slots,)),
            pltpu.SemaphoreType.DMA((slots,)),
            pltpu.SemaphoreType.DMA((4,)),
        ],
        name="feed_forward",
        compiler_params=pltpu.CompilerParams(
            collective_id=4, has_side_effects=True, vmem_limit_bytes=63 * 1024 * 1024
        ),
    )(context, tokens, w_out, w_up, w_down, vectors, up_shift, cotangent)


def lamb_pieces(weight, first, second, grad, decay):
    first_new = BETA_ONE * first + (1.0 - BETA_ONE) * grad
    second_new = BETA_TWO * second + (1.0 - BETA_TWO) * grad * grad
    spread_out = jnp.sqrt(second_new / CORR_TWO) + ADAM_EPS
    update = first_new / CORR_ONE / spread_out + decay * weight
    return (first_new, second_new, update)


def square_sum(values):
    return jnp.sum(jnp.sum(values * values, axis=1, keepdims=True), axis=0, keepdims=True)


def picked(small, rank, vector_size, bias_size):
    width = small.shape[1]
    row = lax.broadcasted_iota(jnp.int32, (width, 128), 0)
    lane = lax.broadcasted_iota(jnp.int32, (width, 128), 1)
    dot = functools.partial(jnp.dot, precision=lax.Precision.HIGHEST, preferred_element_type=FLOAT)
    chosen = (row == lane + rank * vector_size) & (lane < vector_size)
    vector_grad = dot(small[0:8, :], jnp.where(chosen, 1.0, 0.0))[:, :vector_size]
    start = rank * bias_size
    chosen = (row == lane + lax.rem(start, width)) & (lane < bias_size)
    tail = dot(small[8:16, :], jnp.where(chosen, 1.0, 0.0))
    tail_row = lax.broadcasted_iota(jnp.int32, tail.shape, 0)
    tail = jnp.sum(jnp.where(tail_row == lax.div(start, width), tail, 0.0), axis=0, keepdims=True)
    return vector_grad, tail[:, :bias_size]


def scatters_of(here, slots, grads, buffers, partials, own_sem, splits):
    count = len(grads)
    found, loads = [], []
    for index, (grad, partial) in enumerate(zip(grads, partials)):
        own, *arrivals = buffers[index::count]
        load = lambda grad=grad, own=own, index=index: pltpu.make_async_copy(
            grad.at[:, here.core], own, own_sem.at[index]
        )
        loads.append(load)
        for order, pieces in enumerate(parts_of(grad.shape[-2:], splits[index])):
            wait = (lambda load=load: load().wait()) if order == 0 else (lambda: None)
            found.append(Scatter(here, slots, grad, own, *arrivals, partial, pieces, wait))
    return found, loads


def scatter_buffers(shapes, counts):
    half_count, seq_count = counts[0] // 2, counts[1]
    leads = [(half_count, seq_count)] * 2 + [(seq_count - 1, half_count)]
    return [pltpu.VMEM(lead + shape, BRAIN) for lead in leads for shape in shapes]


def scatter_views(grads, shapes, counts):
    lead = (counts[0] // 2, 2, counts[1])
    return [grad.reshape(lead + shape) for grad, shape in zip(grads, shapes)]


class SmallSum(Transfer):
    def __init__(self, here, small, sums, arrived, send_sem, recv_sem):
        self.slots = Slots(send_sem, recv_sem)
        self.small, self.sums, self.arrived = small, sums, arrived
        self.peers = [here.core_peer()]
        self.peers += [here.line_peer(bit) for bit in range(here.seq_bits)]
        self.peers += [{"dp": flipped(here.place, bit + 1)} for bit in range(bits_of(here.half_count))]
        self.stages = len(self.peers)

    def copies(self, stage):
        source = self.sums.at[stage - 1] if stage else self.small
        return [self.slots.copy(stage, source, self.arrived.at[stage], self.peers[stage])]

    def use(self, stage):
        before = self.sums[stage - 1] if stage else self.small[...]
        self.sums[stage] = before + self.arrived[stage]


def scatter_kernel(counts, *refs):
    parts, refs = refs[3:7], (*refs[:3], refs[-1], *refs[7:-1])
    grads, small, input_rows, partials, ready = refs[0:3], refs[3], refs[4], refs[5:7], refs[7]
    norm_sums, shift_sums, sums, hidden_sums = parts
    small[0:2, :] = norm_sums[0:2, :]
    small[2:4, :] = sums[0:2, :]
    small[4:6, :] = shift_sums[0:2, :]
    small[6:8, :] = sums[2:4, :]
    small[8:16, :] = jnp.zeros((8, small.shape[1]), FLOAT)
    for row in range(hidden_sums.shape[1] // small.shape[1]):
        columns = slice(row * small.shape[1], (row + 1) * small.shape[1])
        small[8 + row : 9 + row, :] = hidden_sums[0:1, columns]
    weights, firsts, seconds = refs[8:14], refs[14:20], refs[20:26]
    shares, norm_out, input_grad = refs[26:32], refs[32], refs[33]
    buffers, mine, arrived, bounce = refs[34:43], refs[43:46], refs[46:51], refs[51]
    small_sum, small_in, norm_mine, norm_dp, norm_line, norm_seq = refs[52:58]
    send_sem, recv_sem, own_sem, move_sem, small_send, small_recv, norm_send, norm_recv = refs[58:66]
    here = Here(*counts)
    slots = Slots(send_sem, recv_sem)
    scatters, loads = scatters_of(here, slots, grads, buffers, mine, own_sem, [False] * 3)
    early = [
        ChipSum(here, slots, partial, arrived[index], shares[index + 1], 0)
        for index, partial in enumerate(partials)
    ]
    late = [
        ChipSum(here, slots, mine[at], arrived[2 + at], shares[0], at * grads[at].shape[-1])
        for at in range(3)
    ]
    move = Exchange(here, slots, input_rows, input_grad, False, bounce, move_sem)
    total = SmallSum(here, small, small_sum, small_in, small_send, small_recv)
    for load in loads:
        load().start()
    dp_peers, seq_peers = here.all_peers()[: here.dp_count - 1], here.all_peers()[here.dp_count - 1 :]
    greet(dp_peers + seq_peers)
    lane = lax.broadcasted_iota(jnp.int32, (8, 128), 1)
    row = lax.broadcasted_iota(jnp.int32, (8, 128), 0)

    def with_norms(tile, index, grad):
        decay = DECAY_RATE if index < 4 else 0.0
        weight = weights[index][...]
        update = lamb_pieces(weight, firsts[index][...], seconds[index][...], grad, decay)[2]
        at = row == min(index, 4)
        tile = jnp.where(at & (lane == 0), square_sum(weight), tile)
        return jnp.where(at & (lane == 1), square_sum(update), tile)

    total.start(0)
    begin_all(scatters + early)
    tile = jnp.zeros((8, 128), FLOAT)
    follow(total, 1)
    shares[3][...] = ready[...]
    tile = with_norms(tile, 3, ready[...])
    for stage in range(2, here.seq_bits + 1):
        follow(total, stage)
    stages = scatters[0].stages
    done = here.seq_bits
    for stage in range(1, stages + 1):
        if stage == stages:
            move.start(0)
        for index, scatter in enumerate(scatters):
            follow(scatter, stage)
            if stage == stages:
                late[index].start(0)
        if done < total.stages and stage < stages:
            done += 1
            follow(total, done)
    for stage in range(done + 1, total.stages + 1):
        follow(total, stage)
    for index, chip in enumerate(early):
        chip.finish(0)
        tile = with_norms(tile, index + 1, shares[index + 1][...])

    rank = here.place * here.seq_count + here.line
    vector_grad, bias_grad = picked(
        small_sum[total.stages - 1], rank, shares[4].shape[1], shares[5].shape[1]
    )
    shares[4][...] = vector_grad
    shares[5][...] = bias_grad
    tile = with_norms(tile, 5, bias_grad)
    for chip in late:
        chip.finish(0)
    norm_mine[0:8, :] = with_norms(tile, 0, shares[0][...])
    weight = weights[4][...]
    update = lamb_pieces(weight, firsts[4][...], seconds[4][...], vector_grad, 0.0)[2]
    weight_sq = jnp.sum(weight * weight, axis=1, keepdims=True)
    update_sq = jnp.sum(update * update, axis=1, keepdims=True)
    norm_mine[8:16, :] = jnp.where(lane == 0, weight_sq, jnp.where(lane == 1, update_sq, 0.0))

    norm_slots = Slots(norm_send, norm_recv)

    def exchange(source, held, peers, at):
        base = norm_slots.take(len(peers))
        copies = [
            norm_slots.copy(base + turn, source, held.at[at], peer) for turn, peer in enumerate(peers)
        ]
        for copy in copies:
            copy.start()
        held[at] = source[...]
        for copy in copies:
            copy.wait_recv()
        found = held[0]
        for turn in range(1, held.shape[0]):
            found = found + held[turn]
        return copies, found

    sent, found = exchange(norm_mine, norm_dp, dp_peers, here.place)
    norm_line[...] = found
    also, found = exchange(norm_line, norm_seq, seq_peers, here.line)
    norm_out[...] = found
    move.finish(0)
    for copy in sent + also:
        copy.wait_send()
    drain_all(scatters + early + late + [total, move])


def scatter_last(grads, sums, input_rows, partials, ready, weights, firsts, seconds, counts):
    dp_count, seq_count = counts
    shapes = [weight.shape for weight in weights]
    thirds = [(shapes[0][0], grad.shape[1]) for grad in grads]
    lead, small = (dp_count // 2,), (16, sums[0].shape[1])
    pieces = piece_count(thirds, [False] * 3)
    slots = pieces * seq_count + 5 * (dp_count // 2 - 1) + seq_count - 1
    stages = bits_of(dp_count) + bits_of(seq_count)
    return pl.pallas_call(
        functools.partial(scatter_kernel, counts),
        out_shape=[jax.ShapeDtypeStruct(shape, FLOAT) for shape in shapes]
        + [
            jax.ShapeDtypeStruct((16, 128), FLOAT),
            jax.ShapeDtypeStruct((seq_count,) + input_rows.shape[0:1] + input_rows.shape[2:], BRAIN),
        ],
        in_specs=[ANYWHERE] * 3 + [WHOLE] * 4 + [ANYWHERE] + [WHOLE] * 21,
        out_specs=[WHOLE] * 7 + [ANYWHERE],
        scratch_shapes=scatter_buffers(thirds, counts)
        + [pltpu.VMEM(lead + shape, BRAIN) for shape in thirds]
        + [pltpu.VMEM((lead[0] - 1,) + shape, BRAIN) for shape in shapes[1:3] + thirds]
        + [
            pltpu.VMEM(input_rows.shape[0:1] + input_rows.shape[2:], BRAIN),
            pltpu.VMEM((stages,) + small, FLOAT),
            pltpu.VMEM((stages,) + small, FLOAT),
            pltpu.VMEM((16, 128), FLOAT),
            pltpu.VMEM((dp_count, 16, 128), FLOAT),
            pltpu.VMEM((16, 128), FLOAT),
            pltpu.VMEM((seq_count, 16, 128), FLOAT),
            pltpu.SemaphoreType.DMA((slots,)),
            pltpu.SemaphoreType.DMA((slots,)),
            pltpu.SemaphoreType.DMA((3,)),
            pltpu.SemaphoreType.DMA((2,)),
            pltpu.SemaphoreType.DMA((stages,)),
            pltpu.SemaphoreType.DMA((stages,)),
            pltpu.SemaphoreType.DMA((dp_count + seq_count,)),
            pltpu.SemaphoreType.DMA((dp_count + seq_count,)),
            pltpu.VMEM(small, FLOAT),
        ],
        name="scatter_last",
        compiler_params=pltpu.CompilerParams(
            collective_id=3, has_side_effects=True, vmem_limit_bytes=60 * 1024 * 1024
        ),
    )(
        *scatter_views(grads, thirds, counts),
        *sums,
        input_rows,
        *partials,
        ready,
        *weights,
        *firsts,
        *seconds,
    )


def lamb_kernel(*refs):
    grads, norms = refs[0:6], refs[6]
    weights, firsts, seconds = refs[7:13], refs[13:19], refs[19:25]
    input_rows, refs = refs[25], refs[26:]
    grad_out, first_out, second_out, new_out = refs[0:6], refs[6:12], refs[12:18], refs[18:24]
    copy_out, input_out = refs[24:28], refs[28]
    for row in range(input_rows.shape[0]):
        input_out[row] = input_rows[row].astype(FLOAT)
    weight_norm = jnp.sqrt(norms[:, 0:1])
    scales = weight_norm / (jnp.sqrt(norms[:, 1:2]) + ADAM_EPS)
    for index in range(6):
        grad = grads[index][...]
        weight = weights[index][...]
        decay = DECAY_RATE if index < 4 else 0.0
        first_new, second_new, update = lamb_pieces(
            weight, firsts[index][...], seconds[index][...], grad, decay
        )
        scale = scales[8:16] if index == 4 else scales[min(index, 4) : min(index, 4) + 1]
        new = weight - LEARN_RATE * scale * update
        grad_out[index][...] = grad
        first_out[index][...] = first_new
        second_out[index][...] = second_new
        new_out[index][...] = new
        if index < 4:
            copy_out[index][...] = new.astype(BRAIN)


def lamb_all(grads, norms, weights, firsts, seconds, input_rows):
    vmem = pl.BlockSpec(memory_space=pltpu.VMEM)
    shapes = [jax.ShapeDtypeStruct(weight.shape, FLOAT) for weight in weights]
    copies = [jax.ShapeDtypeStruct(weight.shape, BRAIN) for weight in weights[:4]]
    return pl.pallas_call(
        lamb_kernel,
        out_shape=shapes * 4 + copies + [jax.ShapeDtypeStruct(input_rows.shape, FLOAT)],
        in_specs=[vmem] * 26,
        out_specs=[vmem] * 29,
        name="lamb_update",
        compiler_params=pltpu.CompilerParams(vmem_limit_bytes=63 * 1024 * 1024),
    )(*grads, norms, *weights, *firsts, *seconds, input_rows)


def body(
    tokens,
    cotangent,
    segment_ids,
    w_qkv,
    m_qkv,
    v_qkv,
    w_out,
    m_out,
    v_out,
    w_up,
    m_up,
    v_up,
    w_down,
    m_down,
    v_down,
    vectors,
    m_vectors,
    v_vectors,
    up_bias,
    m_up_bias,
    v_up_bias,
):
    dp_count, seq_count = lax.axis_size("dp"), lax.axis_size("seq")
    vector_size, bias_size = vectors.shape[1], up_bias.shape[0]
    counts = (dp_count, seq_count)
    token_rows, *fulls = gather_first(
        tokens, vectors, up_bias[None], [w_qkv, w_out, w_up, w_down], 2, counts
    )
    small = fulls[0].reshape(dp_count * seq_count, 16, 128)
    full_vectors = small[:, :8, :vector_size].transpose(1, 0, 2)
    vector_rows = full_vectors.reshape(8, -1).astype(FLOAT)
    up_shift = small[:, 8, :bias_size].reshape(-1).astype(FLOAT)
    as_matrix = lambda full: full.reshape(-1, full.shape[-1])
    full_qkv = as_matrix(fulls[1])

    width = tokens.shape[2]
    length = segment_ids.shape[1]
    rows = token_rows.shape[0]
    assert rows == 1
    token_rows = token_rows.reshape(length, width)
    *heads, context, lse_rows, full_out, full_up, full_down = attention_forward(
        segment_ids, token_rows, vector_rows, full_qkv, fulls[2:], counts
    )
    full_out, full_up, full_down = [as_matrix(full) for full in (full_out, full_up, full_down)]
    grad_up, grad_down, grad_up_bias, grad_out, context_grad, resid_grad, sums, mixed = feed_forward(
        context,
        token_rows,
        full_out,
        full_up,
        full_down,
        vector_rows,
        up_shift[None],
        cotangent,
        counts,
    )
    *qkv_grads, shift_sums, norm_sums, input_rows, share_down, sum_up, sum_out = attention_backward(
        segment_ids,
        heads,
        context_grad,
        lse_rows,
        token_rows,
        vector_rows,
        resid_grad,
        full_qkv,
        [grad_down, grad_up, grad_out],
        [w_down.shape, w_up.shape, w_out.shape],
        counts,
    )
    as_row = lambda value: value.reshape(1, -1)
    weights = (w_qkv, w_out, w_up, w_down, vectors, as_row(up_bias))
    firsts = (m_qkv, m_out, m_up, m_down, m_vectors, as_row(m_up_bias))
    seconds = (v_qkv, v_out, v_up, v_down, v_vectors, as_row(v_up_bias))
    *shares, norms, input_grad = scatter_last(
        qkv_grads,
        [norm_sums, shift_sums, sums, grad_up_bias],
        input_rows.reshape(rows, seq_count, length // seq_count, width),
        [sum_out, sum_up],
        share_down,
        weights,
        firsts,
        seconds,
        counts,
    )
    *results, input_grad = lamb_all(
        shares, norms, weights, firsts, seconds, input_grad.reshape(tokens.shape)
    )
    mixed = mixed.reshape(tokens.shape)
    for index in (5, 11, 17, 23):
        results[index] = results[index].reshape(-1)
    return (mixed, input_grad, *results)


def solution(mesh):
    matrix = P(("dp", "seq"), None)
    rows = P("dp", "seq", None)
    vector = P(None, ("dp", "seq"))
    bias = P(("dp", "seq"))
    six = (matrix, matrix, matrix, matrix, vector, bias)
    in_specs = (rows, rows, P("dp", None)) + tuple(spec for spec in six for _ in range(3))
    out_specs = (rows, rows) + six * 4 + (matrix,) * 4
    return jax.shard_map(body, mesh=mesh, in_specs=in_specs, out_specs=out_specs, check_vma=False)
```
